32 devices in a mesh: fsdp: 32 (over z, y, x, core).
Axes of the slice: x: 2, y: 2, z: 4, core: 2. Of those that a mesh axis runs over, the one named last changes fastest.
Arguments:
- tokens: float32 [23328, 1152], P('fsdp'), may hold values from -6 to 6
- image_valid: int32 [32], P('fsdp'), may hold values 0 or 1
- attn_gain: float32 [1152], P('fsdp'), may hold values from 0.1 to 1.9
- attn_shift: float32 [1152], P('fsdp'), may hold values from -1.8 to 1.8
- query_weight: float32 [1327104], P('fsdp'), may hold values from -0.25 to 0.25
- query_bias: float32 [1152], P('fsdp'), may hold values from -3 to 3
- key_weight: float32 [1327104], P('fsdp'), may hold values from -0.25 to 0.25
- value_weight: float32 [1327104], P('fsdp'), may hold values from -0.1875 to 0.1875
- value_bias: float32 [1152], P('fsdp'), may hold values from -0.6 to 0.6
- output_weight: float32 [1327104], P('fsdp'), may hold values from -1 to 1
- output_bias: float32 [1152], P('fsdp'), may hold values from -1.8 to 1.8
- mlp_gain: float32 [1152], P('fsdp'), may hold values from 0.1 to 1.9
- mlp_shift: float32 [1152], P('fsdp'), may hold values from -1.8 to 1.8
- expand_weight: float32 [4958208], P('fsdp'), may hold values from -0.1875 to 0.1875
- expand_bias: float32 [4320], P('fsdp'), may hold values from -3 to 3
- reduce_weight: float32 [4958208], P('fsdp'), may hold values from -0.09375 to 0.09375
- reduce_bias: float32 [1152], P('fsdp'), may hold values from -1.8 to 1.8
- cotangent: float32 [23328, 1152], P('fsdp'), may hold values from -6 to 6
Outputs:
- layer_out: float32 [23328, 1152], P('fsdp')
- tokens_grad: float32 [23328, 1152], P('fsdp')
- attn_gain_grad: float32 [1152], P('fsdp')
- attn_shift_grad: float32 [1152], P('fsdp')
- query_weight_grad: float32 [1327104], P('fsdp')
- query_bias_grad: float32 [1152], P('fsdp')
- key_weight_grad: float32 [1327104], P('fsdp')
- value_weight_grad: float32 [1327104], P('fsdp')
- value_bias_grad: float32 [1152], P('fsdp')
- output_weight_grad: float32 [1327104], P('fsdp')
- output_bias_grad: float32 [1152], P('fsdp')
- mlp_gain_grad: float32 [1152], P('fsdp')
- mlp_shift_grad: float32 [1152], P('fsdp')
- expand_weight_grad: float32 [4958208], P('fsdp')
- expand_bias_grad: float32 [4320], P('fsdp')
- reduce_weight_grad: float32 [4958208], P('fsdp')
- reduce_bias_grad: float32 [1152], P('fsdp')
The draws below stay inside these ranges and needn't reach their ends.
All inputs are finite; a program needn't handle non-finite values. No bound on the sum of `image_valid` on one device may be relied on, other than what follows from the above.
Results may differ from the reference program's by a relative error of at most 0.013.
The reference program's roundings to bfloat16 on the way count: a program that leaves them out, or rounds other values in their place, can miss the bound.
Values may be sent and summed in bfloat16 or wider, within the bound.
No kernel may reach another device: no remote copies, remote signals or barrier semaphores. Data moves between devices by JAX's collectives and lax.ppermute only.
A program may use at most 384 MiB of HBM per device.

```python
import jax
import jax.numpy as jnp
from jax import lax

D = 1152
HEADS = 16
HEAD_DIM = 72
FF = 4304
SEQ = 729
IMAGES = 32
TOKENS = 23328
LEN_VEC = 1152
LEN_HID = 4320
LEN_SQ = 1327104
LEN_MLP = 4958208


def place_ends(drawn, own_key, least, top_value):
    index_at = [jax.random.randint(jax.random.fold_in(own_key, axis), (), 0, length) for axis, length in enumerate(drawn.shape)]
    main_axis = drawn.shape.index(max(drawn.shape))
    neighbour = index_at[:main_axis] + [(index_at[main_axis] + 1) % drawn.shape[main_axis]] + index_at[main_axis + 1:]
    return drawn.at[tuple(index_at)].set(least).at[tuple(neighbour)].set(top_value)


def steps_of(rng, shape, shards, low, high):
    level, own = 1.0, jax.random.fold_in(rng, 6)
    for axis_at, blocks in shards:
        draws = jnp.exp(jax.random.uniform(jax.random.fold_in(own, axis_at), (blocks,), jnp.float32, low / len(shards), high / len(shards)))
        level = level * jnp.repeat(draws, shape[axis_at] // blocks).reshape([-1 if axis == axis_at else 1 for axis in range(len(shape))])
    return level


def centred(rng, dims, width, bound, split=(), held_as=jnp.bfloat16):
    level = steps_of(rng, dims, split, -0.22, 0.18) if split else 1.0
    drawn = jax.random.normal(rng, dims, jnp.float32) * width * level
    return jnp.minimum(jnp.maximum(drawn, -bound), bound).astype(held_as)


def setup_inputs(seed: int = 0) -> dict:
    arg_keys = jax.random.split(jax.random.key(seed), 19)
    tokens = centred(arg_keys[0], (TOKENS, D), 1.0, 6.0, ((0, 32),), jnp.float32)
    image_valid = place_ends((jax.random.randint(arg_keys[1], (IMAGES,), 0, 4) < 3).astype(jnp.int32), jax.random.fold_in(arg_keys[1], 1), 0, 1)
    attn_gain = jnp.clip(1.0 + 0.18 * jax.random.normal(arg_keys[2], (LEN_VEC,), jnp.float32), 0.1, 1.9)
    attn_shift = centred(arg_keys[3], (LEN_VEC,), 0.3, 1.8, ((0, 32),), jnp.float32)
    query_weight = centred(arg_keys[4], (LEN_SQ,), (D // 2) ** -0.5, 0.25, ((0, 32),), jnp.float32)
    query_bias = centred(arg_keys[5], (LEN_VEC,), 0.5, 3.0, ((0, 32),), jnp.float32)
    key_weight = centred(arg_keys[6], (LEN_SQ,), (D // 2) ** -0.5, 0.25, ((0, 32),), jnp.float32)
    value_weight = centred(arg_keys[7], (LEN_SQ,), D ** -0.5, 0.1875, ((0, 32),), jnp.float32)
    value_bias = centred(arg_keys[8], (LEN_VEC,), 0.1, 0.6, ((0, 32),), jnp.float32)
    output_weight = centred(arg_keys[9], (LEN_SQ,), (D // 32) ** -0.5, 1.0, ((0, 32),), jnp.float32)
    output_bias = centred(arg_keys[10], (LEN_VEC,), 0.3, 1.8, ((0, 32),), jnp.float32)
    mlp_gain = jnp.clip(1.0 + 0.18 * jax.random.normal(arg_keys[11], (LEN_VEC,), jnp.float32), 0.1, 1.9)
    mlp_shift = centred(arg_keys[12], (LEN_VEC,), 0.3, 1.8, ((0, 32),), jnp.float32)
    expand_weight = centred(arg_keys[13], (LEN_MLP,), D ** -0.5, 0.1875, ((0, 32),), jnp.float32)
    expand_bias = centred(arg_keys[14], (LEN_HID,), 0.5, 3.0, ((0, 32),), jnp.float32)
    reduce_weight = centred(arg_keys[15], (LEN_MLP,), FF ** -0.5, 0.09375, ((0, 32),), jnp.float32)
    reduce_bias = centred(arg_keys[16], (LEN_VEC,), 0.3, 1.8, ((0, 32),), jnp.float32)
    cotangent = centred(arg_keys[17], (TOKENS, D), 1.0, 6.0, ((0, 32),), jnp.float32)
    return {"tokens": tokens, "image_valid": image_valid, "attn_gain": attn_gain, "attn_shift": attn_shift, "query_weight": query_weight, "query_bias": query_bias, "key_weight": key_weight, "value_weight": value_weight, "value_bias": value_bias, "output_weight": output_weight, "output_bias": output_bias, "mlp_gain": mlp_gain, "mlp_shift": mlp_shift, "expand_weight": expand_weight, "expand_bias": expand_bias, "reduce_weight": reduce_weight, "reduce_bias": reduce_bias, "cotangent": cotangent}


@jax.custom_vjp
def low(v):
    return lax.optimization_barrier(v.astype(jnp.bfloat16)).astype(jnp.float32)

@jax.custom_vjp
def low_back(v):
    return v

def low_keep(v):
    return (low(v), None)

def low_pass(kept, grad):
    return (grad,)

def back_keep(v):
    return (v, None)

def back_low(kept, grad):
    return (low(grad),)
low.defvjp(low_keep, low_pass)
low_back.defvjp(back_keep, back_low)

def layer_norm(values, gain, shift):
    centre = lax.optimization_barrier(jnp.mean(values, axis=-1, keepdims=True))
    centered = values - centre
    spread = lax.optimization_barrier(jnp.mean(centered * centered, axis=-1, keepdims=True))
    return centered * lax.rsqrt(spread + 1e-06) * gain + shift

def product(left, right):
    return jnp.dot(left, right, precision=lax.Precision.HIGHEST, preferred_element_type=jnp.float32)

def both_ways(values):
    return low(low_back(values))

def layout_dims():
    return ((D,), (D,), (D, D), (D,), (D, D), (D, D), (D,), (D, D), (D,), (D,), (D,), (D, FF), (FF,), (FF, D), (D,))

def unpack_flat(flat, shape_dims):
    length = 1
    for extent in shape_dims:
        length = length * extent
    return flat[:length].reshape(shape_dims)

def image_forward(image, image_weight, raw_params):
    params = [low(unpack_flat(flat, shape_dims)) for flat, shape_dims in zip(raw_params, layout_dims())]
    gain_one, shift_one, query_w, query_b, key_w, value_w, value_b, output_w, output_b, gain_two, shift_two, expand_w, expand_b, reduce_w, reduce_b = params
    normed = low(layer_norm(image, gain_one, shift_one))
    query = both_ways(product(normed, query_w) + query_b).reshape(SEQ, HEADS, HEAD_DIM)
    keys = both_ways(product(normed, key_w)).reshape(SEQ, HEADS, HEAD_DIM)
    values = both_ways(product(normed, value_w) + value_b).reshape(SEQ, HEADS, HEAD_DIM)
    scores = low_back(jnp.einsum('qhd,khd->hqk', query, keys, precision=lax.Precision.HIGHEST) * HEAD_DIM ** (-0.5))
    highest = lax.optimization_barrier(jnp.max(scores, axis=-1, keepdims=True))
    expd = jnp.exp(scores - highest)
    probs = low(expd / lax.optimization_barrier(jnp.sum(expd, axis=-1, keepdims=True)))
    mixed = both_ways(jnp.einsum('hqk,khd->qhd', probs, values, precision=lax.Precision.HIGHEST).reshape(SEQ, D))
    resid = image + low_back(product(mixed, output_w) + output_b)
    normed_two = low(layer_norm(resid, gain_two, shift_two))
    hidden = low(jax.nn.gelu(low_back(product(normed_two, expand_w) + expand_b), approximate=True))
    return image_weight * (resid + low_back(product(hidden, reduce_w) + reduce_b))

def reference(tokens, image_valid, attn_gain, attn_shift, query_weight, query_bias, key_weight, value_weight, value_bias, output_weight, output_bias, mlp_gain, mlp_shift, expand_weight, expand_bias, reduce_weight, reduce_bias, cotangent):
    raw_params = (attn_gain, attn_shift, query_weight, query_bias, key_weight, value_weight, value_bias, output_weight, output_bias, mlp_gain, mlp_shift, expand_weight, expand_bias, reduce_weight, reduce_bias)
    images = tokens.reshape(IMAGES, SEQ, D)
    cotangents = cotangent.reshape(IMAGES, SEQ, D)
    weights = image_valid.astype(jnp.float32)

    def one_image(totals, inputs):
        image, image_weight, image_cot = inputs
        result, pullback = jax.vjp(lambda image_in, params_in: image_forward(image_in, image_weight, params_in), image, raw_params)
        image_grad, param_grads = pullback(image_cot)
        summed = tuple((total + grad_part for total, grad_part in zip(totals, param_grads)))
        return (summed, (result, image_grad))
    starting = tuple((jnp.zeros(piece.shape, jnp.float32) for piece in raw_params))
    totals, (results, image_grads) = lax.scan(one_image, starting, (images, weights, cotangents))
    return (results.reshape(TOKENS, D), image_grads.reshape(TOKENS, D), totals[0], totals[1], totals[2], totals[3], totals[4], totals[5], totals[6], totals[7], totals[8], totals[9], totals[10], totals[11], totals[12], totals[13], totals[14])
```

```python
import functools
import itertools
import jax
import jax.numpy as jnp
from jax import lax
from jax.sharding import PartitionSpec as P
from jax.experimental import pallas as pl
from jax.experimental.pallas import tpu as pltpu
D=1152; HEADS=16; HEAD_DIM=72; LANES=128
NEG=-1e30
LOG2E=1.4426950408889634
def nt(a,b): return lax.dot_general(a,b,(((1,),(1,)),((),())),preferred_element_type=jnp.float32)
def nn(a,b): return lax.dot_general(a,b,(((1,),(0,)),((),())),preferred_element_type=jnp.float32)

def fill_heads(dst, src, col, tokens, fill):
    rows=dst.shape[1]
    for h in range(HEADS):
        if fill is not None:
            dst[h]=fill
        dst[h,0:tokens,0:HEAD_DIM]=src[:,col+h*HEAD_DIM:col+(h+1)*HEAD_DIM]

def pad_values(rows, tokens, kind):
    lane=lax.broadcasted_iota(jnp.int32,(rows,LANES),1)
    row=lax.broadcasted_iota(jnp.int32,(rows,LANES),0)
    if kind=="query":
        v=jnp.where(lane==HEAD_DIM,1.0,0.0)
    elif kind=="key":
        v=jnp.where((lane==HEAD_DIM)&(row>=tokens),NEG,0.0)
    else:
        v=jnp.zeros((rows,LANES),jnp.float32)
    return v.astype(jnp.bfloat16)

def fwd_kernel(tokens, krows, qrows, per, qkv_ref, mixed_ref, lse_ref, qs, ks, vs, os):
    step=pl.program_id(0)
    @pl.when(step==0)
    def _():
        fill_heads(qs,qkv_ref,0,tokens,pad_values(qrows,tokens,"query"))
        fill_heads(ks,qkv_ref,D,tokens,pad_values(krows,tokens,"key"))
        zero=pad_values(krows,tokens,"value")
        for h in range(HEADS):
            vs[h]=zero
            vs[h,0:tokens,0:HEAD_DIM]=qkv_ref[:,2*D+h*HEAD_DIM:2*D+(h+1)*HEAD_DIM]
    c=HEAD_DIM**-0.5*LOG2E
    for j in range(per):
        h=step*per+j
        s=nt(ks[h],qs[h])
        m=jnp.max(s,axis=0,keepdims=True)
        e=jnp.exp2((s-m)*c)
        l=jnp.sum(e,axis=0,keepdims=True)
        p=(e*(1.0/l)).astype(jnp.bfloat16)
        vt=vs[h].T
        ot=nn(vt,p)
        os[h]=ot.T.astype(jnp.bfloat16)
        lse_ref[j]=m*c+jnp.log2(l)
    @pl.when(step==pl.num_programs(0)-1)
    def _():
        for h in range(HEADS):
            mixed_ref[:,h*HEAD_DIM:(h+1)*HEAD_DIM]=os[h,0:tokens,0:HEAD_DIM]

def attn_fwd(qkv, per=1):
    tokens=qkv.shape[0]
    krows=-(-tokens//16)*16; qrows=-(-tokens//128)*128
    return pl.pallas_call(functools.partial(fwd_kernel,tokens,krows,qrows,per),
        grid=(HEADS//per,),
        in_specs=[pl.BlockSpec(qkv.shape,lambda i:(0,0),pipeline_mode=pl.Buffered(1))],
        out_specs=[pl.BlockSpec((tokens,D),lambda i:(0,0),pipeline_mode=pl.Buffered(1)),pl.BlockSpec((per,1,qrows),lambda i:(i,0,0))],
        out_shape=[jax.ShapeDtypeStruct((tokens,D),jnp.bfloat16),jax.ShapeDtypeStruct((HEADS,1,qrows),jnp.float32)],
        scratch_shapes=[pltpu.VMEM((HEADS,qrows,LANES),jnp.bfloat16),pltpu.VMEM((HEADS,krows,LANES),jnp.bfloat16),
                        pltpu.VMEM((HEADS,krows,LANES),jnp.bfloat16),pltpu.VMEM((HEADS,qrows,LANES),jnp.bfloat16)],
        compiler_params=pltpu.CompilerParams(vmem_limit_bytes=56<<20,dimension_semantics=("arbitrary",)),
        cost_estimate=pl.CostEstimate(flops=4*HEADS*qrows*krows*LANES,bytes_accessed=4*tokens*D*2,transcendentals=HEADS*qrows*krows),
        name="attention_forward")(qkv)

def bwd_kernel(tokens, krows, qrows, per, qkv_ref, go_ref, lse_ref, dqkv_ref, qs, ks, vs, gs):
    step=pl.program_id(0)
    @pl.when(step==0)
    def _():
        fill_heads(qs,qkv_ref,0,tokens,pad_values(qrows,tokens,"query"))
        fill_heads(ks,qkv_ref,D,tokens,pad_values(krows,tokens,"key"))
        fill_heads(vs,qkv_ref,2*D,tokens,pad_values(krows,tokens,"value"))
        fill_heads(gs,go_ref,0,tokens,pad_values(qrows,tokens,"value"))
    scale=HEAD_DIM**-0.5
    c=scale*LOG2E
    for j in range(per):
        h=step*per+j
        q=qs[h]; k=ks[h]; v=vs[h]; g=gs[h]
        s=nt(k,q)
        p=jnp.exp2(s*c-lse_ref[j])
        dp=nt(v,g)
        dv=nn(p.astype(jnp.bfloat16),g)
        delta=jnp.sum(p*dp,axis=0,keepdims=True)
        ds=(p*(dp-delta)).astype(jnp.bfloat16)
        dk=nn(ds,q)*scale
        dqt=nn(k.T,ds)*scale
        qs[h]=dqt.T.astype(jnp.bfloat16)
        ks[h]=dk.astype(jnp.bfloat16)
        vs[h]=dv.astype(jnp.bfloat16)
    @pl.when(step==pl.num_programs(0)-1)
    def _():
        for i,r in enumerate((qs,ks,vs)):
            for h in range(HEADS):
                dqkv_ref[:,i*D+h*HEAD_DIM:i*D+(h+1)*HEAD_DIM]=r[h,0:tokens,0:HEAD_DIM]

def attn_bwd(qkv, gmixed, lse, per=1):
    tokens=qkv.shape[0]
    krows=-(-tokens//16)*16; qrows=-(-tokens//128)*128
    return pl.pallas_call(functools.partial(bwd_kernel,tokens,krows,qrows,per),
        grid=(HEADS//per,),
        in_specs=[pl.BlockSpec(qkv.shape,lambda i:(0,0),pipeline_mode=pl.Buffered(1)),pl.BlockSpec(gmixed.shape,lambda i:(0,0),pipeline_mode=pl.Buffered(1)),
                  pl.BlockSpec((per,1,qrows),lambda i:(i,0,0))],
        out_specs=pl.BlockSpec((tokens,3*D),lambda i:(0,0),pipeline_mode=pl.Buffered(1)),
        out_shape=jax.ShapeDtypeStruct((tokens,3*D),jnp.bfloat16),
        scratch_shapes=[pltpu.VMEM((HEADS,qrows,LANES),jnp.bfloat16),pltpu.VMEM((HEADS,krows,LANES),jnp.bfloat16),
                        pltpu.VMEM((HEADS,krows,LANES),jnp.bfloat16),pltpu.VMEM((HEADS,qrows,LANES),jnp.bfloat16)],
        compiler_params=pltpu.CompilerParams(vmem_limit_bytes=56<<20,dimension_semantics=("arbitrary",)),
        cost_estimate=pl.CostEstimate(flops=10*HEADS*qrows*krows*LANES,bytes_accessed=7*tokens*D*2,transcendentals=HEADS*qrows*krows),
        name="attention_backward")(qkv,gmixed,lse)


FF = 4304
GROUPS = 16
FF_GROUP = FF // GROUPS
FF_ROWS = 272
FF_PAD = GROUPS * FF_ROWS
PAIR_ROWS = D // GROUPS
HALF_UP = FF_PAD // 2
HALF_DOWN = FF_ROWS // 2
SQUARE_HALF = 2 * D
EXTRA = 128
VECTORS = (0, 1, 3, 6, 8, 9, 10, 12, 14)
bf16 = jnp.bfloat16
f32 = jnp.float32


def product(left, right):
    return jnp.dot(left, right, preferred_element_type=f32)


def product_t(left, right):
    return lax.dot_general(left, right, (((0,), (0,)), ((), ())), preferred_element_type=f32)


def product_bt(left, right):
    return lax.dot_general(left, right, (((1,), (1,)), ((), ())), preferred_element_type=f32)


def swap(value, mask):
    devices = lax.axis_size("fsdp")
    return lax.ppermute(value, "fsdp", [(i, i ^ mask) for i in range(devices)])


def pad_hidden(columns):
    rows = columns.shape[0]
    grouped = columns.reshape(rows, GROUPS, FF_GROUP)
    return jnp.pad(grouped, ((0, 0), (0, 0), (0, FF_ROWS - FF_GROUP))).reshape(rows, FF_PAD)


def trim_hidden(columns):
    rows = columns.shape[0]
    return columns.reshape(rows, GROUPS, FF_ROWS)[:, :, :FF_GROUP].reshape(rows, FF)


def place_kernel(kind, coords, *refs):
    sources, targets, sems = refs[:8], refs[8:-1], refs[-1]
    core, x, y, z = coords[0], coords[1], coords[2], coords[3]
    copies = []
    for stream, part, near, dz in itertools.product(range(2), range(4), range(2), range(4)):
        src = sources[4 * stream + part].at[near * 4 + dz]
        owner = core if part < 2 else 1 - core
        far = part % 2
        dx, dy = (near, far) if stream == 0 else (far, near)
        chip = ((z ^ dz) * 2 + (y ^ dy)) * 2 + (x ^ dx)
        sem = sems.at[len(copies)]
        cols = src.shape[-1]
        if kind == "down":
            groups = src.shape[0]
            first = PAIR_ROWS // 8 if stream else 0
            dst = targets[0].at[chip * 2 + owner, first : first + groups]
        elif kind == "up":
            col = owner * HALF_UP + (D if stream else 0)
            dst = targets[0].at[chip, :, pl.ds(pl.multiple_of(col, 128), cols)]
        elif stream == 0:
            col = owner * SQUARE_HALF
            dst = targets[0].at[chip, :, pl.ds(pl.multiple_of(col, 128), cols)]
        else:
            dst = targets[0].at[chip, :, pl.ds(D, cols)]
            copies.append(pltpu.make_async_copy(src, dst, sem))
            last = pltpu.make_async_copy(src, targets[1].at[chip], sem)
            pl.when(owner == 0)(copies[-1].start)
            pl.when(owner == 1)(last.start)
            continue
        copies.append(pltpu.make_async_copy(src, dst, sem))
        copies[-1].start()
    for copy in copies:
        copy.wait()


def place(streams, coords, kind, shapes):
    sources = list(streams[0]) + list(streams[1])
    if kind == "down":
        sources = [s.reshape(8, -1, 8, D) for s in sources]
    size = sum(s.size for s in sources) * 2
    return pl.pallas_call(
        functools.partial(place_kernel, kind),
        in_specs=[pl.BlockSpec(memory_space=pltpu.SMEM)]
        + [pl.BlockSpec(memory_space=pltpu.HBM)] * 8,
        out_specs=[pl.BlockSpec(memory_space=pltpu.HBM)] * len(shapes),
        out_shape=[jax.ShapeDtypeStruct(s, bf16) for s in shapes],
        scratch_shapes=[pltpu.SemaphoreType.DMA((64,))],
        cost_estimate=pl.CostEstimate(flops=0, bytes_accessed=2 * size, transcendentals=0),
        name="place_" + kind,
    )(coords, *sources)


def spread(block, cut, axis):
    parts = [block] + [swap(block, 8 * step) for step in (1, 2, 3)]
    streams = []
    for stream in range(2):
        if axis == 1:
            own = jnp.stack([p[:, :cut] if stream == 0 else p[:, cut:] for p in parts])
        else:
            own = jnp.stack([p[:cut] if stream == 0 else p[cut:] for p in parts])
        near, far = (2, 4) if stream == 0 else (4, 2)
        first = jnp.concatenate([own, swap(own, near)])
        second = swap(first, far)
        streams.append((first, second, swap(first, 1), swap(second, 1)))
    return streams


def pick(value, index, axis):
    return lax.dynamic_index_in_dim(value, index, axis, keepdims=False)


def collect(keep, send, coords, cut, axis):
    core, x, y, z = coords
    other = swap(send, 1)
    rows, cols = keep.shape[1:]
    whole = (keep.astype(f32) + other.astype(f32)).reshape(4, 2, 2, rows, cols)
    results = []
    for stream in range(2):
        if axis == 1:
            value = whole[..., :cut] if stream == 0 else whole[..., cut:]
        else:
            value = whole[..., :cut, :] if stream == 0 else whole[..., cut:, :]
        if stream == 0:
            got = swap(pick(value, 1 - y, 1).astype(bf16), 4)
            value = pick(value, y, 1) + got.astype(f32)
            got = swap(pick(value, 1 - x, 1).astype(bf16), 2)
            value = pick(value, x, 1) + got.astype(f32)
        else:
            got = swap(pick(value, 1 - x, 2).astype(bf16), 2)
            value = pick(value, x, 2) + got.astype(f32)
            got = swap(pick(value, 1 - y, 1).astype(bf16), 4)
            value = pick(value, y, 1) + got.astype(f32)
        results.append(value)
    value = jnp.concatenate(results, axis=2 if axis == 1 else 1)
    total = pick(value, z, 0)
    for step in (1, 2, 3):
        total = total + swap(pick(value, z ^ step, 0).astype(bf16), 8 * step).astype(f32)
    return total


def fetch_pairs(narrow, core):
    q, k, v, o = (narrow[i].reshape(PAIR_ROWS // 2, D) for i in (2, 4, 5, 7))
    up = pad_hidden(narrow[11].reshape(PAIR_ROWS // 2, FF))
    down = narrow[13]
    first = jnp.concatenate([q, k, up[:, :HALF_UP]], axis=1)
    second = jnp.concatenate([v, o, up[:, HALF_UP:]], axis=1)
    lead = D * HALF_DOWN - down.shape[0]
    rows = PAIR_ROWS // 2
    tail = jnp.pad(down[:lead], (0, rows * EXTRA - lead)).reshape(rows, EXTRA)
    is_first = core == 0
    mine = jnp.where(is_first, first, second)
    theirs = jnp.where(is_first, second, first)
    got = swap(jnp.concatenate([theirs, tail], axis=1), 1)
    other = got[:, : mine.shape[1]]
    block = jnp.where(is_first, jnp.concatenate([mine, other]), jnp.concatenate([other, mine]))
    extra = got[:, mine.shape[1] :].reshape(-1)[:lead]
    end = jnp.zeros((D * HALF_DOWN - (down.shape[0] - lead),), bf16)
    down_block = jnp.where(
        is_first, jnp.concatenate([down, extra]), jnp.concatenate([down[lead:], end])
    ).reshape(HALF_DOWN, D)
    return block[:, :SQUARE_HALF], block[:, SQUARE_HALF:], down_block


def unpair(total, core):
    rows = total.shape[0] // 2
    keep = lax.dynamic_slice_in_dim(total, core * rows, rows, 0)
    got = swap(lax.dynamic_slice_in_dim(total, (1 - core) * rows, rows, 0), 1)
    is_first = core == 0
    return jnp.where(is_first, keep, got), jnp.where(is_first, got, keep)


def normalize(values):
    centre = jnp.mean(values, axis=-1, keepdims=True)
    centered = values - centre
    spread_sq = jnp.mean(centered * centered, axis=-1, keepdims=True)
    inverse = lax.rsqrt(spread_sq + 1e-06)
    return centered * inverse, inverse


def normalize_back(grad, gain, xhat, inverse):
    scaled = grad * gain
    first = jnp.mean(scaled, axis=-1, keepdims=True)
    second = jnp.mean(scaled * xhat, axis=-1, keepdims=True)
    return inverse * (scaled - first - xhat * second)


def gather_vectors(narrow):
    widths = [narrow[i].shape[0] for i in VECTORS]
    joined = jnp.concatenate([narrow[i] for i in VECTORS])
    joined = jnp.pad(joined, (0, 2048 - joined.shape[0])).reshape(16, 128)
    whole = lax.all_gather(joined, "fsdp", axis=0, tiled=True).reshape(-1, 2048)
    found = {}
    position = 0
    for i, width in zip(VECTORS, widths):
        found[i] = whole[:, position : position + width].reshape(-1).astype(f32)
        position += width
    return found


def on_device(*args):
    devices = lax.axis_size("fsdp")
    tokens, image_valid = args[0], args[1]
    shards = args[2:17]
    cotangent = args[17]
    staged = devices == 32
    widths = [piece.shape[0] for piece in shards]
    narrow = [piece.astype(bf16) for piece in shards]
    index = lax.axis_index("fsdp")
    core, x, y, z = index % 2, (index // 2) % 2, (index // 4) % 2, index // 8
    coords = (core, x, y, z)
    image_count = image_valid.shape[0]
    seq_len = tokens.shape[0] // image_count
    weight_img = jnp.repeat(image_valid.astype(f32), seq_len)[:, None]

    vectors = gather_vectors(narrow)
    if staged:
        where = jnp.stack(coords).astype(jnp.int32)
        square_block, up_block, down_block = fetch_pairs(narrow, core)
        blocks = (GROUPS, PAIR_ROWS)
        weight_qkv, weight_o = place(
            spread(square_block, D, 1), where, "square", [blocks + (3 * D,), blocks + (D,)]
        )
        weight_qkv, weight_o = weight_qkv.reshape(D, 3 * D), weight_o.reshape(D, D)
        (weight_up,) = place(spread(up_block, D, 1), where, "up", [blocks + (FF_PAD,)])
        weight_up = weight_up.reshape(D, FF_PAD)
        (weight_down,) = place(
            spread(down_block, PAIR_ROWS, 0), where, "down", [(2 * GROUPS, HALF_DOWN // 8, 8, D)]
        )
        weight_down = weight_down.reshape(FF_PAD, D)
    else:
        whole = {
            i: lax.all_gather(narrow[i], "fsdp", axis=0, tiled=True) for i in (2, 4, 5, 7, 11, 13)
        }
        square = [whole[i][: D * D].reshape(D, D) for i in (2, 4, 5, 7)]
        weight_qkv = jnp.concatenate(square[:3], axis=1)
        weight_o = square[3]
        weight_up = pad_hidden(whole[11][: D * FF].reshape(D, FF))
        weight_down = pad_hidden(whole[13][: D * FF].reshape(FF, D).T).T

    vec = lambda i: vectors[i][:D]
    gain_one, shift_one, gain_two, shift_two = vec(0), vec(1), vec(9), vec(10)
    bias_qkv = jnp.concatenate([vec(3), jnp.zeros((D,), f32), vec(6)])
    bias_o, bias_down = vec(8), vec(14)
    bias_up = pad_hidden(vectors[12][:FF].reshape(1, FF))

    xhat_one, inverse_one = normalize(tokens)
    normed = (xhat_one * gain_one + shift_one).astype(bf16)
    qkv = (product(normed, weight_qkv) + bias_qkv).astype(bf16)
    mixed, lse = attn_fwd(qkv, 2)
    resid = tokens + product(mixed, weight_o) + bias_o
    xhat_two, inverse_two = normalize(resid)
    normed_two = (xhat_two * gain_two + shift_two).astype(bf16)
    pre = product(normed_two, weight_up) + bias_up
    hidden, gelu_back = jax.vjp(lambda t: jax.nn.gelu(t, approximate=True), pre)
    hidden = hidden.astype(bf16)
    layer_out = weight_img * (resid + product(hidden, weight_down) + bias_down)

    grad_out = weight_img * cotangent
    grad_branch = grad_out.astype(bf16)
    grads = {14: jnp.sum(grad_branch.astype(f32), axis=0)}
    down_grad = product_t(hidden, grad_branch).astype(bf16)
    grad_pre = gelu_back(product_bt(grad_branch, weight_down))[0].astype(bf16)
    up_bias_grad = jnp.sum(grad_pre.astype(f32), axis=0)
    up_grad = product_t(normed_two, grad_pre).astype(bf16)
    grad_normed_two = product_bt(grad_pre, weight_up)
    grads[9] = jnp.sum(grad_normed_two * xhat_two, axis=0)
    grads[10] = jnp.sum(grad_normed_two, axis=0)
    grad_resid = grad_out + normalize_back(grad_normed_two, gain_two, xhat_two, inverse_two)
    grad_attn = grad_resid.astype(bf16)
    grads[8] = jnp.sum(grad_attn.astype(f32), axis=0)
    o_grad = product_t(mixed, grad_attn).astype(bf16)
    grad_mixed = product_bt(grad_attn, weight_o).astype(bf16)
    grad_qkv = attn_bwd(qkv, grad_mixed, lse, 2)
    qkv_bias_grad = jnp.sum(grad_qkv.astype(f32), axis=0)
    grads[3], grads[6] = qkv_bias_grad[:D], qkv_bias_grad[2 * D :]
    qkv_grad = product_t(normed, grad_qkv).astype(bf16)
    grad_normed = product_bt(grad_qkv, weight_qkv)
    grads[0] = jnp.sum(grad_normed * xhat_one, axis=0)
    grads[1] = jnp.sum(grad_normed, axis=0)
    tokens_grad = grad_resid + normalize_back(grad_normed, gain_one, xhat_one, inverse_one)
    grads[12] = trim_hidden(up_bias_grad.reshape(1, FF_PAD)).reshape(FF)

    rows = []
    for i in VECTORS:
        row = grads[i]
        row = jnp.pad(row, (0, widths[i] * devices - row.shape[0]))
        rows.append(row.reshape(devices, widths[i]))
    rows = jnp.concatenate(rows, axis=1)
    owned = [None] * 15
    if staged:
        down_halves = down_grad.reshape(GROUPS, 2, HALF_DOWN, D)
        down_total = collect(
            pick(down_halves, core, 1), pick(down_halves, 1 - core, 1), coords, PAIR_ROWS, 0
        )
        flat = down_total.reshape(-1)
        size = widths[13]
        lead = flat.shape[0] - size
        got = swap(flat[size:], 1)
        owned[13] = jnp.where(core == 0, flat[:size], jnp.concatenate([got, flat[: size - lead]]))

        up_grad = up_grad.reshape(GROUPS, PAIR_ROWS, FF_PAD)
        up_total = collect(
            lax.dynamic_slice_in_dim(up_grad, core * HALF_UP, HALF_UP, 2),
            lax.dynamic_slice_in_dim(up_grad, (1 - core) * HALF_UP, HALF_UP, 2),
            coords,
            D,
            1,
        )
        owned[11] = trim_hidden(jnp.concatenate(unpair(up_total, core), axis=1)).reshape(-1)

        rows = jnp.pad(rows, ((0, 0), (0, PAIR_ROWS // 2 * EXTRA - rows.shape[1])))
        rows = rows.reshape(D, EXTRA).astype(bf16)
        first = jnp.concatenate([qkv_grad[:, :SQUARE_HALF], rows], axis=1)
        second = jnp.concatenate([qkv_grad[:, SQUARE_HALF:], o_grad, jnp.zeros_like(rows)], axis=1)
        shape = (GROUPS, PAIR_ROWS, SQUARE_HALF + EXTRA)
        square_total = collect(
            jnp.where(core == 0, first, second).reshape(shape),
            jnp.where(core == 0, second, first).reshape(shape),
            coords,
            D + EXTRA,
            1,
        )
        left, right = unpair(square_total, core)
        owned[2] = left[:, :D].reshape(-1)
        owned[4] = left[:, D : 2 * D].reshape(-1)
        owned[5] = right[:, :D].reshape(-1)
        owned[7] = right[:, D : 2 * D].reshape(-1)
        small = left[:, 2 * D :].reshape(-1)
    else:
        scatter = lambda value: lax.psum_scatter(
            value.astype(f32).reshape(-1), "fsdp", scatter_dimension=0, tiled=True
        )
        fill = lambda value, i: jnp.pad(
            value.reshape(-1), (0, widths[i] * devices - value.size)
        )
        for position, i in enumerate((2, 4, 5)):
            owned[i] = scatter(fill(qkv_grad[:, position * D : (position + 1) * D], i))
        owned[7] = scatter(fill(o_grad, 7))
        owned[11] = scatter(fill(trim_hidden(up_grad), 11))
        owned[13] = scatter(fill(trim_hidden(down_grad.T).T, 13))
        small = scatter(rows)
    position = 0
    for i in VECTORS:
        owned[i] = small[position : position + widths[i]]
        position += widths[i]
    return (layer_out, tokens_grad, *owned)


def solution(mesh):
    row, flat = P("fsdp", None), P("fsdp")
    in_specs = (row, flat) + (flat,) * 15 + (row,)
    out_specs = (row, row) + (flat,) * 15
    return jax.shard_map(
        on_device, mesh=mesh, in_specs=in_specs, out_specs=out_specs, check_vma=False
    )
```

```python
import functools
import itertools
import jax
import jax.numpy as jnp
from jax import lax
from jax.sharding import PartitionSpec as P
from jax.experimental import pallas as pl
from jax.experimental.pallas import tpu as pltpu
D=1152; HEADS=16; HEAD_DIM=72; LANES=128
NEG=-1e30
LOG2E=1.4426950408889634
def nt(a,b): return lax.dot_general(a,b,(((1,),(1,)),((),())),preferred_element_type=jnp.float32)
def nn(a,b): return lax.dot_general(a,b,(((1,),(0,)),((),())),preferred_element_type=jnp.float32)

def fill_heads(dst, src, col, tokens, fill):
    rows=dst.shape[1]
    for h in range(HEADS):
        if fill is not None:
            dst[h]=fill
        dst[h,0:tokens,0:HEAD_DIM]=src[:,col+h*HEAD_DIM:col+(h+1)*HEAD_DIM]

def pad_values(rows, tokens, kind):
    lane=lax.broadcasted_iota(jnp.int32,(rows,LANES),1)
    row=lax.broadcasted_iota(jnp.int32,(rows,LANES),0)
    if kind=="query":
        v=jnp.where(lane==HEAD_DIM,1.0,0.0)
    elif kind=="key":
        v=jnp.where((lane==HEAD_DIM)&(row>=tokens),NEG,0.0)
    else:
        v=jnp.zeros((rows,LANES),jnp.float32)
    return v.astype(jnp.bfloat16)

def fwd_kernel(tokens, krows, qrows, per, qkv_ref, mixed_ref, lse_ref, qs, ks, vs, os):
    step=pl.program_id(0)
    @pl.when(step==0)
    def _():
        fill_heads(qs,qkv_ref,0,tokens,pad_values(qrows,tokens,"query"))
        fill_heads(ks,qkv_ref,D,tokens,pad_values(krows,tokens,"key"))
        zero=pad_values(krows,tokens,"value")
        for h in range(HEADS):
            vs[h]=zero
            vs[h,0:tokens,0:HEAD_DIM]=qkv_ref[:,2*D+h*HEAD_DIM:2*D+(h+1)*HEAD_DIM]
    c=HEAD_DIM**-0.5*LOG2E
    for j in range(per):
        h=step*per+j
        s=nt(ks[h],qs[h])
        m=jnp.max(s,axis=0,keepdims=True)
        e=jnp.exp2((s-m)*c)
        l=jnp.sum(e,axis=0,keepdims=True)
        p=(e*(1.0/l)).astype(jnp.bfloat16)
        vt=vs[h].T
        ot=nn(vt,p)
        os[h]=ot.T.astype(jnp.bfloat16)
        lse_ref[j]=m*c+jnp.log2(l)
    @pl.when(step==pl.num_programs(0)-1)
    def _():
        for h in range(HEADS):
            mixed_ref[:,h*HEAD_DIM:(h+1)*HEAD_DIM]=os[h,0:tokens,0:HEAD_DIM]

def attn_fwd(qkv, per=1):
    tokens=qkv.shape[0]
    krows=-(-tokens//16)*16; qrows=-(-tokens//128)*128
    return pl.pallas_call(functools.partial(fwd_kernel,tokens,krows,qrows,per),
        grid=(HEADS//per,),
        in_specs=[pl.BlockSpec(qkv.shape,lambda i:(0,0),pipeline_mode=pl.Buffered(1))],
        out_specs=[pl.BlockSpec((tokens,D),lambda i:(0,0),pipeline_mode=pl.Buffered(1)),pl.BlockSpec((per,1,qrows),lambda i:(i,0,0))],
        out_shape=[jax.ShapeDtypeStruct((tokens,D),jnp.bfloat16),jax.ShapeDtypeStruct((HEADS,1,qrows),jnp.float32)],
        scratch_shapes=[pltpu.VMEM((HEADS,qrows,LANES),jnp.bfloat16),pltpu.VMEM((HEADS,krows,LANES),jnp.bfloat16),
                        pltpu.VMEM((HEADS,krows,LANES),jnp.bfloat16),pltpu.VMEM((HEADS,qrows,LANES),jnp.bfloat16)],
        compiler_params=pltpu.CompilerParams(vmem_limit_bytes=56<<20,dimension_semantics=("arbitrary",)),
        cost_estimate=pl.CostEstimate(flops=4*HEADS*qrows*krows*LANES,bytes_accessed=4*tokens*D*2,transcendentals=HEADS*qrows*krows),
        name="attention_forward")(qkv)

def bwd_kernel(tokens, krows, qrows, per, qkv_ref, go_ref, lse_ref, dqkv_ref, qs, ks, vs, gs):
    step=pl.program_id(0)
    @pl.when(step==0)
    def _():
        fill_heads(qs,qkv_ref,0,tokens,pad_values(qrows,tokens,"query"))
        fill_heads(ks,qkv_ref,D,tokens,pad_values(krows,tokens,"key"))
        fill_heads(vs,qkv_ref,2*D,tokens,pad_values(krows,tokens,"value"))
        fill_heads(gs,go_ref,0,tokens,pad_values(qrows,tokens,"value"))
    scale=HEAD_DIM**-0.5
    c=scale*LOG2E
    for j in range(per):
        h=step*per+j
        q=qs[h]; k=ks[h]; v=vs[h]; g=gs[h]
        s=nt(k,q)
        p=jnp.exp2(s*c-lse_ref[j])
        dp=nt(v,g)
        dv=nn(p.astype(jnp.bfloat16),g)
        delta=jnp.sum(p*dp,axis=0,keepdims=True)
        ds=(p*(dp-delta)).astype(jnp.bfloat16)
        dk=nn(ds,q)*scale
        dqt=nn(k.T,ds)*scale
        qs[h]=dqt.T.astype(jnp.bfloat16)
        ks[h]=dk.astype(jnp.bfloat16)
        vs[h]=dv.astype(jnp.bfloat16)
    @pl.when(step==pl.num_programs(0)-1)
    def _():
        for i,r in enumerate((qs,ks,vs)):
            for h in range(HEADS):
                dqkv_ref[:,i*D+h*HEAD_DIM:i*D+(h+1)*HEAD_DIM]=r[h,0:tokens,0:HEAD_DIM]

def attn_bwd(qkv, gmixed, lse, per=1):
    tokens=qkv.shape[0]
    krows=-(-tokens//16)*16; qrows=-(-tokens//128)*128
    return pl.pallas_call(functools.partial(bwd_kernel,tokens,krows,qrows,per),
        grid=(HEADS//per,),
        in_specs=[pl.BlockSpec(qkv.shape,lambda i:(0,0),pipeline_mode=pl.Buffered(1)),pl.BlockSpec(gmixed.shape,lambda i:(0,0),pipeline_mode=pl.Buffered(1)),
                  pl.BlockSpec((per,1,qrows),lambda i:(i,0,0))],
        out_specs=pl.BlockSpec((tokens,3*D),lambda i:(0,0),pipeline_mode=pl.Buffered(1)),
        out_shape=jax.ShapeDtypeStruct((tokens,3*D),jnp.bfloat16),
        scratch_shapes=[pltpu.VMEM((HEADS,qrows,LANES),jnp.bfloat16),pltpu.VMEM((HEADS,krows,LANES),jnp.bfloat16),
                        pltpu.VMEM((HEADS,krows,LANES),jnp.bfloat16),pltpu.VMEM((HEADS,qrows,LANES),jnp.bfloat16)],
        compiler_params=pltpu.CompilerParams(vmem_limit_bytes=56<<20,dimension_semantics=("arbitrary",)),
        cost_estimate=pl.CostEstimate(flops=10*HEADS*qrows*krows*LANES,bytes_accessed=7*tokens*D*2,transcendentals=HEADS*qrows*krows),
        name="attention_backward")(qkv,gmixed,lse)


FF = 4304
GROUPS = 16
FF_GROUP = FF // GROUPS
FF_ROWS = 272
FF_PAD = GROUPS * FF_ROWS
PAIR_ROWS = D // GROUPS
HALF_UP = FF_PAD // 2
HALF_DOWN = FF_ROWS // 2
SQUARE_HALF = 2 * D
EXTRA = 128
VECTORS = (0, 1, 3, 6, 8, 9, 10, 12, 14)
bf16 = jnp.bfloat16
f32 = jnp.float32


def product(left, right):
    return jnp.dot(left, right, preferred_element_type=f32)


def product_t(left, right):
    return lax.dot_general(left, right, (((0,), (0,)), ((), ())), preferred_element_type=f32)


def product_bt(left, right):
    return lax.dot_general(left, right, (((1,), (1,)), ((), ())), preferred_element_type=f32)


def swap(value, mask):
    devices = lax.axis_size("fsdp")
    return lax.ppermute(value, "fsdp", [(i, i ^ mask) for i in range(devices)])


def pad_hidden(columns):
    rows = columns.shape[0]
    grouped = columns.reshape(rows, GROUPS, FF_GROUP)
    return jnp.pad(grouped, ((0, 0), (0, 0), (0, FF_ROWS - FF_GROUP))).reshape(rows, FF_PAD)


def trim_hidden(columns):
    rows = columns.shape[0]
    return columns.reshape(rows, GROUPS, FF_ROWS)[:, :, :FF_GROUP].reshape(rows, FF)


def place_kernel(kind, coords, *refs):
    sources, targets = refs[:8], refs[8:-10]
    held, in_sems, out_sems = refs[-10:-2], refs[-2], refs[-1]
    core, x, y, z = coords[0], coords[1], coords[2], coords[3]
    arrivals = [
        pltpu.make_async_copy(sources[i], held[i], in_sems.at[i]) for i in range(8)
    ]
    for arrival in arrivals:
        arrival.start()
    copies = []

    def move(src, dst):
        copies.append(pltpu.make_async_copy(src, dst, out_sems.at[len(copies)]))
        return copies[-1]

    for part, stream in itertools.product(range(4), range(2)):
        arrivals[4 * stream + part].wait()
        for near, dz in itertools.product(range(2), range(4)):
            src = held[4 * stream + part].at[near * 4 + dz]
            owner = core if part < 2 else 1 - core
            far = part % 2
            dx, dy = (near, far) if stream == 0 else (far, near)
            chip = ((z ^ dz) * 2 + (y ^ dy)) * 2 + (x ^ dx)
            cols = src.shape[-1]
            if kind == "down":
                groups = src.shape[0]
                first = PAIR_ROWS // 8 if stream else 0
                row = (chip ^ (core * 8)) * 2 + owner
                move(src, targets[0].at[row, first : first + groups]).start()
            elif kind == "up":
                col = (HALF_UP if part >= 2 else 0) + (D if stream else 0)
                move(src, targets[0].at[chip, :, col : col + cols]).start()
            elif stream == 0:
                col = pl.multiple_of(owner * SQUARE_HALF, 128)
                move(src.at[:, EXTRA:], targets[0].at[chip, :, pl.ds(col, D)]).start()
                move(src.at[:, :EXTRA], targets[2].at[owner * GROUPS + chip]).start()
            else:
                copy = move(src, targets[0].at[chip, :, D : 2 * D])
                last = pltpu.make_async_copy(src, targets[1].at[chip], out_sems.at[len(copies) - 1])
                pl.when(owner == 0)(copy.start)
                pl.when(owner == 1)(last.start)
    for copy in copies:
        copy.wait()


def place(streams, coords, kind, shapes):
    sources = list(streams[0]) + list(streams[1])
    if kind == "down":
        sources = [s.reshape(8, -1, 8, D) for s in sources]
    size = sum(s.size for s in sources) * 2
    return pl.pallas_call(
        functools.partial(place_kernel, kind),
        in_specs=[pl.BlockSpec(memory_space=pltpu.SMEM)]
        + [pl.BlockSpec(memory_space=pltpu.HBM)] * 8,
        out_specs=[pl.BlockSpec(memory_space=pltpu.HBM)] * len(shapes),
        out_shape=[jax.ShapeDtypeStruct(s, bf16) for s in shapes],
        scratch_shapes=[pltpu.VMEM(s.shape, bf16) for s in sources]
        + [pltpu.SemaphoreType.DMA((8,)), pltpu.SemaphoreType.DMA((96,))],
        compiler_params=pltpu.CompilerParams(vmem_limit_bytes=24 << 20),
        cost_estimate=pl.CostEstimate(flops=0, bytes_accessed=2 * size, transcendentals=0),
        name="place_" + kind,
    )(coords, *sources)


def tie(*values):
    leaves, form = jax.tree.flatten(values)
    return form.unflatten(lax.optimization_barrier(leaves))


def gather_z(block):
    return [block] + [swap(block, 8 * step) for step in (1, 2, 3)]


def gather_near(parts, cut, axis):
    streams = []
    for stream in range(2):
        if axis == 1:
            own = jnp.stack([p[:, :cut] if stream == 0 else p[:, cut:] for p in parts])
        else:
            own = jnp.stack([p[:cut] if stream == 0 else p[cut:] for p in parts])
        streams.append((own, swap(own, 4 if stream else 2)))
    return streams


def gather_far(streams):
    results = []
    for stream in range(2):
        first = jnp.concatenate(streams[stream])
        results.append((first, swap(first, 2 if stream else 4), swap(first, 1)))
    return results


def gather_core(streams):
    return [(first, second, third, swap(second, 1)) for first, second, third in streams]


def pick(value, index, axis):
    return lax.dynamic_index_in_dim(value, index, axis, keepdims=False)


def take(value, where):
    for axis in reversed(range(len(where))):
        if where[axis] is not None:
            value = pick(value, where[axis], axis)
    return value


def cut_streams(value, cut, axis):
    if axis == 1:
        return value[..., :cut], value[..., cut:]
    return value[..., :cut, :], value[..., cut:, :]


def total_of(terms):
    total = terms[0].astype(f32)
    for term in terms[1:]:
        total = total + term.astype(f32)
    return total


def sum_far(keep, other, coords, cut, axis):
    core, x, y, z = coords
    keeps, others = cut_streams(keep, cut, axis), cut_streams(other, cut, axis)
    got = []
    for stream in range(2):
        to = (None, None, 1 - x) if stream else (None, 1 - y)
        send = total_of([take(keeps[stream], to), take(others[stream], to)]).astype(bf16)
        got.append(swap(send, 2 if stream else 4))
    return got


def sum_near(keep, other, far, coords, cut, axis):
    core, x, y, z = coords
    keeps, others = cut_streams(keep, cut, axis), cut_streams(other, cut, axis)
    got = []
    for stream in range(2):
        to = (None, 1 - y, x) if stream else (None, y, 1 - x)
        after = (None, 1 - y) if stream else (None, 1 - x)
        terms = [take(keeps[stream], to), take(others[stream], to), take(far[stream], after)]
        got.append(swap(total_of(terms).astype(bf16), 4 if stream else 2))
    return got


def sum_z(keep, other, far, near, coords, cut, axis):
    core, x, y, z = coords
    keeps, others = cut_streams(keep, cut, axis), cut_streams(other, cut, axis)

    def at(plane):
        pieces = []
        for stream in range(2):
            after = (plane, y) if stream else (plane, x)
            terms = [
                take(keeps[stream], (plane, y, x)),
                take(others[stream], (plane, y, x)),
                take(far[stream], after),
                take(near[stream], (plane,)),
            ]
            pieces.append(total_of(terms))
        return jnp.concatenate(pieces, axis=axis)

    got = [swap(at(z ^ step).astype(bf16), 8 * step) for step in (1, 2, 3)]
    return lambda arrived: total_of([at(z)] + arrived), got


def fetch_pairs(narrow, core):
    q, k, v, o = (narrow[i].reshape(PAIR_ROWS // 2, D) for i in (2, 4, 5, 7))
    up = pad_hidden(narrow[11].reshape(PAIR_ROWS // 2, FF))
    down = narrow[13]
    small = jnp.concatenate([narrow[i] for i in VECTORS])
    small = jnp.pad(small, (0, PAIR_ROWS // 2 * EXTRA - small.shape[0]))
    small = small.reshape(PAIR_ROWS // 2, EXTRA)
    first = jnp.concatenate([small, q, k, up[:, :HALF_UP]], axis=1)
    second = jnp.concatenate([small, v, o, up[:, HALF_UP:]], axis=1)
    lead = D * HALF_DOWN - down.shape[0]
    rows = PAIR_ROWS // 2
    tail = jnp.pad(down[:lead], (0, rows * EXTRA - lead)).reshape(rows, EXTRA)
    is_first = core == 0
    mine = jnp.where(is_first, first, second)
    theirs = jnp.where(is_first, second, first)
    got = swap(jnp.concatenate([theirs, tail], axis=1), 1)
    other = got[:, : mine.shape[1]]
    block = jnp.where(is_first, jnp.concatenate([mine, other]), jnp.concatenate([other, mine]))
    extra = got[:, mine.shape[1] :].reshape(-1)[:lead]
    end = jnp.zeros((D * HALF_DOWN - (down.shape[0] - lead),), bf16)
    down_block = jnp.where(
        is_first, jnp.concatenate([down, extra]), jnp.concatenate([down[lead:], end])
    ).reshape(HALF_DOWN, D)
    square = SQUARE_HALF + EXTRA
    return block[:, :square], block[:, square:], down_block


def unpair(total, core):
    rows = total.shape[0] // 2
    keep = lax.dynamic_slice_in_dim(total, core * rows, rows, 0)
    got = swap(lax.dynamic_slice_in_dim(total, (1 - core) * rows, rows, 0), 1)
    is_first = core == 0
    return jnp.where(is_first, keep, got), jnp.where(is_first, got, keep)


def normalize(values):
    centre = jnp.mean(values, axis=-1, keepdims=True)
    centered = values - centre
    spread_sq = jnp.mean(centered * centered, axis=-1, keepdims=True)
    inverse = lax.rsqrt(spread_sq + 1e-06)
    return centered * inverse, inverse


def normalize_back(grad, gain, xhat, inverse):
    scaled = grad * gain
    first = jnp.mean(scaled, axis=-1, keepdims=True)
    second = jnp.mean(scaled * xhat, axis=-1, keepdims=True)
    return inverse * (scaled - first - xhat * second)


def name_vectors(whole, widths):
    found = {}
    position = 0
    for i in VECTORS:
        found[i] = whole[:, position : position + widths[i]].reshape(-1).astype(f32)
        position += widths[i]
    return found


def gather_plain(narrow, widths):
    whole = {
        i: lax.all_gather(narrow[i], "fsdp", axis=0, tiled=True) for i in (2, 4, 5, 7, 11, 13)
    }
    square = [whole[i][: D * D].reshape(D, D) for i in (2, 4, 5, 7)]
    up = pad_hidden(whole[11][: D * FF].reshape(D, FF))
    down = pad_hidden(whole[13][: D * FF].reshape(FF, D).T).T
    joined = jnp.concatenate([narrow[i] for i in VECTORS])
    length = joined.shape[0]
    joined = jnp.pad(joined, (0, 2048 - length)).reshape(16, 128)
    joined = lax.all_gather(joined, "fsdp", axis=0, tiled=True).reshape(-1, 2048)
    return jnp.concatenate(square[:3], axis=1), square[3], up, down, name_vectors(joined, widths)


def on_device(*args):
    devices = lax.axis_size("fsdp")
    tokens, image_valid = args[0], args[1]
    shards = args[2:17]
    cotangent = args[17]
    staged = devices == 32
    widths = [piece.shape[0] for piece in shards]
    narrow = [piece.astype(bf16) for piece in shards]
    index = lax.axis_index("fsdp")
    core, x, y, z = index % 2, (index // 2) % 2, (index // 4) % 2, index // 8
    coords = (core, x, y, z)
    image_count = image_valid.shape[0]
    seq_len = tokens.shape[0] // image_count
    weight_img = jnp.repeat(image_valid.astype(f32), seq_len)[:, None]

    grad_out = weight_img * cotangent
    grad_branch = grad_out.astype(bf16)
    grads = {14: jnp.sum(grad_branch.astype(f32), axis=0)}
    xhat_one, inverse_one = normalize(tokens)
    if staged:
        where = jnp.stack(coords).astype(jnp.int32)
        sq, up, down = fetch_pairs(narrow, core)
        square_cut = D + EXTRA
        sq = gather_z(sq)
        sq, up, down, xhat_one, inverse_one, grad_branch = tie(
            sq, up, down, xhat_one, inverse_one, grad_branch
        )
        sq = gather_near(sq, square_cut, 1)
        up = gather_z(up)
        (sq,) = tie(sq)
        sq = gather_far(sq)
        sq, up, down = tie(sq, up, down)
        sq = gather_core(sq)
        up = gather_near(up, D, 1)
        down = gather_z(down)
        blocks = (GROUPS, PAIR_ROWS)
        weight_qkv, weight_o, small = place(
            sq, where, "square", [blocks + (3 * D,), blocks + (D,), (2 * GROUPS, PAIR_ROWS, EXTRA)]
        )
        weight_qkv, weight_o = weight_qkv.reshape(D, 3 * D), weight_o.reshape(D, D)
        small = small[:GROUPS].reshape(devices, PAIR_ROWS // 2 * EXTRA)
        vectors = name_vectors(small, widths)
    else:
        weight_qkv, weight_o, weight_up, weight_down, vectors = gather_plain(narrow, widths)

    vec = lambda i: vectors[i][:D]
    gain_one, shift_one, gain_two, shift_two = vec(0), vec(1), vec(9), vec(10)
    bias_qkv = jnp.concatenate([vec(3), jnp.zeros((D,), f32), vec(6)])
    bias_o, bias_down = vec(8), vec(14)
    bias_up = pad_hidden(vectors[12][:FF].reshape(1, FF))
    if staged:
        bias_up = jnp.where(core == 0, bias_up, jnp.roll(bias_up, HALF_UP, axis=1))

    normed = (xhat_one * gain_one + shift_one).astype(bf16)
    qkv = (product(normed, weight_qkv) + bias_qkv).astype(bf16)
    if staged:
        qkv, up = tie(qkv, up)
        up = gather_far(up)
    mixed, lse = attn_fwd(qkv, 2)
    if staged:
        mixed, lse, up, down = tie(mixed, lse, up, down)
        up = gather_core(up)
        down = gather_near(down, PAIR_ROWS, 0)
    resid = tokens + product(mixed, weight_o) + bias_o
    xhat_two, inverse_two = normalize(resid)
    normed_two = (xhat_two * gain_two + shift_two).astype(bf16)
    if staged:
        normed_two, up, down = tie(normed_two, up, down)
        down = gather_far(down)
        (weight_up,) = place(up, where, "up", [blocks + (FF_PAD,)])
        weight_up = weight_up.reshape(D, FF_PAD)
    pre = product(normed_two, weight_up) + bias_up
    hidden, gelu_back = jax.vjp(lambda t: jax.nn.gelu(t, approximate=True), pre)
    hidden = hidden.astype(bf16)
    if staged:
        hidden, down = tie(hidden, down)
        down = gather_core(down)
    down_grad = product_t(hidden, grad_branch).astype(bf16)
    if staged:
        down_grad, down = tie(down_grad, down)
        down_grad = down_grad.reshape(4, 2, 2, 2, HALF_DOWN, D)
        down_keep, down_send = pick(down_grad, core, 3), pick(down_grad, 1 - core, 3)
        down_send = jnp.concatenate([down_send[2:], down_send[:2]])
        down_other = swap(down_send, 1)
        (weight_down,) = place(down, where, "down", [(2 * GROUPS, HALF_DOWN // 8, 8, D)])
        weight_down = weight_down.reshape(FF_PAD, D)
    branch = resid + product(hidden, weight_down) + bias_down
    layer_out = weight_img * branch
    if staged:
        down_at = (core, x, y, z ^ (2 * core))
        down_keep, down_other, weight_down, layer_out = tie(
            down_keep, down_other, weight_down, layer_out
        )
        down_far = sum_far(down_keep, down_other, down_at, PAIR_ROWS, 0)
    grad_pre = gelu_back(product_bt(grad_branch, weight_down))[0].astype(bf16)
    up_bias_grad = jnp.sum(grad_pre.astype(f32), axis=0)
    up_grad = product_t(normed_two, grad_pre).astype(bf16)
    if staged:
        down_far, up_grad, grad_pre = tie(down_far, up_grad, grad_pre)
        down_near = sum_near(down_keep, down_other, down_far, down_at, PAIR_ROWS, 0)
        up_grad = up_grad.reshape(4, 2, 2, PAIR_ROWS, FF_PAD)
        up_keep, up_send = up_grad[..., :HALF_UP], up_grad[..., HALF_UP:]
        up_other = swap(up_send, 1)
    grad_normed_two = product_bt(grad_pre, weight_up)
    grads[9] = jnp.sum(grad_normed_two * xhat_two, axis=0)
    grads[10] = jnp.sum(grad_normed_two, axis=0)
    grad_resid = grad_out + normalize_back(grad_normed_two, gain_two, xhat_two, inverse_two)
    grad_attn = grad_resid.astype(bf16)
    grads[8] = jnp.sum(grad_attn.astype(f32), axis=0)
    if staged:
        down_near, up_other, grad_attn = tie(down_near, up_other, grad_attn)
        down_sum, down_z = sum_z(
            down_keep, down_other, down_far, down_near, down_at, PAIR_ROWS, 0
        )
        up_far = sum_far(up_keep, up_other, coords, D, 1)
    o_grad = product_t(mixed, grad_attn).astype(bf16)
    grad_mixed = product_bt(grad_attn, weight_o).astype(bf16)
    grad_qkv = attn_bwd(qkv, grad_mixed, lse, 2)
    if staged:
        grad_qkv, o_grad, down_z, up_far = tie(grad_qkv, o_grad, down_z, up_far)
        up_near = sum_near(up_keep, up_other, up_far, coords, D, 1)
    qkv_bias_grad = jnp.sum(grad_qkv.astype(f32), axis=0)
    grads[3], grads[6] = qkv_bias_grad[:D], qkv_bias_grad[2 * D :]
    qkv_grad = product_t(normed, grad_qkv).astype(bf16)
    grad_normed = product_bt(grad_qkv, weight_qkv)
    grads[0] = jnp.sum(grad_normed * xhat_one, axis=0)
    grads[1] = jnp.sum(grad_normed, axis=0)
    tokens_grad = grad_resid + normalize_back(grad_normed, gain_one, xhat_one, inverse_one)
    if staged:
        up_bias_grad = jnp.where(core == 0, up_bias_grad, jnp.roll(up_bias_grad, HALF_UP))
    grads[12] = trim_hidden(up_bias_grad.reshape(1, FF_PAD)).reshape(FF)

    rows = []
    for i in VECTORS:
        row = grads[i]
        row = jnp.pad(row, (0, widths[i] * devices - row.shape[0]))
        rows.append(row.reshape(devices, widths[i]))
    rows = jnp.concatenate(rows, axis=1)
    owned = [None] * 15
    if staged:
        rows = jnp.pad(rows, ((0, 0), (0, PAIR_ROWS // 2 * EXTRA - rows.shape[1])))
        rows = rows.reshape(D, EXTRA).astype(bf16)
        first = jnp.concatenate([rows, qkv_grad[:, :SQUARE_HALF]], axis=1)
        second = jnp.concatenate([jnp.zeros_like(rows), qkv_grad[:, SQUARE_HALF:], o_grad], axis=1)
        shape = (4, 2, 2, PAIR_ROWS, SQUARE_HALF + EXTRA)
        keep = jnp.where(core == 0, first, second).reshape(shape)
        send = jnp.where(core == 0, second, first).reshape(shape)
        keep, send, up_near = tie(keep, send, up_near)
        up_sum, up_z = sum_z(up_keep, up_other, up_far, up_near, coords, D, 1)
        other = swap(send, 1)
        (other,) = tie(other)
        far = sum_far(keep, other, coords, square_cut, 1)
        far, up_z = tie(far, up_z)
        near = sum_near(keep, other, far, coords, square_cut, 1)

        down_total = down_sum(down_z)
        flat = down_total.reshape(-1)
        size = widths[13]
        lead = flat.shape[0] - size
        got = swap(flat[size:], 1)
        owned[13] = jnp.where(core == 0, flat[:size], jnp.concatenate([got, flat[: size - lead]]))
        up_total = up_sum(up_z)
        owned[11] = trim_hidden(jnp.concatenate(unpair(up_total, core), axis=1)).reshape(-1)
        near, owned[13], owned[11] = tie(near, owned[13], owned[11])

        square_sum, got = sum_z(keep, other, far, near, coords, square_cut, 1)
        left, right = unpair(square_sum(got), core)
        owned[2] = left[:, EXTRA:square_cut].reshape(-1)
        owned[4] = left[:, square_cut:].reshape(-1)
        owned[5] = right[:, EXTRA:square_cut].reshape(-1)
        owned[7] = right[:, square_cut:].reshape(-1)
        small = left[:, :EXTRA].reshape(-1)
    else:
        scatter = lambda value: lax.psum_scatter(
            value.astype(f32).reshape(-1), "fsdp", scatter_dimension=0, tiled=True
        )
        fill = lambda value, i: jnp.pad(
            value.reshape(-1), (0, widths[i] * devices - value.size)
        )
        for position, i in enumerate((2, 4, 5)):
            owned[i] = scatter(fill(qkv_grad[:, position * D : (position + 1) * D], i))
        owned[7] = scatter(fill(o_grad, 7))
        owned[11] = scatter(fill(trim_hidden(up_grad), 11))
        owned[13] = scatter(fill(trim_hidden(down_grad.T).T, 13))
        small = scatter(rows)
    position = 0
    for i in VECTORS:
        owned[i] = small[position : position + widths[i]]
        position += widths[i]
    return (layer_out, tokens_grad, *owned)


def solution(mesh):
    row, flat = P("fsdp", None), P("fsdp")
    in_specs = (row, flat) + (flat,) * 15 + (row,)
    out_specs = (row, row) + (flat,) * 15
    return jax.shard_map(
        on_device, mesh=mesh, in_specs=in_specs, out_specs=out_specs, check_vma=False
    )
```

```python
import functools
import itertools
import jax
import jax.numpy as jnp
from jax import lax
from jax.sharding import PartitionSpec as P
from jax.experimental import pallas as pl
from jax.experimental.pallas import tpu as pltpu
D=1152; HEADS=16; HEAD_DIM=72; LANES=128
NEG=-1e30
LOG2E=1.4426950408889634
def nt(a,b): return lax.dot_general(a,b,(((1,),(1,)),((),())),preferred_element_type=jnp.float32)
def nn(a,b): return lax.dot_general(a,b,(((1,),(0,)),((),())),preferred_element_type=jnp.float32)

def fill_heads(dst, src, col, tokens, fill):
    rows=dst.shape[1]
    for h in range(HEADS):
        if fill is not None:
            dst[h]=fill
        dst[h,0:tokens,0:HEAD_DIM]=src[:,col+h*HEAD_DIM:col+(h+1)*HEAD_DIM]

def pad_values(rows, tokens, kind):
    lane=lax.broadcasted_iota(jnp.int32,(rows,LANES),1)
    row=lax.broadcasted_iota(jnp.int32,(rows,LANES),0)
    if kind=="query":
        v=jnp.where(lane==HEAD_DIM,1.0,0.0)
    elif kind=="key":
        v=jnp.where((lane==HEAD_DIM)&(row>=tokens),NEG,0.0)
    else:
        v=jnp.zeros((rows,LANES),jnp.float32)
    return v.astype(jnp.bfloat16)

def fwd_kernel(tokens, krows, qrows, per, qkv_ref, mixed_ref, lse_ref, qs, ks, vs, os):
    step=pl.program_id(0)
    @pl.when(step==0)
    def _():
        fill_heads(qs,qkv_ref,0,tokens,pad_values(qrows,tokens,"query"))
        fill_heads(ks,qkv_ref,D,tokens,pad_values(krows,tokens,"key"))
        zero=pad_values(krows,tokens,"value")
        for h in range(HEADS):
            vs[h]=zero
            vs[h,0:tokens,0:HEAD_DIM]=qkv_ref[:,2*D+h*HEAD_DIM:2*D+(h+1)*HEAD_DIM]
    c=HEAD_DIM**-0.5*LOG2E
    for j in range(per):
        h=step*per+j
        s=nt(ks[h],qs[h])
        m=jnp.max(s,axis=0,keepdims=True)
        e=jnp.exp2((s-m)*c)
        l=jnp.sum(e,axis=0,keepdims=True)
        p=(e*(1.0/l)).astype(jnp.bfloat16)
        vt=vs[h].T
        ot=nn(vt,p)
        os[h]=ot.T.astype(jnp.bfloat16)
        lse_ref[j]=m*c+jnp.log2(l)
    @pl.when(step==pl.num_programs(0)-1)
    def _():
        for h in range(HEADS):
            mixed_ref[:,h*HEAD_DIM:(h+1)*HEAD_DIM]=os[h,0:tokens,0:HEAD_DIM]

def attn_fwd(qkv, per=1):
    tokens=qkv.shape[0]
    krows=-(-tokens//16)*16; qrows=-(-tokens//128)*128
    return pl.pallas_call(functools.partial(fwd_kernel,tokens,krows,qrows,per),
        grid=(HEADS//per,),
        in_specs=[pl.BlockSpec(qkv.shape,lambda i:(0,0),pipeline_mode=pl.Buffered(1))],
        out_specs=[pl.BlockSpec((tokens,D),lambda i:(0,0),pipeline_mode=pl.Buffered(1)),pl.BlockSpec((per,1,qrows),lambda i:(i,0,0))],
        out_shape=[jax.ShapeDtypeStruct((tokens,D),jnp.bfloat16),jax.ShapeDtypeStruct((HEADS,1,qrows),jnp.float32)],
        scratch_shapes=[pltpu.VMEM((HEADS,qrows,LANES),jnp.bfloat16),pltpu.VMEM((HEADS,krows,LANES),jnp.bfloat16),
                        pltpu.VMEM((HEADS,krows,LANES),jnp.bfloat16),pltpu.VMEM((HEADS,qrows,LANES),jnp.bfloat16)],
        compiler_params=pltpu.CompilerParams(vmem_limit_bytes=56<<20,dimension_semantics=("arbitrary",)),
        cost_estimate=pl.CostEstimate(flops=4*HEADS*qrows*krows*LANES,bytes_accessed=4*tokens*D*2,transcendentals=HEADS*qrows*krows),
        name="attention_forward")(qkv)

def bwd_kernel(tokens, krows, qrows, per, qkv_ref, go_ref, lse_ref, dqkv_ref, qs, ks, vs, gs):
    step=pl.program_id(0)
    @pl.when(step==0)
    def _():
        fill_heads(qs,qkv_ref,0,tokens,pad_values(qrows,tokens,"query"))
        fill_heads(ks,qkv_ref,D,tokens,pad_values(krows,tokens,"key"))
        fill_heads(vs,qkv_ref,2*D,tokens,pad_values(krows,tokens,"value"))
        fill_heads(gs,go_ref,0,tokens,pad_values(qrows,tokens,"value"))
    scale=HEAD_DIM**-0.5
    c=scale*LOG2E
    for j in range(per):
        h=step*per+j
        q=qs[h]; k=ks[h]; v=vs[h]; g=gs[h]
        s=nt(k,q)
        p=jnp.exp2(s*c-lse_ref[j])
        dp=nt(v,g)
        dv=nn(p.astype(jnp.bfloat16),g)
        delta=jnp.sum(p*dp,axis=0,keepdims=True)
        ds=(p*(dp-delta)).astype(jnp.bfloat16)
        dk=nn(ds,q)*scale
        dqt=nn(k.T,ds)*scale
        qs[h]=dqt.T.astype(jnp.bfloat16)
        ks[h]=dk.astype(jnp.bfloat16)
        vs[h]=dv.astype(jnp.bfloat16)
    @pl.when(step==pl.num_programs(0)-1)
    def _():
        for i,r in enumerate((qs,ks,vs)):
            for h in range(HEADS):
                dqkv_ref[:,i*D+h*HEAD_DIM:i*D+(h+1)*HEAD_DIM]=r[h,0:tokens,0:HEAD_DIM]

def attn_bwd(qkv, gmixed, lse, per=1):
    tokens=qkv.shape[0]
    krows=-(-tokens//16)*16; qrows=-(-tokens//128)*128
    return pl.pallas_call(functools.partial(bwd_kernel,tokens,krows,qrows,per),
        grid=(HEADS//per,),
        in_specs=[pl.BlockSpec(qkv.shape,lambda i:(0,0),pipeline_mode=pl.Buffered(1)),pl.BlockSpec(gmixed.shape,lambda i:(0,0),pipeline_mode=pl.Buffered(1)),
                  pl.BlockSpec((per,1,qrows),lambda i:(i,0,0))],
        out_specs=pl.BlockSpec((tokens,3*D),lambda i:(0,0),pipeline_mode=pl.Buffered(1)),
        out_shape=jax.ShapeDtypeStruct((tokens,3*D),jnp.bfloat16),
        scratch_shapes=[pltpu.VMEM((HEADS,qrows,LANES),jnp.bfloat16),pltpu.VMEM((HEADS,krows,LANES),jnp.bfloat16),
                        pltpu.VMEM((HEADS,krows,LANES),jnp.bfloat16),pltpu.VMEM((HEADS,qrows,LANES),jnp.bfloat16)],
        compiler_params=pltpu.CompilerParams(vmem_limit_bytes=56<<20,dimension_semantics=("arbitrary",)),
        cost_estimate=pl.CostEstimate(flops=10*HEADS*qrows*krows*LANES,bytes_accessed=7*tokens*D*2,transcendentals=HEADS*qrows*krows),
        name="attention_backward")(qkv,gmixed,lse)


FF = 4304
GROUPS = 16
FF_GROUP = FF // GROUPS
FF_ROWS = 272
FF_PAD = GROUPS * FF_ROWS
PAIR_ROWS = D // GROUPS
HALF_DOWN = FF_ROWS // 2
OWN_ROWS = PAIR_ROWS // 2
TILE = 8
BLOCK_TILES = 5
PAIR_TILES = PAIR_ROWS // TILE
EXTRA = 128
QKV_CUT = 14 * 128
UP_CUT = 22 * 128
UP_PIECES = 4
REST_ROWS = UP_PIECES * BLOCK_TILES * TILE + BLOCK_TILES * TILE + HALF_DOWN
VECTORS = (0, 1, 3, 6, 8, 9, 10, 12, 14)
bf16 = jnp.bfloat16
f32 = jnp.float32


def product(left, right):
    return jnp.dot(left, right, preferred_element_type=f32)


def product_t(left, right):
    return lax.dot_general(left, right, (((0,), (0,)), ((), ())), preferred_element_type=f32)


def product_bt(left, right):
    return lax.dot_general(left, right, (((1,), (1,)), ((), ())), preferred_element_type=f32)


def swap(value, mask):
    devices = lax.axis_size("fsdp")
    return lax.ppermute(value, "fsdp", [(i, i ^ mask) for i in range(devices)])


def pad_hidden(columns):
    rows = columns.shape[0]
    grouped = columns.reshape(rows, GROUPS, FF_GROUP)
    return jnp.pad(grouped, ((0, 0), (0, 0), (0, FF_ROWS - FF_GROUP))).reshape(rows, FF_PAD)


def trim_hidden(columns):
    rows = columns.shape[0]
    return columns.reshape(rows, GROUPS, FF_ROWS)[:, :, :FF_GROUP].reshape(rows, FF)


def place_square_kernel(coords, *refs):
    sources, (whole, small) = refs[:8], refs[8:10]
    held, in_sems, out_sems = refs[10:18], refs[18], refs[19]
    core, x, y, z = coords[0], coords[1], coords[2], coords[3]
    arrivals = [pltpu.make_async_copy(sources[i], held[i], in_sems.at[i]) for i in range(8)]
    for arrival in arrivals:
        arrival.start()
    copies, extras = [], []
    for part, stream in itertools.product(range(4), range(2)):
        arrivals[4 * stream + part].wait()
        for near, dz in itertools.product(range(2), range(4)):
            src = held[4 * stream + part].at[near * 4 + dz]
            owner = core if part < 2 else 1 - core
            far = part % 2
            dx, dy = (near, far) if stream == 0 else (far, near)
            chip = ((z ^ dz) * 2 + (y ^ dy)) * 2 + (x ^ dx)
            cols = src.shape[-1] - (0 if stream else EXTRA)
            col = QKV_CUT - EXTRA if stream else 0
            src_cols = pl.ds(0 if stream else EXTRA, cols)
            first = PAIR_TILES * chip + BLOCK_TILES * owner
            copies.append(
                pltpu.make_async_copy(
                    src.at[pl.ds(owner, BLOCK_TILES - 1), :, src_cols],
                    whole.at[pl.ds(first, BLOCK_TILES - 1), :, pl.ds(col, cols)],
                    out_sems.at[len(copies)],
                )
            )
            copies[-1].start()
            extra = pltpu.make_async_copy(
                src.at[BLOCK_TILES - 1, :, src_cols],
                whole.at[PAIR_TILES * chip + BLOCK_TILES - 1, :, pl.ds(col, cols)],
                out_sems.at[96 + len(extras)],
            )
            pl.when(owner == 0)(extra.start)
            extras.append((owner, extra))
            if stream == 0:
                copies.append(
                    pltpu.make_async_copy(
                        src.at[:, :, :EXTRA], small.at[chip * 2 + owner], out_sems.at[len(copies)]
                    )
                )
                copies[-1].start()
    for copy in copies:
        copy.wait()
    for owner, extra in extras:
        pl.when(owner == 0)(extra.wait)


def place_square(streams, coords):
    sources = [s.reshape(8, BLOCK_TILES, TILE, -1) for s in (*streams[0], *streams[1])]
    size = sum(s.size for s in sources) * 2
    whole, small = pl.pallas_call(
        place_square_kernel,
        in_specs=[pl.BlockSpec(memory_space=pltpu.SMEM)]
        + [pl.BlockSpec(memory_space=pltpu.HBM)] * 8,
        out_specs=[pl.BlockSpec(memory_space=pltpu.HBM)] * 2,
        out_shape=[
            jax.ShapeDtypeStruct((GROUPS * PAIR_TILES, TILE, 3 * D), bf16),
            jax.ShapeDtypeStruct((2 * GROUPS, BLOCK_TILES, TILE, EXTRA), bf16),
        ],
        scratch_shapes=[pltpu.VMEM(s.shape, bf16) for s in sources]
        + [pltpu.SemaphoreType.DMA((8,)), pltpu.SemaphoreType.DMA((160,))],
        compiler_params=pltpu.CompilerParams(vmem_limit_bytes=40 << 20),
        cost_estimate=pl.CostEstimate(flops=0, bytes_accessed=2 * size, transcendentals=0),
        name="place_square",
    )(coords, *sources)
    return whole.reshape(D, 3 * D), small.reshape(2 * GROUPS, -1)


def place_rest_kernel(source, up, out, down, held, in_sems, out_sems):
    arrivals = [
        pltpu.make_async_copy(source.at[i], held.at[i], in_sems.at[i]) for i in range(2 * GROUPS)
    ]
    for arrival in arrivals:
        arrival.start()
    copies = []
    for device in range(2 * GROUPS):
        chip, owner = device // 2, device % 2
        src = held.at[device]
        arrivals[device].wait()
        jobs = []
        count = BLOCK_TILES - owner
        first = PAIR_TILES * chip + BLOCK_TILES * owner
        for piece in range(UP_PIECES):
            cols = min(D, FF_PAD - piece * D)
            jobs.append(
                (
                    src.at[pl.ds(piece * BLOCK_TILES + owner, count), :, pl.ds(0, cols)],
                    up.at[pl.ds(first, count), :, pl.ds(piece * D, cols)],
                )
            )
        base = UP_PIECES * BLOCK_TILES
        jobs.append((src.at[pl.ds(base + owner, count)], out.at[pl.ds(first, count)]))
        rows = HALF_DOWN // TILE
        jobs.append((src.at[pl.ds(base + BLOCK_TILES, rows)], down.at[pl.ds(device * rows, rows)]))
        for one, other in jobs:
            copies.append(pltpu.make_async_copy(one, other, out_sems.at[len(copies)]))
            copies[-1].start()
    for copy in copies:
        copy.wait()


def place_rest(gathered):
    source = gathered.reshape(2 * GROUPS, REST_ROWS // TILE, TILE, D)
    up, out, down = pl.pallas_call(
        place_rest_kernel,
        in_specs=[pl.BlockSpec(memory_space=pltpu.HBM)],
        out_specs=[pl.BlockSpec(memory_space=pltpu.HBM)] * 3,
        out_shape=[
            jax.ShapeDtypeStruct((D // TILE, TILE, FF_PAD), bf16),
            jax.ShapeDtypeStruct((D // TILE, TILE, D), bf16),
            jax.ShapeDtypeStruct((FF_PAD // TILE, TILE, D), bf16),
        ],
        scratch_shapes=[
            pltpu.VMEM(source.shape, bf16),
            pltpu.SemaphoreType.DMA((2 * GROUPS,)),
            pltpu.SemaphoreType.DMA((2 * GROUPS * (UP_PIECES + 2),)),
        ],
        compiler_params=pltpu.CompilerParams(vmem_limit_bytes=56 << 20),
        cost_estimate=pl.CostEstimate(
            flops=0, bytes_accessed=4 * source.size, transcendentals=0
        ),
        name="place_rest",
    )(source)
    return up.reshape(D, FF_PAD), out.reshape(D, D), down.reshape(FF_PAD, D)


def tie(*values):
    leaves, form = jax.tree.flatten(values)
    return form.unflatten(lax.optimization_barrier(leaves))


def gather_z(block):
    return [block] + [swap(block, 8 * step) for step in (1, 2, 3)]


def gather_near(parts, cut, axis):
    streams = []
    for stream in range(2):
        if axis == 1:
            own = jnp.stack([p[:, :cut] if stream == 0 else p[:, cut:] for p in parts])
        else:
            own = jnp.stack([p[:cut] if stream == 0 else p[cut:] for p in parts])
        streams.append((own, swap(own, 4 if stream else 2)))
    return streams


def gather_far(streams):
    results = []
    for stream in range(2):
        first = jnp.concatenate(streams[stream])
        results.append((first, swap(first, 2 if stream else 4), swap(first, 1)))
    return results


def gather_core(streams):
    return [(first, second, third, swap(second, 1)) for first, second, third in streams]


def window(value, starts, sizes):
    rank = value.ndim
    starts = list(starts) + [0] * (rank - len(starts))
    lengths = list(value.shape)
    for axis, size in enumerate(sizes):
        if size is not None:
            lengths[axis] = size
    starts = [jnp.int32(0) if start is None else jnp.int32(start) for start in starts]
    result = lax.dynamic_slice(value, starts, lengths)
    kept = [
        length for axis, length in enumerate(lengths) if axis >= len(sizes) or sizes[axis] != 1
    ]
    return result.reshape(kept)


class Reduction:
    def __init__(self, matrices, streams, coords):
        self.matrices = [m.reshape(4, 2, 2, PAIR_TILES, TILE, -1) for m in matrices]
        self.streams = streams
        self.coords = coords

    def part(self, arrays, stream, plane, tile):
        sizes = tuple(None if p is None else 1 for p in plane) + (BLOCK_TILES, None)
        pieces = []
        for number, first, last in self.streams[stream]:
            starts = tuple(plane) + (tile, None, first)
            pieces.append(window(arrays[number], starts, sizes + (last - first,)))
        return pieces[0] if len(pieces) == 1 else jnp.concatenate(pieces, axis=-1)

    def terms(self, stream, plane):
        tile = self.coords[0] * (PAIR_TILES - BLOCK_TILES)
        own = self.part(self.matrices, stream, plane, tile)
        return [own, self.part(self.other, stream, plane, 0)]

    def core_step(self):
        tile = (1 - self.coords[0]) * (PAIR_TILES - BLOCK_TILES)
        starts, sizes = (None, None, None, tile), (None, None, None, BLOCK_TILES)
        return [swap(window(m, starts, sizes), 1) for m in self.matrices]

    def far_step(self, other):
        core, x, y, z = self.coords
        self.other = other
        got = []
        for stream in range(2):
            plane = (None, None, 1 - x) if stream else (None, 1 - y, None)
            send = total_of(self.terms(stream, plane)).astype(bf16)
            got.append(swap(send, 2 if stream else 4))
        return got

    def near_step(self, far):
        core, x, y, z = self.coords
        self.far = far
        got = []
        for stream in range(2):
            plane = (None, 1 - y, x) if stream else (None, y, 1 - x)
            after = (None, 1 - y) if stream else (None, 1 - x)
            terms = self.terms(stream, plane) + [window(far[stream], after, (None, 1))]
            got.append(swap(total_of(terms).astype(bf16), 4 if stream else 2))
        return got

    def at(self, plane):
        core, x, y, z = self.coords
        pieces = []
        for stream in range(2):
            after = (plane, y) if stream else (plane, x)
            terms = self.terms(stream, (plane, y, x)) + [
                window(self.far[stream], after, (1, 1)),
                window(self.near[stream], (plane,), (1,)),
            ]
            pieces.append(total_of(terms))
        return jnp.concatenate(pieces, axis=-1)

    def z_step(self, near):
        z = self.coords[3]
        self.near = near
        return [swap(self.at(z ^ step).astype(bf16), 8 * step) for step in (1, 2, 3)]

    def finish(self, arrived):
        core, x, y, z = self.coords
        total = total_of([self.at(z)] + arrived)
        total = total.reshape(BLOCK_TILES * TILE, -1)
        return lax.dynamic_slice_in_dim(
            total, core * (BLOCK_TILES * TILE - OWN_ROWS), OWN_ROWS, 0
        )


def total_of(terms):
    total = terms[0].astype(f32)
    for term in terms[1:]:
        total = total + term.astype(f32)
    return total


def fetch_pairs(narrow, core):
    q, k, v, o = (narrow[i].reshape(OWN_ROWS, D) for i in (2, 4, 5, 7))
    up = pad_hidden(narrow[11].reshape(OWN_ROWS, FF))
    down = narrow[13]
    rows = jnp.concatenate([q, k, v, o, up], axis=1)
    spare = BLOCK_TILES * TILE - OWN_ROWS
    lead = D * HALF_DOWN - down.shape[0]
    tail = jnp.pad(down[:lead].reshape(spare, -1), ((0, 0), (0, 512 - lead // spare)))
    is_first = core == 0
    edge = jnp.where(is_first, rows[OWN_ROWS - spare :], rows[:spare])
    got = swap(jnp.concatenate([edge, tail], axis=1), 1)
    edge = got[:, : rows.shape[1]]
    block = jnp.where(is_first, jnp.concatenate([rows, edge]), jnp.concatenate([edge, rows]))
    extra = got[:, rows.shape[1] : rows.shape[1] + lead // spare].reshape(-1)
    end = jnp.zeros((D * HALF_DOWN - (down.shape[0] - lead),), bf16)
    down_block = jnp.where(
        is_first, jnp.concatenate([down, extra]), jnp.concatenate([down[lead:], end])
    ).reshape(HALF_DOWN, D)
    small = jnp.concatenate([narrow[i] for i in VECTORS])
    small = jnp.pad(small, (0, BLOCK_TILES * TILE * EXTRA - small.shape[0]))
    small = small.reshape(BLOCK_TILES * TILE, EXTRA)
    square = jnp.concatenate([small, block[:, : 3 * D]], axis=1)
    up_block = jnp.pad(block[:, 4 * D :], ((0, 0), (0, UP_PIECES * D - FF_PAD)))
    pieces = [up_block[:, i * D : (i + 1) * D] for i in range(UP_PIECES)]
    rest = jnp.concatenate(pieces + [block[:, 3 * D : 4 * D], down_block])
    return square, rest


def normalize(values):
    centre = jnp.mean(values, axis=-1, keepdims=True)
    centered = values - centre
    spread_sq = jnp.mean(centered * centered, axis=-1, keepdims=True)
    inverse = lax.rsqrt(spread_sq + 1e-06)
    return centered * inverse, inverse


def normalize_back(grad, gain, xhat, inverse):
    scaled = grad * gain
    first = jnp.mean(scaled, axis=-1, keepdims=True)
    second = jnp.mean(scaled * xhat, axis=-1, keepdims=True)
    return inverse * (scaled - first - xhat * second)


def name_vectors(whole, widths):
    found = {}
    position = 0
    for i in VECTORS:
        found[i] = whole[:, position : position + widths[i]].reshape(-1).astype(f32)
        position += widths[i]
    return found


def gather_plain(narrow, widths):
    whole = {
        i: lax.all_gather(narrow[i], "fsdp", axis=0, tiled=True) for i in (2, 4, 5, 7, 11, 13)
    }
    square = [whole[i][: D * D].reshape(D, D) for i in (2, 4, 5, 7)]
    up = pad_hidden(whole[11][: D * FF].reshape(D, FF))
    down = pad_hidden(whole[13][: D * FF].reshape(FF, D).T).T
    joined = jnp.concatenate([narrow[i] for i in VECTORS])
    length = joined.shape[0]
    joined = jnp.pad(joined, (0, 2048 - length)).reshape(16, 128)
    joined = lax.all_gather(joined, "fsdp", axis=0, tiled=True).reshape(-1, 2048)
    return jnp.concatenate(square[:3], axis=1), square[3], up, down, name_vectors(joined, widths)


def on_device(*args):
    devices = lax.axis_size("fsdp")
    tokens, image_valid = args[0], args[1]
    shards = args[2:17]
    cotangent = args[17]
    staged = devices == 32
    widths = [piece.shape[0] for piece in shards]
    narrow = [piece.astype(bf16) for piece in shards]
    index = lax.axis_index("fsdp")
    core, x, y, z = index % 2, (index // 2) % 2, (index // 4) % 2, index // 8
    coords = (core, x, y, z)
    image_count = image_valid.shape[0]
    seq_len = tokens.shape[0] // image_count
    weight_img = jnp.repeat(image_valid.astype(f32), seq_len)[:, None]

    grad_out = weight_img * cotangent
    grad_branch = grad_out.astype(bf16)
    grads = {14: jnp.sum(grad_branch.astype(f32), axis=0)}
    xhat_one, inverse_one = normalize(tokens)
    if staged:
        where = jnp.stack(coords).astype(jnp.int32)
        sq, rest = fetch_pairs(narrow, core)
        rest = lax.all_gather(rest, "fsdp", axis=0, tiled=True)
        sq = gather_z(sq)
        sq, xhat_one, inverse_one, grad_branch = tie(sq, xhat_one, inverse_one, grad_branch)
        sq = gather_near(sq, QKV_CUT, 1)
        sq = gather_far(sq)
        sq = gather_core(sq)
        weight_qkv, small = place_square(sq, where)
        vectors = name_vectors(small, widths)
    else:
        weight_qkv, weight_o, weight_up, weight_down, vectors = gather_plain(narrow, widths)

    vec = lambda i: vectors[i][:D]
    gain_one, shift_one, gain_two, shift_two = vec(0), vec(1), vec(9), vec(10)
    bias_qkv = jnp.concatenate([vec(3), jnp.zeros((D,), f32), vec(6)])
    bias_o, bias_down = vec(8), vec(14)
    bias_up = pad_hidden(vectors[12][:FF].reshape(1, FF))

    normed = (xhat_one * gain_one + shift_one).astype(bf16)
    qkv = (product(normed, weight_qkv) + bias_qkv).astype(bf16)
    mixed, lse = attn_fwd(qkv, 2)
    if staged:
        mixed, lse, rest = tie(mixed, lse, rest)
        weight_up, weight_o, weight_down = place_rest(rest)
    resid = tokens + product(mixed, weight_o) + bias_o
    xhat_two, inverse_two = normalize(resid)
    normed_two = (xhat_two * gain_two + shift_two).astype(bf16)
    pre = product(normed_two, weight_up) + bias_up
    hidden = jax.nn.gelu(pre, approximate=True).astype(bf16)
    down_grad = product_t(hidden, grad_branch).astype(bf16)
    if staged:
        grad_branch, down_grad, pre = tie(grad_branch, down_grad, pre)
        down_sum = lax.psum_scatter(down_grad, "fsdp", scatter_dimension=0, tiled=True)
    layer_out = weight_img * (resid + product(hidden, weight_down) + bias_down)
    gelu_back = jax.vjp(lambda t: jax.nn.gelu(t, approximate=True), pre)[1]
    grad_pre = gelu_back(product_bt(grad_branch, weight_down))[0].astype(bf16)
    up_bias_grad = jnp.sum(grad_pre.astype(f32), axis=0)
    up_grad = product_t(normed_two, grad_pre).astype(bf16)
    grad_normed_two = product_bt(grad_pre, weight_up)
    grads[9] = jnp.sum(grad_normed_two * xhat_two, axis=0)
    grads[10] = jnp.sum(grad_normed_two, axis=0)
    grad_resid = grad_out + normalize_back(grad_normed_two, gain_two, xhat_two, inverse_two)
    grad_attn = grad_resid.astype(bf16)
    grads[8] = jnp.sum(grad_attn.astype(f32), axis=0)
    o_grad = product_t(mixed, grad_attn).astype(bf16)
    if staged:
        up_grad, o_grad, grad_attn = tie(up_grad, o_grad, grad_attn)
        outer = Reduction(
            (up_grad, o_grad), (((0, 0, UP_CUT),), ((0, UP_CUT, FF_PAD), (1, 0, D))), coords
        )
        outer_other = outer.core_step()
    grad_mixed = product_bt(grad_attn, weight_o).astype(bf16)
    if staged:
        grad_mixed, outer_other = tie(grad_mixed, outer_other)
        outer_far = outer.far_step(outer_other)
    grad_qkv = attn_bwd(qkv, grad_mixed, lse, 2)
    if staged:
        grad_qkv, outer_far = tie(grad_qkv, outer_far)
        outer_near = outer.near_step(outer_far)
    qkv_bias_grad = jnp.sum(grad_qkv.astype(f32), axis=0)
    grads[3], grads[6] = qkv_bias_grad[:D], qkv_bias_grad[2 * D :]
    qkv_grad = product_t(normed, grad_qkv).astype(bf16)
    grad_normed = product_bt(grad_qkv, weight_qkv)
    grads[0] = jnp.sum(grad_normed * xhat_one, axis=0)
    grads[1] = jnp.sum(grad_normed, axis=0)
    grads[12] = trim_hidden(up_bias_grad.reshape(1, FF_PAD)).reshape(FF)

    rows = []
    for i in VECTORS:
        row = grads[i]
        row = jnp.pad(row, (0, widths[i] * devices - row.shape[0]))
        rows.append(row.reshape(devices, widths[i]))
    rows = jnp.concatenate(rows, axis=1)
    owned = [None] * 15
    if staged:
        rows = jnp.pad(rows, ((0, 0), (0, OWN_ROWS * EXTRA - rows.shape[1])))
        rows = rows.reshape(D, EXTRA).astype(bf16)
        inner = Reduction(
            (rows, qkv_grad),
            (((0, 0, EXTRA), (1, 0, QKV_CUT - EXTRA)), ((1, QKV_CUT - EXTRA, 3 * D),)),
            coords,
        )
        rows, qkv_grad, outer_near, grad_normed = tie(rows, qkv_grad, outer_near, grad_normed)
        outer_z = outer.z_step(outer_near)
        inner_other = inner.core_step()
        tokens_grad = grad_resid + normalize_back(grad_normed, gain_one, xhat_one, inverse_one)
        (inner_other,) = tie(inner_other)
        inner_far = inner.far_step(inner_other)
        inner_far, outer_z, tokens_grad = tie(inner_far, outer_z, tokens_grad)
        inner_near = inner.near_step(inner_far)

        flat = down_sum.astype(f32).reshape(-1)
        size = widths[13]
        lead = flat.shape[0] - size
        got = swap(down_sum.reshape(-1)[size:], 1).astype(f32)
        owned[13] = jnp.where(core == 0, flat[:size], jnp.concatenate([got, flat[: size - lead]]))
        outer_sum = outer.finish(outer_z)
        owned[11] = trim_hidden(outer_sum[:, :FF_PAD]).reshape(-1)
        owned[7] = outer_sum[:, FF_PAD:].reshape(-1)
        inner_near, owned[13], owned[11], owned[7] = tie(
            inner_near, owned[13], owned[11], owned[7]
        )
        inner_sum = inner.finish(inner.z_step(inner_near))
        for position, i in enumerate((2, 4, 5)):
            first = EXTRA + position * D
            owned[i] = inner_sum[:, first : first + D].reshape(-1)
        small = inner_sum[:, :EXTRA].reshape(-1)
    else:
        tokens_grad = grad_resid + normalize_back(grad_normed, gain_one, xhat_one, inverse_one)
        scatter = lambda value: lax.psum_scatter(
            value.astype(f32).reshape(-1), "fsdp", scatter_dimension=0, tiled=True
        )
        fill = lambda value, i: jnp.pad(
            value.reshape(-1), (0, widths[i] * devices - value.size)
        )
        for position, i in enumerate((2, 4, 5)):
            owned[i] = scatter(fill(qkv_grad[:, position * D : (position + 1) * D], i))
        owned[7] = scatter(fill(o_grad, 7))
        owned[11] = scatter(fill(trim_hidden(up_grad), 11))
        owned[13] = scatter(fill(trim_hidden(down_grad.T).T, 13))
        small = scatter(rows)
    position = 0
    for i in VECTORS:
        owned[i] = small[position : position + widths[i]]
        position += widths[i]
    return (layer_out, tokens_grad, *owned)


def solution(mesh):
    row, flat = P("fsdp", None), P("fsdp")
    in_specs = (row, flat) + (flat,) * 15 + (row,)
    out_specs = (row, row) + (flat,) * 15
    return jax.shard_map(
        on_device, mesh=mesh, in_specs=in_specs, out_specs=out_specs, check_vma=False
    )
```

```python
import functools
import itertools
import jax
import jax.numpy as jnp
from jax import lax
from jax.sharding import PartitionSpec as P
from jax.experimental import pallas as pl
from jax.experimental.pallas import tpu as pltpu
D=1152; HEADS=16; HEAD_DIM=72; LANES=128
NEG=-1e30
LOG2E=1.4426950408889634
def nt(a,b): return lax.dot_general(a,b,(((1,),(1,)),((),())),preferred_element_type=jnp.float32)
def nn(a,b): return lax.dot_general(a,b,(((1,),(0,)),((),())),preferred_element_type=jnp.float32)

def fill_heads(dst, src, col, tokens, fill):
    rows=dst.shape[1]
    for h in range(HEADS):
        if fill is not None:
            dst[h]=fill
        dst[h,0:tokens,0:HEAD_DIM]=src[:,col+h*HEAD_DIM:col+(h+1)*HEAD_DIM]

def pad_values(rows, tokens, kind):
    lane=lax.broadcasted_iota(jnp.int32,(rows,LANES),1)
    row=lax.broadcasted_iota(jnp.int32,(rows,LANES),0)
    if kind=="query":
        v=jnp.where(lane==HEAD_DIM,1.0,0.0)
    elif kind=="key":
        v=jnp.where((lane==HEAD_DIM)&(row>=tokens),NEG,0.0)
    else:
        v=jnp.zeros((rows,LANES),jnp.float32)
    return v.astype(jnp.bfloat16)

def fwd_kernel(tokens, krows, qrows, per, qkv_ref, mixed_ref, lse_ref, qs, ks, vs, os):
    step=pl.program_id(0)
    @pl.when(step==0)
    def _():
        fill_heads(qs,qkv_ref,0,tokens,pad_values(qrows,tokens,"query"))
        fill_heads(ks,qkv_ref,D,tokens,pad_values(krows,tokens,"key"))
        zero=pad_values(krows,tokens,"value")
        for h in range(HEADS):
            vs[h]=zero
            vs[h,0:tokens,0:HEAD_DIM]=qkv_ref[:,2*D+h*HEAD_DIM:2*D+(h+1)*HEAD_DIM]
    c=HEAD_DIM**-0.5*LOG2E
    for j in range(per):
        h=step*per+j
        s=nt(ks[h],qs[h])
        m=jnp.max(s,axis=0,keepdims=True)
        e=jnp.exp2((s-m)*c)
        l=jnp.sum(e,axis=0,keepdims=True)
        p=(e*(1.0/l)).astype(jnp.bfloat16)
        vt=vs[h].T
        ot=nn(vt,p)
        os[h]=ot.T.astype(jnp.bfloat16)
        lse_ref[j]=m*c+jnp.log2(l)
    @pl.when(step==pl.num_programs(0)-1)
    def _():
        for h in range(HEADS):
            mixed_ref[:,h*HEAD_DIM:(h+1)*HEAD_DIM]=os[h,0:tokens,0:HEAD_DIM]

def attn_fwd(qkv, per=1):
    tokens=qkv.shape[0]
    krows=-(-tokens//16)*16; qrows=-(-tokens//128)*128
    return pl.pallas_call(functools.partial(fwd_kernel,tokens,krows,qrows,per),
        grid=(HEADS//per,),
        in_specs=[pl.BlockSpec(qkv.shape,lambda i:(0,0),pipeline_mode=pl.Buffered(1))],
        out_specs=[pl.BlockSpec((tokens,D),lambda i:(0,0),pipeline_mode=pl.Buffered(1)),pl.BlockSpec((per,1,qrows),lambda i:(i,0,0))],
        out_shape=[jax.ShapeDtypeStruct((tokens,D),jnp.bfloat16),jax.ShapeDtypeStruct((HEADS,1,qrows),jnp.float32)],
        scratch_shapes=[pltpu.VMEM((HEADS,qrows,LANES),jnp.bfloat16),pltpu.VMEM((HEADS,krows,LANES),jnp.bfloat16),
                        pltpu.VMEM((HEADS,krows,LANES),jnp.bfloat16),pltpu.VMEM((HEADS,qrows,LANES),jnp.bfloat16)],
        compiler_params=pltpu.CompilerParams(vmem_limit_bytes=56<<20,dimension_semantics=("arbitrary",)),
        cost_estimate=pl.CostEstimate(flops=4*HEADS*qrows*krows*LANES,bytes_accessed=4*tokens*D*2,transcendentals=HEADS*qrows*krows),
        name="attention_forward")(qkv)

def bwd_kernel(tokens, krows, qrows, per, qkv_ref, go_ref, lse_ref, dqkv_ref, qs, ks, vs, gs):
    step=pl.program_id(0)
    @pl.when(step==0)
    def _():
        fill_heads(qs,qkv_ref,0,tokens,pad_values(qrows,tokens,"query"))
        fill_heads(ks,qkv_ref,D,tokens,pad_values(krows,tokens,"key"))
        fill_heads(vs,qkv_ref,2*D,tokens,pad_values(krows,tokens,"value"))
        fill_heads(gs,go_ref,0,tokens,pad_values(qrows,tokens,"value"))
    scale=HEAD_DIM**-0.5
    c=scale*LOG2E
    for j in range(per):
        h=step*per+j
        q=qs[h]; k=ks[h]; v=vs[h]; g=gs[h]
        s=nt(k,q)
        p=jnp.exp2(s*c-lse_ref[j])
        dp=nt(v,g)
        dv=nn(p.astype(jnp.bfloat16),g)
        delta=jnp.sum(p*dp,axis=0,keepdims=True)
        ds=(p*(dp-delta)).astype(jnp.bfloat16)
        dk=nn(ds,q)*scale
        dqt=nn(k.T,ds)*scale
        qs[h]=dqt.T.astype(jnp.bfloat16)
        ks[h]=dk.astype(jnp.bfloat16)
        vs[h]=dv.astype(jnp.bfloat16)
    @pl.when(step==pl.num_programs(0)-1)
    def _():
        for i,r in enumerate((qs,ks,vs)):
            for h in range(HEADS):
                dqkv_ref[:,i*D+h*HEAD_DIM:i*D+(h+1)*HEAD_DIM]=r[h,0:tokens,0:HEAD_DIM]

def attn_bwd(qkv, gmixed, lse, per=1):
    tokens=qkv.shape[0]
    krows=-(-tokens//16)*16; qrows=-(-tokens//128)*128
    return pl.pallas_call(functools.partial(bwd_kernel,tokens,krows,qrows,per),
        grid=(HEADS//per,),
        in_specs=[pl.BlockSpec(qkv.shape,lambda i:(0,0),pipeline_mode=pl.Buffered(1)),pl.BlockSpec(gmixed.shape,lambda i:(0,0),pipeline_mode=pl.Buffered(1)),
                  pl.BlockSpec((per,1,qrows),lambda i:(i,0,0))],
        out_specs=pl.BlockSpec((tokens,3*D),lambda i:(0,0),pipeline_mode=pl.Buffered(1)),
        out_shape=jax.ShapeDtypeStruct((tokens,3*D),jnp.bfloat16),
        scratch_shapes=[pltpu.VMEM((HEADS,qrows,LANES),jnp.bfloat16),pltpu.VMEM((HEADS,krows,LANES),jnp.bfloat16),
                        pltpu.VMEM((HEADS,krows,LANES),jnp.bfloat16),pltpu.VMEM((HEADS,qrows,LANES),jnp.bfloat16)],
        compiler_params=pltpu.CompilerParams(vmem_limit_bytes=56<<20,dimension_semantics=("arbitrary",)),
        cost_estimate=pl.CostEstimate(flops=1000000,bytes_accessed=1000000,transcendentals=0),
        name="attention_backward")(qkv,gmixed,lse)


GELU_A = 0.7978845608028654
GELU_B = 0.044715


def mlp_kernel(normed_ref, grad_ref, up_ref, bias_ref, down_ref, out_ref, back_ref,
               up_grad_ref, bias_grad_ref, down_grad_ref, normed, normed_t, grad, out, back):
    step = pl.program_id(0)
    tokens = normed_ref.shape[0]

    @pl.when(step == 0)
    def _():
        for held, source in ((normed, normed_ref), (grad, grad_ref)):
            held[...] = jnp.zeros_like(held)
            held[0:tokens] = source[...]
        normed_t[...] = normed[...].T
        out[...] = jnp.zeros_like(out)
        back[...] = jnp.zeros_like(back)

    pre = nn(normed[...], up_ref[...]) + bias_ref[...]
    square = pre * pre
    bend = jnp.tanh(pre * (GELU_A + GELU_A * GELU_B * square))
    hidden = (0.5 * pre * (1.0 + bend)).astype(jnp.bfloat16)
    slope = 0.5 * (1.0 + bend) + 0.5 * pre * (1.0 - bend * bend) * (
        GELU_A + 3.0 * GELU_A * GELU_B * square
    )
    grad_pre = (nt(grad[...], down_ref[...]) * slope).astype(jnp.bfloat16)
    out[...] += nn(hidden, down_ref[...])
    back[...] += nt(grad_pre, up_ref[...])
    down_grad_ref[...] = nn(hidden.T, grad[...]).astype(jnp.bfloat16)
    up_grad_ref[...] = nn(normed_t[...], grad_pre).astype(jnp.bfloat16)
    bias_grad_ref[...] = jnp.sum(grad_pre.astype(jnp.float32), axis=0, keepdims=True)

    @pl.when(step == pl.num_programs(0) - 1)
    def _():
        out_ref[...] = out[0:tokens]
        back_ref[...] = back[0:tokens]


def mlp(normed, grad, up, bias, down):
    tokens, hidden = normed.shape[0], up.shape[1]
    rows = -(-tokens // 16) * 16
    tile = 256
    whole = lambda shape: pl.BlockSpec(shape, lambda i: (0, 0), pipeline_mode=pl.Buffered(1))
    return pl.pallas_call(
        mlp_kernel,
        grid=(hidden // tile,),
        in_specs=[
            whole((tokens, D)),
            whole((tokens, D)),
            pl.BlockSpec((D, tile), lambda i: (0, i)),
            pl.BlockSpec((1, tile), lambda i: (0, i)),
            pl.BlockSpec((tile, D), lambda i: (i, 0)),
        ],
        out_specs=[
            whole((tokens, D)),
            whole((tokens, D)),
            pl.BlockSpec((D, tile), lambda i: (0, i)),
            pl.BlockSpec((1, tile), lambda i: (0, i)),
            pl.BlockSpec((tile, D), lambda i: (i, 0)),
        ],
        out_shape=[
            jax.ShapeDtypeStruct((tokens, D), jnp.float32),
            jax.ShapeDtypeStruct((tokens, D), jnp.float32),
            jax.ShapeDtypeStruct((D, hidden), jnp.bfloat16),
            jax.ShapeDtypeStruct((1, hidden), jnp.float32),
            jax.ShapeDtypeStruct((hidden, D), jnp.bfloat16),
        ],
        scratch_shapes=[
            pltpu.VMEM((rows, D), jnp.bfloat16),
            pltpu.VMEM((D, rows), jnp.bfloat16),
            pltpu.VMEM((rows, D), jnp.bfloat16),
            pltpu.VMEM((rows, D), jnp.float32),
            pltpu.VMEM((rows, D), jnp.float32),
        ],
        compiler_params=pltpu.CompilerParams(
            vmem_limit_bytes=56 << 20, dimension_semantics=("arbitrary",)
        ),
        cost_estimate=pl.CostEstimate(flops=1000000, bytes_accessed=1000000, transcendentals=0),
        name="mlp_forward_backward",
    )(normed, grad, up, bias, down)


def qkv_back_kernel(grad_ref, normed_ref, weight_ref, xhat_ref, inverse_ref, gain_ref, resid_ref,
                    weight_grad_ref, bias_grad_ref, sums_ref, tokens_ref, grad, normed_t, total):
    step = pl.program_id(0)
    tokens = normed_ref.shape[0]

    @pl.when(step == 0)
    def _():
        grad[...] = jnp.zeros_like(grad)
        grad[0:tokens] = normed_ref[...]
        normed_t[...] = grad[...].T
        grad[...] = jnp.zeros_like(grad)
        total[...] = jnp.zeros_like(total)

    grad[0:tokens] = grad_ref[...]
    weight_grad_ref[...] = nn(normed_t[...], grad[...]).astype(jnp.bfloat16)
    bias_grad_ref[...] = jnp.sum(grad[...].astype(jnp.float32), axis=0, keepdims=True)
    total[...] += nt(grad[...], weight_ref[...])

    @pl.when(step == pl.num_programs(0) - 1)
    def _():
        back = total[0:tokens]
        xhat = xhat_ref[...]
        sums_ref[0:1] = jnp.sum(back * xhat, axis=0, keepdims=True)
        sums_ref[1:2] = jnp.sum(back, axis=0, keepdims=True)
        scaled = back * gain_ref[...]
        first = jnp.mean(scaled, axis=-1, keepdims=True)
        second = jnp.mean(scaled * xhat, axis=-1, keepdims=True)
        tokens_ref[...] = resid_ref[...] + inverse_ref[...] * (scaled - first - xhat * second)


def qkv_back(grad, normed, weight, xhat, inverse, gain, resid):
    tokens = normed.shape[0]
    rows = -(-tokens // 16) * 16
    whole = lambda shape: pl.BlockSpec(shape, lambda i: (0, 0), pipeline_mode=pl.Buffered(1))
    part = lambda shape: pl.BlockSpec(shape, lambda i: (0, i))
    return pl.pallas_call(
        qkv_back_kernel,
        grid=(3,),
        in_specs=[
            part((tokens, D)),
            whole((tokens, D)),
            part((D, D)),
            whole((tokens, D)),
            whole((tokens, 1)),
            whole((1, D)),
            whole((tokens, D)),
        ],
        out_specs=[part((D, D)), part((1, D)), whole((8, D)), whole((tokens, D))],
        out_shape=[
            jax.ShapeDtypeStruct((D, 3 * D), jnp.bfloat16),
            jax.ShapeDtypeStruct((1, 3 * D), jnp.float32),
            jax.ShapeDtypeStruct((8, D), jnp.float32),
            jax.ShapeDtypeStruct((tokens, D), jnp.float32),
        ],
        scratch_shapes=[
            pltpu.VMEM((rows, D), jnp.bfloat16),
            pltpu.VMEM((D, rows), jnp.bfloat16),
            pltpu.VMEM((rows, D), jnp.float32),
        ],
        compiler_params=pltpu.CompilerParams(
            vmem_limit_bytes=56 << 20, dimension_semantics=("arbitrary",)
        ),
        cost_estimate=pl.CostEstimate(flops=1000000, bytes_accessed=1000000, transcendentals=0),
        name="qkv_backward",
    )(grad, normed, weight, xhat, inverse, gain, resid)


FF = 4304
GROUPS = 16
FF_GROUP = FF // GROUPS
FF_ROWS = 272
FF_PAD = GROUPS * FF_ROWS
PAIR_ROWS = D // GROUPS
HALF_DOWN = FF_ROWS // 2
OWN_ROWS = PAIR_ROWS // 2
TILE = 8
BLOCK_TILES = 5
PAIR_TILES = PAIR_ROWS // TILE
EXTRA = 128
QKV_CUT = 14 * 128
UP_CUT = 22 * 128
UP_PIECES = 4
REST_ROWS = UP_PIECES * BLOCK_TILES * TILE + BLOCK_TILES * TILE + HALF_DOWN
VECTORS = (0, 1, 3, 6, 8, 9, 10, 12, 14)
bf16 = jnp.bfloat16
f32 = jnp.float32


def product(left, right):
    return jnp.dot(left, right, preferred_element_type=f32)


def product_t(left, right):
    return lax.dot_general(left, right, (((0,), (0,)), ((), ())), preferred_element_type=f32)


def product_bt(left, right):
    return lax.dot_general(left, right, (((1,), (1,)), ((), ())), preferred_element_type=f32)


def swap(value, mask):
    devices = lax.axis_size("fsdp")
    return lax.ppermute(value, "fsdp", [(i, i ^ mask) for i in range(devices)])


def pad_hidden(columns):
    rows = columns.shape[0]
    grouped = columns.reshape(rows, GROUPS, FF_GROUP)
    return jnp.pad(grouped, ((0, 0), (0, 0), (0, FF_ROWS - FF_GROUP))).reshape(rows, FF_PAD)


def trim_hidden(columns):
    rows = columns.shape[0]
    return columns.reshape(rows, GROUPS, FF_ROWS)[:, :, :FF_GROUP].reshape(rows, FF)


def place_square_kernel(coords, *refs):
    sources, (whole, small) = refs[:8], refs[8:10]
    held, in_sems, out_sems = refs[10:18], refs[18], refs[19]
    core, x, y, z = coords[0], coords[1], coords[2], coords[3]
    arrivals = [pltpu.make_async_copy(sources[i], held[i], in_sems.at[i]) for i in range(8)]
    for arrival in arrivals:
        arrival.start()
    copies, extras = [], []
    for part, stream in itertools.product(range(4), range(2)):
        arrivals[4 * stream + part].wait()
        for near, dz in itertools.product(range(2), range(4)):
            src = held[4 * stream + part].at[near * 4 + dz]
            owner = core if part < 2 else 1 - core
            far = part % 2
            dx, dy = (near, far) if stream == 0 else (far, near)
            chip = ((z ^ dz) * 2 + (y ^ dy)) * 2 + (x ^ dx)
            cols = src.shape[-1] - (0 if stream else EXTRA)
            col = QKV_CUT - EXTRA if stream else 0
            src_cols = pl.ds(0 if stream else EXTRA, cols)
            first = PAIR_TILES * chip + BLOCK_TILES * owner
            copies.append(
                pltpu.make_async_copy(
                    src.at[pl.ds(owner, BLOCK_TILES - 1), :, src_cols],
                    whole.at[pl.ds(first, BLOCK_TILES - 1), :, pl.ds(col, cols)],
                    out_sems.at[len(copies)],
                )
            )
            copies[-1].start()
            extra = pltpu.make_async_copy(
                src.at[BLOCK_TILES - 1, :, src_cols],
                whole.at[PAIR_TILES * chip + BLOCK_TILES - 1, :, pl.ds(col, cols)],
                out_sems.at[96 + len(extras)],
            )
            pl.when(owner == 0)(extra.start)
            extras.append((owner, extra))
            if stream == 0:
                copies.append(
                    pltpu.make_async_copy(
                        src.at[:, :, :EXTRA], small.at[chip * 2 + owner], out_sems.at[len(copies)]
                    )
                )
                copies[-1].start()
    for copy in copies:
        copy.wait()
    for owner, extra in extras:
        pl.when(owner == 0)(extra.wait)


def place_square(streams, coords):
    sources = [s.reshape(8, BLOCK_TILES, TILE, -1) for s in (*streams[0], *streams[1])]
    size = sum(s.size for s in sources) * 2
    whole, small = pl.pallas_call(
        place_square_kernel,
        in_specs=[pl.BlockSpec(memory_space=pltpu.SMEM)]
        + [pl.BlockSpec(memory_space=pltpu.HBM)] * 8,
        out_specs=[pl.BlockSpec(memory_space=pltpu.HBM)] * 2,
        out_shape=[
            jax.ShapeDtypeStruct((GROUPS * PAIR_TILES, TILE, 3 * D), bf16),
            jax.ShapeDtypeStruct((2 * GROUPS, BLOCK_TILES, TILE, EXTRA), bf16),
        ],
        scratch_shapes=[pltpu.VMEM(s.shape, bf16) for s in sources]
        + [pltpu.SemaphoreType.DMA((8,)), pltpu.SemaphoreType.DMA((160,))],
        compiler_params=pltpu.CompilerParams(vmem_limit_bytes=40 << 20),
        cost_estimate=pl.CostEstimate(flops=0, bytes_accessed=2 * size, transcendentals=0),
        name="place_square",
    )(coords, *sources)
    return whole.reshape(D, 3 * D), small.reshape(2 * GROUPS, -1)


def place_rest_kernel(source, up, out, down, held, in_sems, out_sems):
    arrivals = [
        pltpu.make_async_copy(source.at[i], held.at[i], in_sems.at[i]) for i in range(2 * GROUPS)
    ]
    for arrival in arrivals:
        arrival.start()
    copies = []
    for device in range(2 * GROUPS):
        chip, owner = device // 2, device % 2
        src = held.at[device]
        arrivals[device].wait()
        jobs = []
        count = BLOCK_TILES - owner
        first = PAIR_TILES * chip + BLOCK_TILES * owner
        for piece in range(UP_PIECES):
            cols = min(D, FF_PAD - piece * D)
            jobs.append(
                (
                    src.at[pl.ds(piece * BLOCK_TILES + owner, count), :, pl.ds(0, cols)],
                    up.at[pl.ds(first, count), :, pl.ds(piece * D, cols)],
                )
            )
        base = UP_PIECES * BLOCK_TILES
        jobs.append((src.at[pl.ds(base + owner, count)], out.at[pl.ds(first, count)]))
        rows = HALF_DOWN // TILE
        jobs.append((src.at[pl.ds(base + BLOCK_TILES, rows)], down.at[pl.ds(device * rows, rows)]))
        for one, other in jobs:
            copies.append(pltpu.make_async_copy(one, other, out_sems.at[len(copies)]))
            copies[-1].start()
    for copy in copies:
        copy.wait()


def place_rest(gathered):
    source = gathered.reshape(2 * GROUPS, REST_ROWS // TILE, TILE, D)
    up, out, down = pl.pallas_call(
        place_rest_kernel,
        in_specs=[pl.BlockSpec(memory_space=pltpu.HBM)],
        out_specs=[pl.BlockSpec(memory_space=pltpu.HBM)] * 3,
        out_shape=[
            jax.ShapeDtypeStruct((D // TILE, TILE, FF_PAD), bf16),
            jax.ShapeDtypeStruct((D // TILE, TILE, D), bf16),
            jax.ShapeDtypeStruct((FF_PAD // TILE, TILE, D), bf16),
        ],
        scratch_shapes=[
            pltpu.VMEM(source.shape, bf16),
            pltpu.SemaphoreType.DMA((2 * GROUPS,)),
            pltpu.SemaphoreType.DMA((2 * GROUPS * (UP_PIECES + 2),)),
        ],
        compiler_params=pltpu.CompilerParams(vmem_limit_bytes=56 << 20),
        cost_estimate=pl.CostEstimate(
            flops=0, bytes_accessed=4 * source.size, transcendentals=0
        ),
        name="place_rest",
    )(source)
    return up.reshape(D, FF_PAD), out.reshape(D, D), down.reshape(FF_PAD, D)


def tie(*values):
    leaves, form = jax.tree.flatten(values)
    return form.unflatten(lax.optimization_barrier(leaves))


def gather_z(block):
    return [block] + [swap(block, 8 * step) for step in (1, 2, 3)]


def gather_near(parts, cut, axis):
    streams = []
    for stream in range(2):
        if axis == 1:
            own = jnp.stack([p[:, :cut] if stream == 0 else p[:, cut:] for p in parts])
        else:
            own = jnp.stack([p[:cut] if stream == 0 else p[cut:] for p in parts])
        streams.append((own, swap(own, 4 if stream else 2)))
    return streams


def gather_far(streams):
    results = []
    for stream in range(2):
        first = jnp.concatenate(streams[stream])
        results.append((first, swap(first, 2 if stream else 4), swap(first, 1)))
    return results


def gather_core(streams):
    return [(first, second, third, swap(second, 1)) for first, second, third in streams]


def window(value, starts, sizes):
    rank = value.ndim
    starts = list(starts) + [0] * (rank - len(starts))
    lengths = list(value.shape)
    for axis, size in enumerate(sizes):
        if size is not None:
            lengths[axis] = size
    starts = [jnp.int32(0) if start is None else jnp.int32(start) for start in starts]
    result = lax.dynamic_slice(value, starts, lengths)
    kept = [
        length for axis, length in enumerate(lengths) if axis >= len(sizes) or sizes[axis] != 1
    ]
    return result.reshape(kept)


class Reduction:
    def __init__(self, matrices, streams, coords):
        self.matrices = [m.reshape(4, 2, 2, PAIR_TILES, TILE, -1) for m in matrices]
        self.streams = streams
        self.coords = coords

    def part(self, arrays, stream, plane, tile):
        sizes = tuple(None if p is None else 1 for p in plane) + (BLOCK_TILES, None)
        pieces = []
        for number, first, last in self.streams[stream]:
            starts = tuple(plane) + (tile, None, first)
            pieces.append(window(arrays[number], starts, sizes + (last - first,)))
        return pieces[0] if len(pieces) == 1 else jnp.concatenate(pieces, axis=-1)

    def terms(self, stream, plane):
        tile = self.coords[0] * (PAIR_TILES - BLOCK_TILES)
        own = self.part(self.matrices, stream, plane, tile)
        return [own, self.part(self.other, stream, plane, 0)]

    def core_step(self):
        tile = (1 - self.coords[0]) * (PAIR_TILES - BLOCK_TILES)
        starts, sizes = (None, None, None, tile), (None, None, None, BLOCK_TILES)
        return [swap(window(m, starts, sizes), 1) for m in self.matrices]

    def far_step(self, other, streams=(0, 1), pieces=slice(None)):
        core, x, y, z = self.coords
        self.other = other
        got = []
        every = self.streams
        for stream in streams:
            plane = (None, None, 1 - x) if stream else (None, 1 - y, None)
            self.streams = {stream: every[stream][pieces]}
            send = total_of(self.terms(stream, plane)).astype(bf16)
            got.append(swap(send, 2 if stream else 4))
        self.streams = every
        return got

    def near_step(self, far):
        core, x, y, z = self.coords
        self.far = far
        got = []
        for stream in range(2):
            plane = (None, 1 - y, x) if stream else (None, y, 1 - x)
            after = (None, 1 - y) if stream else (None, 1 - x)
            terms = self.terms(stream, plane) + [window(far[stream], after, (None, 1))]
            got.append(swap(total_of(terms).astype(bf16), 4 if stream else 2))
        return got

    def at(self, plane):
        core, x, y, z = self.coords
        pieces = []
        for stream in range(2):
            after = (plane, y) if stream else (plane, x)
            terms = self.terms(stream, (plane, y, x)) + [
                window(self.far[stream], after, (1, 1)),
                window(self.near[stream], (plane,), (1,)),
            ]
            pieces.append(total_of(terms))
        return jnp.concatenate(pieces, axis=-1)

    def z_step(self, near):
        z = self.coords[3]
        self.near = near
        return [swap(self.at(z ^ step).astype(bf16), 8 * step) for step in (1, 2, 3)]

    def finish(self, arrived):
        core, x, y, z = self.coords
        total = total_of([self.at(z)] + arrived)
        total = total.reshape(BLOCK_TILES * TILE, -1)
        return lax.dynamic_slice_in_dim(
            total, core * (BLOCK_TILES * TILE - OWN_ROWS), OWN_ROWS, 0
        )


def total_of(terms):
    total = terms[0].astype(f32)
    for term in terms[1:]:
        total = total + term.astype(f32)
    return total


def fetch_pairs(narrow, core):
    q, k, v, o = (narrow[i].reshape(OWN_ROWS, D) for i in (2, 4, 5, 7))
    up = pad_hidden(narrow[11].reshape(OWN_ROWS, FF))
    down = narrow[13]
    rows = jnp.concatenate([q, k, v, o, up], axis=1)
    spare = BLOCK_TILES * TILE - OWN_ROWS
    lead = D * HALF_DOWN - down.shape[0]
    tail = jnp.pad(down[:lead].reshape(spare, -1), ((0, 0), (0, 512 - lead // spare)))
    is_first = core == 0
    edge = jnp.where(is_first, rows[OWN_ROWS - spare :], rows[:spare])
    got = swap(jnp.concatenate([edge, tail], axis=1), 1)
    edge = got[:, : rows.shape[1]]
    block = jnp.where(is_first, jnp.concatenate([rows, edge]), jnp.concatenate([edge, rows]))
    extra = got[:, rows.shape[1] : rows.shape[1] + lead // spare].reshape(-1)
    end = jnp.zeros((D * HALF_DOWN - (down.shape[0] - lead),), bf16)
    down_block = jnp.where(
        is_first, jnp.concatenate([down, extra]), jnp.concatenate([down[lead:], end])
    ).reshape(HALF_DOWN, D)
    small = jnp.concatenate([narrow[i] for i in VECTORS])
    small = jnp.pad(small, (0, BLOCK_TILES * TILE * EXTRA - small.shape[0]))
    small = small.reshape(BLOCK_TILES * TILE, EXTRA)
    square = jnp.concatenate([small, block[:, : 3 * D]], axis=1)
    up_block = jnp.pad(block[:, 4 * D :], ((0, 0), (0, UP_PIECES * D - FF_PAD)))
    pieces = [up_block[:, i * D : (i + 1) * D] for i in range(UP_PIECES)]
    rest = jnp.concatenate(pieces + [block[:, 3 * D : 4 * D], down_block])
    return square, rest


def normalize(values):
    centre = jnp.mean(values, axis=-1, keepdims=True)
    centered = values - centre
    spread_sq = jnp.mean(centered * centered, axis=-1, keepdims=True)
    inverse = lax.rsqrt(spread_sq + 1e-06)
    return centered * inverse, inverse


def normalize_back(grad, gain, xhat, inverse):
    scaled = grad * gain
    first = jnp.mean(scaled, axis=-1, keepdims=True)
    second = jnp.mean(scaled * xhat, axis=-1, keepdims=True)
    return inverse * (scaled - first - xhat * second)


def name_vectors(whole, widths):
    found = {}
    position = 0
    for i in VECTORS:
        found[i] = whole[:, position : position + widths[i]].reshape(-1).astype(f32)
        position += widths[i]
    return found


def gather_plain(narrow, widths):
    whole = {
        i: lax.all_gather(narrow[i], "fsdp", axis=0, tiled=True) for i in (2, 4, 5, 7, 11, 13)
    }
    square = [whole[i][: D * D].reshape(D, D) for i in (2, 4, 5, 7)]
    up = pad_hidden(whole[11][: D * FF].reshape(D, FF))
    down = pad_hidden(whole[13][: D * FF].reshape(FF, D).T).T
    joined = jnp.concatenate([narrow[i] for i in VECTORS])
    length = joined.shape[0]
    joined = jnp.pad(joined, (0, 2048 - length)).reshape(16, 128)
    joined = lax.all_gather(joined, "fsdp", axis=0, tiled=True).reshape(-1, 2048)
    return jnp.concatenate(square[:3], axis=1), square[3], up, down, name_vectors(joined, widths)


def on_device(*args):
    devices = lax.axis_size("fsdp")
    tokens, image_valid = args[0], args[1]
    shards = args[2:17]
    cotangent = args[17]
    staged = devices == 32
    widths = [piece.shape[0] for piece in shards]
    narrow = [piece.astype(bf16) for piece in shards]
    index = lax.axis_index("fsdp")
    core, x, y, z = index % 2, (index // 2) % 2, (index // 4) % 2, index // 8
    coords = (core, x, y, z)
    image_count = image_valid.shape[0]
    seq_len = tokens.shape[0] // image_count
    weight_img = jnp.repeat(image_valid.astype(f32), seq_len)[:, None]

    grad_out = weight_img * cotangent
    grad_branch = grad_out.astype(bf16)
    grads = {14: jnp.sum(grad_branch.astype(f32), axis=0)}
    xhat_one, inverse_one = normalize(tokens)
    if staged:
        where = jnp.stack(coords).astype(jnp.int32)
        sq, rest = fetch_pairs(narrow, core)
        rest = lax.all_gather(rest, "fsdp", axis=0, tiled=True)
        sq = gather_z(sq)
        sq, xhat_one, inverse_one, grad_branch = tie(sq, xhat_one, inverse_one, grad_branch)
        sq = gather_near(sq, QKV_CUT, 1)
        sq = gather_far(sq)
        sq = gather_core(sq)
        weight_qkv, small = place_square(sq, where)
        vectors = name_vectors(small, widths)
    else:
        weight_qkv, weight_o, weight_up, weight_down, vectors = gather_plain(narrow, widths)

    vec = lambda i: vectors[i][:D]
    gain_one, shift_one, gain_two, shift_two = vec(0), vec(1), vec(9), vec(10)
    bias_qkv = jnp.concatenate([vec(3), jnp.zeros((D,), f32), vec(6)])
    bias_o, bias_down = vec(8), vec(14)
    bias_up = pad_hidden(vectors[12][:FF].reshape(1, FF))

    normed = (xhat_one * gain_one + shift_one).astype(bf16)
    qkv = (product(normed, weight_qkv) + bias_qkv).astype(bf16)
    mixed, lse = attn_fwd(qkv, 2)
    if staged:
        mixed, lse, rest = tie(mixed, lse, rest)
        weight_up, weight_o, weight_down = place_rest(rest)
    resid = tokens + product(mixed, weight_o) + bias_o
    xhat_two, inverse_two = normalize(resid)
    normed_two = (xhat_two * gain_two + shift_two).astype(bf16)
    branch, grad_normed_two, up_grad, up_bias_grad, down_grad = mlp(
        normed_two, grad_branch, weight_up, bias_up, weight_down
    )
    up_bias_grad = up_bias_grad.reshape(FF_PAD)
    layer_out = weight_img * (resid + branch + bias_down)
    if staged:
        down_sum = lax.psum_scatter(down_grad, "fsdp", scatter_dimension=0, tiled=True)
    grads[9] = jnp.sum(grad_normed_two * xhat_two, axis=0)
    grads[10] = jnp.sum(grad_normed_two, axis=0)
    grad_resid = grad_out + normalize_back(grad_normed_two, gain_two, xhat_two, inverse_two)
    grad_attn = grad_resid.astype(bf16)
    grads[8] = jnp.sum(grad_attn.astype(f32), axis=0)
    o_grad = product_t(mixed, grad_attn).astype(bf16)
    if staged:
        up_grad, o_grad, grad_attn = tie(up_grad, o_grad, grad_attn)
        outer = Reduction(
            (up_grad, o_grad), (((0, 0, UP_CUT),), ((0, UP_CUT, FF_PAD), (1, 0, D))), coords
        )
        outer_other = outer.core_step()
    grad_mixed = product_bt(grad_attn, weight_o).astype(bf16)
    if staged:
        grad_mixed, outer_other = tie(grad_mixed, outer_other)
        outer_far = outer.far_step(outer_other)
    grad_qkv = attn_bwd(qkv, grad_mixed, lse, 2)
    if staged:
        grad_qkv, outer_far = tie(grad_qkv, outer_far)
        outer_near = outer.near_step(outer_far)
    qkv_grad, qkv_bias_grad, norm_sums, tokens_grad = qkv_back(
        grad_qkv, normed, weight_qkv, xhat_one, inverse_one, gain_one.reshape(1, D), grad_resid
    )
    grads[3], grads[6] = qkv_bias_grad[0, :D], qkv_bias_grad[0, 2 * D :]
    grads[0], grads[1] = norm_sums[0], norm_sums[1]
    if staged:
        inner = Reduction((qkv_grad,), (((0, 0, QKV_CUT - EXTRA),),) * 2, coords)
        inner_other = inner.core_step()
        inner_other, outer_near, qkv_grad, norm_sums, qkv_bias_grad = tie(
            inner_other, outer_near, qkv_grad, norm_sums, qkv_bias_grad
        )
        inner = Reduction(
            (qkv_grad, qkv_grad),
            (((0, 0, QKV_CUT - EXTRA), (1, 0, EXTRA)), ((0, QKV_CUT - EXTRA, 3 * D),)),
            coords,
        )
        inner_far = inner.far_step(inner_other, (0, 1), slice(0, 1))
        outer_z = outer.z_step(outer_near)
    grads[12] = trim_hidden(up_bias_grad.reshape(1, FF_PAD)).reshape(FF)

    rows = []
    for i in VECTORS:
        row = grads[i]
        row = jnp.pad(row, (0, widths[i] * devices - row.shape[0]))
        rows.append(row.reshape(devices, widths[i]))
    rows = jnp.concatenate(rows, axis=1)
    owned = [None] * 15
    if staged:
        rows = jnp.pad(rows, ((0, 0), (0, OWN_ROWS * EXTRA - rows.shape[1])))
        rows = rows.reshape(D, EXTRA).astype(bf16)
        inner.matrices[1] = rows.reshape(4, 2, 2, PAIR_TILES, TILE, EXTRA)
        rows_other = Reduction((rows,), None, coords).core_step()
        inner.other = inner_other + rows_other
        rows_far = inner.far_step(inner.other, (0,), slice(1, 2))
        inner_far, rows_far = tie(inner_far, rows_far)
        inner_far = [jnp.concatenate([inner_far[0], rows_far[0]], axis=-1), inner_far[1]]
        inner_near = inner.near_step(inner_far)
        inner_near, outer_z = tie(inner_near, outer_z)
        inner_z = inner.z_step(inner_near)
        inner_z, down_sum = tie(inner_z, down_sum)

        flat = down_sum.astype(f32).reshape(-1)
        size = widths[13]
        lead = flat.shape[0] - size
        got = swap(down_sum.reshape(-1)[size:], 1).astype(f32)
        owned[13] = jnp.where(core == 0, flat[:size], jnp.concatenate([got, flat[: size - lead]]))
        outer_sum = outer.finish(outer_z)
        owned[11] = trim_hidden(outer_sum[:, :FF_PAD]).reshape(-1)
        owned[7] = outer_sum[:, FF_PAD:].reshape(-1)
        inner_sum = inner.finish(inner_z)
        first = QKV_CUT - EXTRA
        owned[2] = inner_sum[:, :D].reshape(-1)
        owned[4] = jnp.concatenate(
            [inner_sum[:, D:first], inner_sum[:, QKV_CUT : 2 * D + EXTRA]], axis=1
        ).reshape(-1)
        owned[5] = inner_sum[:, 2 * D + EXTRA :].reshape(-1)
        small = inner_sum[:, first:QKV_CUT].reshape(-1)
    else:
        scatter = lambda value: lax.psum_scatter(
            value.astype(f32).reshape(-1), "fsdp", scatter_dimension=0, tiled=True
        )
        fill = lambda value, i: jnp.pad(
            value.reshape(-1), (0, widths[i] * devices - value.size)
        )
        for position, i in enumerate((2, 4, 5)):
            owned[i] = scatter(fill(qkv_grad[:, position * D : (position + 1) * D], i))
        owned[7] = scatter(fill(o_grad, 7))
        owned[11] = scatter(fill(trim_hidden(up_grad), 11))
        owned[13] = scatter(fill(trim_hidden(down_grad.T).T, 13))
        small = scatter(rows)
    position = 0
    for i in VECTORS:
        owned[i] = small[position : position + widths[i]]
        position += widths[i]
    return (layer_out, tokens_grad, *owned)


def solution(mesh):
    row, flat = P("fsdp", None), P("fsdp")
    in_specs = (row, flat) + (flat,) * 15 + (row,)
    out_specs = (row, row) + (flat,) * 15
    return jax.shard_map(
        on_device, mesh=mesh, in_specs=in_specs, out_specs=out_specs, check_vma=False
    )
```

```python
import functools
import itertools
import jax
import jax.numpy as jnp
from jax import lax
from jax.sharding import PartitionSpec as P
from jax.experimental import pallas as pl
from jax.experimental.pallas import tpu as pltpu
D=1152; HEADS=16; HEAD_DIM=72; LANES=128
NEG=-1e30
LOG2E=1.4426950408889634
def nt(a,b): return lax.dot_general(a,b,(((1,),(1,)),((),())),preferred_element_type=jnp.float32)
def nn(a,b): return lax.dot_general(a,b,(((1,),(0,)),((),())),preferred_element_type=jnp.float32)

def fill_heads(dst, src, col, tokens, fill):
    rows=dst.shape[1]
    for h in range(HEADS):
        if fill is not None:
            dst[h]=fill
        dst[h,0:tokens,0:HEAD_DIM]=src[:,col+h*HEAD_DIM:col+(h+1)*HEAD_DIM]

def pad_values(rows, tokens, kind):
    lane=lax.broadcasted_iota(jnp.int32,(rows,LANES),1)
    row=lax.broadcasted_iota(jnp.int32,(rows,LANES),0)
    if kind=="query":
        v=jnp.where(lane==HEAD_DIM,1.0,0.0)
    elif kind=="key":
        v=jnp.where((lane==HEAD_DIM)&(row>=tokens),NEG,0.0)
    else:
        v=jnp.zeros((rows,LANES),jnp.float32)
    return v.astype(jnp.bfloat16)

def fwd_kernel(tokens, krows, qrows, per, qkv_ref, mixed_ref, lse_ref, qs, ks, vs, os):
    step=pl.program_id(0)
    @pl.when(step==0)
    def _():
        fill_heads(qs,qkv_ref,0,tokens,pad_values(qrows,tokens,"query"))
        fill_heads(ks,qkv_ref,D,tokens,pad_values(krows,tokens,"key"))
        zero=pad_values(krows,tokens,"value")
        for h in range(HEADS):
            vs[h]=zero
            vs[h,0:tokens,0:HEAD_DIM]=qkv_ref[:,2*D+h*HEAD_DIM:2*D+(h+1)*HEAD_DIM]
    c=HEAD_DIM**-0.5*LOG2E
    for j in range(per):
        h=step*per+j
        s=nt(ks[h],qs[h])
        m=jnp.max(s,axis=0,keepdims=True)
        e=jnp.exp2((s-m)*c)
        l=jnp.sum(e,axis=0,keepdims=True)
        p=(e*(1.0/l)).astype(jnp.bfloat16)
        vt=vs[h].T
        ot=nn(vt,p)
        os[h]=ot.T.astype(jnp.bfloat16)
        lse_ref[j]=m*c+jnp.log2(l)
    @pl.when(step==pl.num_programs(0)-1)
    def _():
        for h in range(HEADS):
            mixed_ref[:,h*HEAD_DIM:(h+1)*HEAD_DIM]=os[h,0:tokens,0:HEAD_DIM]

def attn_fwd(qkv, per=1):
    tokens=qkv.shape[0]
    krows=-(-tokens//16)*16; qrows=-(-tokens//128)*128
    return pl.pallas_call(functools.partial(fwd_kernel,tokens,krows,qrows,per),
        grid=(HEADS//per,),
        in_specs=[pl.BlockSpec(qkv.shape,lambda i:(0,0),pipeline_mode=pl.Buffered(1))],
        out_specs=[pl.BlockSpec((tokens,D),lambda i:(0,0),pipeline_mode=pl.Buffered(1)),pl.BlockSpec((per,1,qrows),lambda i:(i,0,0))],
        out_shape=[jax.ShapeDtypeStruct((tokens,D),jnp.bfloat16),jax.ShapeDtypeStruct((HEADS,1,qrows),jnp.float32)],
        scratch_shapes=[pltpu.VMEM((HEADS,qrows,LANES),jnp.bfloat16),pltpu.VMEM((HEADS,krows,LANES),jnp.bfloat16),
                        pltpu.VMEM((HEADS,krows,LANES),jnp.bfloat16),pltpu.VMEM((HEADS,qrows,LANES),jnp.bfloat16)],
        compiler_params=pltpu.CompilerParams(vmem_limit_bytes=56<<20,dimension_semantics=("arbitrary",)),
        cost_estimate=pl.CostEstimate(flops=4*HEADS*qrows*krows*LANES,bytes_accessed=4*tokens*D*2,transcendentals=HEADS*qrows*krows),
        name="attention_forward")(qkv)

def bwd_kernel(tokens, krows, qrows, per, qkv_ref, go_ref, lse_ref, dqkv_ref, qs, ks, vs, gs):
    step=pl.program_id(0)
    @pl.when(step==0)
    def _():
        fill_heads(qs,qkv_ref,0,tokens,pad_values(qrows,tokens,"query"))
        fill_heads(ks,qkv_ref,D,tokens,pad_values(krows,tokens,"key"))
        fill_heads(vs,qkv_ref,2*D,tokens,pad_values(krows,tokens,"value"))
        fill_heads(gs,go_ref,0,tokens,pad_values(qrows,tokens,"value"))
    scale=HEAD_DIM**-0.5
    c=scale*LOG2E
    for j in range(per):
        h=step*per+j
        q=qs[h]; k=ks[h]; v=vs[h]; g=gs[h]
        s=nt(k,q)
        p=jnp.exp2(s*c-lse_ref[j])
        dp=nt(v,g)
        dv=nn(p.astype(jnp.bfloat16),g)
        delta=jnp.sum(p*dp,axis=0,keepdims=True)
        ds=(p*(dp-delta)).astype(jnp.bfloat16)
        dk=nn(ds,q)*scale
        dqt=nn(k.T,ds)*scale
        qs[h]=dqt.T.astype(jnp.bfloat16)
        ks[h]=dk.astype(jnp.bfloat16)
        vs[h]=dv.astype(jnp.bfloat16)
    @pl.when(step==pl.num_programs(0)-1)
    def _():
        for i,r in enumerate((qs,ks,vs)):
            for h in range(HEADS):
                dqkv_ref[:,i*D+h*HEAD_DIM:i*D+(h+1)*HEAD_DIM]=r[h,0:tokens,0:HEAD_DIM]

def attn_bwd(qkv, gmixed, lse, per=1):
    tokens=qkv.shape[0]
    krows=-(-tokens//16)*16; qrows=-(-tokens//128)*128
    return pl.pallas_call(functools.partial(bwd_kernel,tokens,krows,qrows,per),
        grid=(HEADS//per,),
        in_specs=[pl.BlockSpec(qkv.shape,lambda i:(0,0),pipeline_mode=pl.Buffered(1)),pl.BlockSpec(gmixed.shape,lambda i:(0,0),pipeline_mode=pl.Buffered(1)),
                  pl.BlockSpec((per,1,qrows),lambda i:(i,0,0))],
        out_specs=pl.BlockSpec((tokens,3*D),lambda i:(0,0),pipeline_mode=pl.Buffered(1)),
        out_shape=jax.ShapeDtypeStruct((tokens,3*D),jnp.bfloat16),
        scratch_shapes=[pltpu.VMEM((HEADS,qrows,LANES),jnp.bfloat16),pltpu.VMEM((HEADS,krows,LANES),jnp.bfloat16),
                        pltpu.VMEM((HEADS,krows,LANES),jnp.bfloat16),pltpu.VMEM((HEADS,qrows,LANES),jnp.bfloat16)],
        compiler_params=pltpu.CompilerParams(vmem_limit_bytes=56<<20,dimension_semantics=("arbitrary",)),
        cost_estimate=pl.CostEstimate(flops=1000000,bytes_accessed=1000000,transcendentals=0),
        name="attention_backward")(qkv,gmixed,lse)


GELU_A = 0.7978845608028654
GELU_B = 0.044715


def mlp_kernel(normed_ref, grad_ref, up_ref, bias_ref, down_ref, xhat_ref, inverse_ref, gain_ref,
               grad_out_ref, mixed_ref, output_ref, out_ref, up_grad_ref, bias_grad_ref,
               down_grad_ref, sums_ref, resid_grad_ref, output_grad_ref, mixed_grad_ref,
               normed, normed_t, grad, out, back):
    step = pl.program_id(0)
    tokens = normed_ref.shape[0]

    @pl.when(step == 0)
    def _():
        for held, source in ((normed, normed_ref), (grad, grad_ref)):
            held[...] = jnp.zeros_like(held)
            held[0:tokens] = source[...]
        normed_t[...] = normed[...].T
        out[...] = jnp.zeros_like(out)
        back[...] = jnp.zeros_like(back)

    pre = nn(normed[...], up_ref[...]) + bias_ref[...]
    square = pre * pre
    bend = jnp.tanh(pre * (GELU_A + GELU_A * GELU_B * square))
    hidden = (0.5 * pre * (1.0 + bend)).astype(jnp.bfloat16)
    slope = 0.5 * (1.0 + bend) + 0.5 * pre * (1.0 - bend * bend) * (
        GELU_A + 3.0 * GELU_A * GELU_B * square
    )
    grad_pre = (nt(grad[...], down_ref[...]) * slope).astype(jnp.bfloat16)
    out[...] += nn(hidden, down_ref[...])
    back[...] += nt(grad_pre, up_ref[...])
    down_grad_ref[...] = nn(hidden.T, grad[...]).astype(jnp.bfloat16)
    up_grad_ref[...] = nn(normed_t[...], grad_pre).astype(jnp.bfloat16)
    bias_grad_ref[...] = jnp.sum(grad_pre.astype(jnp.float32), axis=0, keepdims=True)

    @pl.when(step == pl.num_programs(0) - 1)
    def _():
        out_ref[...] = out[0:tokens]
        total = back[0:tokens]
        xhat = xhat_ref[...]
        sums_ref[0:1] = jnp.sum(total * xhat, axis=0, keepdims=True)
        sums_ref[1:2] = jnp.sum(total, axis=0, keepdims=True)
        scaled = total * gain_ref[...]
        first = jnp.mean(scaled, axis=-1, keepdims=True)
        second = jnp.mean(scaled * xhat, axis=-1, keepdims=True)
        resid_grad = grad_out_ref[...] + inverse_ref[...] * (scaled - first - xhat * second)
        resid_grad_ref[...] = resid_grad
        grad[0:tokens] = resid_grad.astype(jnp.bfloat16)
        low = grad[...]
        sums_ref[2:3] = jnp.sum(low.astype(jnp.float32), axis=0, keepdims=True)
        mixed_grad_ref[...] = nt(low, output_ref[...]).astype(jnp.bfloat16)[0:tokens]
        normed[0:tokens] = mixed_ref[...]
        normed_t[...] = normed[...].T
        output_grad_ref[...] = nn(normed_t[...], low).astype(jnp.bfloat16)


def whole_block(shape):
    return pl.BlockSpec(shape, lambda i: (0, 0), pipeline_mode=pl.Buffered(1))


def mlp(normed, grad, up, bias, down, xhat, inverse, gain, grad_out, mixed, output):
    tokens, hidden = normed.shape[0], up.shape[1]
    rows = -(-tokens // 16) * 16
    tile = 256
    full = whole_block((tokens, D))
    columns = pl.BlockSpec((D, tile), lambda i: (0, i))
    line = pl.BlockSpec((1, tile), lambda i: (0, i))
    band = pl.BlockSpec((tile, D), lambda i: (i, 0))
    square = whole_block((D, D))
    return pl.pallas_call(
        mlp_kernel,
        grid=(hidden // tile,),
        in_specs=[full, full, columns, line, band, full, whole_block((tokens, 1)),
                  whole_block((1, D)), full, full, square],
        out_specs=[full, columns, line, band, whole_block((8, D)), full, square, full],
        out_shape=[
            jax.ShapeDtypeStruct((tokens, D), jnp.float32),
            jax.ShapeDtypeStruct((D, hidden), jnp.bfloat16),
            jax.ShapeDtypeStruct((1, hidden), jnp.float32),
            jax.ShapeDtypeStruct((hidden, D), jnp.bfloat16),
            jax.ShapeDtypeStruct((8, D), jnp.float32),
            jax.ShapeDtypeStruct((tokens, D), jnp.float32),
            jax.ShapeDtypeStruct((D, D), jnp.bfloat16),
            jax.ShapeDtypeStruct((tokens, D), jnp.bfloat16),
        ],
        scratch_shapes=[
            pltpu.VMEM((rows, D), jnp.bfloat16),
            pltpu.VMEM((D, rows), jnp.bfloat16),
            pltpu.VMEM((rows, D), jnp.bfloat16),
            pltpu.VMEM((rows, D), jnp.float32),
            pltpu.VMEM((rows, D), jnp.float32),
        ],
        compiler_params=pltpu.CompilerParams(
            vmem_limit_bytes=56 << 20, dimension_semantics=("arbitrary",)
        ),
        cost_estimate=pl.CostEstimate(flops=1000000, bytes_accessed=1000000, transcendentals=0),
        name="mlp_forward_backward",
    )(normed, grad, up, bias, down, xhat, inverse, gain, grad_out, mixed, output)


def qkv_back_kernel(grad_ref, normed_ref, weight_ref, xhat_ref, inverse_ref, gain_ref, resid_ref,
                    weight_grad_ref, bias_grad_ref, sums_ref, tokens_ref, grad, normed_t, total):
    step = pl.program_id(0)
    tokens = normed_ref.shape[0]

    @pl.when(step == 0)
    def _():
        grad[...] = jnp.zeros_like(grad)
        grad[0:tokens] = normed_ref[...]
        normed_t[...] = grad[...].T
        grad[...] = jnp.zeros_like(grad)
        total[...] = jnp.zeros_like(total)

    grad[0:tokens] = grad_ref[...]
    weight_grad_ref[...] = nn(normed_t[...], grad[...]).astype(jnp.bfloat16)
    bias_grad_ref[...] = jnp.sum(grad[...].astype(jnp.float32), axis=0, keepdims=True)
    total[...] += nt(grad[...], weight_ref[...])

    @pl.when(step == pl.num_programs(0) - 1)
    def _():
        back = total[0:tokens]
        xhat = xhat_ref[...]
        sums_ref[0:1] = jnp.sum(back * xhat, axis=0, keepdims=True)
        sums_ref[1:2] = jnp.sum(back, axis=0, keepdims=True)
        scaled = back * gain_ref[...]
        first = jnp.mean(scaled, axis=-1, keepdims=True)
        second = jnp.mean(scaled * xhat, axis=-1, keepdims=True)
        tokens_ref[...] = resid_ref[...] + inverse_ref[...] * (scaled - first - xhat * second)


def qkv_back(grad, normed, weight, xhat, inverse, gain, resid):
    tokens = normed.shape[0]
    rows = -(-tokens // 16) * 16
    whole = lambda shape: pl.BlockSpec(shape, lambda i: (0, 0), pipeline_mode=pl.Buffered(1))
    part = lambda shape: pl.BlockSpec(shape, lambda i: (0, i))
    return pl.pallas_call(
        qkv_back_kernel,
        grid=(3,),
        in_specs=[
            part((tokens, D)),
            whole((tokens, D)),
            part((D, D)),
            whole((tokens, D)),
            whole((tokens, 1)),
            whole((1, D)),
            whole((tokens, D)),
        ],
        out_specs=[part((D, D)), part((1, D)), whole((8, D)), whole((tokens, D))],
        out_shape=[
            jax.ShapeDtypeStruct((D, 3 * D), jnp.bfloat16),
            jax.ShapeDtypeStruct((1, 3 * D), jnp.float32),
            jax.ShapeDtypeStruct((8, D), jnp.float32),
            jax.ShapeDtypeStruct((tokens, D), jnp.float32),
        ],
        scratch_shapes=[
            pltpu.VMEM((rows, D), jnp.bfloat16),
            pltpu.VMEM((D, rows), jnp.bfloat16),
            pltpu.VMEM((rows, D), jnp.float32),
        ],
        compiler_params=pltpu.CompilerParams(
            vmem_limit_bytes=56 << 20, dimension_semantics=("arbitrary",)
        ),
        cost_estimate=pl.CostEstimate(flops=1000000, bytes_accessed=1000000, transcendentals=0),
        name="qkv_backward",
    )(grad, normed, weight, xhat, inverse, gain, resid)


FF = 4304
GROUPS = 16
FF_GROUP = FF // GROUPS
FF_ROWS = 272
FF_PAD = GROUPS * FF_ROWS
PAIR_ROWS = D // GROUPS
HALF_DOWN = FF_ROWS // 2
OWN_ROWS = PAIR_ROWS // 2
TILE = 8
BLOCK_TILES = 5
PAIR_TILES = PAIR_ROWS // TILE
EXTRA = 128
QKV_CUT = 14 * 128
UP_CUT = 22 * 128
UP_PIECES = 4
DOWN_CUT = 72
REST_ROWS = UP_PIECES * BLOCK_TILES * TILE + BLOCK_TILES * TILE
VECTORS = (0, 1, 3, 6, 8, 9, 10, 12, 14)
bf16 = jnp.bfloat16
f32 = jnp.float32


def product(left, right):
    return jnp.dot(left, right, preferred_element_type=f32)


def product_t(left, right):
    return lax.dot_general(left, right, (((0,), (0,)), ((), ())), preferred_element_type=f32)


def product_bt(left, right):
    return lax.dot_general(left, right, (((1,), (1,)), ((), ())), preferred_element_type=f32)


def swap(value, mask):
    devices = lax.axis_size("fsdp")
    return lax.ppermute(value, "fsdp", [(i, i ^ mask) for i in range(devices)])


def pad_hidden(columns):
    rows = columns.shape[0]
    grouped = columns.reshape(rows, GROUPS, FF_GROUP)
    return jnp.pad(grouped, ((0, 0), (0, 0), (0, FF_ROWS - FF_GROUP))).reshape(rows, FF_PAD)


def trim_hidden(columns):
    rows = columns.shape[0]
    return columns.reshape(rows, GROUPS, FF_ROWS)[:, :, :FF_GROUP].reshape(rows, FF)


def place_square_kernel(coords, *refs):
    sources, (whole, small) = refs[:8], refs[8:10]
    held, in_sems, out_sems = refs[10:18], refs[18], refs[19]
    core, x, y, z = coords[0], coords[1], coords[2], coords[3]
    arrivals = [pltpu.make_async_copy(sources[i], held[i], in_sems.at[i]) for i in range(8)]
    for arrival in arrivals:
        arrival.start()
    copies, extras = [], []
    for part, stream in itertools.product(range(4), range(2)):
        arrivals[4 * stream + part].wait()
        for near, dz in itertools.product(range(2), range(4)):
            src = held[4 * stream + part].at[near * 4 + dz]
            owner = core if part < 2 else 1 - core
            far = part % 2
            dx, dy = (near, far) if stream == 0 else (far, near)
            chip = ((z ^ dz) * 2 + (y ^ dy)) * 2 + (x ^ dx)
            cols = src.shape[-1] - (0 if stream else EXTRA)
            col = QKV_CUT - EXTRA if stream else 0
            src_cols = pl.ds(0 if stream else EXTRA, cols)
            first = PAIR_TILES * chip + BLOCK_TILES * owner
            copies.append(
                pltpu.make_async_copy(
                    src.at[pl.ds(owner, BLOCK_TILES - 1), :, src_cols],
                    whole.at[pl.ds(first, BLOCK_TILES - 1), :, pl.ds(col, cols)],
                    out_sems.at[len(copies)],
                )
            )
            copies[-1].start()
            extra = pltpu.make_async_copy(
                src.at[BLOCK_TILES - 1, :, src_cols],
                whole.at[PAIR_TILES * chip + BLOCK_TILES - 1, :, pl.ds(col, cols)],
                out_sems.at[96 + len(extras)],
            )
            pl.when(owner == 0)(extra.start)
            extras.append((owner, extra))
            if stream == 0:
                copies.append(
                    pltpu.make_async_copy(
                        src.at[:, :, :EXTRA], small.at[chip * 2 + owner], out_sems.at[len(copies)]
                    )
                )
                copies[-1].start()
    for copy in copies:
        copy.wait()
    for owner, extra in extras:
        pl.when(owner == 0)(extra.wait)


def place_square(streams, coords):
    sources = [s.reshape(8, BLOCK_TILES, TILE, -1) for s in (*streams[0], *streams[1])]
    size = sum(s.size for s in sources) * 2
    whole, small = pl.pallas_call(
        place_square_kernel,
        in_specs=[pl.BlockSpec(memory_space=pltpu.SMEM)]
        + [pl.BlockSpec(memory_space=pltpu.HBM)] * 8,
        out_specs=[pl.BlockSpec(memory_space=pltpu.HBM)] * 2,
        out_shape=[
            jax.ShapeDtypeStruct((GROUPS * PAIR_TILES, TILE, 3 * D), bf16),
            jax.ShapeDtypeStruct((2 * GROUPS, BLOCK_TILES, TILE, EXTRA), bf16),
        ],
        scratch_shapes=[pltpu.VMEM(s.shape, bf16) for s in sources]
        + [pltpu.SemaphoreType.DMA((8,)), pltpu.SemaphoreType.DMA((160,))],
        compiler_params=pltpu.CompilerParams(vmem_limit_bytes=40 << 20),
        cost_estimate=pl.CostEstimate(flops=0, bytes_accessed=2 * size, transcendentals=0),
        name="place_square",
    )(coords, *sources)
    return whole.reshape(D, 3 * D), small.reshape(2 * GROUPS, -1)


def place_rest_kernel(source, up, out, held, in_sems, out_sems):
    arrivals = [
        pltpu.make_async_copy(source.at[i], held.at[i], in_sems.at[i]) for i in range(2 * GROUPS)
    ]
    for arrival in arrivals:
        arrival.start()
    copies = []
    for device in range(2 * GROUPS):
        chip, owner = device // 2, device % 2
        src = held.at[device]
        arrivals[device].wait()
        jobs = []
        count = BLOCK_TILES - owner
        first = PAIR_TILES * chip + BLOCK_TILES * owner
        for piece in range(UP_PIECES):
            cols = min(D, FF_PAD - piece * D)
            jobs.append(
                (
                    src.at[pl.ds(piece * BLOCK_TILES + owner, count), :, pl.ds(0, cols)],
                    up.at[pl.ds(first, count), :, pl.ds(piece * D, cols)],
                )
            )
        base = UP_PIECES * BLOCK_TILES
        jobs.append((src.at[pl.ds(base + owner, count)], out.at[pl.ds(first, count)]))
        for one, other in jobs:
            copies.append(pltpu.make_async_copy(one, other, out_sems.at[len(copies)]))
            copies[-1].start()
    for copy in copies:
        copy.wait()


def place_rest(gathered):
    source = gathered.reshape(2 * GROUPS, REST_ROWS // TILE, TILE, D)
    up, out = pl.pallas_call(
        place_rest_kernel,
        in_specs=[pl.BlockSpec(memory_space=pltpu.HBM)],
        out_specs=[pl.BlockSpec(memory_space=pltpu.HBM)] * 2,
        out_shape=[
            jax.ShapeDtypeStruct((D // TILE, TILE, FF_PAD), bf16),
            jax.ShapeDtypeStruct((D // TILE, TILE, D), bf16),
        ],
        scratch_shapes=[
            pltpu.VMEM(source.shape, bf16),
            pltpu.SemaphoreType.DMA((2 * GROUPS,)),
            pltpu.SemaphoreType.DMA((2 * GROUPS * (UP_PIECES + 1),)),
        ],
        compiler_params=pltpu.CompilerParams(vmem_limit_bytes=56 << 20),
        cost_estimate=pl.CostEstimate(
            flops=0, bytes_accessed=4 * source.size, transcendentals=0
        ),
        name="place_rest",
    )(source)
    return up.reshape(D, FF_PAD), out.reshape(D, D)


def place_down_kernel(coords, *refs):
    sources, whole = refs[:8], refs[8]
    held, in_sems, out_sems = refs[9:17], refs[17], refs[18]
    core, x, y, z = coords[0], coords[1], coords[2], coords[3]
    arrivals = [pltpu.make_async_copy(sources[i], held[i], in_sems.at[i]) for i in range(8)]
    for arrival in arrivals:
        arrival.start()
    copies = []
    for part, stream in itertools.product(range(4), range(2)):
        arrivals[4 * stream + part].wait()
        for near, dz in itertools.product(range(2), range(4)):
            src = held[4 * stream + part].at[near * 4 + dz]
            owner = core if part < 2 else 1 - core
            far = part % 2
            dx, dy = (near, far) if stream == 0 else (far, near)
            chip = ((z ^ dz) * 2 + (y ^ dy)) * 2 + (x ^ dx)
            first = DOWN_CUT // TILE if stream else 0
            dst = whole.at[chip * 2 + owner, first : first + src.shape[0]]
            copies.append(pltpu.make_async_copy(src, dst, out_sems.at[len(copies)]))
            copies[-1].start()
    for copy in copies:
        copy.wait()


def place_down(streams, coords):
    sources = [s.reshape(8, -1, TILE, D) for s in (*streams[0], *streams[1])]
    size = sum(s.size for s in sources) * 2
    return pl.pallas_call(
        place_down_kernel,
        in_specs=[pl.BlockSpec(memory_space=pltpu.SMEM)]
        + [pl.BlockSpec(memory_space=pltpu.HBM)] * 8,
        out_specs=pl.BlockSpec(memory_space=pltpu.HBM),
        out_shape=jax.ShapeDtypeStruct((2 * GROUPS, HALF_DOWN // TILE, TILE, D), bf16),
        scratch_shapes=[pltpu.VMEM(s.shape, bf16) for s in sources]
        + [pltpu.SemaphoreType.DMA((8,)), pltpu.SemaphoreType.DMA((64,))],
        compiler_params=pltpu.CompilerParams(vmem_limit_bytes=40 << 20),
        cost_estimate=pl.CostEstimate(flops=0, bytes_accessed=2 * size, transcendentals=0),
        name="place_down",
    )(coords, *sources).reshape(FF_PAD, D)


def tie(*values):
    leaves, form = jax.tree.flatten(values)
    return form.unflatten(lax.optimization_barrier(leaves))


def gather_z(block):
    return [block] + [swap(block, 8 * step) for step in (1, 2, 3)]


def gather_near(parts, cut, axis):
    streams = []
    for stream in range(2):
        if axis == 1:
            own = jnp.stack([p[:, :cut] if stream == 0 else p[:, cut:] for p in parts])
        else:
            own = jnp.stack([p[:cut] if stream == 0 else p[cut:] for p in parts])
        streams.append((own, swap(own, 4 if stream else 2)))
    return streams


def gather_far(streams):
    results = []
    for stream in range(2):
        first = jnp.concatenate(streams[stream])
        results.append((first, swap(first, 2 if stream else 4)))
    return results


def gather_core(streams):
    return [(first, second, swap(first, 1), swap(second, 1)) for first, second in streams]


def window(value, starts, sizes):
    rank = value.ndim
    starts = list(starts) + [0] * (rank - len(starts))
    lengths = list(value.shape)
    for axis, size in enumerate(sizes):
        if size is not None:
            lengths[axis] = size
    starts = [jnp.int32(0) if start is None else jnp.int32(start) for start in starts]
    result = lax.dynamic_slice(value, starts, lengths)
    kept = [
        length for axis, length in enumerate(lengths) if axis >= len(sizes) or sizes[axis] != 1
    ]
    return result.reshape(kept)


class Reduction:
    def __init__(self, matrices, streams, coords):
        self.matrices = [m.reshape(4, 2, 2, PAIR_TILES, TILE, -1) for m in matrices]
        self.streams = streams
        self.coords = coords

    def part(self, arrays, stream, plane, tile):
        sizes = tuple(None if p is None else 1 for p in plane) + (BLOCK_TILES, None)
        pieces = []
        for number, first, last in self.streams[stream]:
            starts = tuple(plane) + (tile, None, first)
            pieces.append(window(arrays[number], starts, sizes + (last - first,)))
        return pieces[0] if len(pieces) == 1 else jnp.concatenate(pieces, axis=-1)

    def terms(self, stream, plane):
        tile = self.coords[0] * (PAIR_TILES - BLOCK_TILES)
        own = self.part(self.matrices, stream, plane, tile)
        return [own, self.part(self.other, stream, plane, 0)]

    def core_step(self):
        tile = (1 - self.coords[0]) * (PAIR_TILES - BLOCK_TILES)
        starts, sizes = (None, None, None, tile), (None, None, None, BLOCK_TILES)
        return [swap(window(m, starts, sizes), 1) for m in self.matrices]

    def far_step(self, other, streams=(0, 1), pieces=slice(None)):
        core, x, y, z = self.coords
        self.other = other
        got = []
        every = self.streams
        for stream in streams:
            plane = (None, None, 1 - x) if stream else (None, 1 - y, None)
            self.streams = {stream: every[stream][pieces]}
            send = total_of(self.terms(stream, plane)).astype(bf16)
            got.append(swap(send, 2 if stream else 4))
        self.streams = every
        return got

    def near_step(self, far):
        core, x, y, z = self.coords
        self.far = far
        got = []
        for stream in range(2):
            plane = (None, 1 - y, x) if stream else (None, y, 1 - x)
            after = (None, 1 - y) if stream else (None, 1 - x)
            terms = self.terms(stream, plane) + [window(far[stream], after, (None, 1))]
            got.append(swap(total_of(terms).astype(bf16), 4 if stream else 2))
        return got

    def at(self, plane):
        core, x, y, z = self.coords
        pieces = []
        for stream in range(2):
            after = (plane, y) if stream else (plane, x)
            terms = self.terms(stream, (plane, y, x)) + [
                window(self.far[stream], after, (1, 1)),
                window(self.near[stream], (plane,), (1,)),
            ]
            pieces.append(total_of(terms))
        return jnp.concatenate(pieces, axis=-1)

    def z_step(self, near):
        z = self.coords[3]
        self.near = near
        return [swap(self.at(z ^ step).astype(bf16), 8 * step) for step in (1, 2, 3)]

    def finish(self, arrived):
        core, x, y, z = self.coords
        total = total_of([self.at(z)] + arrived)
        total = total.reshape(BLOCK_TILES * TILE, -1)
        return lax.dynamic_slice_in_dim(
            total, core * (BLOCK_TILES * TILE - OWN_ROWS), OWN_ROWS, 0
        )


def total_of(terms):
    total = terms[0].astype(f32)
    for term in terms[1:]:
        total = total + term.astype(f32)
    return total


def fetch_pairs(narrow, core):
    q, k, v, o = (narrow[i].reshape(OWN_ROWS, D) for i in (2, 4, 5, 7))
    up = pad_hidden(narrow[11].reshape(OWN_ROWS, FF))
    down = narrow[13]
    rows = jnp.concatenate([q, k, v, o, up], axis=1)
    spare = BLOCK_TILES * TILE - OWN_ROWS
    lead = D * HALF_DOWN - down.shape[0]
    tail = jnp.pad(down[:lead].reshape(spare, -1), ((0, 0), (0, 512 - lead // spare)))
    is_first = core == 0
    edge = jnp.where(is_first, rows[OWN_ROWS - spare :], rows[:spare])
    got = swap(jnp.concatenate([edge, tail], axis=1), 1)
    edge = got[:, : rows.shape[1]]
    block = jnp.where(is_first, jnp.concatenate([rows, edge]), jnp.concatenate([edge, rows]))
    extra = got[:, rows.shape[1] : rows.shape[1] + lead // spare].reshape(-1)
    end = jnp.zeros((D * HALF_DOWN - (down.shape[0] - lead),), bf16)
    down_block = jnp.where(
        is_first, jnp.concatenate([down, extra]), jnp.concatenate([down[lead:], end])
    ).reshape(HALF_DOWN, D)
    small = jnp.concatenate([narrow[i] for i in VECTORS])
    small = jnp.pad(small, (0, BLOCK_TILES * TILE * EXTRA - small.shape[0]))
    small = small.reshape(BLOCK_TILES * TILE, EXTRA)
    square = jnp.concatenate([small, block[:, : 3 * D]], axis=1)
    up_block = jnp.pad(block[:, 4 * D :], ((0, 0), (0, UP_PIECES * D - FF_PAD)))
    pieces = [up_block[:, i * D : (i + 1) * D] for i in range(UP_PIECES)]
    rest = jnp.concatenate(pieces + [block[:, 3 * D : 4 * D]])
    return square, rest, down_block


def normalize(values):
    centre = jnp.mean(values, axis=-1, keepdims=True)
    centered = values - centre
    spread_sq = jnp.mean(centered * centered, axis=-1, keepdims=True)
    inverse = lax.rsqrt(spread_sq + 1e-06)
    return centered * inverse, inverse


def normalize_back(grad, gain, xhat, inverse):
    scaled = grad * gain
    first = jnp.mean(scaled, axis=-1, keepdims=True)
    second = jnp.mean(scaled * xhat, axis=-1, keepdims=True)
    return inverse * (scaled - first - xhat * second)


def name_vectors(whole, widths):
    found = {}
    position = 0
    for i in VECTORS:
        found[i] = whole[:, position : position + widths[i]].reshape(-1).astype(f32)
        position += widths[i]
    return found


def gather_plain(narrow, widths):
    whole = {
        i: lax.all_gather(narrow[i], "fsdp", axis=0, tiled=True) for i in (2, 4, 5, 7, 11, 13)
    }
    square = [whole[i][: D * D].reshape(D, D) for i in (2, 4, 5, 7)]
    up = pad_hidden(whole[11][: D * FF].reshape(D, FF))
    down = pad_hidden(whole[13][: D * FF].reshape(FF, D).T).T
    joined = jnp.concatenate([narrow[i] for i in VECTORS])
    length = joined.shape[0]
    joined = jnp.pad(joined, (0, 2048 - length)).reshape(16, 128)
    joined = lax.all_gather(joined, "fsdp", axis=0, tiled=True).reshape(-1, 2048)
    return jnp.concatenate(square[:3], axis=1), square[3], up, down, name_vectors(joined, widths)


def on_device(*args):
    devices = lax.axis_size("fsdp")
    tokens, image_valid = args[0], args[1]
    shards = args[2:17]
    cotangent = args[17]
    staged = devices == 32
    widths = [piece.shape[0] for piece in shards]
    narrow = [piece.astype(bf16) for piece in shards]
    index = lax.axis_index("fsdp")
    core, x, y, z = index % 2, (index // 2) % 2, (index // 4) % 2, index // 8
    coords = (core, x, y, z)
    image_count = image_valid.shape[0]
    seq_len = tokens.shape[0] // image_count
    weight_img = jnp.repeat(image_valid.astype(f32), seq_len)[:, None]

    grad_out = weight_img * cotangent
    grad_branch = grad_out.astype(bf16)
    grads = {14: jnp.sum(grad_branch.astype(f32), axis=0)}
    xhat_one, inverse_one = normalize(tokens)
    if staged:
        where = jnp.stack(coords).astype(jnp.int32)
        sq, rest, down = fetch_pairs(narrow, core)
        rest = lax.all_gather(rest, "fsdp", axis=0, tiled=True)
        sq = gather_z(sq)
        sq, down, xhat_one, inverse_one, grad_branch = tie(
            sq, down, xhat_one, inverse_one, grad_branch
        )
        sq = gather_near(sq, QKV_CUT, 1)
        down = gather_z(down)
        sq = gather_far(sq)
        sq, down = tie(sq, down)
        sq = gather_core(sq)
        down = gather_near(down, DOWN_CUT, 0)
        weight_qkv, small = place_square(sq, where)
        vectors = name_vectors(small, widths)
    else:
        weight_qkv, weight_o, weight_up, weight_down, vectors = gather_plain(narrow, widths)

    vec = lambda i: vectors[i][:D]
    gain_one, shift_one, gain_two, shift_two = vec(0), vec(1), vec(9), vec(10)
    bias_qkv = jnp.concatenate([vec(3), jnp.zeros((D,), f32), vec(6)])
    bias_o, bias_down = vec(8), vec(14)
    bias_up = pad_hidden(vectors[12][:FF].reshape(1, FF))

    normed = (xhat_one * gain_one + shift_one).astype(bf16)
    qkv = (product(normed, weight_qkv) + bias_qkv).astype(bf16)
    if staged:
        qkv, down = tie(qkv, down)
        down = gather_far(down)
    mixed, lse = attn_fwd(qkv, 2)
    if staged:
        mixed, lse, rest, down = tie(mixed, lse, rest, down)
        down = gather_core(down)
        weight_up, weight_o = place_rest(rest)
    resid = tokens + product(mixed, weight_o) + bias_o
    xhat_two, inverse_two = normalize(resid)
    normed_two = (xhat_two * gain_two + shift_two).astype(bf16)
    if staged:
        normed_two, down = tie(normed_two, down)
        weight_down = place_down(down, where)
    branch, up_grad, up_bias_grad, down_grad, sums_two, grad_resid, o_grad, grad_mixed = mlp(
        normed_two,
        grad_branch,
        weight_up,
        bias_up,
        weight_down,
        xhat_two,
        inverse_two,
        gain_two.reshape(1, D),
        grad_out,
        mixed,
        weight_o,
    )
    up_bias_grad = up_bias_grad.reshape(FF_PAD)
    layer_out = weight_img * (resid + branch + bias_down)
    grads[9], grads[10], grads[8] = sums_two[0], sums_two[1], sums_two[2]
    if staged:
        down_sum = lax.psum_scatter(down_grad, "fsdp", scatter_dimension=0, tiled=True)
    if staged:
        outer = Reduction(
            (up_grad, o_grad), (((0, 0, UP_CUT),), ((0, UP_CUT, FF_PAD), (1, 0, D))), coords
        )
        outer_other = outer.core_step()
    if staged:
        grad_mixed, outer_other = tie(grad_mixed, outer_other)
        outer_far = outer.far_step(outer_other)
    grad_qkv = attn_bwd(qkv, grad_mixed, lse, 2)
    if staged:
        grad_qkv, outer_far = tie(grad_qkv, outer_far)
        outer_near = outer.near_step(outer_far)
    qkv_grad, qkv_bias_grad, norm_sums, tokens_grad = qkv_back(
        grad_qkv, normed, weight_qkv, xhat_one, inverse_one, gain_one.reshape(1, D), grad_resid
    )
    grads[3], grads[6] = qkv_bias_grad[0, :D], qkv_bias_grad[0, 2 * D :]
    grads[0], grads[1] = norm_sums[0], norm_sums[1]
    if staged:
        inner = Reduction((qkv_grad,), (((0, 0, QKV_CUT - EXTRA),),) * 2, coords)
        inner_other = inner.core_step()
        inner_other, outer_near, qkv_grad, norm_sums, qkv_bias_grad = tie(
            inner_other, outer_near, qkv_grad, norm_sums, qkv_bias_grad
        )
        inner = Reduction(
            (qkv_grad, qkv_grad),
            (((0, 0, QKV_CUT - EXTRA), (1, 0, EXTRA)), ((0, QKV_CUT - EXTRA, 3 * D),)),
            coords,
        )
        inner_far = inner.far_step(inner_other, (0, 1), slice(0, 1))
        outer_z = outer.z_step(outer_near)
    grads[12] = trim_hidden(up_bias_grad.reshape(1, FF_PAD)).reshape(FF)

    rows = []
    for i in VECTORS:
        row = grads[i]
        row = jnp.pad(row, (0, widths[i] * devices - row.shape[0]))
        rows.append(row.reshape(devices, widths[i]))
    rows = jnp.concatenate(rows, axis=1)
    owned = [None] * 15
    if staged:
        rows = jnp.pad(rows, ((0, 0), (0, OWN_ROWS * EXTRA - rows.shape[1])))
        rows = rows.reshape(D, EXTRA).astype(bf16)
        inner.matrices[1] = rows.reshape(4, 2, 2, PAIR_TILES, TILE, EXTRA)
        rows_other = Reduction((rows,), None, coords).core_step()
        inner.other = inner_other + rows_other
        rows_far = inner.far_step(inner.other, (0,), slice(1, 2))
        inner_far, rows_far = tie(inner_far, rows_far)
        inner_far = [jnp.concatenate([inner_far[0], rows_far[0]], axis=-1), inner_far[1]]
        inner_near = inner.near_step(inner_far)
        inner_near, outer_z = tie(inner_near, outer_z)
        inner_z = inner.z_step(inner_near)
        inner_near, down_sum = tie(inner_near, down_sum)

        flat = down_sum.astype(f32).reshape(-1)
        size = widths[13]
        lead = flat.shape[0] - size
        got = swap(down_sum.reshape(-1)[size:], 1).astype(f32)
        owned[13] = jnp.where(core == 0, flat[:size], jnp.concatenate([got, flat[: size - lead]]))
        outer_sum = outer.finish(outer_z)
        owned[11] = trim_hidden(outer_sum[:, :FF_PAD]).reshape(-1)
        owned[7] = outer_sum[:, FF_PAD:].reshape(-1)
        inner_sum = inner.finish(inner_z)
        first = QKV_CUT - EXTRA
        owned[2] = inner_sum[:, :D].reshape(-1)
        owned[4] = jnp.concatenate(
            [inner_sum[:, D:first], inner_sum[:, QKV_CUT : 2 * D + EXTRA]], axis=1
        ).reshape(-1)
        owned[5] = inner_sum[:, 2 * D + EXTRA :].reshape(-1)
        small = inner_sum[:, first:QKV_CUT].reshape(-1)
    else:
        scatter = lambda value: lax.psum_scatter(
            value.astype(f32).reshape(-1), "fsdp", scatter_dimension=0, tiled=True
        )
        fill = lambda value, i: jnp.pad(
            value.reshape(-1), (0, widths[i] * devices - value.size)
        )
        for position, i in enumerate((2, 4, 5)):
            owned[i] = scatter(fill(qkv_grad[:, position * D : (position + 1) * D], i))
        owned[7] = scatter(fill(o_grad, 7))
        owned[11] = scatter(fill(trim_hidden(up_grad), 11))
        owned[13] = scatter(fill(trim_hidden(down_grad.T).T, 13))
        small = scatter(rows)
    position = 0
    for i in VECTORS:
        owned[i] = small[position : position + widths[i]]
        position += widths[i]
    return (layer_out, tokens_grad, *owned)


def solution(mesh):
    row, flat = P("fsdp", None), P("fsdp")
    in_specs = (row, flat) + (flat,) * 15 + (row,)
    out_specs = (row, row) + (flat,) * 15
    return jax.shard_map(
        on_device, mesh=mesh, in_specs=in_specs, out_specs=out_specs, check_vma=False
    )
```

```python
import functools
import itertools
import jax
import jax.numpy as jnp
from jax import lax
from jax.sharding import PartitionSpec as P
from jax.experimental import pallas as pl
from jax.experimental.pallas import tpu as pltpu
D=1152; HEADS=16; HEAD_DIM=72; LANES=128
NEG=-1e30
LOG2E=1.4426950408889634
def nt(a,b): return lax.dot_general(a,b,(((1,),(1,)),((),())),preferred_element_type=jnp.float32)
def nn(a,b): return lax.dot_general(a,b,(((1,),(0,)),((),())),preferred_element_type=jnp.float32)

def fill_heads(dst, src, col, tokens, fill):
    rows=dst.shape[1]
    for h in range(HEADS):
        if fill is not None:
            dst[h]=fill
        dst[h,0:tokens,0:HEAD_DIM]=src[:,col+h*HEAD_DIM:col+(h+1)*HEAD_DIM]

def pad_values(rows, tokens, kind):
    lane=lax.broadcasted_iota(jnp.int32,(rows,LANES),1)
    row=lax.broadcasted_iota(jnp.int32,(rows,LANES),0)
    if kind=="query":
        v=jnp.where(lane==HEAD_DIM,1.0,0.0)
    elif kind=="key":
        v=jnp.where((lane==HEAD_DIM)&(row>=tokens),NEG,0.0)
    else:
        v=jnp.zeros((rows,LANES),jnp.float32)
    return v.astype(jnp.bfloat16)

def fwd_kernel(tokens, krows, qrows, per, qkv_ref, mixed_ref, lse_ref, qs, ks, vs, os):
    step=pl.program_id(0)
    @pl.when(step==0)
    def _():
        fill_heads(qs,qkv_ref,0,tokens,pad_values(qrows,tokens,"query"))
        fill_heads(ks,qkv_ref,D,tokens,pad_values(krows,tokens,"key"))
        zero=pad_values(krows,tokens,"value")
        for h in range(HEADS):
            vs[h]=zero
            vs[h,0:tokens,0:HEAD_DIM]=qkv_ref[:,2*D+h*HEAD_DIM:2*D+(h+1)*HEAD_DIM]
    c=HEAD_DIM**-0.5*LOG2E
    for j in range(per):
        h=step*per+j
        s=nt(ks[h],qs[h])
        m=jnp.max(s,axis=0,keepdims=True)
        e=jnp.exp2((s-m)*c)
        l=jnp.sum(e,axis=0,keepdims=True)
        p=(e*(1.0/l)).astype(jnp.bfloat16)
        vt=vs[h].T
        ot=nn(vt,p)
        os[h]=ot.T.astype(jnp.bfloat16)
        lse_ref[j]=m*c+jnp.log2(l)
    @pl.when(step==pl.num_programs(0)-1)
    def _():
        for h in range(HEADS):
            mixed_ref[:,h*HEAD_DIM:(h+1)*HEAD_DIM]=os[h,0:tokens,0:HEAD_DIM]

def attn_fwd(qkv, per=1):
    tokens=qkv.shape[0]
    krows=-(-tokens//16)*16; qrows=-(-tokens//128)*128
    return pl.pallas_call(functools.partial(fwd_kernel,tokens,krows,qrows,per),
        grid=(HEADS//per,),
        in_specs=[pl.BlockSpec(qkv.shape,lambda i:(0,0),pipeline_mode=pl.Buffered(1))],
        out_specs=[pl.BlockSpec((tokens,D),lambda i:(0,0),pipeline_mode=pl.Buffered(1)),pl.BlockSpec((per,1,qrows),lambda i:(i,0,0))],
        out_shape=[jax.ShapeDtypeStruct((tokens,D),jnp.bfloat16),jax.ShapeDtypeStruct((HEADS,1,qrows),jnp.float32)],
        scratch_shapes=[pltpu.VMEM((HEADS,qrows,LANES),jnp.bfloat16),pltpu.VMEM((HEADS,krows,LANES),jnp.bfloat16),
                        pltpu.VMEM((HEADS,krows,LANES),jnp.bfloat16),pltpu.VMEM((HEADS,qrows,LANES),jnp.bfloat16)],
        compiler_params=pltpu.CompilerParams(vmem_limit_bytes=56<<20,dimension_semantics=("arbitrary",)),
        cost_estimate=pl.CostEstimate(flops=4*HEADS*qrows*krows*LANES,bytes_accessed=4*tokens*D*2,transcendentals=HEADS*qrows*krows),
        name="attention_forward")(qkv)

def bwd_kernel(tokens, krows, qrows, per, qkv_ref, go_ref, lse_ref, dqkv_ref, qs, ks, vs, gs):
    step=pl.program_id(0)
    @pl.when(step==0)
    def _():
        fill_heads(qs,qkv_ref,0,tokens,pad_values(qrows,tokens,"query"))
        fill_heads(ks,qkv_ref,D,tokens,pad_values(krows,tokens,"key"))
        fill_heads(vs,qkv_ref,2*D,tokens,pad_values(krows,tokens,"value"))
        fill_heads(gs,go_ref,0,tokens,pad_values(qrows,tokens,"value"))
    scale=HEAD_DIM**-0.5
    c=scale*LOG2E
    for j in range(per):
        h=step*per+j
        q=qs[h]; k=ks[h]; v=vs[h]; g=gs[h]
        s=nt(k,q)
        p=jnp.exp2(s*c-lse_ref[j])
        dp=nt(v,g)
        dv=nn(p.astype(jnp.bfloat16),g)
        delta=jnp.sum(p*dp,axis=0,keepdims=True)
        ds=(p*(dp-delta)).astype(jnp.bfloat16)
        dk=nn(ds,q)*scale
        dqt=nn(k.T,ds)*scale
        qs[h]=dqt.T.astype(jnp.bfloat16)
        ks[h]=dk.astype(jnp.bfloat16)
        vs[h]=dv.astype(jnp.bfloat16)
    @pl.when(step==pl.num_programs(0)-1)
    def _():
        for i,r in enumerate((qs,ks,vs)):
            for h in range(HEADS):
                dqkv_ref[:,i*D+h*HEAD_DIM:i*D+(h+1)*HEAD_DIM]=r[h,0:tokens,0:HEAD_DIM]

def attn_bwd(qkv, gmixed, lse, per=1):
    tokens=qkv.shape[0]
    krows=-(-tokens//16)*16; qrows=-(-tokens//128)*128
    return pl.pallas_call(functools.partial(bwd_kernel,tokens,krows,qrows,per),
        grid=(HEADS//per,),
        in_specs=[pl.BlockSpec(qkv.shape,lambda i:(0,0),pipeline_mode=pl.Buffered(1)),pl.BlockSpec(gmixed.shape,lambda i:(0,0),pipeline_mode=pl.Buffered(1)),
                  pl.BlockSpec((per,1,qrows),lambda i:(i,0,0))],
        out_specs=pl.BlockSpec((tokens,3*D),lambda i:(0,0),pipeline_mode=pl.Buffered(1)),
        out_shape=jax.ShapeDtypeStruct((tokens,3*D),jnp.bfloat16),
        scratch_shapes=[pltpu.VMEM((HEADS,qrows,LANES),jnp.bfloat16),pltpu.VMEM((HEADS,krows,LANES),jnp.bfloat16),
                        pltpu.VMEM((HEADS,krows,LANES),jnp.bfloat16),pltpu.VMEM((HEADS,qrows,LANES),jnp.bfloat16)],
        compiler_params=pltpu.CompilerParams(vmem_limit_bytes=56<<20,dimension_semantics=("arbitrary",)),
        cost_estimate=pl.CostEstimate(flops=1000000,bytes_accessed=1000000,transcendentals=0),
        name="attention_backward")(qkv,gmixed,lse)


GELU_A = 0.7978845608028654
GELU_B = 0.044715


def mlp_kernel(normed_ref, grad_ref, up_ref, bias_ref, down_ref, xhat_ref, inverse_ref, gain_ref,
               grad_out_ref, mixed_ref, output_ref, out_ref, up_grad_ref, bias_grad_ref,
               down_grad_ref, sums_ref, resid_grad_ref, output_grad_ref, mixed_grad_ref,
               normed, normed_t, grad, out, back):
    step = pl.program_id(0)
    tokens = normed_ref.shape[0]

    @pl.when(step == 0)
    def _():
        for held, source in ((normed, normed_ref), (grad, grad_ref)):
            held[...] = jnp.zeros_like(held)
            held[0:tokens] = source[...]
        normed_t[...] = normed[...].T
        out[...] = jnp.zeros_like(out)
        back[...] = jnp.zeros_like(back)

    pre = nn(normed[...], up_ref[...]) + bias_ref[...]
    square = pre * pre
    bend = jnp.tanh(pre * (GELU_A + GELU_A * GELU_B * square))
    hidden = (0.5 * pre * (1.0 + bend)).astype(jnp.bfloat16)
    slope = 0.5 * (1.0 + bend) + 0.5 * pre * (1.0 - bend * bend) * (
        GELU_A + 3.0 * GELU_A * GELU_B * square
    )
    grad_pre = (nt(grad[...], down_ref[...]) * slope).astype(jnp.bfloat16)
    out[...] += nn(hidden, down_ref[...])
    back[...] += nt(grad_pre, up_ref[...])
    down_grad_ref[...] = nn(hidden.T, grad[...]).astype(jnp.bfloat16)
    up_grad_ref[...] = nn(normed_t[...], grad_pre).astype(jnp.bfloat16)
    bias_grad_ref[...] = jnp.sum(grad_pre.astype(jnp.float32), axis=0, keepdims=True)

    @pl.when(step == pl.num_programs(0) - 1)
    def _():
        out_ref[...] = out[0:tokens]
        total = back[0:tokens]
        xhat = xhat_ref[...]
        sums_ref[0:1] = jnp.sum(total * xhat, axis=0, keepdims=True)
        sums_ref[1:2] = jnp.sum(total, axis=0, keepdims=True)
        scaled = total * gain_ref[...]
        first = jnp.mean(scaled, axis=-1, keepdims=True)
        second = jnp.mean(scaled * xhat, axis=-1, keepdims=True)
        resid_grad = grad_out_ref[...] + inverse_ref[...] * (scaled - first - xhat * second)
        resid_grad_ref[...] = resid_grad
        grad[0:tokens] = resid_grad.astype(jnp.bfloat16)
        low = grad[...]
        sums_ref[2:3] = jnp.sum(low.astype(jnp.float32), axis=0, keepdims=True)
        mixed_grad_ref[...] = nt(low, output_ref[...]).astype(jnp.bfloat16)[0:tokens]
        normed[0:tokens] = mixed_ref[...]
        normed_t[...] = normed[...].T
        output_grad_ref[...] = nn(normed_t[...], low).astype(jnp.bfloat16)


def whole_block(shape):
    return pl.BlockSpec(shape, lambda i: (0, 0), pipeline_mode=pl.Buffered(1))


def mlp(normed, grad, up, bias, down, xhat, inverse, gain, grad_out, mixed, output):
    tokens, hidden = normed.shape[0], up.shape[1]
    rows = -(-tokens // 16) * 16
    tile = 256
    full = whole_block((tokens, D))
    columns = pl.BlockSpec((D, tile), lambda i: (0, i))
    line = pl.BlockSpec((1, tile), lambda i: (0, i))
    band = pl.BlockSpec((tile, D), lambda i: (i, 0))
    square = whole_block((D, D))
    return pl.pallas_call(
        mlp_kernel,
        grid=(hidden // tile,),
        in_specs=[full, full, columns, line, band, full, whole_block((tokens, 1)),
                  whole_block((1, D)), full, full, square],
        out_specs=[full, columns, line, band, whole_block((8, D)), full, square, full],
        out_shape=[
            jax.ShapeDtypeStruct((tokens, D), jnp.float32),
            jax.ShapeDtypeStruct((D, hidden), jnp.bfloat16),
            jax.ShapeDtypeStruct((1, hidden), jnp.float32),
            jax.ShapeDtypeStruct((hidden, D), jnp.bfloat16),
            jax.ShapeDtypeStruct((8, D), jnp.float32),
            jax.ShapeDtypeStruct((tokens, D), jnp.float32),
            jax.ShapeDtypeStruct((D, D), jnp.bfloat16),
            jax.ShapeDtypeStruct((tokens, D), jnp.bfloat16),
        ],
        scratch_shapes=[
            pltpu.VMEM((rows, D), jnp.bfloat16),
            pltpu.VMEM((D, rows), jnp.bfloat16),
            pltpu.VMEM((rows, D), jnp.bfloat16),
            pltpu.VMEM((rows, D), jnp.float32),
            pltpu.VMEM((rows, D), jnp.float32),
        ],
        compiler_params=pltpu.CompilerParams(
            vmem_limit_bytes=56 << 20, dimension_semantics=("arbitrary",)
        ),
        cost_estimate=pl.CostEstimate(flops=1000000, bytes_accessed=1000000, transcendentals=0),
        name="mlp_forward_backward",
    )(normed, grad, up, bias, down, xhat, inverse, gain, grad_out, mixed, output)


def qkv_back_kernel(grad_ref, normed_ref, weight_ref, xhat_ref, inverse_ref, gain_ref, resid_ref,
                    weight_grad_ref, bias_grad_ref, sums_ref, tokens_ref, grad, normed_t, total):
    step = pl.program_id(0)
    tokens = normed_ref.shape[0]

    @pl.when(step == 0)
    def _():
        grad[...] = jnp.zeros_like(grad)
        grad[0:tokens] = normed_ref[...]
        normed_t[...] = grad[...].T
        grad[...] = jnp.zeros_like(grad)
        total[...] = jnp.zeros_like(total)

    grad[0:tokens] = grad_ref[...]
    weight_grad_ref[...] = nn(normed_t[...], grad[...]).astype(jnp.bfloat16)
    bias_grad_ref[...] = jnp.sum(grad[...].astype(jnp.float32), axis=0, keepdims=True)
    total[...] += nt(grad[...], weight_ref[...])

    @pl.when(step == pl.num_programs(0) - 1)
    def _():
        back = total[0:tokens]
        xhat = xhat_ref[...]
        sums_ref[0:1] = jnp.sum(back * xhat, axis=0, keepdims=True)
        sums_ref[1:2] = jnp.sum(back, axis=0, keepdims=True)
        scaled = back * gain_ref[...]
        first = jnp.mean(scaled, axis=-1, keepdims=True)
        second = jnp.mean(scaled * xhat, axis=-1, keepdims=True)
        tokens_ref[...] = resid_ref[...] + inverse_ref[...] * (scaled - first - xhat * second)


def qkv_back(grad, normed, weight, xhat, inverse, gain, resid):
    tokens = normed.shape[0]
    rows = -(-tokens // 16) * 16
    whole = lambda shape: pl.BlockSpec(shape, lambda i: (0, 0), pipeline_mode=pl.Buffered(1))
    part = lambda shape: pl.BlockSpec(shape, lambda i: (0, i))
    return pl.pallas_call(
        qkv_back_kernel,
        grid=(3,),
        in_specs=[
            part((tokens, D)),
            whole((tokens, D)),
            part((D, D)),
            whole((tokens, D)),
            whole((tokens, 1)),
            whole((1, D)),
            whole((tokens, D)),
        ],
        out_specs=[part((D, D)), part((1, D)), whole((8, D)), whole((tokens, D))],
        out_shape=[
            jax.ShapeDtypeStruct((D, 3 * D), jnp.bfloat16),
            jax.ShapeDtypeStruct((1, 3 * D), jnp.float32),
            jax.ShapeDtypeStruct((8, D), jnp.float32),
            jax.ShapeDtypeStruct((tokens, D), jnp.float32),
        ],
        scratch_shapes=[
            pltpu.VMEM((rows, D), jnp.bfloat16),
            pltpu.VMEM((D, rows), jnp.bfloat16),
            pltpu.VMEM((rows, D), jnp.float32),
        ],
        compiler_params=pltpu.CompilerParams(
            vmem_limit_bytes=56 << 20, dimension_semantics=("arbitrary",)
        ),
        cost_estimate=pl.CostEstimate(flops=1000000, bytes_accessed=1000000, transcendentals=0),
        name="qkv_backward",
    )(grad, normed, weight, xhat, inverse, gain, resid)


FF = 4304
GROUPS = 16
FF_GROUP = FF // GROUPS
FF_ROWS = 272
FF_PAD = GROUPS * FF_ROWS
PAIR_ROWS = D // GROUPS
HALF_DOWN = FF_ROWS // 2
OWN_ROWS = PAIR_ROWS // 2
TILE = 8
BLOCK_TILES = 5
PAIR_TILES = PAIR_ROWS // TILE
EXTRA = 128
QKV_CUT = 14 * 128
UP_CUT = 22 * 128
UP_PIECES = 4
DOWN_CUT = 40
DOWN_FIRST = 64
REST_ROWS = UP_PIECES * BLOCK_TILES * TILE + BLOCK_TILES * TILE + DOWN_FIRST
VECTORS = (0, 1, 3, 6, 8, 9, 10, 12, 14)
bf16 = jnp.bfloat16
f32 = jnp.float32


def product(left, right):
    return jnp.dot(left, right, preferred_element_type=f32)


def product_t(left, right):
    return lax.dot_general(left, right, (((0,), (0,)), ((), ())), preferred_element_type=f32)


def product_bt(left, right):
    return lax.dot_general(left, right, (((1,), (1,)), ((), ())), preferred_element_type=f32)


def swap(value, mask):
    devices = lax.axis_size("fsdp")
    return lax.ppermute(value, "fsdp", [(i, i ^ mask) for i in range(devices)])


def pad_hidden(columns):
    rows = columns.shape[0]
    grouped = columns.reshape(rows, GROUPS, FF_GROUP)
    return jnp.pad(grouped, ((0, 0), (0, 0), (0, FF_ROWS - FF_GROUP))).reshape(rows, FF_PAD)


def trim_hidden(columns):
    rows = columns.shape[0]
    return columns.reshape(rows, GROUPS, FF_ROWS)[:, :, :FF_GROUP].reshape(rows, FF)


def place_square_kernel(coords, *refs):
    sources, (whole, small) = refs[:8], refs[8:10]
    held, in_sems, out_sems = refs[10:18], refs[18], refs[19]
    core, x, y, z = coords[0], coords[1], coords[2], coords[3]
    arrivals = [pltpu.make_async_copy(sources[i], held[i], in_sems.at[i]) for i in range(8)]
    for arrival in arrivals:
        arrival.start()
    copies, extras = [], []
    for part, stream in itertools.product(range(4), range(2)):
        arrivals[4 * stream + part].wait()
        for near, dz in itertools.product(range(2), range(4)):
            src = held[4 * stream + part].at[near * 4 + dz]
            owner = core if part < 2 else 1 - core
            far = part % 2
            dx, dy = (near, far) if stream == 0 else (far, near)
            chip = ((z ^ dz) * 2 + (y ^ dy)) * 2 + (x ^ dx)
            cols = src.shape[-1] - (0 if stream else EXTRA)
            col = QKV_CUT - EXTRA if stream else 0
            src_cols = pl.ds(0 if stream else EXTRA, cols)
            first = PAIR_TILES * chip + BLOCK_TILES * owner
            copies.append(
                pltpu.make_async_copy(
                    src.at[pl.ds(owner, BLOCK_TILES - 1), :, src_cols],
                    whole.at[pl.ds(first, BLOCK_TILES - 1), :, pl.ds(col, cols)],
                    out_sems.at[len(copies)],
                )
            )
            copies[-1].start()
            extra = pltpu.make_async_copy(
                src.at[BLOCK_TILES - 1, :, src_cols],
                whole.at[PAIR_TILES * chip + BLOCK_TILES - 1, :, pl.ds(col, cols)],
                out_sems.at[96 + len(extras)],
            )
            pl.when(owner == 0)(extra.start)
            extras.append((owner, extra))
            if stream == 0:
                copies.append(
                    pltpu.make_async_copy(
                        src.at[:, :, :EXTRA], small.at[chip * 2 + owner], out_sems.at[len(copies)]
                    )
                )
                copies[-1].start()
    for copy in copies:
        copy.wait()
    for owner, extra in extras:
        pl.when(owner == 0)(extra.wait)


def place_square(streams, coords):
    sources = [s.reshape(8, BLOCK_TILES, TILE, -1) for s in (*streams[0], *streams[1])]
    size = sum(s.size for s in sources) * 2
    whole, small = pl.pallas_call(
        place_square_kernel,
        in_specs=[pl.BlockSpec(memory_space=pltpu.SMEM)]
        + [pl.BlockSpec(memory_space=pltpu.HBM)] * 8,
        out_specs=[pl.BlockSpec(memory_space=pltpu.HBM)] * 2,
        out_shape=[
            jax.ShapeDtypeStruct((GROUPS * PAIR_TILES, TILE, 3 * D), bf16),
            jax.ShapeDtypeStruct((2 * GROUPS, BLOCK_TILES, TILE, EXTRA), bf16),
        ],
        scratch_shapes=[pltpu.VMEM(s.shape, bf16) for s in sources]
        + [pltpu.SemaphoreType.DMA((8,)), pltpu.SemaphoreType.DMA((160,))],
        compiler_params=pltpu.CompilerParams(vmem_limit_bytes=40 << 20),
        cost_estimate=pl.CostEstimate(flops=0, bytes_accessed=2 * size, transcendentals=0),
        name="place_square",
    )(coords, *sources)
    return whole.reshape(D, 3 * D), small.reshape(2 * GROUPS, -1)


def place_rest_kernel(coords, *refs):
    source, streams, (up, out, down) = refs[0], refs[1:9], refs[9:12]
    held, in_sems, out_sems = refs[12], refs[13], refs[14]
    parts, part_sems = refs[15:23], refs[23]
    core, x, y, z = coords[0], coords[1], coords[2], coords[3]
    arrivals = [
        pltpu.make_async_copy(source.at[i], held.at[i], in_sems.at[i]) for i in range(2 * GROUPS)
    ]
    others = [pltpu.make_async_copy(streams[i], parts[i], part_sems.at[i]) for i in range(8)]
    for arrival in arrivals + others:
        arrival.start()
    copies = []

    def move(one, other):
        copies.append(pltpu.make_async_copy(one, other, out_sems.at[len(copies)]))
        copies[-1].start()

    lead = DOWN_FIRST // TILE
    for device in range(2 * GROUPS):
        chip, owner = device // 2, device % 2
        src = held.at[device]
        arrivals[device].wait()
        count = BLOCK_TILES - owner
        first = PAIR_TILES * chip + BLOCK_TILES * owner
        for piece in range(UP_PIECES):
            cols = min(D, FF_PAD - piece * D)
            move(
                src.at[pl.ds(piece * BLOCK_TILES + owner, count), :, pl.ds(0, cols)],
                up.at[pl.ds(first, count), :, pl.ds(piece * D, cols)],
            )
        base = UP_PIECES * BLOCK_TILES
        move(src.at[pl.ds(base + owner, count)], out.at[pl.ds(first, count)])
        move(src.at[pl.ds(base + BLOCK_TILES, lead)], down.at[device, pl.ds(0, lead)])
    for part, stream in itertools.product(range(4), range(2)):
        others[4 * stream + part].wait()
        for near, dz in itertools.product(range(2), range(4)):
            src = parts[4 * stream + part].at[near * 4 + dz]
            owner = core if part < 2 else 1 - core
            far = part % 2
            dx, dy = (near, far) if stream == 0 else (far, near)
            chip = ((z ^ dz) * 2 + (y ^ dy)) * 2 + (x ^ dx)
            first = lead + (DOWN_CUT // TILE if stream else 0)
            move(src, down.at[chip * 2 + owner, pl.ds(first, src.shape[0])])
    for copy in copies:
        copy.wait()


def place_rest(gathered, streams, coords):
    source = gathered.reshape(2 * GROUPS, REST_ROWS // TILE, TILE, D)
    sources = [s.reshape(8, -1, TILE, D) for s in (*streams[0], *streams[1])]
    up, out, down = pl.pallas_call(
        place_rest_kernel,
        in_specs=[pl.BlockSpec(memory_space=pltpu.SMEM)]
        + [pl.BlockSpec(memory_space=pltpu.HBM)] * 9,
        out_specs=[pl.BlockSpec(memory_space=pltpu.HBM)] * 3,
        out_shape=[
            jax.ShapeDtypeStruct((D // TILE, TILE, FF_PAD), bf16),
            jax.ShapeDtypeStruct((D // TILE, TILE, D), bf16),
            jax.ShapeDtypeStruct((2 * GROUPS, HALF_DOWN // TILE, TILE, D), bf16),
        ],
        scratch_shapes=[
            pltpu.VMEM(source.shape, bf16),
            pltpu.SemaphoreType.DMA((2 * GROUPS,)),
            pltpu.SemaphoreType.DMA((2 * GROUPS * (UP_PIECES + 2) + 64,)),
        ]
        + [pltpu.VMEM(s.shape, bf16) for s in sources]
        + [pltpu.SemaphoreType.DMA((8,))],
        compiler_params=pltpu.CompilerParams(vmem_limit_bytes=60 << 20),
        cost_estimate=pl.CostEstimate(
            flops=0, bytes_accessed=4 * source.size, transcendentals=0
        ),
        name="place_rest",
    )(coords, source, *sources)
    return up.reshape(D, FF_PAD), out.reshape(D, D), down.reshape(FF_PAD, D)


def tie(*values):
    leaves, form = jax.tree.flatten(values)
    return form.unflatten(lax.optimization_barrier(leaves))


def gather_z(block):
    return [block] + [swap(block, 8 * step) for step in (1, 2, 3)]


def gather_near(parts, cut, axis):
    streams = []
    for stream in range(2):
        if axis == 1:
            own = jnp.stack([p[:, :cut] if stream == 0 else p[:, cut:] for p in parts])
        else:
            own = jnp.stack([p[:cut] if stream == 0 else p[cut:] for p in parts])
        streams.append((own, swap(own, 4 if stream else 2)))
    return streams


def gather_far(streams):
    results = []
    for stream in range(2):
        first = jnp.concatenate(streams[stream])
        results.append((first, swap(first, 2 if stream else 4)))
    return results


def gather_core(streams):
    return [(first, second, swap(first, 1), swap(second, 1)) for first, second in streams]


def window(value, starts, sizes):
    rank = value.ndim
    starts = list(starts) + [0] * (rank - len(starts))
    lengths = list(value.shape)
    for axis, size in enumerate(sizes):
        if size is not None:
            lengths[axis] = size
    starts = [jnp.int32(0) if start is None else jnp.int32(start) for start in starts]
    result = lax.dynamic_slice(value, starts, lengths)
    kept = [
        length for axis, length in enumerate(lengths) if axis >= len(sizes) or sizes[axis] != 1
    ]
    return result.reshape(kept)


class Reduction:
    def __init__(self, matrices, streams, coords):
        self.matrices = [m.reshape(4, 2, 2, PAIR_TILES, TILE, -1) for m in matrices]
        self.streams = streams
        self.coords = coords

    def part(self, arrays, stream, plane, tile):
        sizes = tuple(None if p is None else 1 for p in plane) + (BLOCK_TILES, None)
        pieces = []
        for number, first, last in self.streams[stream]:
            starts = tuple(plane) + (tile, None, first)
            pieces.append(window(arrays[number], starts, sizes + (last - first,)))
        return pieces[0] if len(pieces) == 1 else jnp.concatenate(pieces, axis=-1)

    def terms(self, stream, plane):
        tile = self.coords[0] * (PAIR_TILES - BLOCK_TILES)
        own = self.part(self.matrices, stream, plane, tile)
        return [own, self.part(self.other, stream, plane, 0)]

    def core_step(self):
        tile = (1 - self.coords[0]) * (PAIR_TILES - BLOCK_TILES)
        starts, sizes = (None, None, None, tile), (None, None, None, BLOCK_TILES)
        return [swap(window(m, starts, sizes), 1) for m in self.matrices]

    def far_step(self, other, streams=(0, 1), pieces=slice(None)):
        core, x, y, z = self.coords
        self.other = other
        got = []
        every = self.streams
        for stream in streams:
            plane = (None, None, 1 - x) if stream else (None, 1 - y, None)
            self.streams = {stream: every[stream][pieces]}
            send = total_of(self.terms(stream, plane)).astype(bf16)
            got.append(swap(send, 2 if stream else 4))
        self.streams = every
        return got

    def near_step(self, far):
        core, x, y, z = self.coords
        self.far = far
        got = []
        for stream in range(2):
            plane = (None, 1 - y, x) if stream else (None, y, 1 - x)
            after = (None, 1 - y) if stream else (None, 1 - x)
            terms = self.terms(stream, plane) + [window(far[stream], after, (None, 1))]
            got.append(swap(total_of(terms).astype(bf16), 4 if stream else 2))
        return got

    def at(self, plane):
        core, x, y, z = self.coords
        pieces = []
        for stream in range(2):
            after = (plane, y) if stream else (plane, x)
            terms = self.terms(stream, (plane, y, x)) + [
                window(self.far[stream], after, (1, 1)),
                window(self.near[stream], (plane,), (1,)),
            ]
            pieces.append(total_of(terms))
        return jnp.concatenate(pieces, axis=-1)

    def z_step(self, near):
        z = self.coords[3]
        self.near = near
        return [swap(self.at(z ^ step).astype(bf16), 8 * step) for step in (1, 2, 3)]

    def finish(self, arrived):
        core, x, y, z = self.coords
        total = total_of([self.at(z)] + arrived)
        total = total.reshape(BLOCK_TILES * TILE, -1)
        return lax.dynamic_slice_in_dim(
            total, core * (BLOCK_TILES * TILE - OWN_ROWS), OWN_ROWS, 0
        )


def total_of(terms):
    total = terms[0].astype(f32)
    for term in terms[1:]:
        total = total + term.astype(f32)
    return total


def fetch_pairs(narrow, core):
    q, k, v, o = (narrow[i].reshape(OWN_ROWS, D) for i in (2, 4, 5, 7))
    up = pad_hidden(narrow[11].reshape(OWN_ROWS, FF))
    down = narrow[13]
    rows = jnp.concatenate([q, k, v, o, up], axis=1)
    spare = BLOCK_TILES * TILE - OWN_ROWS
    lead = D * HALF_DOWN - down.shape[0]
    tail = jnp.pad(down[:lead].reshape(spare, -1), ((0, 0), (0, 512 - lead // spare)))
    is_first = core == 0
    edge = jnp.where(is_first, rows[OWN_ROWS - spare :], rows[:spare])
    got = swap(jnp.concatenate([edge, tail], axis=1), 1)
    edge = got[:, : rows.shape[1]]
    block = jnp.where(is_first, jnp.concatenate([rows, edge]), jnp.concatenate([edge, rows]))
    extra = got[:, rows.shape[1] : rows.shape[1] + lead // spare].reshape(-1)
    end = jnp.zeros((D * HALF_DOWN - (down.shape[0] - lead),), bf16)
    down_block = jnp.where(
        is_first, jnp.concatenate([down, extra]), jnp.concatenate([down[lead:], end])
    ).reshape(HALF_DOWN, D)
    small = jnp.concatenate([narrow[i] for i in VECTORS])
    small = jnp.pad(small, (0, BLOCK_TILES * TILE * EXTRA - small.shape[0]))
    small = small.reshape(BLOCK_TILES * TILE, EXTRA)
    square = jnp.concatenate([small, block[:, : 3 * D]], axis=1)
    up_block = jnp.pad(block[:, 4 * D :], ((0, 0), (0, UP_PIECES * D - FF_PAD)))
    pieces = [up_block[:, i * D : (i + 1) * D] for i in range(UP_PIECES)]
    rest = jnp.concatenate(pieces + [block[:, 3 * D : 4 * D], down_block[:DOWN_FIRST]])
    return square, rest, down_block[DOWN_FIRST:]


def normalize(values):
    centre = jnp.mean(values, axis=-1, keepdims=True)
    centered = values - centre
    spread_sq = jnp.mean(centered * centered, axis=-1, keepdims=True)
    inverse = lax.rsqrt(spread_sq + 1e-06)
    return centered * inverse, inverse


def normalize_back(grad, gain, xhat, inverse):
    scaled = grad * gain
    first = jnp.mean(scaled, axis=-1, keepdims=True)
    second = jnp.mean(scaled * xhat, axis=-1, keepdims=True)
    return inverse * (scaled - first - xhat * second)


def name_vectors(whole, widths):
    found = {}
    position = 0
    for i in VECTORS:
        found[i] = whole[:, position : position + widths[i]].reshape(-1).astype(f32)
        position += widths[i]
    return found


def gather_plain(narrow, widths):
    whole = {
        i: lax.all_gather(narrow[i], "fsdp", axis=0, tiled=True) for i in (2, 4, 5, 7, 11, 13)
    }
    square = [whole[i][: D * D].reshape(D, D) for i in (2, 4, 5, 7)]
    up = pad_hidden(whole[11][: D * FF].reshape(D, FF))
    down = pad_hidden(whole[13][: D * FF].reshape(FF, D).T).T
    joined = jnp.concatenate([narrow[i] for i in VECTORS])
    length = joined.shape[0]
    joined = jnp.pad(joined, (0, 2048 - length)).reshape(16, 128)
    joined = lax.all_gather(joined, "fsdp", axis=0, tiled=True).reshape(-1, 2048)
    return jnp.concatenate(square[:3], axis=1), square[3], up, down, name_vectors(joined, widths)


def on_device(*args):
    devices = lax.axis_size("fsdp")
    tokens, image_valid = args[0], args[1]
    shards = args[2:17]
    cotangent = args[17]
    staged = devices == 32
    widths = [piece.shape[0] for piece in shards]
    narrow = [piece.astype(bf16) for piece in shards]
    index = lax.axis_index("fsdp")
    core, x, y, z = index % 2, (index // 2) % 2, (index // 4) % 2, index // 8
    coords = (core, x, y, z)
    image_count = image_valid.shape[0]
    seq_len = tokens.shape[0] // image_count
    weight_img = jnp.repeat(image_valid.astype(f32), seq_len)[:, None]

    grad_out = weight_img * cotangent
    grad_branch = grad_out.astype(bf16)
    grads = {14: jnp.sum(grad_branch.astype(f32), axis=0)}
    xhat_one, inverse_one = normalize(tokens)
    if staged:
        where = jnp.stack(coords).astype(jnp.int32)
        sq, rest, down = fetch_pairs(narrow, core)
        rest = lax.all_gather(rest, "fsdp", axis=0, tiled=True)
        sq = gather_z(sq)
        sq, down, xhat_one, inverse_one, grad_branch = tie(
            sq, down, xhat_one, inverse_one, grad_branch
        )
        sq = gather_near(sq, QKV_CUT, 1)
        down = gather_z(down)
        sq = gather_far(sq)
        sq, down = tie(sq, down)
        sq = gather_core(sq)
        down = gather_near(down, DOWN_CUT, 0)
        weight_qkv, small = place_square(sq, where)
        vectors = name_vectors(small, widths)
    else:
        weight_qkv, weight_o, weight_up, weight_down, vectors = gather_plain(narrow, widths)

    vec = lambda i: vectors[i][:D]
    gain_one, shift_one, gain_two, shift_two = vec(0), vec(1), vec(9), vec(10)
    bias_qkv = jnp.concatenate([vec(3), jnp.zeros((D,), f32), vec(6)])
    bias_o, bias_down = vec(8), vec(14)
    bias_up = pad_hidden(vectors[12][:FF].reshape(1, FF))

    normed = (xhat_one * gain_one + shift_one).astype(bf16)
    qkv = (product(normed, weight_qkv) + bias_qkv).astype(bf16)
    if staged:
        qkv, down = tie(qkv, down)
        down = gather_far(down)
    mixed, lse = attn_fwd(qkv, 2)
    if staged:
        mixed, lse, down = tie(mixed, lse, down)
        down = gather_core(down)
        weight_up, weight_o, weight_down = place_rest(rest, down, where)
    resid = tokens + product(mixed, weight_o) + bias_o
    xhat_two, inverse_two = normalize(resid)
    normed_two = (xhat_two * gain_two + shift_two).astype(bf16)
    branch, up_grad, up_bias_grad, down_grad, sums_two, grad_resid, o_grad, grad_mixed = mlp(
        normed_two,
        grad_branch,
        weight_up,
        bias_up,
        weight_down,
        xhat_two,
        inverse_two,
        gain_two.reshape(1, D),
        grad_out,
        mixed,
        weight_o,
    )
    up_bias_grad = up_bias_grad.reshape(FF_PAD)
    layer_out = weight_img * (resid + branch + bias_down)
    grads[9], grads[10], grads[8] = sums_two[0], sums_two[1], sums_two[2]
    if staged:
        down_sum = lax.psum_scatter(down_grad, "fsdp", scatter_dimension=0, tiled=True)
    if staged:
        outer = Reduction(
            (up_grad, o_grad), (((0, 0, UP_CUT),), ((0, UP_CUT, FF_PAD), (1, 0, D))), coords
        )
        outer_other = outer.core_step()
    if staged:
        grad_mixed, outer_other = tie(grad_mixed, outer_other)
        outer_far = outer.far_step(outer_other)
    grad_qkv = attn_bwd(qkv, grad_mixed, lse, 2)
    if staged:
        grad_qkv, outer_far = tie(grad_qkv, outer_far)
        outer_near = outer.near_step(outer_far)
    qkv_grad, qkv_bias_grad, norm_sums, tokens_grad = qkv_back(
        grad_qkv, normed, weight_qkv, xhat_one, inverse_one, gain_one.reshape(1, D), grad_resid
    )
    grads[3], grads[6] = qkv_bias_grad[0, :D], qkv_bias_grad[0, 2 * D :]
    grads[0], grads[1] = norm_sums[0], norm_sums[1]
    if staged:
        qkv_grad, outer_near = tie(qkv_grad, outer_near)
        inner = Reduction((qkv_grad,), (((0, 0, QKV_CUT - EXTRA),),) * 2, coords)
        inner_other = inner.core_step()
        inner_other, outer_near, qkv_grad, norm_sums, qkv_bias_grad = tie(
            inner_other, outer_near, qkv_grad, norm_sums, qkv_bias_grad
        )
        inner = Reduction(
            (qkv_grad, qkv_grad),
            (((0, 0, QKV_CUT - EXTRA), (1, 0, EXTRA)), ((0, QKV_CUT - EXTRA, 3 * D),)),
            coords,
        )
        inner_far = inner.far_step(inner_other, (0, 1), slice(0, 1))
        outer_z = outer.z_step(outer_near)
    grads[12] = trim_hidden(up_bias_grad.reshape(1, FF_PAD)).reshape(FF)

    rows = []
    for i in VECTORS:
        row = grads[i]
        row = jnp.pad(row, (0, widths[i] * devices - row.shape[0]))
        rows.append(row.reshape(devices, widths[i]))
    rows = jnp.concatenate(rows, axis=1)
    owned = [None] * 15
    if staged:
        rows = jnp.pad(rows, ((0, 0), (0, OWN_ROWS * EXTRA - rows.shape[1])))
        rows = rows.reshape(D, EXTRA).astype(bf16)
        inner.matrices[1] = rows.reshape(4, 2, 2, PAIR_TILES, TILE, EXTRA)
        rows_other = Reduction((rows,), None, coords).core_step()
        inner.other = inner_other + rows_other
        rows_far = inner.far_step(inner.other, (0,), slice(1, 2))
        inner_far, rows_far = tie(inner_far, rows_far)
        inner_far = [jnp.concatenate([inner_far[0], rows_far[0]], axis=-1), inner_far[1]]
        inner_near = inner.near_step(inner_far)
        inner_near, outer_z = tie(inner_near, outer_z)
        inner_z = inner.z_step(inner_near)
        inner_near, down_sum = tie(inner_near, down_sum)

        flat = down_sum.astype(f32).reshape(-1)
        size = widths[13]
        lead = flat.shape[0] - size
        got = swap(down_sum.reshape(-1)[size:], 1).astype(f32)
        owned[13] = jnp.where(core == 0, flat[:size], jnp.concatenate([got, flat[: size - lead]]))
        outer_sum = outer.finish(outer_z)
        owned[11] = trim_hidden(outer_sum[:, :FF_PAD]).reshape(-1)
        owned[7] = outer_sum[:, FF_PAD:].reshape(-1)
        inner_sum = inner.finish(inner_z)
        first = QKV_CUT - EXTRA
        owned[2] = inner_sum[:, :D].reshape(-1)
        owned[4] = jnp.concatenate(
            [inner_sum[:, D:first], inner_sum[:, QKV_CUT : 2 * D + EXTRA]], axis=1
        ).reshape(-1)
        owned[5] = inner_sum[:, 2 * D + EXTRA :].reshape(-1)
        small = inner_sum[:, first:QKV_CUT].reshape(-1)
    else:
        scatter = lambda value: lax.psum_scatter(
            value.astype(f32).reshape(-1), "fsdp", scatter_dimension=0, tiled=True
        )
        fill = lambda value, i: jnp.pad(
            value.reshape(-1), (0, widths[i] * devices - value.size)
        )
        for position, i in enumerate((2, 4, 5)):
            owned[i] = scatter(fill(qkv_grad[:, position * D : (position + 1) * D], i))
        owned[7] = scatter(fill(o_grad, 7))
        owned[11] = scatter(fill(trim_hidden(up_grad), 11))
        owned[13] = scatter(fill(trim_hidden(down_grad.T).T, 13))
        small = scatter(rows)
    position = 0
    for i in VECTORS:
        owned[i] = small[position : position + widths[i]]
        position += widths[i]
    return (layer_out, tokens_grad, *owned)


def solution(mesh):
    row, flat = P("fsdp", None), P("fsdp")
    in_specs = (row, flat) + (flat,) * 15 + (row,)
    out_specs = (row, row) + (flat,) * 15
    return jax.shard_map(
        on_device, mesh=mesh, in_specs=in_specs, out_specs=out_specs, check_vma=False
    )
```

```python
import functools
import itertools
import jax
import jax.numpy as jnp
from jax import lax
from jax.sharding import PartitionSpec as P
from jax.experimental import pallas as pl
from jax.experimental.pallas import tpu as pltpu
D=1152; HEADS=16; HEAD_DIM=72; LANES=128
NEG=-1e30
LOG2E=1.4426950408889634
def nt(a,b): return lax.dot_general(a,b,(((1,),(1,)),((),())),preferred_element_type=jnp.float32)
def nn(a,b): return lax.dot_general(a,b,(((1,),(0,)),((),())),preferred_element_type=jnp.float32)

def fill_heads(dst, src, col, tokens, fill):
    rows=dst.shape[1]
    for h in range(HEADS):
        if fill is not None:
            dst[h]=fill
        dst[h,0:tokens,0:HEAD_DIM]=src[:,col+h*HEAD_DIM:col+(h+1)*HEAD_DIM]

def pad_values(rows, tokens, kind):
    lane=lax.broadcasted_iota(jnp.int32,(rows,LANES),1)
    row=lax.broadcasted_iota(jnp.int32,(rows,LANES),0)
    if kind=="query":
        v=jnp.where(lane==HEAD_DIM,1.0,0.0)
    elif kind=="key":
        v=jnp.where((lane==HEAD_DIM)&(row>=tokens),NEG,0.0)
    else:
        v=jnp.zeros((rows,LANES),jnp.float32)
    return v.astype(jnp.bfloat16)

def fwd_kernel(tokens, krows, qrows, per, qkv_ref, mixed_ref, lse_ref, qs, ks, vs, os):
    step=pl.program_id(0)
    @pl.when(step==0)
    def _():
        fill_heads(qs,qkv_ref,0,tokens,pad_values(qrows,tokens,"query"))
        fill_heads(ks,qkv_ref,D,tokens,pad_values(krows,tokens,"key"))
        zero=pad_values(krows,tokens,"value")
        for h in range(HEADS):
            vs[h]=zero
            vs[h,0:tokens,0:HEAD_DIM]=qkv_ref[:,2*D+h*HEAD_DIM:2*D+(h+1)*HEAD_DIM]
    c=HEAD_DIM**-0.5*LOG2E
    for j in range(per):
        h=step*per+j
        s=nt(ks[h],qs[h])
        m=jnp.max(s,axis=0,keepdims=True)
        e=jnp.exp2((s-m)*c)
        l=jnp.sum(e,axis=0,keepdims=True)
        p=(e*(1.0/l)).astype(jnp.bfloat16)
        vt=vs[h].T
        ot=nn(vt,p)
        os[h]=ot.T.astype(jnp.bfloat16)
        lse_ref[j]=m*c+jnp.log2(l)
    @pl.when(step==pl.num_programs(0)-1)
    def _():
        for h in range(HEADS):
            mixed_ref[:,h*HEAD_DIM:(h+1)*HEAD_DIM]=os[h,0:tokens,0:HEAD_DIM]

def attn_fwd(qkv, per=1):
    tokens=qkv.shape[0]
    krows=-(-tokens//16)*16; qrows=-(-tokens//128)*128
    return pl.pallas_call(functools.partial(fwd_kernel,tokens,krows,qrows,per),
        grid=(HEADS//per,),
        in_specs=[pl.BlockSpec(qkv.shape,lambda i:(0,0),pipeline_mode=pl.Buffered(1))],
        out_specs=[pl.BlockSpec((tokens,D),lambda i:(0,0),pipeline_mode=pl.Buffered(1)),pl.BlockSpec((per,1,qrows),lambda i:(i,0,0))],
        out_shape=[jax.ShapeDtypeStruct((tokens,D),jnp.bfloat16),jax.ShapeDtypeStruct((HEADS,1,qrows),jnp.float32)],
        scratch_shapes=[pltpu.VMEM((HEADS,qrows,LANES),jnp.bfloat16),pltpu.VMEM((HEADS,krows,LANES),jnp.bfloat16),
                        pltpu.VMEM((HEADS,krows,LANES),jnp.bfloat16),pltpu.VMEM((HEADS,qrows,LANES),jnp.bfloat16)],
        compiler_params=pltpu.CompilerParams(vmem_limit_bytes=56<<20,dimension_semantics=("arbitrary",)),
        cost_estimate=pl.CostEstimate(flops=4*HEADS*qrows*krows*LANES,bytes_accessed=4*tokens*D*2,transcendentals=HEADS*qrows*krows),
        name="attention_forward")(qkv)

def bwd_kernel(tokens, krows, qrows, per, qkv_ref, go_ref, lse_ref, dqkv_ref, qs, ks, vs, gs):
    step=pl.program_id(0)
    @pl.when(step==0)
    def _():
        fill_heads(qs,qkv_ref,0,tokens,pad_values(qrows,tokens,"query"))
        fill_heads(ks,qkv_ref,D,tokens,pad_values(krows,tokens,"key"))
        fill_heads(vs,qkv_ref,2*D,tokens,pad_values(krows,tokens,"value"))
        fill_heads(gs,go_ref,0,tokens,pad_values(qrows,tokens,"value"))
    scale=HEAD_DIM**-0.5
    c=scale*LOG2E
    for j in range(per):
        h=step*per+j
        q=qs[h]; k=ks[h]; v=vs[h]; g=gs[h]
        s=nt(k,q)
        p=jnp.exp2(s*c-lse_ref[j])
        dp=nt(v,g)
        dv=nn(p.astype(jnp.bfloat16),g)
        delta=jnp.sum(p*dp,axis=0,keepdims=True)
        ds=(p*(dp-delta)).astype(jnp.bfloat16)
        dk=nn(ds,q)*scale
        dqt=nn(k.T,ds)*scale
        qs[h]=dqt.T.astype(jnp.bfloat16)
        ks[h]=dk.astype(jnp.bfloat16)
        vs[h]=dv.astype(jnp.bfloat16)
    @pl.when(step==pl.num_programs(0)-1)
    def _():
        for i,r in enumerate((qs,ks,vs)):
            for h in range(HEADS):
                dqkv_ref[:,i*D+h*HEAD_DIM:i*D+(h+1)*HEAD_DIM]=r[h,0:tokens,0:HEAD_DIM]

def attn_bwd(qkv, gmixed, lse, per=1):
    tokens=qkv.shape[0]
    krows=-(-tokens//16)*16; qrows=-(-tokens//128)*128
    return pl.pallas_call(functools.partial(bwd_kernel,tokens,krows,qrows,per),
        grid=(HEADS//per,),
        in_specs=[pl.BlockSpec(qkv.shape,lambda i:(0,0),pipeline_mode=pl.Buffered(1)),pl.BlockSpec(gmixed.shape,lambda i:(0,0),pipeline_mode=pl.Buffered(1)),
                  pl.BlockSpec((per,1,qrows),lambda i:(i,0,0))],
        out_specs=pl.BlockSpec((tokens,3*D),lambda i:(0,0),pipeline_mode=pl.Buffered(1)),
        out_shape=jax.ShapeDtypeStruct((tokens,3*D),jnp.bfloat16),
        scratch_shapes=[pltpu.VMEM((HEADS,qrows,LANES),jnp.bfloat16),pltpu.VMEM((HEADS,krows,LANES),jnp.bfloat16),
                        pltpu.VMEM((HEADS,krows,LANES),jnp.bfloat16),pltpu.VMEM((HEADS,qrows,LANES),jnp.bfloat16)],
        compiler_params=pltpu.CompilerParams(vmem_limit_bytes=56<<20,dimension_semantics=("arbitrary",)),
        cost_estimate=pl.CostEstimate(flops=1000000,bytes_accessed=1000000,transcendentals=0),
        name="attention_backward")(qkv,gmixed,lse)


GELU_A = 0.7978845608028654
GELU_B = 0.044715


PAIR_ROWS = D // HEADS
BLOCK_ROWS = 40


def share_rows(core, value, keep_ref, send_ref):
    for chip in range(value.shape[0] // PAIR_ROWS):
        first = value[chip * PAIR_ROWS : chip * PAIR_ROWS + BLOCK_ROWS]
        last = value[(chip + 1) * PAIR_ROWS - BLOCK_ROWS : (chip + 1) * PAIR_ROWS]
        keep_ref[chip] = jnp.where(core == 0, first, last).astype(jnp.bfloat16)
        send_ref[chip] = jnp.where(core == 0, last, first).astype(jnp.bfloat16)


def mlp_kernel(coords, normed_ref, grad_ref, up_ref, bias_ref, down_ref, xhat_ref, inverse_ref, gain_ref,
               grad_out_ref, mixed_ref, output_ref, out_ref, up_keep_ref, up_send_ref, bias_grad_ref,
               down_grad_ref, sums_ref, resid_grad_ref, output_keep_ref, output_send_ref, mixed_grad_ref,
               normed, normed_t, grad, out, back):
    step = pl.program_id(0)
    tokens = normed_ref.shape[0]

    @pl.when(step == 0)
    def _():
        for held, source in ((normed, normed_ref), (grad, grad_ref)):
            held[...] = jnp.zeros_like(held)
            held[0:tokens] = source[...]
        normed_t[...] = normed[...].T
        out[...] = jnp.zeros_like(out)
        back[...] = jnp.zeros_like(back)

    pre = nn(normed[...], up_ref[...]) + bias_ref[...]
    square = pre * pre
    bend = jnp.tanh(pre * (GELU_A + GELU_A * GELU_B * square))
    hidden = (0.5 * pre * (1.0 + bend)).astype(jnp.bfloat16)
    slope = 0.5 * (1.0 + bend) + 0.5 * pre * (1.0 - bend * bend) * (
        GELU_A + 3.0 * GELU_A * GELU_B * square
    )
    grad_pre = (nt(grad[...], down_ref[...]) * slope).astype(jnp.bfloat16)
    out[...] += nn(hidden, down_ref[...])
    back[...] += nt(grad_pre, up_ref[...])
    down_grad_ref[...] = nn(hidden.T, grad[...]).astype(jnp.bfloat16)
    share_rows(coords[0], nn(normed_t[...], grad_pre), up_keep_ref, up_send_ref)
    bias_grad_ref[...] = jnp.sum(grad_pre.astype(jnp.float32), axis=0, keepdims=True)

    @pl.when(step == pl.num_programs(0) - 1)
    def _():
        out_ref[...] = out[0:tokens]
        total = back[0:tokens]
        xhat = xhat_ref[...]
        sums_ref[0:1] = jnp.sum(total * xhat, axis=0, keepdims=True)
        sums_ref[1:2] = jnp.sum(total, axis=0, keepdims=True)
        scaled = total * gain_ref[...]
        first = jnp.mean(scaled, axis=-1, keepdims=True)
        second = jnp.mean(scaled * xhat, axis=-1, keepdims=True)
        resid_grad = grad_out_ref[...] + inverse_ref[...] * (scaled - first - xhat * second)
        resid_grad_ref[...] = resid_grad
        grad[0:tokens] = resid_grad.astype(jnp.bfloat16)
        low = grad[...]
        sums_ref[2:3] = jnp.sum(low.astype(jnp.float32), axis=0, keepdims=True)
        mixed_grad_ref[...] = nt(low, output_ref[...]).astype(jnp.bfloat16)[0:tokens]
        normed[0:tokens] = mixed_ref[...]
        normed_t[...] = normed[...].T
        share_rows(coords[0], nn(normed_t[...], low), output_keep_ref, output_send_ref)


def whole_block(shape):
    return pl.BlockSpec(shape, lambda i: (0, 0), pipeline_mode=pl.Buffered(1))


def mlp(coords, normed, grad, up, bias, down, xhat, inverse, gain, grad_out, mixed, output):
    tokens, hidden = normed.shape[0], up.shape[1]
    rows = -(-tokens // 16) * 16
    tile = 256
    full = whole_block((tokens, D))
    columns = pl.BlockSpec((D, tile), lambda i: (0, i))
    line = pl.BlockSpec((1, tile), lambda i: (0, i))
    band = pl.BlockSpec((tile, D), lambda i: (i, 0))
    square = whole_block((D, D))
    shares = (D // PAIR_ROWS, BLOCK_ROWS)
    part = pl.BlockSpec(shares + (tile,), lambda i: (0, 0, i))
    full_part = pl.BlockSpec(
        shares + (D,), lambda i: (0, 0, 0), pipeline_mode=pl.Buffered(1)
    )
    return pl.pallas_call(
        mlp_kernel,
        grid=(hidden // tile,),
        in_specs=[pl.BlockSpec(memory_space=pltpu.SMEM), full, full, columns, line, band, full, whole_block((tokens, 1)),
                  whole_block((1, D)), full, full, square],
        out_specs=[full, part, part, line, band, whole_block((8, D)), full, full_part, full_part,
                   full],
        out_shape=[
            jax.ShapeDtypeStruct((tokens, D), jnp.float32),
            jax.ShapeDtypeStruct(shares + (hidden,), jnp.bfloat16),
            jax.ShapeDtypeStruct(shares + (hidden,), jnp.bfloat16),
            jax.ShapeDtypeStruct((1, hidden), jnp.float32),
            jax.ShapeDtypeStruct((hidden, D), jnp.bfloat16),
            jax.ShapeDtypeStruct((8, D), jnp.float32),
            jax.ShapeDtypeStruct((tokens, D), jnp.float32),
            jax.ShapeDtypeStruct(shares + (D,), jnp.bfloat16),
            jax.ShapeDtypeStruct(shares + (D,), jnp.bfloat16),
            jax.ShapeDtypeStruct((tokens, D), jnp.bfloat16),
        ],
        scratch_shapes=[
            pltpu.VMEM((rows, D), jnp.bfloat16),
            pltpu.VMEM((D, rows), jnp.bfloat16),
            pltpu.VMEM((rows, D), jnp.bfloat16),
            pltpu.VMEM((rows, D), jnp.float32),
            pltpu.VMEM((rows, D), jnp.float32),
        ],
        compiler_params=pltpu.CompilerParams(
            vmem_limit_bytes=56 << 20, dimension_semantics=("arbitrary",)
        ),
        cost_estimate=pl.CostEstimate(flops=1000000, bytes_accessed=1000000, transcendentals=0),
        name="mlp_forward_backward",
    )(coords, normed, grad, up, bias, down, xhat, inverse, gain, grad_out, mixed, output)


def qkv_back_kernel(coords, grad_ref, normed_ref, weight_ref, xhat_ref, inverse_ref, gain_ref, resid_ref,
                    keep_ref, send_ref, bias_grad_ref, sums_ref, tokens_ref, grad, normed_t, total):
    step = pl.program_id(0)
    tokens = normed_ref.shape[0]

    @pl.when(step == 0)
    def _():
        grad[...] = jnp.zeros_like(grad)
        grad[0:tokens] = normed_ref[...]
        normed_t[...] = grad[...].T
        grad[...] = jnp.zeros_like(grad)
        total[...] = jnp.zeros_like(total)

    grad[0:tokens] = grad_ref[...]
    share_rows(coords[0], nn(normed_t[...], grad[...]), keep_ref, send_ref)
    bias_grad_ref[...] = jnp.sum(grad[...].astype(jnp.float32), axis=0, keepdims=True)
    total[...] += nt(grad[...], weight_ref[...])

    @pl.when(step == pl.num_programs(0) - 1)
    def _():
        back = total[0:tokens]
        xhat = xhat_ref[...]
        sums_ref[0:1] = jnp.sum(back * xhat, axis=0, keepdims=True)
        sums_ref[1:2] = jnp.sum(back, axis=0, keepdims=True)
        scaled = back * gain_ref[...]
        first = jnp.mean(scaled, axis=-1, keepdims=True)
        second = jnp.mean(scaled * xhat, axis=-1, keepdims=True)
        tokens_ref[...] = resid_ref[...] + inverse_ref[...] * (scaled - first - xhat * second)


def qkv_back(coords, grad, normed, weight, xhat, inverse, gain, resid):
    tokens = normed.shape[0]
    rows = -(-tokens // 16) * 16
    whole = lambda shape: pl.BlockSpec(shape, lambda i: (0, 0), pipeline_mode=pl.Buffered(1))
    part = lambda shape: pl.BlockSpec(shape, lambda i: (0, i))
    shares = (D // PAIR_ROWS, BLOCK_ROWS)
    share = pl.BlockSpec(shares + (D,), lambda i: (0, 0, i))
    return pl.pallas_call(
        qkv_back_kernel,
        grid=(3,),
        in_specs=[
            pl.BlockSpec(memory_space=pltpu.SMEM),
            part((tokens, D)),
            whole((tokens, D)),
            part((D, D)),
            whole((tokens, D)),
            whole((tokens, 1)),
            whole((1, D)),
            whole((tokens, D)),
        ],
        out_specs=[share, share, part((1, D)), whole((8, D)), whole((tokens, D))],
        out_shape=[
            jax.ShapeDtypeStruct(shares + (3 * D,), jnp.bfloat16),
            jax.ShapeDtypeStruct(shares + (3 * D,), jnp.bfloat16),
            jax.ShapeDtypeStruct((1, 3 * D), jnp.float32),
            jax.ShapeDtypeStruct((8, D), jnp.float32),
            jax.ShapeDtypeStruct((tokens, D), jnp.float32),
        ],
        scratch_shapes=[
            pltpu.VMEM((rows, D), jnp.bfloat16),
            pltpu.VMEM((D, rows), jnp.bfloat16),
            pltpu.VMEM((rows, D), jnp.float32),
        ],
        compiler_params=pltpu.CompilerParams(
            vmem_limit_bytes=56 << 20, dimension_semantics=("arbitrary",)
        ),
        cost_estimate=pl.CostEstimate(flops=1000000, bytes_accessed=1000000, transcendentals=0),
        name="qkv_backward",
    )(coords, grad, normed, weight, xhat, inverse, gain, resid)


FF = 4304
GROUPS = 16
FF_GROUP = FF // GROUPS
FF_ROWS = 272
FF_PAD = GROUPS * FF_ROWS
HALF_DOWN = FF_ROWS // 2
OWN_ROWS = PAIR_ROWS // 2
TILE = 8
BLOCK_TILES = 5
PAIR_TILES = PAIR_ROWS // TILE
EXTRA = 128
QKV_CUT = 14 * 128
UP_CUT = 22 * 128
UP_PIECES = 4
DOWN_CUT = 40
DOWN_FIRST = 64
REST_ROWS = UP_PIECES * BLOCK_TILES * TILE + BLOCK_TILES * TILE + DOWN_FIRST
VECTORS = (0, 1, 3, 6, 8, 9, 10, 14, 12)
bf16 = jnp.bfloat16
f32 = jnp.float32


def product(left, right):
    return jnp.dot(left, right, preferred_element_type=f32)


def product_t(left, right):
    return lax.dot_general(left, right, (((0,), (0,)), ((), ())), preferred_element_type=f32)


def product_bt(left, right):
    return lax.dot_general(left, right, (((1,), (1,)), ((), ())), preferred_element_type=f32)


def swap(value, mask):
    devices = lax.axis_size("fsdp")
    return lax.ppermute(value, "fsdp", [(i, i ^ mask) for i in range(devices)])


def pad_hidden(columns):
    rows = columns.shape[0]
    grouped = columns.reshape(rows, GROUPS, FF_GROUP)
    return jnp.pad(grouped, ((0, 0), (0, 0), (0, FF_ROWS - FF_GROUP))).reshape(rows, FF_PAD)


def trim_hidden(columns):
    rows = columns.shape[0]
    return columns.reshape(rows, GROUPS, FF_ROWS)[:, :, :FF_GROUP].reshape(rows, FF)


def place_square_kernel(coords, *refs):
    sources, (whole, small) = refs[:8], refs[8:10]
    held, in_sems, out_sems = refs[10:18], refs[18], refs[19]
    core, x, y, z = coords[0], coords[1], coords[2], coords[3]
    arrivals = [pltpu.make_async_copy(sources[i], held[i], in_sems.at[i]) for i in range(8)]
    for arrival in arrivals:
        arrival.start()
    copies, extras = [], []
    for part, stream in itertools.product(range(4), range(2)):
        arrivals[4 * stream + part].wait()
        for near, dz in itertools.product(range(2), range(4)):
            src = held[4 * stream + part].at[near * 4 + dz]
            owner = core if part < 2 else 1 - core
            far = part % 2
            dx, dy = (near, far) if stream == 0 else (far, near)
            chip = ((z ^ dz) * 2 + (y ^ dy)) * 2 + (x ^ dx)
            cols = src.shape[-1] - (0 if stream else EXTRA)
            col = QKV_CUT - EXTRA if stream else 0
            src_cols = pl.ds(0 if stream else EXTRA, cols)
            first = PAIR_TILES * chip + BLOCK_TILES * owner
            copies.append(
                pltpu.make_async_copy(
                    src.at[pl.ds(owner, BLOCK_TILES - 1), :, src_cols],
                    whole.at[pl.ds(first, BLOCK_TILES - 1), :, pl.ds(col, cols)],
                    out_sems.at[len(copies)],
                )
            )
            copies[-1].start()
            extra = pltpu.make_async_copy(
                src.at[BLOCK_TILES - 1, :, src_cols],
                whole.at[PAIR_TILES * chip + BLOCK_TILES - 1, :, pl.ds(col, cols)],
                out_sems.at[96 + len(extras)],
            )
            pl.when(owner == 0)(extra.start)
            extras.append((owner, extra))
            if stream == 0:
                copies.append(
                    pltpu.make_async_copy(
                        src.at[:, :, :EXTRA], small.at[chip * 2 + owner], out_sems.at[len(copies)]
                    )
                )
                copies[-1].start()
    for copy in copies:
        copy.wait()
    for owner, extra in extras:
        pl.when(owner == 0)(extra.wait)


def place_square(streams, coords):
    sources = [s.reshape(8, BLOCK_TILES, TILE, -1) for s in (*streams[0], *streams[1])]
    size = sum(s.size for s in sources) * 2
    whole, small = pl.pallas_call(
        place_square_kernel,
        in_specs=[pl.BlockSpec(memory_space=pltpu.SMEM)]
        + [pl.BlockSpec(memory_space=pltpu.HBM)] * 8,
        out_specs=[pl.BlockSpec(memory_space=pltpu.HBM)] * 2,
        out_shape=[
            jax.ShapeDtypeStruct((GROUPS * PAIR_TILES, TILE, 3 * D), bf16),
            jax.ShapeDtypeStruct((2 * GROUPS, BLOCK_TILES, TILE, EXTRA), bf16),
        ],
        scratch_shapes=[pltpu.VMEM(s.shape, bf16) for s in sources]
        + [pltpu.SemaphoreType.DMA((8,)), pltpu.SemaphoreType.DMA((160,))],
        compiler_params=pltpu.CompilerParams(vmem_limit_bytes=40 << 20),
        cost_estimate=pl.CostEstimate(flops=0, bytes_accessed=2 * size, transcendentals=0),
        name="place_square",
    )(coords, *sources)
    return whole.reshape(D, 3 * D), small.reshape(2 * GROUPS, -1)


def place_rest_kernel(coords, *refs):
    source, streams, (up, out, down) = refs[0], refs[1:9], refs[9:12]
    held, in_sems, out_sems = refs[12], refs[13], refs[14]
    parts, part_sems = refs[15:23], refs[23]
    core, x, y, z = coords[0], coords[1], coords[2], coords[3]
    arrivals = [
        pltpu.make_async_copy(source.at[i], held.at[i], in_sems.at[i]) for i in range(2 * GROUPS)
    ]
    others = [pltpu.make_async_copy(streams[i], parts[i], part_sems.at[i]) for i in range(8)]
    for arrival in arrivals + others:
        arrival.start()
    copies = []

    def move(one, other):
        copies.append(pltpu.make_async_copy(one, other, out_sems.at[len(copies)]))
        copies[-1].start()

    lead = DOWN_FIRST // TILE
    for device in range(2 * GROUPS):
        chip, owner = device // 2, device % 2
        src = held.at[device]
        arrivals[device].wait()
        count = BLOCK_TILES - owner
        first = PAIR_TILES * chip + BLOCK_TILES * owner
        for piece in range(UP_PIECES):
            cols = min(D, FF_PAD - piece * D)
            move(
                src.at[pl.ds(piece * BLOCK_TILES + owner, count), :, pl.ds(0, cols)],
                up.at[pl.ds(first, count), :, pl.ds(piece * D, cols)],
            )
        base = UP_PIECES * BLOCK_TILES
        move(src.at[pl.ds(base + owner, count)], out.at[pl.ds(first, count)])
        move(src.at[pl.ds(base + BLOCK_TILES, lead)], down.at[device, pl.ds(0, lead)])
    for part, stream in itertools.product(range(4), range(2)):
        others[4 * stream + part].wait()
        for near, dz in itertools.product(range(2), range(4)):
            src = parts[4 * stream + part].at[near * 4 + dz]
            owner = core if part < 2 else 1 - core
            far = part % 2
            dx, dy = (near, far) if stream == 0 else (far, near)
            chip = ((z ^ dz) * 2 + (y ^ dy)) * 2 + (x ^ dx)
            first = lead + (DOWN_CUT // TILE if stream else 0)
            move(src, down.at[chip * 2 + owner, pl.ds(first, src.shape[0])])
    for copy in copies:
        copy.wait()


def place_rest(gathered, streams, coords):
    source = gathered.reshape(2 * GROUPS, REST_ROWS // TILE, TILE, D)
    sources = [s.reshape(8, -1, TILE, D) for s in (*streams[0], *streams[1])]
    up, out, down = pl.pallas_call(
        place_rest_kernel,
        in_specs=[pl.BlockSpec(memory_space=pltpu.SMEM)]
        + [pl.BlockSpec(memory_space=pltpu.HBM)] * 9,
        out_specs=[pl.BlockSpec(memory_space=pltpu.HBM)] * 3,
        out_shape=[
            jax.ShapeDtypeStruct((D // TILE, TILE, FF_PAD), bf16),
            jax.ShapeDtypeStruct((D // TILE, TILE, D), bf16),
            jax.ShapeDtypeStruct((2 * GROUPS, HALF_DOWN // TILE, TILE, D), bf16),
        ],
        scratch_shapes=[
            pltpu.VMEM(source.shape, bf16),
            pltpu.SemaphoreType.DMA((2 * GROUPS,)),
            pltpu.SemaphoreType.DMA((2 * GROUPS * (UP_PIECES + 2) + 64,)),
        ]
        + [pltpu.VMEM(s.shape, bf16) for s in sources]
        + [pltpu.SemaphoreType.DMA((8,))],
        compiler_params=pltpu.CompilerParams(vmem_limit_bytes=60 << 20),
        cost_estimate=pl.CostEstimate(
            flops=0, bytes_accessed=4 * source.size, transcendentals=0
        ),
        name="place_rest",
    )(coords, source, *sources)
    return up.reshape(D, FF_PAD), out.reshape(D, D), down.reshape(FF_PAD, D)


def tie(*values):
    leaves, form = jax.tree.flatten(values)
    return form.unflatten(lax.optimization_barrier(leaves))


def gather_z(block):
    return [block] + [swap(block, 8 * step) for step in (1, 2, 3)]


def gather_near(parts, cut, axis):
    streams = []
    for stream in range(2):
        if axis == 1:
            own = jnp.stack([p[:, :cut] if stream == 0 else p[:, cut:] for p in parts])
        else:
            own = jnp.stack([p[:cut] if stream == 0 else p[cut:] for p in parts])
        streams.append((own, swap(own, 4 if stream else 2)))
    return streams


def gather_far(streams):
    results = []
    for stream in range(2):
        first = jnp.concatenate(streams[stream])
        results.append((first, swap(first, 2 if stream else 4)))
    return results


def gather_core(streams):
    return [(first, second, swap(first, 1), swap(second, 1)) for first, second in streams]


def window(value, starts, sizes):
    rank = value.ndim
    starts = list(starts) + [0] * (rank - len(starts))
    lengths = list(value.shape)
    for axis, size in enumerate(sizes):
        if size is not None:
            lengths[axis] = size
    starts = [jnp.int32(0) if start is None else jnp.int32(start) for start in starts]
    result = lax.dynamic_slice(value, starts, lengths)
    kept = [
        length for axis, length in enumerate(lengths) if axis >= len(sizes) or sizes[axis] != 1
    ]
    return result.reshape(kept)


class Reduction:
    def __init__(self, keeps, streams, coords):
        self.keeps = [k.reshape(4, 2, 2, BLOCK_TILES, TILE, -1) for k in keeps]
        self.streams = streams
        self.coords = coords

    def part(self, arrays, stream, plane):
        sizes = tuple(None if p is None else 1 for p in plane) + (None, None)
        pieces = []
        for number, first, last in self.streams[stream]:
            starts = tuple(plane) + (None, None, first)
            pieces.append(window(arrays[number], starts, sizes + (last - first,)))
        return pieces[0] if len(pieces) == 1 else jnp.concatenate(pieces, axis=-1)

    def terms(self, stream, plane):
        return [self.part(self.keeps, stream, plane), self.part(self.other, stream, plane)]

    def core_step(self, sends):
        return [swap(send.reshape(4, 2, 2, BLOCK_TILES, TILE, -1), 1) for send in sends]

    def far_sends(self, other, streams=(0, 1), pieces=slice(None)):
        core, x, y, z = self.coords
        self.other = other
        sends = []
        every = self.streams
        for stream in streams:
            plane = (None, None, 1 - x) if stream else (None, 1 - y, None)
            self.streams = {stream: every[stream][pieces]}
            sends.append(total_of(self.terms(stream, plane)).astype(bf16))
        self.streams = every
        return sends

    def far_swap(self, sends):
        return [swap(send, 2 if stream else 4) for stream, send in enumerate(sends)]

    def near_sends(self, far):
        core, x, y, z = self.coords
        self.far = far
        sends = []
        for stream in range(2):
            plane = (None, 1 - y, x) if stream else (None, y, 1 - x)
            after = (None, 1 - y) if stream else (None, 1 - x)
            terms = self.terms(stream, plane) + [window(far[stream], after, (None, 1))]
            sends.append(total_of(terms).astype(bf16))
        return sends

    def near_swap(self, sends):
        return [swap(send, 4 if stream else 2) for stream, send in enumerate(sends)]

    def at(self, plane):
        core, x, y, z = self.coords
        pieces = []
        for stream in range(2):
            after = (plane, y) if stream else (plane, x)
            terms = self.terms(stream, (plane, y, x)) + [
                window(self.far[stream], after, (1, 1)),
                window(self.near[stream], (plane,), (1,)),
            ]
            pieces.append(total_of(terms))
        return jnp.concatenate(pieces, axis=-1)

    def z_sends(self, near):
        z = self.coords[3]
        self.near = near
        return [self.at(z ^ step).astype(bf16) for step in (1, 2, 3)]

    def z_swap(self, sends):
        return [swap(send, 8 * step) for step, send in zip((1, 2, 3), sends)]

    def finish(self, arrived):
        core, x, y, z = self.coords
        total = total_of([self.at(z)] + arrived)
        total = total.reshape(BLOCK_TILES * TILE, -1)
        return lax.dynamic_slice_in_dim(
            total, core * (BLOCK_TILES * TILE - OWN_ROWS), OWN_ROWS, 0
        )


def join_rows(keep, send):
    whole = jnp.concatenate([keep, send[:, 2 * BLOCK_ROWS - PAIR_ROWS :]], axis=1)
    return whole.reshape(D, -1)


def total_of(terms):
    total = terms[0].astype(f32)
    for term in terms[1:]:
        total = total + term.astype(f32)
    return total


def fetch_pairs(narrow, core):
    q, k, v, o = (narrow[i].reshape(OWN_ROWS, D) for i in (2, 4, 5, 7))
    up = pad_hidden(narrow[11].reshape(OWN_ROWS, FF))
    down = narrow[13]
    rows = jnp.concatenate([q, k, v, o, up], axis=1)
    spare = BLOCK_TILES * TILE - OWN_ROWS
    lead = D * HALF_DOWN - down.shape[0]
    tail = jnp.pad(down[:lead].reshape(spare, -1), ((0, 0), (0, 512 - lead // spare)))
    is_first = core == 0
    edge = jnp.where(is_first, rows[OWN_ROWS - spare :], rows[:spare])
    got = swap(jnp.concatenate([edge, tail], axis=1), 1)
    edge = got[:, : rows.shape[1]]
    block = jnp.where(is_first, jnp.concatenate([rows, edge]), jnp.concatenate([edge, rows]))
    extra = got[:, rows.shape[1] : rows.shape[1] + lead // spare].reshape(-1)
    end = jnp.zeros((D * HALF_DOWN - (down.shape[0] - lead),), bf16)
    down_block = jnp.where(
        is_first, jnp.concatenate([down, extra]), jnp.concatenate([down[lead:], end])
    ).reshape(HALF_DOWN, D)
    small = jnp.concatenate([narrow[i] for i in VECTORS])
    small = jnp.pad(small, (0, BLOCK_TILES * TILE * EXTRA - small.shape[0]))
    small = small.reshape(BLOCK_TILES * TILE, EXTRA)
    square = jnp.concatenate([small, block[:, : 3 * D]], axis=1)
    up_block = jnp.pad(block[:, 4 * D :], ((0, 0), (0, UP_PIECES * D - FF_PAD)))
    pieces = [up_block[:, i * D : (i + 1) * D] for i in range(UP_PIECES)]
    rest = jnp.concatenate(pieces + [block[:, 3 * D : 4 * D], down_block[:DOWN_FIRST]])
    return square, rest, down_block[DOWN_FIRST:]


def normalize(values):
    centre = jnp.mean(values, axis=-1, keepdims=True)
    centered = values - centre
    spread_sq = jnp.mean(centered * centered, axis=-1, keepdims=True)
    inverse = lax.rsqrt(spread_sq + 1e-06)
    return centered * inverse, inverse


def normalize_back(grad, gain, xhat, inverse):
    scaled = grad * gain
    first = jnp.mean(scaled, axis=-1, keepdims=True)
    second = jnp.mean(scaled * xhat, axis=-1, keepdims=True)
    return inverse * (scaled - first - xhat * second)


def name_vectors(whole, widths):
    count = len(VECTORS) - 1
    width = widths[VECTORS[0]]
    pieces = whole[:, : count * width].reshape(-1, count, width)
    pieces = pieces.transpose(1, 0, 2).reshape(count, -1).astype(f32)
    found = {i: pieces[position] for position, i in enumerate(VECTORS[:-1])}
    last = widths[VECTORS[-1]]
    found[VECTORS[-1]] = whole[:, count * width : count * width + last].reshape(-1).astype(f32)
    return found


def pack_vectors(grads, widths, devices):
    count = len(VECTORS) - 1
    width = widths[VECTORS[0]]
    rows = jnp.stack([grads[i] for i in VECTORS[:-1]])
    rows = jnp.pad(rows, ((0, 0), (0, width * devices - rows.shape[1])))
    rows = rows.reshape(count, devices, width).transpose(1, 0, 2).reshape(devices, -1)
    last = grads[VECTORS[-1]]
    last = jnp.pad(last, (0, widths[VECTORS[-1]] * devices - last.shape[0]))
    return jnp.concatenate([rows, last.reshape(devices, -1)], axis=1)


def gather_plain(narrow, widths):
    whole = {
        i: lax.all_gather(narrow[i], "fsdp", axis=0, tiled=True) for i in (2, 4, 5, 7, 11, 13)
    }
    square = [whole[i][: D * D].reshape(D, D) for i in (2, 4, 5, 7)]
    up = pad_hidden(whole[11][: D * FF].reshape(D, FF))
    down = pad_hidden(whole[13][: D * FF].reshape(FF, D).T).T
    joined = jnp.concatenate([narrow[i] for i in VECTORS])
    length = joined.shape[0]
    joined = jnp.pad(joined, (0, 2048 - length)).reshape(16, 128)
    joined = lax.all_gather(joined, "fsdp", axis=0, tiled=True).reshape(-1, 2048)
    return jnp.concatenate(square[:3], axis=1), square[3], up, down, name_vectors(joined, widths)


def on_device(*args):
    devices = lax.axis_size("fsdp")
    tokens, image_valid = args[0], args[1]
    shards = args[2:17]
    cotangent = args[17]
    staged = devices == 32
    widths = [piece.shape[0] for piece in shards]
    narrow = [piece.astype(bf16) for piece in shards]
    index = lax.axis_index("fsdp")
    core, x, y, z = index % 2, (index // 2) % 2, (index // 4) % 2, index // 8
    coords = (core, x, y, z)
    image_count = image_valid.shape[0]
    seq_len = tokens.shape[0] // image_count
    weight_img = jnp.repeat(image_valid.astype(f32), seq_len)[:, None]

    grad_out = weight_img * cotangent
    grad_branch = grad_out.astype(bf16)
    grads = {14: jnp.sum(grad_branch.astype(f32), axis=0)}
    xhat_one, inverse_one = normalize(tokens)
    where = jnp.stack(coords if staged else (jnp.int32(0),) * 4).astype(jnp.int32)
    if staged:
        sq, rest, down = fetch_pairs(narrow, core)
        rest = lax.all_gather(rest, "fsdp", axis=0, tiled=True)
        sq = gather_z(sq)
        sq, down, xhat_one, inverse_one, grad_branch = tie(
            sq, down, xhat_one, inverse_one, grad_branch
        )
        sq = gather_near(sq, QKV_CUT, 1)
        down = gather_z(down)
        sq = gather_far(sq)
        sq, down = tie(sq, down)
        sq = gather_core(sq)
        down = gather_near(down, DOWN_CUT, 0)
        weight_qkv, small = place_square(sq, where)
        vectors = name_vectors(small, widths)
    else:
        weight_qkv, weight_o, weight_up, weight_down, vectors = gather_plain(narrow, widths)

    vec = lambda i: vectors[i][:D]
    gain_one, shift_one, gain_two, shift_two = vec(0), vec(1), vec(9), vec(10)
    bias_qkv = jnp.concatenate([vec(3), jnp.zeros((D,), f32), vec(6)])
    bias_o, bias_down = vec(8), vec(14)
    bias_up = pad_hidden(vectors[12][:FF].reshape(1, FF))

    normed = (xhat_one * gain_one + shift_one).astype(bf16)
    qkv = (product(normed, weight_qkv) + bias_qkv).astype(bf16)
    if staged:
        qkv, down = tie(qkv, down)
        down = gather_far(down)
    mixed, lse = attn_fwd(qkv, 2)
    if staged:
        mixed, lse, down = tie(mixed, lse, down)
        down = gather_core(down)
        weight_up, weight_o, weight_down = place_rest(rest, down, where)
    resid = tokens + product(mixed, weight_o) + bias_o
    xhat_two, inverse_two = normalize(resid)
    normed_two = (xhat_two * gain_two + shift_two).astype(bf16)
    (
        branch,
        up_keep,
        up_send,
        up_bias_grad,
        down_grad,
        sums_two,
        grad_resid,
        o_keep,
        o_send,
        grad_mixed,
    ) = mlp(
        where,
        normed_two,
        grad_branch,
        weight_up,
        bias_up,
        weight_down,
        xhat_two,
        inverse_two,
        gain_two.reshape(1, D),
        grad_out,
        mixed,
        weight_o,
    )
    up_bias_grad = up_bias_grad.reshape(FF_PAD)
    layer_out = weight_img * (resid + branch + bias_down)
    grads[9], grads[10], grads[8] = sums_two[0], sums_two[1], sums_two[2]
    if staged:
        down_sum = lax.psum_scatter(down_grad, "fsdp", scatter_dimension=0, tiled=True)
    if staged:
        outer = Reduction(
            (up_keep, o_keep), (((0, 0, UP_CUT),), ((0, UP_CUT, FF_PAD), (1, 0, D))), coords
        )
        outer_other = outer.core_step((up_send, o_send))
        grad_mixed, outer_other = tie(grad_mixed, outer_other)
        outer_far = outer.far_swap(outer.far_sends(outer_other))
    grad_qkv = attn_bwd(qkv, grad_mixed, lse, 2)
    if staged:
        grad_qkv, outer_far = tie(grad_qkv, outer_far)
        outer_near = outer.near_sends(outer_far)
        grad_qkv, outer_near = tie(grad_qkv, outer_near)
        outer_near = outer.near_swap(outer_near)
    qkv_keep, qkv_send, qkv_bias_grad, norm_sums, tokens_grad = qkv_back(
        where,
        grad_qkv,
        normed,
        weight_qkv,
        xhat_one,
        inverse_one,
        gain_one.reshape(1, D),
        grad_resid,
    )
    if staged:
        qkv_keep, qkv_send, norm_sums, qkv_bias_grad, outer_near = tie(
            qkv_keep, qkv_send, norm_sums, qkv_bias_grad, outer_near
        )
        outer_z = outer.z_sends(outer_near)
        qkv_other = outer.core_step((qkv_send,))[0]
    grads[3], grads[6] = qkv_bias_grad[0, :D], qkv_bias_grad[0, 2 * D :]
    grads[0], grads[1] = norm_sums[0], norm_sums[1]
    grads[12] = trim_hidden(up_bias_grad.reshape(1, FF_PAD)).reshape(FF)

    rows = pack_vectors(grads, widths, devices)
    owned = [None] * 15
    if staged:
        rows = jnp.pad(rows, ((0, 0), (0, OWN_ROWS * EXTRA - rows.shape[1])))
        rows = rows.reshape(GROUPS, PAIR_ROWS, EXTRA).astype(bf16)
        top, bottom = rows[:, :BLOCK_ROWS], rows[:, PAIR_ROWS - BLOCK_ROWS :]
        rows_keep = jnp.where(core == 0, top, bottom)
        rows_send = jnp.where(core == 0, bottom, top)
        rows_other = outer.core_step((rows_send,))[0]
        cut = QKV_CUT - EXTRA
        inner = Reduction(
            (qkv_keep, rows_keep), (((0, 0, cut), (1, 0, EXTRA)), ((0, cut, 3 * D),)), coords
        )
        qkv_other, rows_other, outer_z = tie(qkv_other, rows_other, outer_z)
        inner_far = inner.far_swap(inner.far_sends((qkv_other, rows_other)))
        outer_z = outer.z_swap(outer_z)
        inner_far, layer_out = tie(inner_far, layer_out)
        inner_near = inner.near_swap(inner.near_sends(inner_far))
        outer_sum = outer.finish(outer_z)
        owned[11] = trim_hidden(outer_sum[:, :FF_PAD]).reshape(-1)
        owned[7] = outer_sum[:, FF_PAD:].reshape(-1)
        inner_near, down_sum, owned[11], owned[7] = tie(
            inner_near, down_sum, owned[11], owned[7]
        )
        inner_z = inner.z_sends(inner_near)
        inner_z, down_sum = tie(inner_z, down_sum)
        inner_z = inner.z_swap(inner_z)

        flat = down_sum.astype(f32).reshape(-1)
        size = widths[13]
        lead = flat.shape[0] - size
        got = swap(down_sum.reshape(-1)[size:], 1).astype(f32)
        owned[13] = jnp.where(core == 0, flat[:size], jnp.concatenate([got, flat[: size - lead]]))
        inner_sum = inner.finish(inner_z)
        first = QKV_CUT - EXTRA
        owned[2] = inner_sum[:, :D].reshape(-1)
        owned[4] = jnp.concatenate(
            [inner_sum[:, D:first], inner_sum[:, QKV_CUT : 2 * D + EXTRA]], axis=1
        ).reshape(-1)
        owned[5] = inner_sum[:, 2 * D + EXTRA :].reshape(-1)
        small = inner_sum[:, first:QKV_CUT].reshape(-1)
    else:
        scatter = lambda value: lax.psum_scatter(
            value.astype(f32).reshape(-1), "fsdp", scatter_dimension=0, tiled=True
        )
        fill = lambda value, i: jnp.pad(
            value.reshape(-1), (0, widths[i] * devices - value.size)
        )
        qkv_grad = join_rows(qkv_keep, qkv_send)
        for position, i in enumerate((2, 4, 5)):
            owned[i] = scatter(fill(qkv_grad[:, position * D : (position + 1) * D], i))
        owned[7] = scatter(fill(join_rows(o_keep, o_send), 7))
        owned[11] = scatter(fill(trim_hidden(join_rows(up_keep, up_send)), 11))
        owned[13] = scatter(fill(trim_hidden(down_grad.T).T, 13))
        small = scatter(rows)
    position = 0
    for i in VECTORS:
        owned[i] = small[position : position + widths[i]]
        position += widths[i]
    return (layer_out, tokens_grad, *owned)


def solution(mesh):
    row, flat = P("fsdp", None), P("fsdp")
    in_specs = (row, flat) + (flat,) * 15 + (row,)
    out_specs = (row, row) + (flat,) * 15
    return jax.shard_map(
        on_device, mesh=mesh, in_specs=in_specs, out_specs=out_specs, check_vma=False
    )
```

```python
import functools
import itertools
import jax
import jax.numpy as jnp
from jax import lax
from jax.sharding import PartitionSpec as P
from jax.experimental import pallas as pl
from jax.experimental.pallas import tpu as pltpu
D=1152; HEADS=16; HEAD_DIM=72; LANES=128
NEG=-1e30
LOG2E=1.4426950408889634
def nt(a,b): return lax.dot_general(a,b,(((1,),(1,)),((),())),preferred_element_type=jnp.float32)
def nn(a,b): return lax.dot_general(a,b,(((1,),(0,)),((),())),preferred_element_type=jnp.float32)

def fill_heads(dst, src, col, tokens, fill, first=0):
    for h in range(dst.shape[0]):
        start=col+(first+h)*HEAD_DIM
        dst[h]=fill
        dst[h,0:tokens,0:HEAD_DIM]=src[:,start:start+HEAD_DIM]

def pad_values(rows, tokens, kind):
    lane=lax.broadcasted_iota(jnp.int32,(rows,LANES),1)
    row=lax.broadcasted_iota(jnp.int32,(rows,LANES),0)
    if kind=="query":
        v=jnp.where(lane==HEAD_DIM,1.0,0.0)
    elif kind=="key":
        v=jnp.where((lane==HEAD_DIM)&(row>=tokens),NEG,0.0)
    else:
        v=jnp.zeros((rows,LANES),jnp.float32)
    return v.astype(jnp.bfloat16)

def fwd_kernel(tokens, krows, qrows, per, qkv_ref, mixed_ref, lse_ref, qs, ks, vs, os):
    step=pl.program_id(0)
    @pl.when(step==0)
    def _():
        fill_heads(qs,qkv_ref,0,tokens,pad_values(qrows,tokens,"query"))
        fill_heads(ks,qkv_ref,D,tokens,pad_values(krows,tokens,"key"))
        zero=pad_values(krows,tokens,"value")
        for h in range(HEADS):
            vs[h]=zero
            vs[h,0:tokens,0:HEAD_DIM]=qkv_ref[:,2*D+h*HEAD_DIM:2*D+(h+1)*HEAD_DIM]
    c=HEAD_DIM**-0.5*LOG2E
    for j in range(per):
        h=step*per+j
        s=nt(ks[h],qs[h])
        m=jnp.max(s,axis=0,keepdims=True)
        e=jnp.exp2((s-m)*c)
        l=jnp.sum(e,axis=0,keepdims=True)
        p=(e*(1.0/l)).astype(jnp.bfloat16)
        vt=vs[h].T
        ot=nn(vt,p)
        os[h]=ot.T.astype(jnp.bfloat16)
        lse_ref[j]=m*c+jnp.log2(l)
    @pl.when(step==pl.num_programs(0)-1)
    def _():
        for h in range(HEADS):
            mixed_ref[:,h*HEAD_DIM:(h+1)*HEAD_DIM]=os[h,0:tokens,0:HEAD_DIM]

def attn_fwd(qkv, per=1):
    tokens=qkv.shape[0]
    krows=-(-tokens//16)*16; qrows=-(-tokens//128)*128
    return pl.pallas_call(functools.partial(fwd_kernel,tokens,krows,qrows,per),
        grid=(HEADS//per,),
        in_specs=[pl.BlockSpec(qkv.shape,lambda i:(0,0),pipeline_mode=pl.Buffered(1))],
        out_specs=[pl.BlockSpec((tokens,D),lambda i:(0,0),pipeline_mode=pl.Buffered(1)),pl.BlockSpec((per,1,qrows),lambda i:(i,0,0))],
        out_shape=[jax.ShapeDtypeStruct((tokens,D),jnp.bfloat16),jax.ShapeDtypeStruct((HEADS,1,qrows),jnp.float32)],
        scratch_shapes=[pltpu.VMEM((HEADS,qrows,LANES),jnp.bfloat16),pltpu.VMEM((HEADS,krows,LANES),jnp.bfloat16),
                        pltpu.VMEM((HEADS,krows,LANES),jnp.bfloat16),pltpu.VMEM((HEADS,qrows,LANES),jnp.bfloat16)],
        compiler_params=pltpu.CompilerParams(vmem_limit_bytes=56<<20,dimension_semantics=("arbitrary",)),
        cost_estimate=pl.CostEstimate(flops=4*HEADS*qrows*krows*LANES,bytes_accessed=4*tokens*D*2,transcendentals=HEADS*qrows*krows),
        name="attention_forward")(qkv)

def bwd_kernel(tokens, krows, qrows, per, first, qkv_ref, go_ref, lse_ref, dqkv_ref, qs, ks, vs, gs):
    step=pl.program_id(0)
    @pl.when(step==0)
    def _():
        fill_heads(qs,qkv_ref,0,tokens,pad_values(qrows,tokens,"query"),first)
        fill_heads(ks,qkv_ref,D,tokens,pad_values(krows,tokens,"key"),first)
        fill_heads(vs,qkv_ref,2*D,tokens,pad_values(krows,tokens,"value"),first)
        fill_heads(gs,go_ref,0,tokens,pad_values(qrows,tokens,"value"),first)
    scale=HEAD_DIM**-0.5
    c=scale*LOG2E
    for j in range(per):
        h=step*per+j
        q=qs[h]; k=ks[h]; v=vs[h]; g=gs[h]
        s=nt(k,q)
        p=jnp.exp2(s*c-lse_ref[j])
        dp=nt(v,g)
        dv=nn(p.astype(jnp.bfloat16),g)
        delta=jnp.sum(p*dp,axis=0,keepdims=True)
        ds=(p*(dp-delta)).astype(jnp.bfloat16)
        dk=nn(ds,q)*scale
        dqt=nn(k.T,ds)*scale
        qs[h]=dqt.T.astype(jnp.bfloat16)
        ks[h]=dk.astype(jnp.bfloat16)
        vs[h]=dv.astype(jnp.bfloat16)
    @pl.when(step==pl.num_programs(0)-1)
    def _():
        for i,r in enumerate((qs,ks,vs)):
            for h in range(qs.shape[0]):
                dqkv_ref[i,:,h*HEAD_DIM:(h+1)*HEAD_DIM]=r[h,0:tokens,0:HEAD_DIM]

def attn_bwd(qkv, gmixed, lse, per, first, count):
    tokens=qkv.shape[0]
    krows=-(-tokens//16)*16; qrows=-(-tokens//128)*128
    return pl.pallas_call(functools.partial(bwd_kernel,tokens,krows,qrows,per,first),
        grid=(count//per,),
        in_specs=[pl.BlockSpec(qkv.shape,lambda i:(0,0),pipeline_mode=pl.Buffered(1)),pl.BlockSpec(gmixed.shape,lambda i:(0,0),pipeline_mode=pl.Buffered(1)),
                  pl.BlockSpec((per,1,qrows),lambda i:(i+first//per,0,0))],
        out_specs=pl.BlockSpec((3,tokens,count*HEAD_DIM),lambda i:(0,0,0),pipeline_mode=pl.Buffered(1)),
        out_shape=jax.ShapeDtypeStruct((3,tokens,count*HEAD_DIM),jnp.bfloat16),
        scratch_shapes=[pltpu.VMEM((count,qrows,LANES),jnp.bfloat16),pltpu.VMEM((count,krows,LANES),jnp.bfloat16),
                        pltpu.VMEM((count,krows,LANES),jnp.bfloat16),pltpu.VMEM((count,qrows,LANES),jnp.bfloat16)],
        compiler_params=pltpu.CompilerParams(vmem_limit_bytes=56<<20,dimension_semantics=("arbitrary",)),
        cost_estimate=pl.CostEstimate(flops=1000000,bytes_accessed=1000000,transcendentals=0),
        name="attention_backward")(qkv,gmixed,lse)


GELU_A = 0.7978845608028654
GELU_B = 0.044715


PAIR_ROWS = D // HEADS
BLOCK_ROWS = 40


def share_rows(core, value, keep_ref, send_ref):
    for chip in range(value.shape[0] // PAIR_ROWS):
        first = value[chip * PAIR_ROWS : chip * PAIR_ROWS + BLOCK_ROWS]
        last = value[(chip + 1) * PAIR_ROWS - BLOCK_ROWS : (chip + 1) * PAIR_ROWS]
        keep_ref[chip] = jnp.where(core == 0, first, last).astype(jnp.bfloat16)
        send_ref[chip] = jnp.where(core == 0, last, first).astype(jnp.bfloat16)


def mlp_kernel(coords, normed_ref, grad_ref, up_ref, bias_ref, down_ref, xhat_ref, inverse_ref, gain_ref,
               grad_out_ref, mixed_ref, output_ref, out_ref, up_keep_ref, up_send_ref, bias_grad_ref,
               down_grad_ref, sums_ref, resid_grad_ref, output_keep_ref, output_send_ref, mixed_grad_ref,
               normed, normed_t, grad, out, back):
    step = pl.program_id(0)
    tokens = normed_ref.shape[0]

    @pl.when(step == 0)
    def _():
        for held, source in ((normed, normed_ref), (grad, grad_ref)):
            held[...] = jnp.zeros_like(held)
            held[0:tokens] = source[...]
        normed_t[...] = normed[...].T
        out[...] = jnp.zeros_like(out)
        back[...] = jnp.zeros_like(back)

    pre = nn(normed[...], up_ref[...]) + bias_ref[...]
    square = pre * pre
    bend = jnp.tanh(pre * (GELU_A + GELU_A * GELU_B * square))
    hidden = (0.5 * pre * (1.0 + bend)).astype(jnp.bfloat16)
    slope = 0.5 * (1.0 + bend) + 0.5 * pre * (1.0 - bend * bend) * (
        GELU_A + 3.0 * GELU_A * GELU_B * square
    )
    grad_pre = (nt(grad[...], down_ref[...]) * slope).astype(jnp.bfloat16)
    out[...] += nn(hidden, down_ref[...])
    back[...] += nt(grad_pre, up_ref[...])
    down_grad_ref[...] = nn(hidden.T, grad[...]).astype(jnp.bfloat16)
    share_rows(coords[0], nn(normed_t[...], grad_pre), up_keep_ref, up_send_ref)
    bias_grad_ref[...] = jnp.sum(grad_pre.astype(jnp.float32), axis=0, keepdims=True)

    @pl.when(step == pl.num_programs(0) - 1)
    def _():
        out_ref[...] = out[0:tokens]
        total = back[0:tokens]
        xhat = xhat_ref[...]
        sums_ref[0:1] = jnp.sum(total * xhat, axis=0, keepdims=True)
        sums_ref[1:2] = jnp.sum(total, axis=0, keepdims=True)
        scaled = total * gain_ref[...]
        first = jnp.mean(scaled, axis=-1, keepdims=True)
        second = jnp.mean(scaled * xhat, axis=-1, keepdims=True)
        resid_grad = grad_out_ref[...] + inverse_ref[...] * (scaled - first - xhat * second)
        resid_grad_ref[...] = resid_grad
        grad[0:tokens] = resid_grad.astype(jnp.bfloat16)
        low = grad[...]
        sums_ref[2:3] = jnp.sum(low.astype(jnp.float32), axis=0, keepdims=True)
        mixed_grad_ref[...] = nt(low, output_ref[...]).astype(jnp.bfloat16)[0:tokens]
        normed[0:tokens] = mixed_ref[...]
        normed_t[...] = normed[...].T
        share_rows(coords[0], nn(normed_t[...], low), output_keep_ref, output_send_ref)


def whole_block(shape):
    return pl.BlockSpec(shape, lambda i: (0, 0), pipeline_mode=pl.Buffered(1))


def mlp(coords, normed, grad, up, bias, down, xhat, inverse, gain, grad_out, mixed, output):
    tokens, hidden = normed.shape[0], up.shape[1]
    rows = -(-tokens // 16) * 16
    tile = 256
    full = whole_block((tokens, D))
    columns = pl.BlockSpec((D, tile), lambda i: (0, i))
    line = pl.BlockSpec((1, tile), lambda i: (0, i))
    band = pl.BlockSpec((tile, D), lambda i: (i, 0))
    square = whole_block((D, D))
    shares = (D // PAIR_ROWS, BLOCK_ROWS)
    part = pl.BlockSpec(shares + (tile,), lambda i: (0, 0, i))
    full_part = pl.BlockSpec(
        shares + (D,), lambda i: (0, 0, 0), pipeline_mode=pl.Buffered(1)
    )
    return pl.pallas_call(
        mlp_kernel,
        grid=(hidden // tile,),
        in_specs=[pl.BlockSpec(memory_space=pltpu.SMEM), full, full, columns, line, band, full, whole_block((tokens, 1)),
                  whole_block((1, D)), full, full, square],
        out_specs=[full, part, part, line, band, whole_block((8, D)), full, full_part, full_part,
                   full],
        out_shape=[
            jax.ShapeDtypeStruct((tokens, D), jnp.float32),
            jax.ShapeDtypeStruct(shares + (hidden,), jnp.bfloat16),
            jax.ShapeDtypeStruct(shares + (hidden,), jnp.bfloat16),
            jax.ShapeDtypeStruct((1, hidden), jnp.float32),
            jax.ShapeDtypeStruct((hidden, D), jnp.bfloat16),
            jax.ShapeDtypeStruct((8, D), jnp.float32),
            jax.ShapeDtypeStruct((tokens, D), jnp.float32),
            jax.ShapeDtypeStruct(shares + (D,), jnp.bfloat16),
            jax.ShapeDtypeStruct(shares + (D,), jnp.bfloat16),
            jax.ShapeDtypeStruct((tokens, D), jnp.bfloat16),
        ],
        scratch_shapes=[
            pltpu.VMEM((rows, D), jnp.bfloat16),
            pltpu.VMEM((D, rows), jnp.bfloat16),
            pltpu.VMEM((rows, D), jnp.bfloat16),
            pltpu.VMEM((rows, D), jnp.float32),
            pltpu.VMEM((rows, D), jnp.float32),
        ],
        compiler_params=pltpu.CompilerParams(
            vmem_limit_bytes=56 << 20, dimension_semantics=("arbitrary",)
        ),
        cost_estimate=pl.CostEstimate(flops=1000000, bytes_accessed=1000000, transcendentals=0),
        name="mlp_forward_backward",
    )(coords, normed, grad, up, bias, down, xhat, inverse, gain, grad_out, mixed, output)


def qkv_back_kernel(coords, first_ref, second_ref, normed_ref, weight_ref, xhat_ref, inverse_ref, gain_ref, resid_ref,
                    keep_ref, send_ref, bias_grad_ref, sums_ref, tokens_ref, grad, normed_t, total):
    step = pl.program_id(0)
    tokens = normed_ref.shape[0]

    @pl.when(step == 0)
    def _():
        grad[...] = jnp.zeros_like(grad)
        grad[0:tokens] = normed_ref[...]
        normed_t[...] = grad[...].T
        grad[...] = jnp.zeros_like(grad)
        total[...] = jnp.zeros_like(total)

    cut = first_ref.shape[-1]
    grad[0:tokens, 0:cut] = first_ref[0]
    grad[0:tokens, cut:D] = second_ref[0]
    share_rows(coords[0], nn(normed_t[...], grad[...]), keep_ref, send_ref)
    bias_grad_ref[...] = jnp.sum(grad[...].astype(jnp.float32), axis=0, keepdims=True)
    total[...] += nt(grad[...], weight_ref[...])

    @pl.when(step == pl.num_programs(0) - 1)
    def _():
        back = total[0:tokens]
        xhat = xhat_ref[...]
        sums_ref[0:1] = jnp.sum(back * xhat, axis=0, keepdims=True)
        sums_ref[1:2] = jnp.sum(back, axis=0, keepdims=True)
        scaled = back * gain_ref[...]
        first = jnp.mean(scaled, axis=-1, keepdims=True)
        second = jnp.mean(scaled * xhat, axis=-1, keepdims=True)
        tokens_ref[...] = resid_ref[...] + inverse_ref[...] * (scaled - first - xhat * second)


def qkv_back(coords, first, second, normed, weight, xhat, inverse, gain, resid):
    tokens = normed.shape[0]
    rows = -(-tokens // 16) * 16
    whole = lambda shape: pl.BlockSpec(shape, lambda i: (0, 0), pipeline_mode=pl.Buffered(1))
    part = lambda shape: pl.BlockSpec(shape, lambda i: (0, i))
    shares = (D // PAIR_ROWS, BLOCK_ROWS)
    share = pl.BlockSpec(shares + (D,), lambda i: (0, 0, i))
    return pl.pallas_call(
        qkv_back_kernel,
        grid=(3,),
        in_specs=[
            pl.BlockSpec(memory_space=pltpu.SMEM),
            pl.BlockSpec((1,) + first.shape[1:], lambda i: (i, 0, 0)),
            pl.BlockSpec((1,) + second.shape[1:], lambda i: (i, 0, 0)),
            whole((tokens, D)),
            part((D, D)),
            whole((tokens, D)),
            whole((tokens, 1)),
            whole((1, D)),
            whole((tokens, D)),
        ],
        out_specs=[share, share, part((1, D)), whole((8, D)), whole((tokens, D))],
        out_shape=[
            jax.ShapeDtypeStruct(shares + (3 * D,), jnp.bfloat16),
            jax.ShapeDtypeStruct(shares + (3 * D,), jnp.bfloat16),
            jax.ShapeDtypeStruct((1, 3 * D), jnp.float32),
            jax.ShapeDtypeStruct((8, D), jnp.float32),
            jax.ShapeDtypeStruct((tokens, D), jnp.float32),
        ],
        scratch_shapes=[
            pltpu.VMEM((rows, D), jnp.bfloat16),
            pltpu.VMEM((D, rows), jnp.bfloat16),
            pltpu.VMEM((rows, D), jnp.float32),
        ],
        compiler_params=pltpu.CompilerParams(
            vmem_limit_bytes=56 << 20, dimension_semantics=("arbitrary",)
        ),
        cost_estimate=pl.CostEstimate(flops=1000000, bytes_accessed=1000000, transcendentals=0),
        name="qkv_backward",
    )(coords, first, second, normed, weight, xhat, inverse, gain, resid)


FF = 4304
GROUPS = 16
FF_GROUP = FF // GROUPS
FF_ROWS = 272
FF_PAD = GROUPS * FF_ROWS
HALF_DOWN = FF_ROWS // 2
OWN_ROWS = PAIR_ROWS // 2
TILE = 8
BLOCK_TILES = 5
PAIR_TILES = PAIR_ROWS // TILE
EXTRA = 128
QKV_CUT = 14 * 128
UP_CUT = 22 * 128
UP_PIECES = 4
DOWN_CUT = 40
DOWN_FIRST = 64
REST_ROWS = UP_PIECES * BLOCK_TILES * TILE + BLOCK_TILES * TILE + DOWN_FIRST
VECTORS = (0, 1, 3, 6, 8, 9, 10, 14, 12)
bf16 = jnp.bfloat16
f32 = jnp.float32


def product(left, right):
    return jnp.dot(left, right, preferred_element_type=f32)


def product_t(left, right):
    return lax.dot_general(left, right, (((0,), (0,)), ((), ())), preferred_element_type=f32)


def product_bt(left, right):
    return lax.dot_general(left, right, (((1,), (1,)), ((), ())), preferred_element_type=f32)


def swap(value, mask):
    devices = lax.axis_size("fsdp")
    return lax.ppermute(value, "fsdp", [(i, i ^ mask) for i in range(devices)])


def pad_hidden(columns):
    rows = columns.shape[0]
    grouped = columns.reshape(rows, GROUPS, FF_GROUP)
    return jnp.pad(grouped, ((0, 0), (0, 0), (0, FF_ROWS - FF_GROUP))).reshape(rows, FF_PAD)


def trim_hidden(columns):
    rows = columns.shape[0]
    return columns.reshape(rows, GROUPS, FF_ROWS)[:, :, :FF_GROUP].reshape(rows, FF)


def place_square_kernel(coords, *refs):
    sources, (whole, small) = refs[:8], refs[8:10]
    held, in_sems, out_sems = refs[10:18], refs[18], refs[19]
    core, x, y, z = coords[0], coords[1], coords[2], coords[3]
    arrivals = [pltpu.make_async_copy(sources[i], held[i], in_sems.at[i]) for i in range(8)]
    for arrival in arrivals:
        arrival.start()
    copies, extras = [], []
    for part, stream in itertools.product(range(4), range(2)):
        arrivals[4 * stream + part].wait()
        for near, dz in itertools.product(range(2), range(4)):
            src = held[4 * stream + part].at[near * 4 + dz]
            owner = core if part < 2 else 1 - core
            far = part % 2
            dx, dy = (near, far) if stream == 0 else (far, near)
            chip = ((z ^ dz) * 2 + (y ^ dy)) * 2 + (x ^ dx)
            cols = src.shape[-1] - (0 if stream else EXTRA)
            col = QKV_CUT - EXTRA if stream else 0
            src_cols = pl.ds(0 if stream else EXTRA, cols)
            first = PAIR_TILES * chip + BLOCK_TILES * owner
            copies.append(
                pltpu.make_async_copy(
                    src.at[pl.ds(owner, BLOCK_TILES - 1), :, src_cols],
                    whole.at[pl.ds(first, BLOCK_TILES - 1), :, pl.ds(col, cols)],
                    out_sems.at[len(copies)],
                )
            )
            copies[-1].start()
            extra = pltpu.make_async_copy(
                src.at[BLOCK_TILES - 1, :, src_cols],
                whole.at[PAIR_TILES * chip + BLOCK_TILES - 1, :, pl.ds(col, cols)],
                out_sems.at[96 + len(extras)],
            )
            pl.when(owner == 0)(extra.start)
            extras.append((owner, extra))
            if stream == 0:
                copies.append(
                    pltpu.make_async_copy(
                        src.at[:, :, :EXTRA], small.at[chip * 2 + owner], out_sems.at[len(copies)]
                    )
                )
                copies[-1].start()
    for copy in copies:
        copy.wait()
    for owner, extra in extras:
        pl.when(owner == 0)(extra.wait)


def place_square(streams, coords):
    sources = [s.reshape(8, BLOCK_TILES, TILE, -1) for s in (*streams[0], *streams[1])]
    size = sum(s.size for s in sources) * 2
    whole, small = pl.pallas_call(
        place_square_kernel,
        in_specs=[pl.BlockSpec(memory_space=pltpu.SMEM)]
        + [pl.BlockSpec(memory_space=pltpu.HBM)] * 8,
        out_specs=[pl.BlockSpec(memory_space=pltpu.HBM)] * 2,
        out_shape=[
            jax.ShapeDtypeStruct((GROUPS * PAIR_TILES, TILE, 3 * D), bf16),
            jax.ShapeDtypeStruct((2 * GROUPS, BLOCK_TILES, TILE, EXTRA), bf16),
        ],
        scratch_shapes=[pltpu.VMEM(s.shape, bf16) for s in sources]
        + [pltpu.SemaphoreType.DMA((8,)), pltpu.SemaphoreType.DMA((160,))],
        compiler_params=pltpu.CompilerParams(vmem_limit_bytes=40 << 20),
        cost_estimate=pl.CostEstimate(flops=0, bytes_accessed=2 * size, transcendentals=0),
        name="place_square",
    )(coords, *sources)
    return whole.reshape(D, 3 * D), small.reshape(2 * GROUPS, -1)


def place_rest_kernel(coords, *refs):
    source, streams, (up, out, down) = refs[0], refs[1:9], refs[9:12]
    held, in_sems, out_sems = refs[12], refs[13], refs[14]
    parts, part_sems = refs[15:23], refs[23]
    core, x, y, z = coords[0], coords[1], coords[2], coords[3]
    arrivals = [
        pltpu.make_async_copy(source.at[i], held.at[i], in_sems.at[i]) for i in range(2 * GROUPS)
    ]
    others = [pltpu.make_async_copy(streams[i], parts[i], part_sems.at[i]) for i in range(8)]
    for arrival in arrivals + others:
        arrival.start()
    copies = []

    def move(one, other):
        copies.append(pltpu.make_async_copy(one, other, out_sems.at[len(copies)]))
        copies[-1].start()

    lead = DOWN_FIRST // TILE
    for device in range(2 * GROUPS):
        chip, owner = device // 2, device % 2
        src = held.at[device]
        arrivals[device].wait()
        count = BLOCK_TILES - owner
        first = PAIR_TILES * chip + BLOCK_TILES * owner
        for piece in range(UP_PIECES):
            cols = min(D, FF_PAD - piece * D)
            move(
                src.at[pl.ds(piece * BLOCK_TILES + owner, count), :, pl.ds(0, cols)],
                up.at[pl.ds(first, count), :, pl.ds(piece * D, cols)],
            )
        base = UP_PIECES * BLOCK_TILES
        move(src.at[pl.ds(base + owner, count)], out.at[pl.ds(first, count)])
        move(src.at[pl.ds(base + BLOCK_TILES, lead)], down.at[device, pl.ds(0, lead)])
    for part, stream in itertools.product(range(4), range(2)):
        others[4 * stream + part].wait()
        for near, dz in itertools.product(range(2), range(4)):
            src = parts[4 * stream + part].at[near * 4 + dz]
            owner = core if part < 2 else 1 - core
            far = part % 2
            dx, dy = (near, far) if stream == 0 else (far, near)
            chip = ((z ^ dz) * 2 + (y ^ dy)) * 2 + (x ^ dx)
            first = lead + (DOWN_CUT // TILE if stream else 0)
            move(src, down.at[chip * 2 + owner, pl.ds(first, src.shape[0])])
    for copy in copies:
        copy.wait()


def place_rest(gathered, streams, coords):
    source = gathered.reshape(2 * GROUPS, REST_ROWS // TILE, TILE, D)
    sources = [s.reshape(8, -1, TILE, D) for s in (*streams[0], *streams[1])]
    up, out, down = pl.pallas_call(
        place_rest_kernel,
        in_specs=[pl.BlockSpec(memory_space=pltpu.SMEM)]
        + [pl.BlockSpec(memory_space=pltpu.HBM)] * 9,
        out_specs=[pl.BlockSpec(memory_space=pltpu.HBM)] * 3,
        out_shape=[
            jax.ShapeDtypeStruct((D // TILE, TILE, FF_PAD), bf16),
            jax.ShapeDtypeStruct((D // TILE, TILE, D), bf16),
            jax.ShapeDtypeStruct((2 * GROUPS, HALF_DOWN // TILE, TILE, D), bf16),
        ],
        scratch_shapes=[
            pltpu.VMEM(source.shape, bf16),
            pltpu.SemaphoreType.DMA((2 * GROUPS,)),
            pltpu.SemaphoreType.DMA((2 * GROUPS * (UP_PIECES + 2) + 64,)),
        ]
        + [pltpu.VMEM(s.shape, bf16) for s in sources]
        + [pltpu.SemaphoreType.DMA((8,))],
        compiler_params=pltpu.CompilerParams(vmem_limit_bytes=60 << 20),
        cost_estimate=pl.CostEstimate(
            flops=0, bytes_accessed=4 * source.size, transcendentals=0
        ),
        name="place_rest",
    )(coords, source, *sources)
    return up.reshape(D, FF_PAD), out.reshape(D, D), down.reshape(FF_PAD, D)


def tie(*values):
    leaves, form = jax.tree.flatten(values)
    return form.unflatten(lax.optimization_barrier(leaves))


def gather_z(block):
    return [block] + [swap(block, 8 * step) for step in (1, 2, 3)]


def gather_near(parts, cut, axis):
    streams = []
    for stream in range(2):
        if axis == 1:
            own = jnp.stack([p[:, :cut] if stream == 0 else p[:, cut:] for p in parts])
        else:
            own = jnp.stack([p[:cut] if stream == 0 else p[cut:] for p in parts])
        streams.append((own, swap(own, 4 if stream else 2)))
    return streams


def gather_far(streams):
    results = []
    for stream in range(2):
        first = jnp.concatenate(streams[stream])
        results.append((first, swap(first, 2 if stream else 4)))
    return results


def gather_core(streams):
    return [(first, second, swap(first, 1), swap(second, 1)) for first, second in streams]


def window(value, starts, sizes):
    rank = value.ndim
    starts = list(starts) + [0] * (rank - len(starts))
    lengths = list(value.shape)
    for axis, size in enumerate(sizes):
        if size is not None:
            lengths[axis] = size
    starts = [jnp.int32(0) if start is None else jnp.int32(start) for start in starts]
    result = lax.dynamic_slice(value, starts, lengths)
    kept = [
        length for axis, length in enumerate(lengths) if axis >= len(sizes) or sizes[axis] != 1
    ]
    return result.reshape(kept)


class Reduction:
    def __init__(self, keeps, streams, coords):
        self.keeps = [k.reshape(4, 2, 2, BLOCK_TILES, TILE, -1) for k in keeps]
        self.streams = streams
        self.coords = coords

    def part(self, arrays, stream, plane):
        sizes = tuple(None if p is None else 1 for p in plane) + (None, None)
        pieces = []
        for number, first, last in self.streams[stream]:
            starts = tuple(plane) + (None, None, first)
            pieces.append(window(arrays[number], starts, sizes + (last - first,)))
        return pieces[0] if len(pieces) == 1 else jnp.concatenate(pieces, axis=-1)

    def terms(self, stream, plane):
        return [self.part(self.keeps, stream, plane), self.part(self.other, stream, plane)]

    def core_step(self, sends):
        return [swap(send.reshape(4, 2, 2, BLOCK_TILES, TILE, -1), 1) for send in sends]

    def far_sends(self, other, streams=(0, 1), pieces=slice(None)):
        core, x, y, z = self.coords
        self.other = other
        sends = []
        every = self.streams
        for stream in streams:
            plane = (None, None, 1 - x) if stream else (None, 1 - y, None)
            self.streams = {stream: every[stream][pieces]}
            sends.append(total_of(self.terms(stream, plane)).astype(bf16))
        self.streams = every
        return sends

    def far_swap(self, sends):
        return [swap(send, 2 if stream else 4) for stream, send in enumerate(sends)]

    def near_sends(self, far):
        core, x, y, z = self.coords
        self.far = far
        sends = []
        for stream in range(2):
            plane = (None, 1 - y, x) if stream else (None, y, 1 - x)
            after = (None, 1 - y) if stream else (None, 1 - x)
            terms = self.terms(stream, plane) + [window(far[stream], after, (None, 1))]
            sends.append(total_of(terms).astype(bf16))
        return sends

    def near_swap(self, sends):
        return [swap(send, 4 if stream else 2) for stream, send in enumerate(sends)]

    def at(self, plane):
        core, x, y, z = self.coords
        pieces = []
        for stream in range(2):
            after = (plane, y) if stream else (plane, x)
            terms = self.terms(stream, (plane, y, x)) + [
                window(self.far[stream], after, (1, 1)),
                window(self.near[stream], (plane,), (1,)),
            ]
            pieces.append(total_of(terms))
        return jnp.concatenate(pieces, axis=-1)

    def z_sends(self, near):
        z = self.coords[3]
        self.near = near
        return [self.at(z ^ step).astype(bf16) for step in (1, 2, 3)]

    def z_swap(self, sends):
        return [swap(send, 8 * step) for step, send in zip((1, 2, 3), sends)]

    def finish(self, arrived):
        core, x, y, z = self.coords
        total = total_of([self.at(z)] + arrived)
        total = total.reshape(BLOCK_TILES * TILE, -1)
        return lax.dynamic_slice_in_dim(
            total, core * (BLOCK_TILES * TILE - OWN_ROWS), OWN_ROWS, 0
        )


def join_rows(keep, send):
    whole = jnp.concatenate([keep, send[:, 2 * BLOCK_ROWS - PAIR_ROWS :]], axis=1)
    return whole.reshape(D, -1)


def total_of(terms):
    total = terms[0].astype(f32)
    for term in terms[1:]:
        total = total + term.astype(f32)
    return total


def fetch_pairs(narrow, core):
    q, k, v, o = (narrow[i].reshape(OWN_ROWS, D) for i in (2, 4, 5, 7))
    up = pad_hidden(narrow[11].reshape(OWN_ROWS, FF))
    down = narrow[13]
    rows = jnp.concatenate([q, k, v, o, up], axis=1)
    spare = BLOCK_TILES * TILE - OWN_ROWS
    lead = D * HALF_DOWN - down.shape[0]
    tail = jnp.pad(down[:lead].reshape(spare, -1), ((0, 0), (0, 512 - lead // spare)))
    is_first = core == 0
    edge = jnp.where(is_first, rows[OWN_ROWS - spare :], rows[:spare])
    got = swap(jnp.concatenate([edge, tail], axis=1), 1)
    edge = got[:, : rows.shape[1]]
    block = jnp.where(is_first, jnp.concatenate([rows, edge]), jnp.concatenate([edge, rows]))
    extra = got[:, rows.shape[1] : rows.shape[1] + lead // spare].reshape(-1)
    end = jnp.zeros((D * HALF_DOWN - (down.shape[0] - lead),), bf16)
    down_block = jnp.where(
        is_first, jnp.concatenate([down, extra]), jnp.concatenate([down[lead:], end])
    ).reshape(HALF_DOWN, D)
    small = jnp.concatenate([narrow[i] for i in VECTORS])
    small = jnp.pad(small, (0, BLOCK_TILES * TILE * EXTRA - small.shape[0]))
    small = small.reshape(BLOCK_TILES * TILE, EXTRA)
    square = jnp.concatenate([small, block[:, : 3 * D]], axis=1)
    up_block = jnp.pad(block[:, 4 * D :], ((0, 0), (0, UP_PIECES * D - FF_PAD)))
    pieces = [up_block[:, i * D : (i + 1) * D] for i in range(UP_PIECES)]
    rest = jnp.concatenate(pieces + [block[:, 3 * D : 4 * D], down_block[:DOWN_FIRST]])
    return square, rest, down_block[DOWN_FIRST:]


def normalize(values):
    centre = jnp.mean(values, axis=-1, keepdims=True)
    centered = values - centre
    spread_sq = jnp.mean(centered * centered, axis=-1, keepdims=True)
    inverse = lax.rsqrt(spread_sq + 1e-06)
    return centered * inverse, inverse


def normalize_back(grad, gain, xhat, inverse):
    scaled = grad * gain
    first = jnp.mean(scaled, axis=-1, keepdims=True)
    second = jnp.mean(scaled * xhat, axis=-1, keepdims=True)
    return inverse * (scaled - first - xhat * second)


def name_vectors(whole, widths):
    count = len(VECTORS) - 1
    width = widths[VECTORS[0]]
    pieces = whole[:, : count * width].reshape(-1, count, width)
    pieces = pieces.transpose(1, 0, 2).reshape(count, -1).astype(f32)
    found = {i: pieces[position : position + 1] for position, i in enumerate(VECTORS[:-1])}
    last = widths[VECTORS[-1]]
    found[VECTORS[-1]] = whole[:, count * width : count * width + last].reshape(-1).astype(f32)
    return found


def pack_vectors(grads, widths, devices):
    count = len(VECTORS) - 1
    width = widths[VECTORS[0]]
    rows = jnp.stack([grads[i] for i in VECTORS[:-1]])
    rows = jnp.pad(rows, ((0, 0), (0, width * devices - rows.shape[1])))
    rows = rows.reshape(count, devices, width).transpose(1, 0, 2).reshape(devices, -1)
    last = grads[VECTORS[-1]]
    last = jnp.pad(last, (0, widths[VECTORS[-1]] * devices - last.shape[0]))
    return jnp.concatenate([rows, last.reshape(devices, -1)], axis=1)


def gather_plain(narrow, widths):
    whole = {
        i: lax.all_gather(narrow[i], "fsdp", axis=0, tiled=True) for i in (2, 4, 5, 7, 11, 13)
    }
    square = [whole[i][: D * D].reshape(D, D) for i in (2, 4, 5, 7)]
    up = pad_hidden(whole[11][: D * FF].reshape(D, FF))
    down = pad_hidden(whole[13][: D * FF].reshape(FF, D).T).T
    joined = jnp.concatenate([narrow[i] for i in VECTORS])
    length = joined.shape[0]
    joined = jnp.pad(joined, (0, 2048 - length)).reshape(16, 128)
    joined = lax.all_gather(joined, "fsdp", axis=0, tiled=True).reshape(-1, 2048)
    return jnp.concatenate(square[:3], axis=1), square[3], up, down, name_vectors(joined, widths)


def on_device(*args):
    devices = lax.axis_size("fsdp")
    tokens, image_valid = args[0], args[1]
    shards = args[2:17]
    cotangent = args[17]
    staged = devices == 32
    widths = [piece.shape[0] for piece in shards]
    narrow = [piece.astype(bf16) for piece in shards]
    index = lax.axis_index("fsdp")
    core, x, y, z = index % 2, (index // 2) % 2, (index // 4) % 2, index // 8
    coords = (core, x, y, z)
    image_count = image_valid.shape[0]
    seq_len = tokens.shape[0] // image_count
    weight_img = jnp.repeat(image_valid.astype(f32), seq_len)[:, None]

    grad_out = weight_img * cotangent
    grad_branch = grad_out.astype(bf16)
    grads = {14: jnp.sum(grad_branch.astype(f32), axis=0)}
    xhat_one, inverse_one = normalize(tokens)
    where = jnp.stack(coords if staged else (jnp.int32(0),) * 4).astype(jnp.int32)
    if staged:
        sq, rest, down = fetch_pairs(narrow, core)
        rest = lax.all_gather(rest, "fsdp", axis=0, tiled=True)
        sq, tokens = tie(sq, tokens)
        sq = gather_z(sq)
        xhat_one, inverse_one = normalize(tokens)
        sq, down, xhat_one, inverse_one, grad_branch = tie(
            sq, down, xhat_one, inverse_one, grad_branch
        )
        sq = gather_near(sq, QKV_CUT, 1)
        down = gather_z(down)
        sq = gather_far(sq)
        sq, down = tie(sq, down)
        sq = gather_core(sq)
        down = gather_near(down, DOWN_CUT, 0)
        weight_qkv, small = place_square(sq, where)
        vectors = name_vectors(small, widths)
    else:
        weight_qkv, weight_o, weight_up, weight_down, vectors = gather_plain(narrow, widths)

    vec = lambda i: vectors[i][:, :D]
    gain_one, shift_one, gain_two, shift_two = vec(0), vec(1), vec(9), vec(10)
    bias_qkv = jnp.concatenate([vec(3), jnp.zeros((1, D), f32), vec(6)], axis=1)
    bias_o, bias_down = vec(8), vec(14)
    bias_up = pad_hidden(vectors[12][:FF].reshape(1, FF))

    normed = (xhat_one * gain_one + shift_one).astype(bf16)
    qkv = (product(normed, weight_qkv) + bias_qkv).astype(bf16)
    if staged:
        qkv, down = tie(qkv, down)
        down = gather_far(down)
    mixed, lse = attn_fwd(qkv, 2)
    if staged:
        mixed, lse, down = tie(mixed, lse, down)
        down = gather_core(down)
        weight_up, weight_o, weight_down = place_rest(rest, down, where)
    resid = tokens + product(mixed, weight_o) + bias_o
    xhat_two, inverse_two = normalize(resid)
    normed_two = (xhat_two * gain_two + shift_two).astype(bf16)
    (
        branch,
        up_keep,
        up_send,
        up_bias_grad,
        down_grad,
        sums_two,
        grad_resid,
        o_keep,
        o_send,
        grad_mixed,
    ) = mlp(
        where,
        normed_two,
        grad_branch,
        weight_up,
        bias_up,
        weight_down,
        xhat_two,
        inverse_two,
        gain_two.reshape(1, D),
        grad_out,
        mixed,
        weight_o,
    )
    up_bias_grad = up_bias_grad.reshape(FF_PAD)
    layer_out = weight_img * (resid + branch + bias_down)
    grads[9], grads[10], grads[8] = sums_two[0], sums_two[1], sums_two[2]
    if staged:
        down_sum = lax.psum_scatter(down_grad, "fsdp", scatter_dimension=0, tiled=True)
    if staged:
        outer = Reduction(
            (up_keep, o_keep), (((0, 0, UP_CUT),), ((0, UP_CUT, FF_PAD), (1, 0, D))), coords
        )
        outer_other = outer.core_step((up_send, o_send))
        grad_mixed, outer_other = tie(grad_mixed, outer_other)
        outer_far = outer.far_swap(outer.far_sends(outer_other))
    grads_first = attn_bwd(qkv, grad_mixed, lse, 2, 0, 12)
    if staged:
        grads_first, outer_far, grad_mixed = tie(grads_first, outer_far, grad_mixed)
        outer_near = outer.near_sends(outer_far)
        grad_mixed, outer_near = tie(grad_mixed, outer_near)
        outer_near = outer.near_swap(outer_near)
    grads_second = attn_bwd(qkv, grad_mixed, lse, 2, 12, 4)
    if staged:
        grads_second, outer_near = tie(grads_second, outer_near)
        outer_z = outer.z_sends(outer_near)
        grads_second, outer_z = tie(grads_second, outer_z)
        outer_z = outer.z_swap(outer_z)
    qkv_keep, qkv_send, qkv_bias_grad, norm_sums, tokens_grad = qkv_back(
        where,
        grads_first,
        grads_second,
        normed,
        weight_qkv,
        xhat_one,
        inverse_one,
        gain_one.reshape(1, D),
        grad_resid,
    )
    if staged:
        qkv_keep, qkv_send, norm_sums, qkv_bias_grad, outer_z = tie(
            qkv_keep, qkv_send, norm_sums, qkv_bias_grad, outer_z
        )
        qkv_other = outer.core_step((qkv_send,))[0]
    grads[3], grads[6] = qkv_bias_grad[0, :D], qkv_bias_grad[0, 2 * D :]
    grads[0], grads[1] = norm_sums[0], norm_sums[1]
    grads[12] = trim_hidden(up_bias_grad.reshape(1, FF_PAD)).reshape(FF)

    rows = pack_vectors(grads, widths, devices)
    owned = [None] * 15
    if staged:
        rows = jnp.pad(rows, ((0, 0), (0, OWN_ROWS * EXTRA - rows.shape[1])))
        rows = rows.reshape(GROUPS, PAIR_ROWS, EXTRA).astype(bf16)
        top, bottom = rows[:, :BLOCK_ROWS], rows[:, PAIR_ROWS - BLOCK_ROWS :]
        rows_keep = jnp.where(core == 0, top, bottom)
        rows_send = jnp.where(core == 0, bottom, top)
        rows_other = outer.core_step((rows_send,))[0]
        cut = QKV_CUT - EXTRA
        inner = Reduction(
            (qkv_keep, rows_keep), (((0, 0, cut), (1, 0, EXTRA)), ((0, cut, 3 * D),)), coords
        )
        qkv_other, rows_other = tie(qkv_other, rows_other)
        inner_far = inner.far_swap(inner.far_sends((qkv_other, rows_other)))
        inner_far, layer_out = tie(inner_far, layer_out)
        inner_near = inner.near_swap(inner.near_sends(inner_far))
        outer_sum = outer.finish(outer_z)
        owned[11] = trim_hidden(outer_sum[:, :FF_PAD]).reshape(-1)
        owned[7] = outer_sum[:, FF_PAD:].reshape(-1)
        inner_near, down_sum, owned[11], owned[7] = tie(
            inner_near, down_sum, owned[11], owned[7]
        )
        inner_z = inner.z_sends(inner_near)
        inner_z, down_sum = tie(inner_z, down_sum)
        inner_z = inner.z_swap(inner_z)

        flat = down_sum.astype(f32).reshape(-1)
        size = widths[13]
        lead = flat.shape[0] - size
        got = swap(down_sum.reshape(-1)[size:], 1).astype(f32)
        owned[13] = jnp.where(core == 0, flat[:size], jnp.concatenate([got, flat[: size - lead]]))
        inner_sum = inner.finish(inner_z)
        first = QKV_CUT - EXTRA
        owned[2] = inner_sum[:, :D].reshape(-1)
        owned[4] = jnp.concatenate(
            [inner_sum[:, D:first], inner_sum[:, QKV_CUT : 2 * D + EXTRA]], axis=1
        ).reshape(-1)
        owned[5] = inner_sum[:, 2 * D + EXTRA :].reshape(-1)
        small = inner_sum[:, first:QKV_CUT].reshape(-1)
    else:
        scatter = lambda value: lax.psum_scatter(
            value.astype(f32).reshape(-1), "fsdp", scatter_dimension=0, tiled=True
        )
        fill = lambda value, i: jnp.pad(
            value.reshape(-1), (0, widths[i] * devices - value.size)
        )
        qkv_grad = join_rows(qkv_keep, qkv_send)
        for position, i in enumerate((2, 4, 5)):
            owned[i] = scatter(fill(qkv_grad[:, position * D : (position + 1) * D], i))
        owned[7] = scatter(fill(join_rows(o_keep, o_send), 7))
        owned[11] = scatter(fill(trim_hidden(join_rows(up_keep, up_send)), 11))
        owned[13] = scatter(fill(trim_hidden(down_grad.T).T, 13))
        small = scatter(rows)
    position = 0
    for i in VECTORS:
        owned[i] = small[position : position + widths[i]]
        position += widths[i]
    return (layer_out, tokens_grad, *owned)


def solution(mesh):
    row, flat = P("fsdp", None), P("fsdp")
    in_specs = (row, flat) + (flat,) * 15 + (row,)
    out_specs = (row, row) + (flat,) * 15
    return jax.shard_map(
        on_device, mesh=mesh, in_specs=in_specs, out_specs=out_specs, check_vma=False
    )
```

```python
import functools
import itertools
import jax
import jax.numpy as jnp
from jax import lax
from jax.sharding import PartitionSpec as P
from jax.experimental import pallas as pl
from jax.experimental.pallas import tpu as pltpu
D=1152; HEADS=16; HEAD_DIM=72; LANES=128
NEG=-1e30
LOG2E=1.4426950408889634
def nt(a,b): return lax.dot_general(a,b,(((1,),(1,)),((),())),preferred_element_type=jnp.float32)
def nn(a,b): return lax.dot_general(a,b,(((1,),(0,)),((),())),preferred_element_type=jnp.float32)

def fill_heads(dst, src, col, tokens, fill):
    rows=dst.shape[1]
    for h in range(HEADS):
        if fill is not None:
            dst[h]=fill
        dst[h,0:tokens,0:HEAD_DIM]=src[:,col+h*HEAD_DIM:col+(h+1)*HEAD_DIM]

def pad_values(rows, tokens, kind):
    lane=lax.broadcasted_iota(jnp.int32,(rows,LANES),1)
    row=lax.broadcasted_iota(jnp.int32,(rows,LANES),0)
    if kind=="query":
        v=jnp.where(lane==HEAD_DIM,1.0,0.0)
    elif kind=="key":
        v=jnp.where((lane==HEAD_DIM)&(row>=tokens),NEG,0.0)
    else:
        v=jnp.zeros((rows,LANES),jnp.float32)
    return v.astype(jnp.bfloat16)

def fwd_kernel(tokens, krows, qrows, per, qkv_ref, mixed_ref, lse_ref, qs, ks, vs, os):
    step=pl.program_id(0)
    @pl.when(step==0)
    def _():
        fill_heads(qs,qkv_ref,0,tokens,pad_values(qrows,tokens,"query"))
        fill_heads(ks,qkv_ref,D,tokens,pad_values(krows,tokens,"key"))
        zero=pad_values(krows,tokens,"value")
        for h in range(HEADS):
            vs[h]=zero
            vs[h,0:tokens,0:HEAD_DIM]=qkv_ref[:,2*D+h*HEAD_DIM:2*D+(h+1)*HEAD_DIM]
    c=HEAD_DIM**-0.5*LOG2E
    for j in range(per):
        h=step*per+j
        s=nt(ks[h],qs[h])
        m=jnp.max(s,axis=0,keepdims=True)
        e=jnp.exp2((s-m)*c)
        l=jnp.sum(e,axis=0,keepdims=True)
        p=(e*(1.0/l)).astype(jnp.bfloat16)
        vt=vs[h].T
        ot=nn(vt,p)
        os[h]=ot.T.astype(jnp.bfloat16)
        lse_ref[j]=m*c+jnp.log2(l)
    @pl.when(step==pl.num_programs(0)-1)
    def _():
        for h in range(HEADS):
            mixed_ref[:,h*HEAD_DIM:(h+1)*HEAD_DIM]=os[h,0:tokens,0:HEAD_DIM]

def attn_fwd(qkv, per=1):
    tokens=qkv.shape[0]
    krows=-(-tokens//16)*16; qrows=-(-tokens//128)*128
    return pl.pallas_call(functools.partial(fwd_kernel,tokens,krows,qrows,per),
        grid=(HEADS//per,),
        in_specs=[pl.BlockSpec(qkv.shape,lambda i:(0,0),pipeline_mode=pl.Buffered(1))],
        out_specs=[pl.BlockSpec((tokens,D),lambda i:(0,0),pipeline_mode=pl.Buffered(1)),pl.BlockSpec((per,1,qrows),lambda i:(i,0,0))],
        out_shape=[jax.ShapeDtypeStruct((tokens,D),jnp.bfloat16),jax.ShapeDtypeStruct((HEADS,1,qrows),jnp.float32)],
        scratch_shapes=[pltpu.VMEM((HEADS,qrows,LANES),jnp.bfloat16),pltpu.VMEM((HEADS,krows,LANES),jnp.bfloat16),
                        pltpu.VMEM((HEADS,krows,LANES),jnp.bfloat16),pltpu.VMEM((HEADS,qrows,LANES),jnp.bfloat16)],
        compiler_params=pltpu.CompilerParams(vmem_limit_bytes=56<<20,dimension_semantics=("arbitrary",)),
        cost_estimate=pl.CostEstimate(flops=4*HEADS*qrows*krows*LANES,bytes_accessed=4*tokens*D*2,transcendentals=HEADS*qrows*krows),
        name="attention_forward")(qkv)

def bwd_kernel(tokens, krows, qrows, per, qkv_ref, go_ref, lse_ref, dqkv_ref, qs, ks, vs, gs):
    step=pl.program_id(0)
    @pl.when(step==0)
    def _():
        fill_heads(qs,qkv_ref,0,tokens,pad_values(qrows,tokens,"query"))
        fill_heads(ks,qkv_ref,D,tokens,pad_values(krows,tokens,"key"))
        fill_heads(vs,qkv_ref,2*D,tokens,pad_values(krows,tokens,"value"))
        fill_heads(gs,go_ref,0,tokens,pad_values(qrows,tokens,"value"))
    scale=HEAD_DIM**-0.5
    c=scale*LOG2E
    for j in range(per):
        h=step*per+j
        q=qs[h]; k=ks[h]; v=vs[h]; g=gs[h]
        s=nt(k,q)
        p=jnp.exp2(s*c-lse_ref[j])
        dp=nt(v,g)
        dv=nn(p.astype(jnp.bfloat16),g)
        delta=jnp.sum(p*dp,axis=0,keepdims=True)
        ds=(p*(dp-delta)).astype(jnp.bfloat16)
        dk=nn(ds,q)*scale
        dqt=nn(k.T,ds)*scale
        qs[h]=dqt.T.astype(jnp.bfloat16)
        ks[h]=dk.astype(jnp.bfloat16)
        vs[h]=dv.astype(jnp.bfloat16)
    @pl.when(step==pl.num_programs(0)-1)
    def _():
        for i,r in enumerate((qs,ks,vs)):
            for h in range(HEADS):
                dqkv_ref[:,i*D+h*HEAD_DIM:i*D+(h+1)*HEAD_DIM]=r[h,0:tokens,0:HEAD_DIM]

def attn_bwd(qkv, gmixed, lse, per=1):
    tokens=qkv.shape[0]
    krows=-(-tokens//16)*16; qrows=-(-tokens//128)*128
    return pl.pallas_call(functools.partial(bwd_kernel,tokens,krows,qrows,per),
        grid=(HEADS//per,),
        in_specs=[pl.BlockSpec(qkv.shape,lambda i:(0,0),pipeline_mode=pl.Buffered(1)),pl.BlockSpec(gmixed.shape,lambda i:(0,0),pipeline_mode=pl.Buffered(1)),
                  pl.BlockSpec((per,1,qrows),lambda i:(i,0,0))],
        out_specs=pl.BlockSpec((tokens,3*D),lambda i:(0,0),pipeline_mode=pl.Buffered(1)),
        out_shape=jax.ShapeDtypeStruct((tokens,3*D),jnp.bfloat16),
        scratch_shapes=[pltpu.VMEM((HEADS,qrows,LANES),jnp.bfloat16),pltpu.VMEM((HEADS,krows,LANES),jnp.bfloat16),
                        pltpu.VMEM((HEADS,krows,LANES),jnp.bfloat16),pltpu.VMEM((HEADS,qrows,LANES),jnp.bfloat16)],
        compiler_params=pltpu.CompilerParams(vmem_limit_bytes=56<<20,dimension_semantics=("arbitrary",)),
        cost_estimate=pl.CostEstimate(flops=1000000,bytes_accessed=1000000,transcendentals=0),
        name="attention_backward")(qkv,gmixed,lse)


GELU_A = 0.7978845608028654
GELU_B = 0.044715


PAIR_ROWS = D // HEADS
BLOCK_ROWS = 40


def share_rows(core, value, keep_ref, send_ref):
    for chip in range(value.shape[0] // PAIR_ROWS):
        first = value[chip * PAIR_ROWS : chip * PAIR_ROWS + BLOCK_ROWS]
        last = value[(chip + 1) * PAIR_ROWS - BLOCK_ROWS : (chip + 1) * PAIR_ROWS]
        keep_ref[chip] = jnp.where(core == 0, first, last).astype(jnp.bfloat16)
        send_ref[chip] = jnp.where(core == 0, last, first).astype(jnp.bfloat16)


def mlp_kernel(coords, normed_ref, grad_ref, up_ref, bias_ref, down_ref, xhat_ref, inverse_ref, gain_ref,
               grad_out_ref, mixed_ref, output_ref, out_ref, up_keep_ref, up_send_ref, bias_grad_ref,
               down_grad_ref, sums_ref, resid_grad_ref, output_keep_ref, output_send_ref, mixed_grad_ref,
               normed, normed_t, grad, out, back):
    step = pl.program_id(0)
    tokens = normed_ref.shape[0]

    @pl.when(step == 0)
    def _():
        for held, source in ((normed, normed_ref), (grad, grad_ref)):
            held[...] = jnp.zeros_like(held)
            held[0:tokens] = source[...]
        normed_t[...] = normed[...].T
        out[...] = jnp.zeros_like(out)
        back[...] = jnp.zeros_like(back)

    pre = nn(normed[...], up_ref[...]) + bias_ref[...]
    square = pre * pre
    bend = jnp.tanh(pre * (GELU_A + GELU_A * GELU_B * square))
    hidden = (0.5 * pre * (1.0 + bend)).astype(jnp.bfloat16)
    slope = 0.5 * (1.0 + bend) + 0.5 * pre * (1.0 - bend * bend) * (
        GELU_A + 3.0 * GELU_A * GELU_B * square
    )
    grad_pre = (nt(grad[...], down_ref[...]) * slope).astype(jnp.bfloat16)
    out[...] += nn(hidden, down_ref[...])
    back[...] += nt(grad_pre, up_ref[...])
    down_grad_ref[...] = nn(hidden.T, grad[...]).astype(jnp.bfloat16)
    share_rows(coords[0], nn(normed_t[...], grad_pre), up_keep_ref, up_send_ref)
    bias_grad_ref[...] = jnp.sum(grad_pre.astype(jnp.float32), axis=0, keepdims=True)

    @pl.when(step == pl.num_programs(0) - 1)
    def _():
        out_ref[...] = out[0:tokens]
        total = back[0:tokens]
        xhat = xhat_ref[...]
        sums_ref[0:1] = jnp.sum(total * xhat, axis=0, keepdims=True)
        sums_ref[1:2] = jnp.sum(total, axis=0, keepdims=True)
        scaled = total * gain_ref[...]
        first = jnp.mean(scaled, axis=-1, keepdims=True)
        second = jnp.mean(scaled * xhat, axis=-1, keepdims=True)
        resid_grad = grad_out_ref[...] + inverse_ref[...] * (scaled - first - xhat * second)
        resid_grad_ref[...] = resid_grad
        grad[0:tokens] = resid_grad.astype(jnp.bfloat16)
        low = grad[...]
        sums_ref[2:3] = jnp.sum(low.astype(jnp.float32), axis=0, keepdims=True)
        mixed_grad_ref[...] = nt(low, output_ref[...]).astype(jnp.bfloat16)[0:tokens]
        normed[0:tokens] = mixed_ref[...]
        normed_t[...] = normed[...].T
        share_rows(coords[0], nn(normed_t[...], low), output_keep_ref, output_send_ref)


def whole_block(shape):
    return pl.BlockSpec(shape, lambda i: (0, 0), pipeline_mode=pl.Buffered(1))


def mlp(coords, normed, grad, up, bias, down, xhat, inverse, gain, grad_out, mixed, output):
    tokens, hidden = normed.shape[0], up.shape[1]
    rows = -(-tokens // 16) * 16
    tile = 256
    full = whole_block((tokens, D))
    columns = pl.BlockSpec((D, tile), lambda i: (0, i))
    line = pl.BlockSpec((1, tile), lambda i: (0, i))
    band = pl.BlockSpec((tile, D), lambda i: (i, 0))
    square = whole_block((D, D))
    shares = (D // PAIR_ROWS, BLOCK_ROWS)
    part = pl.BlockSpec(shares + (tile,), lambda i: (0, 0, i))
    full_part = pl.BlockSpec(
        shares + (D,), lambda i: (0, 0, 0), pipeline_mode=pl.Buffered(1)
    )
    return pl.pallas_call(
        mlp_kernel,
        grid=(hidden // tile,),
        in_specs=[pl.BlockSpec(memory_space=pltpu.SMEM), full, full, columns, line, band, full, whole_block((tokens, 1)),
                  whole_block((1, D)), full, full, square],
        out_specs=[full, part, part, line, band, whole_block((8, D)), full, full_part, full_part,
                   full],
        out_shape=[
            jax.ShapeDtypeStruct((tokens, D), jnp.float32),
            jax.ShapeDtypeStruct(shares + (hidden,), jnp.bfloat16),
            jax.ShapeDtypeStruct(shares + (hidden,), jnp.bfloat16),
            jax.ShapeDtypeStruct((1, hidden), jnp.float32),
            jax.ShapeDtypeStruct((hidden, D), jnp.bfloat16),
            jax.ShapeDtypeStruct((8, D), jnp.float32),
            jax.ShapeDtypeStruct((tokens, D), jnp.float32),
            jax.ShapeDtypeStruct(shares + (D,), jnp.bfloat16),
            jax.ShapeDtypeStruct(shares + (D,), jnp.bfloat16),
            jax.ShapeDtypeStruct((tokens, D), jnp.bfloat16),
        ],
        scratch_shapes=[
            pltpu.VMEM((rows, D), jnp.bfloat16),
            pltpu.VMEM((D, rows), jnp.bfloat16),
            pltpu.VMEM((rows, D), jnp.bfloat16),
            pltpu.VMEM((rows, D), jnp.float32),
            pltpu.VMEM((rows, D), jnp.float32),
        ],
        compiler_params=pltpu.CompilerParams(
            vmem_limit_bytes=56 << 20, dimension_semantics=("arbitrary",)
        ),
        cost_estimate=pl.CostEstimate(flops=1000000, bytes_accessed=1000000, transcendentals=0),
        name="mlp_forward_backward",
    )(coords, normed, grad, up, bias, down, xhat, inverse, gain, grad_out, mixed, output)


def qkv_back_kernel(coords, grad_ref, normed_ref, weight_ref, xhat_ref, inverse_ref, gain_ref, resid_ref,
                    keep_ref, send_ref, bias_grad_ref, sums_ref, tokens_ref, grad, normed_t, total):
    step = pl.program_id(0)
    tokens = normed_ref.shape[0]

    @pl.when(step == 0)
    def _():
        grad[...] = jnp.zeros_like(grad)
        grad[0:tokens] = normed_ref[...]
        normed_t[...] = grad[...].T
        grad[...] = jnp.zeros_like(grad)
        total[...] = jnp.zeros_like(total)

    grad[0:tokens] = grad_ref[...]
    share_rows(coords[0], nn(normed_t[...], grad[...]), keep_ref, send_ref)
    bias_grad_ref[...] = jnp.sum(grad[...].astype(jnp.float32), axis=0, keepdims=True)
    total[...] += nt(grad[...], weight_ref[...])

    @pl.when(step == pl.num_programs(0) - 1)
    def _():
        back = total[0:tokens]
        xhat = xhat_ref[...]
        sums_ref[0:1] = jnp.sum(back * xhat, axis=0, keepdims=True)
        sums_ref[1:2] = jnp.sum(back, axis=0, keepdims=True)
        scaled = back * gain_ref[...]
        first = jnp.mean(scaled, axis=-1, keepdims=True)
        second = jnp.mean(scaled * xhat, axis=-1, keepdims=True)
        tokens_ref[...] = resid_ref[...] + inverse_ref[...] * (scaled - first - xhat * second)


def qkv_back(coords, grad, normed, weight, xhat, inverse, gain, resid):
    tokens = normed.shape[0]
    rows = -(-tokens // 16) * 16
    whole = lambda shape: pl.BlockSpec(shape, lambda i: (0, 0), pipeline_mode=pl.Buffered(1))
    part = lambda shape: pl.BlockSpec(shape, lambda i: (0, i))
    shares = (D // PAIR_ROWS, BLOCK_ROWS)
    share = pl.BlockSpec(shares + (D,), lambda i: (0, 0, i))
    return pl.pallas_call(
        qkv_back_kernel,
        grid=(3,),
        in_specs=[
            pl.BlockSpec(memory_space=pltpu.SMEM),
            part((tokens, D)),
            whole((tokens, D)),
            part((D, D)),
            whole((tokens, D)),
            whole((tokens, 1)),
            whole((1, D)),
            whole((tokens, D)),
        ],
        out_specs=[share, share, part((1, D)), whole((8, D)), whole((tokens, D))],
        out_shape=[
            jax.ShapeDtypeStruct(shares + (3 * D,), jnp.bfloat16),
            jax.ShapeDtypeStruct(shares + (3 * D,), jnp.bfloat16),
            jax.ShapeDtypeStruct((1, 3 * D), jnp.float32),
            jax.ShapeDtypeStruct((8, D), jnp.float32),
            jax.ShapeDtypeStruct((tokens, D), jnp.float32),
        ],
        scratch_shapes=[
            pltpu.VMEM((rows, D), jnp.bfloat16),
            pltpu.VMEM((D, rows), jnp.bfloat16),
            pltpu.VMEM((rows, D), jnp.float32),
        ],
        compiler_params=pltpu.CompilerParams(
            vmem_limit_bytes=56 << 20, dimension_semantics=("arbitrary",)
        ),
        cost_estimate=pl.CostEstimate(flops=1000000, bytes_accessed=1000000, transcendentals=0),
        name="qkv_backward",
    )(coords, grad, normed, weight, xhat, inverse, gain, resid)


FF = 4304
GROUPS = 16
FF_GROUP = FF // GROUPS
FF_ROWS = 272
FF_PAD = GROUPS * FF_ROWS
HALF_DOWN = FF_ROWS // 2
OWN_ROWS = PAIR_ROWS // 2
TILE = 8
BLOCK_TILES = 5
PAIR_TILES = PAIR_ROWS // TILE
EXTRA = 128
QKV_CUT = 14 * 128
UP_CUT = 22 * 128
UP_PIECES = 4
DOWN_CUT = 40
DOWN_FIRST = 64
REST_ROWS = UP_PIECES * BLOCK_TILES * TILE + BLOCK_TILES * TILE + DOWN_FIRST
VECTORS = (0, 1, 3, 6, 8, 9, 10, 14, 12)
bf16 = jnp.bfloat16
f32 = jnp.float32


def product(left, right):
    return jnp.dot(left, right, preferred_element_type=f32)


def product_t(left, right):
    return lax.dot_general(left, right, (((0,), (0,)), ((), ())), preferred_element_type=f32)


def product_bt(left, right):
    return lax.dot_general(left, right, (((1,), (1,)), ((), ())), preferred_element_type=f32)


def swap(value, mask):
    devices = lax.axis_size("fsdp")
    return lax.ppermute(value, "fsdp", [(i, i ^ mask) for i in range(devices)])


def pad_hidden(columns):
    rows = columns.shape[0]
    grouped = columns.reshape(rows, GROUPS, FF_GROUP)
    return jnp.pad(grouped, ((0, 0), (0, 0), (0, FF_ROWS - FF_GROUP))).reshape(rows, FF_PAD)


def trim_hidden(columns):
    rows = columns.shape[0]
    return columns.reshape(rows, GROUPS, FF_ROWS)[:, :, :FF_GROUP].reshape(rows, FF)


def place_square_kernel(coords, *refs):
    sources, (whole, small) = refs[:8], refs[8:10]
    held, in_sems, out_sems = refs[10:18], refs[18], refs[19]
    core, x, y, z = coords[0], coords[1], coords[2], coords[3]
    arrivals = [pltpu.make_async_copy(sources[i], held[i], in_sems.at[i]) for i in range(8)]
    for arrival in arrivals:
        arrival.start()
    copies, extras = [], []
    for part, stream in itertools.product(range(4), range(2)):
        arrivals[4 * stream + part].wait()
        for near, dz in itertools.product(range(2), range(4)):
            src = held[4 * stream + part].at[near * 4 + dz]
            owner = core if part < 2 else 1 - core
            far = part % 2
            dx, dy = (near, far) if stream == 0 else (far, near)
            chip = ((z ^ dz) * 2 + (y ^ dy)) * 2 + (x ^ dx)
            cols = src.shape[-1] - (0 if stream else EXTRA)
            col = QKV_CUT - EXTRA if stream else 0
            src_cols = pl.ds(0 if stream else EXTRA, cols)
            first = PAIR_TILES * chip + BLOCK_TILES * owner
            copies.append(
                pltpu.make_async_copy(
                    src.at[pl.ds(owner, BLOCK_TILES - 1), :, src_cols],
                    whole.at[pl.ds(first, BLOCK_TILES - 1), :, pl.ds(col, cols)],
                    out_sems.at[len(copies)],
                )
            )
            copies[-1].start()
            extra = pltpu.make_async_copy(
                src.at[BLOCK_TILES - 1, :, src_cols],
                whole.at[PAIR_TILES * chip + BLOCK_TILES - 1, :, pl.ds(col, cols)],
                out_sems.at[96 + len(extras)],
            )
            pl.when(owner == 0)(extra.start)
            extras.append((owner, extra))
            if stream == 0:
                copies.append(
                    pltpu.make_async_copy(
                        src.at[:, :, :EXTRA], small.at[chip * 2 + owner], out_sems.at[len(copies)]
                    )
                )
                copies[-1].start()
    for copy in copies:
        copy.wait()
    for owner, extra in extras:
        pl.when(owner == 0)(extra.wait)


def place_square(streams, coords):
    sources = [s.reshape(8, BLOCK_TILES, TILE, -1) for s in (*streams[0], *streams[1])]
    size = sum(s.size for s in sources) * 2
    whole, small = pl.pallas_call(
        place_square_kernel,
        in_specs=[pl.BlockSpec(memory_space=pltpu.SMEM)]
        + [pl.BlockSpec(memory_space=pltpu.HBM)] * 8,
        out_specs=[pl.BlockSpec(memory_space=pltpu.HBM)] * 2,
        out_shape=[
            jax.ShapeDtypeStruct((GROUPS * PAIR_TILES, TILE, 3 * D), bf16),
            jax.ShapeDtypeStruct((2 * GROUPS, BLOCK_TILES, TILE, EXTRA), bf16),
        ],
        scratch_shapes=[pltpu.VMEM(s.shape, bf16) for s in sources]
        + [pltpu.SemaphoreType.DMA((8,)), pltpu.SemaphoreType.DMA((160,))],
        compiler_params=pltpu.CompilerParams(vmem_limit_bytes=40 << 20),
        cost_estimate=pl.CostEstimate(flops=0, bytes_accessed=2 * size, transcendentals=0),
        name="place_square",
    )(coords, *sources)
    return whole.reshape(D, 3 * D), small.reshape(2 * GROUPS, -1)


def place_rest_kernel(coords, *refs):
    source, streams, (up, out, down) = refs[0], refs[1:9], refs[9:12]
    held, in_sems, out_sems = refs[12], refs[13], refs[14]
    parts, part_sems = refs[15:23], refs[23]
    core, x, y, z = coords[0], coords[1], coords[2], coords[3]
    arrivals = [
        pltpu.make_async_copy(source.at[i], held.at[i], in_sems.at[i]) for i in range(2 * GROUPS)
    ]
    others = [pltpu.make_async_copy(streams[i], parts[i], part_sems.at[i]) for i in range(8)]
    for arrival in arrivals + others:
        arrival.start()
    copies = []

    def move(one, other):
        copies.append(pltpu.make_async_copy(one, other, out_sems.at[len(copies)]))
        copies[-1].start()

    lead = DOWN_FIRST // TILE
    for device in range(2 * GROUPS):
        chip, owner = device // 2, device % 2
        src = held.at[device]
        arrivals[device].wait()
        count = BLOCK_TILES - owner
        first = PAIR_TILES * chip + BLOCK_TILES * owner
        for piece in range(UP_PIECES):
            cols = min(D, FF_PAD - piece * D)
            move(
                src.at[pl.ds(piece * BLOCK_TILES + owner, count), :, pl.ds(0, cols)],
                up.at[pl.ds(first, count), :, pl.ds(piece * D, cols)],
            )
        base = UP_PIECES * BLOCK_TILES
        move(src.at[pl.ds(base + owner, count)], out.at[pl.ds(first, count)])
        move(src.at[pl.ds(base + BLOCK_TILES, lead)], down.at[device, pl.ds(0, lead)])
    for part, stream in itertools.product(range(4), range(2)):
        others[4 * stream + part].wait()
        for near, dz in itertools.product(range(2), range(4)):
            src = parts[4 * stream + part].at[near * 4 + dz]
            owner = core if part < 2 else 1 - core
            far = part % 2
            dx, dy = (near, far) if stream == 0 else (far, near)
            chip = ((z ^ dz) * 2 + (y ^ dy)) * 2 + (x ^ dx)
            first = lead + (DOWN_CUT // TILE if stream else 0)
            move(src, down.at[chip * 2 + owner, pl.ds(first, src.shape[0])])
    for copy in copies:
        copy.wait()


def place_rest(gathered, streams, coords):
    source = gathered.reshape(2 * GROUPS, REST_ROWS // TILE, TILE, D)
    sources = [s.reshape(8, -1, TILE, D) for s in (*streams[0], *streams[1])]
    up, out, down = pl.pallas_call(
        place_rest_kernel,
        in_specs=[pl.BlockSpec(memory_space=pltpu.SMEM)]
        + [pl.BlockSpec(memory_space=pltpu.HBM)] * 9,
        out_specs=[pl.BlockSpec(memory_space=pltpu.HBM)] * 3,
        out_shape=[
            jax.ShapeDtypeStruct((D // TILE, TILE, FF_PAD), bf16),
            jax.ShapeDtypeStruct((D // TILE, TILE, D), bf16),
            jax.ShapeDtypeStruct((2 * GROUPS, HALF_DOWN // TILE, TILE, D), bf16),
        ],
        scratch_shapes=[
            pltpu.VMEM(source.shape, bf16),
            pltpu.SemaphoreType.DMA((2 * GROUPS,)),
            pltpu.SemaphoreType.DMA((2 * GROUPS * (UP_PIECES + 2) + 64,)),
        ]
        + [pltpu.VMEM(s.shape, bf16) for s in sources]
        + [pltpu.SemaphoreType.DMA((8,))],
        compiler_params=pltpu.CompilerParams(vmem_limit_bytes=60 << 20),
        cost_estimate=pl.CostEstimate(
            flops=0, bytes_accessed=4 * source.size, transcendentals=0
        ),
        name="place_rest",
    )(coords, source, *sources)
    return up.reshape(D, FF_PAD), out.reshape(D, D), down.reshape(FF_PAD, D)


def tie(*values):
    leaves, form = jax.tree.flatten(values)
    return form.unflatten(lax.optimization_barrier(leaves))


def gather_z(block):
    return [block] + [swap(block, 8 * step) for step in (1, 2, 3)]


def gather_near(parts, cut, axis):
    streams = []
    for stream in range(2):
        if axis == 1:
            own = jnp.stack([p[:, :cut] if stream == 0 else p[:, cut:] for p in parts])
        else:
            own = jnp.stack([p[:cut] if stream == 0 else p[cut:] for p in parts])
        streams.append((own, swap(own, 4 if stream else 2)))
    return streams


def gather_far(streams):
    results = []
    for stream in range(2):
        first = jnp.concatenate(streams[stream])
        results.append((first, swap(first, 2 if stream else 4)))
    return results


def gather_core(streams):
    return [(first, second, swap(first, 1), swap(second, 1)) for first, second in streams]


def window(value, starts, sizes):
    rank = value.ndim
    starts = list(starts) + [0] * (rank - len(starts))
    lengths = list(value.shape)
    for axis, size in enumerate(sizes):
        if size is not None:
            lengths[axis] = size
    starts = [jnp.int32(0) if start is None else jnp.int32(start) for start in starts]
    result = lax.dynamic_slice(value, starts, lengths)
    kept = [
        length for axis, length in enumerate(lengths) if axis >= len(sizes) or sizes[axis] != 1
    ]
    return result.reshape(kept)


class Reduction:
    def __init__(self, keeps, streams, coords):
        self.keeps = [k.reshape(4, 2, 2, BLOCK_TILES, TILE, -1) for k in keeps]
        self.streams = streams
        self.coords = coords

    def part(self, arrays, stream, plane):
        sizes = tuple(None if p is None else 1 for p in plane) + (None, None)
        pieces = []
        for number, first, last in self.streams[stream]:
            starts = tuple(plane) + (None, None, first)
            pieces.append(window(arrays[number], starts, sizes + (last - first,)))
        return pieces[0] if len(pieces) == 1 else jnp.concatenate(pieces, axis=-1)

    def terms(self, stream, plane):
        return [self.part(self.keeps, stream, plane), self.part(self.other, stream, plane)]

    def core_step(self, sends):
        return [swap(send.reshape(4, 2, 2, BLOCK_TILES, TILE, -1), 1) for send in sends]

    def far_sends(self, other, streams=(0, 1), pieces=slice(None)):
        core, x, y, z = self.coords
        self.other = other
        sends = []
        every = self.streams
        for stream in streams:
            plane = (None, None, 1 - x) if stream else (None, 1 - y, None)
            self.streams = {stream: every[stream][pieces]}
            sends.append(total_of(self.terms(stream, plane)).astype(bf16))
        self.streams = every
        return sends

    def far_swap(self, sends):
        return [swap(send, 2 if stream else 4) for stream, send in enumerate(sends)]

    def near_sends(self, far):
        core, x, y, z = self.coords
        self.far = far
        sends = []
        for stream in range(2):
            plane = (None, 1 - y, x) if stream else (None, y, 1 - x)
            after = (None, 1 - y) if stream else (None, 1 - x)
            terms = self.terms(stream, plane) + [window(far[stream], after, (None, 1))]
            sends.append(total_of(terms).astype(bf16))
        return sends

    def near_swap(self, sends):
        return [swap(send, 4 if stream else 2) for stream, send in enumerate(sends)]

    def at(self, plane):
        core, x, y, z = self.coords
        pieces = []
        for stream in range(2):
            after = (plane, y) if stream else (plane, x)
            terms = self.terms(stream, (plane, y, x)) + [
                window(self.far[stream], after, (1, 1)),
                window(self.near[stream], (plane,), (1,)),
            ]
            pieces.append(total_of(terms))
        return jnp.concatenate(pieces, axis=-1)

    def z_sends(self, near):
        z = self.coords[3]
        self.near = near
        return [self.at(z ^ step).astype(bf16) for step in (1, 2, 3)]

    def z_swap(self, sends):
        return [swap(send, 8 * step) for step, send in zip((1, 2, 3), sends)]

    def finish(self, arrived):
        core, x, y, z = self.coords
        total = total_of([self.at(z)] + arrived)
        total = total.reshape(BLOCK_TILES * TILE, -1)
        return lax.dynamic_slice_in_dim(
            total, core * (BLOCK_TILES * TILE - OWN_ROWS), OWN_ROWS, 0
        )


def join_rows(keep, send):
    whole = jnp.concatenate([keep, send[:, 2 * BLOCK_ROWS - PAIR_ROWS :]], axis=1)
    return whole.reshape(D, -1)


def total_of(terms):
    total = terms[0].astype(f32)
    for term in terms[1:]:
        total = total + term.astype(f32)
    return total


def fetch_pairs(narrow, core):
    q, k, v, o = (narrow[i].reshape(OWN_ROWS, D) for i in (2, 4, 5, 7))
    up = pad_hidden(narrow[11].reshape(OWN_ROWS, FF))
    down = narrow[13]
    rows = jnp.concatenate([q, k, v, o, up], axis=1)
    spare = BLOCK_TILES * TILE - OWN_ROWS
    lead = D * HALF_DOWN - down.shape[0]
    tail = jnp.pad(down[:lead].reshape(spare, -1), ((0, 0), (0, 512 - lead // spare)))
    is_first = core == 0
    edge = jnp.where(is_first, rows[OWN_ROWS - spare :], rows[:spare])
    got = swap(jnp.concatenate([edge, tail], axis=1), 1)
    edge = got[:, : rows.shape[1]]
    block = jnp.where(is_first, jnp.concatenate([rows, edge]), jnp.concatenate([edge, rows]))
    extra = got[:, rows.shape[1] : rows.shape[1] + lead // spare].reshape(-1)
    end = jnp.zeros((D * HALF_DOWN - (down.shape[0] - lead),), bf16)
    down_block = jnp.where(
        is_first, jnp.concatenate([down, extra]), jnp.concatenate([down[lead:], end])
    ).reshape(HALF_DOWN, D)
    small = jnp.concatenate([narrow[i] for i in VECTORS])
    small = jnp.pad(small, (0, BLOCK_TILES * TILE * EXTRA - small.shape[0]))
    small = small.reshape(BLOCK_TILES * TILE, EXTRA)
    square = jnp.concatenate([small, block[:, : 3 * D]], axis=1)
    up_block = jnp.pad(block[:, 4 * D :], ((0, 0), (0, UP_PIECES * D - FF_PAD)))
    pieces = [up_block[:, i * D : (i + 1) * D] for i in range(UP_PIECES)]
    rest = jnp.concatenate(pieces + [block[:, 3 * D : 4 * D], down_block[:DOWN_FIRST]])
    return square, rest, down_block[DOWN_FIRST:]


def normalize(values):
    centre = jnp.mean(values, axis=-1, keepdims=True)
    centered = values - centre
    spread_sq = jnp.mean(centered * centered, axis=-1, keepdims=True)
    inverse = lax.rsqrt(spread_sq + 1e-06)
    return centered * inverse, inverse


def normalize_back(grad, gain, xhat, inverse):
    scaled = grad * gain
    first = jnp.mean(scaled, axis=-1, keepdims=True)
    second = jnp.mean(scaled * xhat, axis=-1, keepdims=True)
    return inverse * (scaled - first - xhat * second)


def name_vectors(whole, widths):
    count = len(VECTORS) - 1
    width = widths[VECTORS[0]]
    pieces = whole[:, : count * width].reshape(-1, count, width)
    pieces = pieces.transpose(1, 0, 2).reshape(count, -1).astype(f32)
    found = {i: pieces[position : position + 1] for position, i in enumerate(VECTORS[:-1])}
    last = widths[VECTORS[-1]]
    found[VECTORS[-1]] = whole[:, count * width : count * width + last].reshape(-1).astype(f32)
    return found


def pack_vectors(grads, widths, devices):
    count = len(VECTORS) - 1
    width = widths[VECTORS[0]]
    rows = jnp.stack([grads[i] for i in VECTORS[:-1]])
    rows = jnp.pad(rows, ((0, 0), (0, width * devices - rows.shape[1])))
    rows = rows.reshape(count, devices, width).transpose(1, 0, 2).reshape(devices, -1)
    last = grads[VECTORS[-1]]
    last = jnp.pad(last, (0, widths[VECTORS[-1]] * devices - last.shape[0]))
    return jnp.concatenate([rows, last.reshape(devices, -1)], axis=1)


def gather_plain(narrow, widths):
    whole = {
        i: lax.all_gather(narrow[i], "fsdp", axis=0, tiled=True) for i in (2, 4, 5, 7, 11, 13)
    }
    square = [whole[i][: D * D].reshape(D, D) for i in (2, 4, 5, 7)]
    up = pad_hidden(whole[11][: D * FF].reshape(D, FF))
    down = pad_hidden(whole[13][: D * FF].reshape(FF, D).T).T
    joined = jnp.concatenate([narrow[i] for i in VECTORS])
    length = joined.shape[0]
    joined = jnp.pad(joined, (0, 2048 - length)).reshape(16, 128)
    joined = lax.all_gather(joined, "fsdp", axis=0, tiled=True).reshape(-1, 2048)
    return jnp.concatenate(square[:3], axis=1), square[3], up, down, name_vectors(joined, widths)


def on_device(*args):
    devices = lax.axis_size("fsdp")
    tokens, image_valid = args[0], args[1]
    shards = args[2:17]
    cotangent = args[17]
    staged = devices == 32
    widths = [piece.shape[0] for piece in shards]
    narrow = [piece.astype(bf16) for piece in shards]
    index = lax.axis_index("fsdp")
    core, x, y, z = index % 2, (index // 2) % 2, (index // 4) % 2, index // 8
    coords = (core, x, y, z)
    image_count = image_valid.shape[0]
    seq_len = tokens.shape[0] // image_count
    weight_img = jnp.repeat(image_valid.astype(f32), seq_len)[:, None]

    grad_out = weight_img * cotangent
    grad_branch = grad_out.astype(bf16)
    grads = {14: jnp.sum(grad_branch.astype(f32), axis=0)}
    xhat_one, inverse_one = normalize(tokens)
    where = jnp.stack(coords if staged else (jnp.int32(0),) * 4).astype(jnp.int32)
    if staged:
        sq, rest, down = fetch_pairs(narrow, core)
        rest = lax.all_gather(rest, "fsdp", axis=0, tiled=True)
        sq, tokens = tie(sq, tokens)
        sq = gather_z(sq)
        xhat_one, inverse_one = normalize(tokens)
        sq, down, xhat_one, inverse_one, grad_branch = tie(
            sq, down, xhat_one, inverse_one, grad_branch
        )
        sq = gather_near(sq, QKV_CUT, 1)
        down = gather_z(down)
        sq = gather_far(sq)
        sq, down = tie(sq, down)
        sq = gather_core(sq)
        down = gather_near(down, DOWN_CUT, 0)
        weight_qkv, small = place_square(sq, where)
        vectors = name_vectors(small, widths)
    else:
        weight_qkv, weight_o, weight_up, weight_down, vectors = gather_plain(narrow, widths)

    vec = lambda i: vectors[i][:, :D]
    gain_one, shift_one, gain_two, shift_two = vec(0), vec(1), vec(9), vec(10)
    bias_qkv = jnp.concatenate([vec(3), jnp.zeros((1, D), f32), vec(6)], axis=1)
    bias_o, bias_down = vec(8), vec(14)
    bias_up = pad_hidden(vectors[12][:FF].reshape(1, FF))

    normed = (xhat_one * gain_one + shift_one).astype(bf16)
    qkv = (product(normed, weight_qkv) + bias_qkv).astype(bf16)
    if staged:
        qkv, down = tie(qkv, down)
        down = [(*pair, swap(pair[0], 1)) for pair in gather_far(down)]
    mixed, lse = attn_fwd(qkv, 2)
    if staged:
        mixed, lse, down = tie(mixed, lse, down)
        down = [(*parts, swap(parts[1], 1)) for parts in down]
        weight_up, weight_o, weight_down = place_rest(rest, down, where)
    resid = tokens + product(mixed, weight_o) + bias_o
    xhat_two, inverse_two = normalize(resid)
    normed_two = (xhat_two * gain_two + shift_two).astype(bf16)
    (
        branch,
        up_keep,
        up_send,
        up_bias_grad,
        down_grad,
        sums_two,
        grad_resid,
        o_keep,
        o_send,
        grad_mixed,
    ) = mlp(
        where,
        normed_two,
        grad_branch,
        weight_up,
        bias_up,
        weight_down,
        xhat_two,
        inverse_two,
        gain_two.reshape(1, D),
        grad_out,
        mixed,
        weight_o,
    )
    up_bias_grad = up_bias_grad.reshape(FF_PAD)
    layer_out = weight_img * (resid + branch + bias_down)
    grads[9], grads[10], grads[8] = sums_two[0], sums_two[1], sums_two[2]
    if staged:
        down_sum = lax.psum_scatter(down_grad, "fsdp", scatter_dimension=0, tiled=True)
    if staged:
        outer = Reduction(
            (up_keep, o_keep), (((0, 0, UP_CUT),), ((0, UP_CUT, FF_PAD), (1, 0, D))), coords
        )
        outer_other = outer.core_step((up_send, o_send))
        grad_mixed, outer_other = tie(grad_mixed, outer_other)
        outer_far = outer.far_swap(outer.far_sends(outer_other))
    grad_qkv = attn_bwd(qkv, grad_mixed, lse, 2)
    if staged:
        grad_qkv, outer_far = tie(grad_qkv, outer_far)
        outer_near = outer.near_sends(outer_far)
        grad_qkv, outer_near = tie(grad_qkv, outer_near)
        outer_near = outer.near_swap(outer_near)
    qkv_keep, qkv_send, qkv_bias_grad, norm_sums, tokens_grad = qkv_back(
        where,
        grad_qkv,
        normed,
        weight_qkv,
        xhat_one,
        inverse_one,
        gain_one.reshape(1, D),
        grad_resid,
    )
    if staged:
        qkv_keep, qkv_send, norm_sums, qkv_bias_grad, outer_near = tie(
            qkv_keep, qkv_send, norm_sums, qkv_bias_grad, outer_near
        )
        outer_z = outer.z_sends(outer_near)
        qkv_other = outer.core_step((qkv_send,))[0]
    grads[3], grads[6] = qkv_bias_grad[0, :D], qkv_bias_grad[0, 2 * D :]
    grads[0], grads[1] = norm_sums[0], norm_sums[1]
    grads[12] = trim_hidden(up_bias_grad.reshape(1, FF_PAD)).reshape(FF)

    rows = pack_vectors(grads, widths, devices)
    owned = [None] * 15
    if staged:
        rows = jnp.pad(rows, ((0, 0), (0, OWN_ROWS * EXTRA - rows.shape[1])))
        rows = rows.reshape(GROUPS, PAIR_ROWS, EXTRA).astype(bf16)
        top, bottom = rows[:, :BLOCK_ROWS], rows[:, PAIR_ROWS - BLOCK_ROWS :]
        rows_keep = jnp.where(core == 0, top, bottom)
        rows_send = jnp.where(core == 0, bottom, top)
        rows_other = outer.core_step((rows_send,))[0]
        cut = QKV_CUT - EXTRA
        inner = Reduction(
            (qkv_keep, rows_keep), (((0, 0, cut), (1, 0, EXTRA)), ((0, cut, 3 * D),)), coords
        )
        qkv_other, rows_other, outer_z = tie(qkv_other, rows_other, outer_z)
        inner_far = inner.far_swap(inner.far_sends((qkv_other, rows_other)))
        outer_z = outer.z_swap(outer_z)
        inner_far, layer_out = tie(inner_far, layer_out)
        inner_near, outer.near = tie(inner.near_sends(inner_far), outer.near)
        inner_near = inner.near_swap(inner_near)
        outer_sum = outer.finish(outer_z)
        owned[11] = trim_hidden(outer_sum[:, :FF_PAD]).reshape(-1)
        owned[7] = outer_sum[:, FF_PAD:].reshape(-1)
        inner_near, down_sum, owned[11], owned[7] = tie(
            inner_near, down_sum, owned[11], owned[7]
        )
        inner_z = inner.z_sends(inner_near)
        inner_z, down_sum = tie(inner_z, down_sum)
        inner_z = inner.z_swap(inner_z)

        flat = down_sum.astype(f32).reshape(-1)
        size = widths[13]
        lead = flat.shape[0] - size
        got = swap(down_sum.reshape(-1)[size:], 1).astype(f32)
        owned[13] = jnp.where(core == 0, flat[:size], jnp.concatenate([got, flat[: size - lead]]))
        inner_sum = inner.finish(inner_z)
        first = QKV_CUT - EXTRA
        owned[2] = inner_sum[:, :D].reshape(-1)
        owned[4] = jnp.concatenate(
            [inner_sum[:, D:first], inner_sum[:, QKV_CUT : 2 * D + EXTRA]], axis=1
        ).reshape(-1)
        owned[5] = inner_sum[:, 2 * D + EXTRA :].reshape(-1)
        small = inner_sum[:, first:QKV_CUT].reshape(-1)
    else:
        scatter = lambda value: lax.psum_scatter(
            value.astype(f32).reshape(-1), "fsdp", scatter_dimension=0, tiled=True
        )
        fill = lambda value, i: jnp.pad(
            value.reshape(-1), (0, widths[i] * devices - value.size)
        )
        qkv_grad = join_rows(qkv_keep, qkv_send)
        for position, i in enumerate((2, 4, 5)):
            owned[i] = scatter(fill(qkv_grad[:, position * D : (position + 1) * D], i))
        owned[7] = scatter(fill(join_rows(o_keep, o_send), 7))
        owned[11] = scatter(fill(trim_hidden(join_rows(up_keep, up_send)), 11))
        owned[13] = scatter(fill(trim_hidden(down_grad.T).T, 13))
        small = scatter(rows)
    position = 0
    for i in VECTORS:
        owned[i] = small[position : position + widths[i]]
        position += widths[i]
    return (layer_out, tokens_grad, *owned)


def solution(mesh):
    row, flat = P("fsdp", None), P("fsdp")
    in_specs = (row, flat) + (flat,) * 15 + (row,)
    out_specs = (row, row) + (flat,) * 15
    return jax.shard_map(
        on_device, mesh=mesh, in_specs=in_specs, out_specs=out_specs, check_vma=False
    )
```

```python
import functools
import itertools
import jax
import jax.numpy as jnp
from jax import lax
from jax.sharding import PartitionSpec as P
from jax.experimental import pallas as pl
from jax.experimental.pallas import tpu as pltpu
D=1152; HEADS=16; HEAD_DIM=72; LANES=128
NEG=-1e30
LOG2E=1.4426950408889634
def nt(a,b): return lax.dot_general(a,b,(((1,),(1,)),((),())),preferred_element_type=jnp.float32)
def nn(a,b): return lax.dot_general(a,b,(((1,),(0,)),((),())),preferred_element_type=jnp.float32)

def fill_heads(dst, src, col, tokens, fill):
    rows=dst.shape[1]
    for h in range(HEADS):
        if fill is not None:
            dst[h]=fill
        dst[h,0:tokens,0:HEAD_DIM]=src[:,col+h*HEAD_DIM:col+(h+1)*HEAD_DIM]

def pad_values(rows, tokens, kind):
    lane=lax.broadcasted_iota(jnp.int32,(rows,LANES),1)
    row=lax.broadcasted_iota(jnp.int32,(rows,LANES),0)
    if kind=="query":
        v=jnp.where(lane==HEAD_DIM,1.0,0.0)
    elif kind=="key":
        v=jnp.where((lane==HEAD_DIM)&(row>=tokens),NEG,0.0)
    else:
        v=jnp.zeros((rows,LANES),jnp.float32)
    return v.astype(jnp.bfloat16)

def fwd_kernel(tokens, krows, qrows, per, qkv_ref, mixed_ref, lse_ref, qs, ks, vs, os):
    step=pl.program_id(0)
    @pl.when(step==0)
    def _():
        fill_heads(qs,qkv_ref,0,tokens,pad_values(qrows,tokens,"query"))
        fill_heads(ks,qkv_ref,D,tokens,pad_values(krows,tokens,"key"))
        zero=pad_values(krows,tokens,"value")
        for h in range(HEADS):
            vs[h]=zero
            vs[h,0:tokens,0:HEAD_DIM]=qkv_ref[:,2*D+h*HEAD_DIM:2*D+(h+1)*HEAD_DIM]
    c=HEAD_DIM**-0.5*LOG2E
    for j in range(per):
        h=step*per+j
        s=nt(ks[h],qs[h])
        m=jnp.max(s,axis=0,keepdims=True)
        e=jnp.exp2((s-m)*c)
        l=jnp.sum(e,axis=0,keepdims=True)
        p=(e*(1.0/l)).astype(jnp.bfloat16)
        vt=vs[h].T
        ot=nn(vt,p)
        os[h]=ot.T.astype(jnp.bfloat16)
        lse_ref[j]=m*c+jnp.log2(l)
    @pl.when(step==pl.num_programs(0)-1)
    def _():
        for h in range(HEADS):
            mixed_ref[:,h*HEAD_DIM:(h+1)*HEAD_DIM]=os[h,0:tokens,0:HEAD_DIM]

def attn_fwd(qkv, per=1):
    tokens=qkv.shape[0]
    krows=-(-tokens//16)*16; qrows=-(-tokens//128)*128
    return pl.pallas_call(functools.partial(fwd_kernel,tokens,krows,qrows,per),
        grid=(HEADS//per,),
        in_specs=[pl.BlockSpec(qkv.shape,lambda i:(0,0),pipeline_mode=pl.Buffered(1))],
        out_specs=[pl.BlockSpec((tokens,D),lambda i:(0,0),pipeline_mode=pl.Buffered(1)),pl.BlockSpec((per,1,qrows),lambda i:(i,0,0))],
        out_shape=[jax.ShapeDtypeStruct((tokens,D),jnp.bfloat16),jax.ShapeDtypeStruct((HEADS,1,qrows),jnp.float32)],
        scratch_shapes=[pltpu.VMEM((HEADS,qrows,LANES),jnp.bfloat16),pltpu.VMEM((HEADS,krows,LANES),jnp.bfloat16),
                        pltpu.VMEM((HEADS,krows,LANES),jnp.bfloat16),pltpu.VMEM((HEADS,qrows,LANES),jnp.bfloat16)],
        compiler_params=pltpu.CompilerParams(vmem_limit_bytes=56<<20,dimension_semantics=("arbitrary",)),
        cost_estimate=pl.CostEstimate(flops=4*HEADS*qrows*krows*LANES,bytes_accessed=4*tokens*D*2,transcendentals=HEADS*qrows*krows),
        name="attention_forward")(qkv)

def bwd_kernel(tokens, krows, qrows, per, qkv_ref, go_ref, lse_ref, dqkv_ref, qs, ks, vs, gs):
    step=pl.program_id(0)
    @pl.when(step==0)
    def _():
        fill_heads(qs,qkv_ref,0,tokens,pad_values(qrows,tokens,"query"))
        fill_heads(ks,qkv_ref,D,tokens,pad_values(krows,tokens,"key"))
        fill_heads(vs,qkv_ref,2*D,tokens,pad_values(krows,tokens,"value"))
        fill_heads(gs,go_ref,0,tokens,pad_values(qrows,tokens,"value"))
    scale=HEAD_DIM**-0.5
    c=scale*LOG2E
    for j in range(per):
        h=step*per+j
        q=qs[h]; k=ks[h]; v=vs[h]; g=gs[h]
        s=nt(k,q)
        p=jnp.exp2(s*c-lse_ref[j])
        dp=nt(v,g)
        dv=nn(p.astype(jnp.bfloat16),g)
        delta=jnp.sum(p*dp,axis=0,keepdims=True)
        ds=(p*(dp-delta)).astype(jnp.bfloat16)
        dk=nn(ds,q)*scale
        dqt=nn(k.T,ds)*scale
        qs[h]=dqt.T.astype(jnp.bfloat16)
        ks[h]=dk.astype(jnp.bfloat16)
        vs[h]=dv.astype(jnp.bfloat16)
    @pl.when(step==pl.num_programs(0)-1)
    def _():
        for i,r in enumerate((qs,ks,vs)):
            for h in range(HEADS):
                dqkv_ref[:,i*D+h*HEAD_DIM:i*D+(h+1)*HEAD_DIM]=r[h,0:tokens,0:HEAD_DIM]

def attn_bwd(qkv, gmixed, lse, per=1):
    tokens=qkv.shape[0]
    krows=-(-tokens//16)*16; qrows=-(-tokens//128)*128
    return pl.pallas_call(functools.partial(bwd_kernel,tokens,krows,qrows,per),
        grid=(HEADS//per,),
        in_specs=[pl.BlockSpec(qkv.shape,lambda i:(0,0),pipeline_mode=pl.Buffered(1)),pl.BlockSpec(gmixed.shape,lambda i:(0,0),pipeline_mode=pl.Buffered(1)),
                  pl.BlockSpec((per,1,qrows),lambda i:(i,0,0))],
        out_specs=pl.BlockSpec((tokens,3*D),lambda i:(0,0),pipeline_mode=pl.Buffered(1)),
        out_shape=jax.ShapeDtypeStruct((tokens,3*D),jnp.bfloat16),
        scratch_shapes=[pltpu.VMEM((HEADS,qrows,LANES),jnp.bfloat16),pltpu.VMEM((HEADS,krows,LANES),jnp.bfloat16),
                        pltpu.VMEM((HEADS,krows,LANES),jnp.bfloat16),pltpu.VMEM((HEADS,qrows,LANES),jnp.bfloat16)],
        compiler_params=pltpu.CompilerParams(vmem_limit_bytes=56<<20,dimension_semantics=("arbitrary",)),
        cost_estimate=pl.CostEstimate(flops=1000000,bytes_accessed=1000000,transcendentals=0),
        name="attention_backward")(qkv,gmixed,lse)


GELU_A = 0.7978845608028654
GELU_B = 0.044715


PAIR_ROWS = D // HEADS
BLOCK_ROWS = 40


def share_rows(core, value, keep_ref, send_ref):
    for chip in range(value.shape[0] // PAIR_ROWS):
        first = value[chip * PAIR_ROWS : chip * PAIR_ROWS + BLOCK_ROWS]
        last = value[(chip + 1) * PAIR_ROWS - BLOCK_ROWS : (chip + 1) * PAIR_ROWS]
        keep_ref[chip] = jnp.where(core == 0, first, last).astype(jnp.bfloat16)
        send_ref[chip] = jnp.where(core == 0, last, first).astype(jnp.bfloat16)


def mlp_kernel(coords, normed_ref, grad_ref, up_ref, bias_ref, down_ref, xhat_ref, inverse_ref, gain_ref,
               grad_out_ref, mixed_ref, output_ref, out_ref, up_keep_ref, up_send_ref, bias_grad_ref,
               down_grad_ref, sums_ref, resid_grad_ref, output_keep_ref, output_send_ref, mixed_grad_ref,
               normed, normed_t, grad, out, back):
    step = pl.program_id(0)
    tokens = normed_ref.shape[0]

    @pl.when(step == 0)
    def _():
        for held, source in ((normed, normed_ref), (grad, grad_ref)):
            held[...] = jnp.zeros_like(held)
            held[0:tokens] = source[...]
        normed_t[...] = normed[...].T
        out[...] = jnp.zeros_like(out)
        back[...] = jnp.zeros_like(back)

    pre = nn(normed[...], up_ref[...]) + bias_ref[...]
    square = pre * pre
    bend = jnp.tanh(pre * (GELU_A + GELU_A * GELU_B * square))
    hidden = (0.5 * pre * (1.0 + bend)).astype(jnp.bfloat16)
    slope = 0.5 * (1.0 + bend) + 0.5 * pre * (1.0 - bend * bend) * (
        GELU_A + 3.0 * GELU_A * GELU_B * square
    )
    grad_pre = (nt(grad[...], down_ref[...]) * slope).astype(jnp.bfloat16)
    out[...] += nn(hidden, down_ref[...])
    back[...] += nt(grad_pre, up_ref[...])
    down_grad_ref[...] = nn(hidden.T, grad[...]).astype(jnp.bfloat16)
    share_rows(coords[0], nn(normed_t[...], grad_pre), up_keep_ref, up_send_ref)
    bias_grad_ref[...] = jnp.sum(grad_pre.astype(jnp.float32), axis=0, keepdims=True)

    @pl.when(step == pl.num_programs(0) - 1)
    def _():
        out_ref[...] = out[0:tokens]
        total = back[0:tokens]
        xhat = xhat_ref[...]
        sums_ref[0:1] = jnp.sum(total * xhat, axis=0, keepdims=True)
        sums_ref[1:2] = jnp.sum(total, axis=0, keepdims=True)
        scaled = total * gain_ref[...]
        first = jnp.mean(scaled, axis=-1, keepdims=True)
        second = jnp.mean(scaled * xhat, axis=-1, keepdims=True)
        resid_grad = grad_out_ref[...] + inverse_ref[...] * (scaled - first - xhat * second)
        resid_grad_ref[...] = resid_grad
        grad[0:tokens] = resid_grad.astype(jnp.bfloat16)
        low = grad[...]
        sums_ref[2:3] = jnp.sum(low.astype(jnp.float32), axis=0, keepdims=True)
        mixed_grad_ref[...] = nt(low, output_ref[...]).astype(jnp.bfloat16)[0:tokens]
        normed[0:tokens] = mixed_ref[...]
        normed_t[...] = normed[...].T
        share_rows(coords[0], nn(normed_t[...], low), output_keep_ref, output_send_ref)


def whole_block(shape):
    return pl.BlockSpec(shape, lambda i: (0, 0), pipeline_mode=pl.Buffered(1))


def mlp(coords, normed, grad, up, bias, down, xhat, inverse, gain, grad_out, mixed, output):
    tokens, hidden = normed.shape[0], up.shape[1]
    rows = -(-tokens // 16) * 16
    tile = 256
    full = whole_block((tokens, D))
    columns = pl.BlockSpec((D, tile), lambda i: (0, i))
    line = pl.BlockSpec((1, tile), lambda i: (0, i))
    band = pl.BlockSpec((tile, D), lambda i: (i, 0))
    square = whole_block((D, D))
    shares = (D // PAIR_ROWS, BLOCK_ROWS)
    part = pl.BlockSpec(shares + (tile,), lambda i: (0, 0, i))
    full_part = pl.BlockSpec(
        shares + (D,), lambda i: (0, 0, 0), pipeline_mode=pl.Buffered(1)
    )
    return pl.pallas_call(
        mlp_kernel,
        grid=(hidden // tile,),
        in_specs=[pl.BlockSpec(memory_space=pltpu.SMEM), full, full, columns, line, band, full, whole_block((tokens, 1)),
                  whole_block((1, D)), full, full, square],
        out_specs=[full, part, part, line, band, whole_block((8, D)), full, full_part, full_part,
                   full],
        out_shape=[
            jax.ShapeDtypeStruct((tokens, D), jnp.float32),
            jax.ShapeDtypeStruct(shares + (hidden,), jnp.bfloat16),
            jax.ShapeDtypeStruct(shares + (hidden,), jnp.bfloat16),
            jax.ShapeDtypeStruct((1, hidden), jnp.float32),
            jax.ShapeDtypeStruct((hidden, D), jnp.bfloat16),
            jax.ShapeDtypeStruct((8, D), jnp.float32),
            jax.ShapeDtypeStruct((tokens, D), jnp.float32),
            jax.ShapeDtypeStruct(shares + (D,), jnp.bfloat16),
            jax.ShapeDtypeStruct(shares + (D,), jnp.bfloat16),
            jax.ShapeDtypeStruct((tokens, D), jnp.bfloat16),
        ],
        scratch_shapes=[
            pltpu.VMEM((rows, D), jnp.bfloat16),
            pltpu.VMEM((D, rows), jnp.bfloat16),
            pltpu.VMEM((rows, D), jnp.bfloat16),
            pltpu.VMEM((rows, D), jnp.float32),
            pltpu.VMEM((rows, D), jnp.float32),
        ],
        compiler_params=pltpu.CompilerParams(
            vmem_limit_bytes=56 << 20, dimension_semantics=("arbitrary",)
        ),
        cost_estimate=pl.CostEstimate(flops=1000000, bytes_accessed=1000000, transcendentals=0),
        name="mlp_forward_backward",
    )(coords, normed, grad, up, bias, down, xhat, inverse, gain, grad_out, mixed, output)


def qkv_back_kernel(coords, grad_ref, normed_ref, weight_ref, xhat_ref, inverse_ref, gain_ref, resid_ref,
                    keep_ref, send_ref, bias_grad_ref, sums_ref, tokens_ref, grad, normed_t, total):
    step = pl.program_id(0)
    tokens = normed_ref.shape[0]

    @pl.when(step == 0)
    def _():
        grad[...] = jnp.zeros_like(grad)
        grad[0:tokens] = normed_ref[...]
        normed_t[...] = grad[...].T
        grad[...] = jnp.zeros_like(grad)
        total[...] = jnp.zeros_like(total)

    grad[0:tokens] = grad_ref[...]
    share_rows(coords[0], nn(normed_t[...], grad[...]), keep_ref, send_ref)
    bias_grad_ref[...] = jnp.sum(grad[...].astype(jnp.float32), axis=0, keepdims=True)
    total[...] += nt(grad[...], weight_ref[...])

    @pl.when(step == pl.num_programs(0) - 1)
    def _():
        back = total[0:tokens]
        xhat = xhat_ref[...]
        sums_ref[0:1] = jnp.sum(back * xhat, axis=0, keepdims=True)
        sums_ref[1:2] = jnp.sum(back, axis=0, keepdims=True)
        scaled = back * gain_ref[...]
        first = jnp.mean(scaled, axis=-1, keepdims=True)
        second = jnp.mean(scaled * xhat, axis=-1, keepdims=True)
        tokens_ref[...] = resid_ref[...] + inverse_ref[...] * (scaled - first - xhat * second)


def qkv_back(coords, grad, normed, weight, xhat, inverse, gain, resid):
    tokens = normed.shape[0]
    rows = -(-tokens // 16) * 16
    whole = lambda shape: pl.BlockSpec(shape, lambda i: (0, 0), pipeline_mode=pl.Buffered(1))
    part = lambda shape: pl.BlockSpec(shape, lambda i: (0, i))
    shares = (D // PAIR_ROWS, BLOCK_ROWS)
    share = pl.BlockSpec(shares + (D,), lambda i: (0, 0, i))
    return pl.pallas_call(
        qkv_back_kernel,
        grid=(3,),
        in_specs=[
            pl.BlockSpec(memory_space=pltpu.SMEM),
            part((tokens, D)),
            whole((tokens, D)),
            part((D, D)),
            whole((tokens, D)),
            whole((tokens, 1)),
            whole((1, D)),
            whole((tokens, D)),
        ],
        out_specs=[share, share, part((1, D)), whole((8, D)), whole((tokens, D))],
        out_shape=[
            jax.ShapeDtypeStruct(shares + (3 * D,), jnp.bfloat16),
            jax.ShapeDtypeStruct(shares + (3 * D,), jnp.bfloat16),
            jax.ShapeDtypeStruct((1, 3 * D), jnp.float32),
            jax.ShapeDtypeStruct((8, D), jnp.float32),
            jax.ShapeDtypeStruct((tokens, D), jnp.float32),
        ],
        scratch_shapes=[
            pltpu.VMEM((rows, D), jnp.bfloat16),
            pltpu.VMEM((D, rows), jnp.bfloat16),
            pltpu.VMEM((rows, D), jnp.float32),
        ],
        compiler_params=pltpu.CompilerParams(
            vmem_limit_bytes=56 << 20, dimension_semantics=("arbitrary",)
        ),
        cost_estimate=pl.CostEstimate(flops=1000000, bytes_accessed=1000000, transcendentals=0),
        name="qkv_backward",
    )(coords, grad, normed, weight, xhat, inverse, gain, resid)


FF = 4304
GROUPS = 16
FF_GROUP = FF // GROUPS
FF_ROWS = 272
FF_PAD = GROUPS * FF_ROWS
HALF_DOWN = FF_ROWS // 2
OWN_ROWS = PAIR_ROWS // 2
TILE = 8
BLOCK_TILES = 5
PAIR_TILES = PAIR_ROWS // TILE
EXTRA = 128
QKV_CUT = 14 * 128
UP_CUT = 22 * 128
UP_PIECES = 4
DOWN_CUT = 40
DOWN_FIRST = 64
REST_ROWS = UP_PIECES * BLOCK_TILES * TILE + BLOCK_TILES * TILE + DOWN_FIRST
VECTORS = (0, 1, 3, 6, 8, 9, 10, 14, 12)
bf16 = jnp.bfloat16
f32 = jnp.float32


def product(left, right):
    return jnp.dot(left, right, preferred_element_type=f32)


def product_t(left, right):
    return lax.dot_general(left, right, (((0,), (0,)), ((), ())), preferred_element_type=f32)


def product_bt(left, right):
    return lax.dot_general(left, right, (((1,), (1,)), ((), ())), preferred_element_type=f32)


def swap(value, mask):
    devices = lax.axis_size("fsdp")
    return lax.ppermute(value, "fsdp", [(i, i ^ mask) for i in range(devices)])


def pad_hidden(columns):
    rows = columns.shape[0]
    grouped = columns.reshape(rows, GROUPS, FF_GROUP)
    return jnp.pad(grouped, ((0, 0), (0, 0), (0, FF_ROWS - FF_GROUP))).reshape(rows, FF_PAD)


def trim_hidden(columns):
    rows = columns.shape[0]
    return columns.reshape(rows, GROUPS, FF_ROWS)[:, :, :FF_GROUP].reshape(rows, FF)


def place_square_kernel(coords, *refs):
    sources, (whole, small) = refs[:8], refs[8:10]
    held, in_sems, out_sems = refs[10:18], refs[18], refs[19]
    core, x, y, z = coords[0], coords[1], coords[2], coords[3]
    arrivals = [pltpu.make_async_copy(sources[i], held[i], in_sems.at[i]) for i in range(8)]
    for arrival in arrivals:
        arrival.start()
    copies, extras = [], []
    for part, stream in itertools.product(range(4), range(2)):
        arrivals[4 * stream + part].wait()
        for near, dz in itertools.product(range(2), range(4)):
            src = held[4 * stream + part].at[near * 4 + dz]
            owner = core if part < 2 else 1 - core
            far = part % 2
            dx, dy = (near, far) if stream == 0 else (far, near)
            chip = ((z ^ dz) * 2 + (y ^ dy)) * 2 + (x ^ dx)
            cols = src.shape[-1] - (0 if stream else EXTRA)
            col = QKV_CUT - EXTRA if stream else 0
            src_cols = pl.ds(0 if stream else EXTRA, cols)
            first = PAIR_TILES * chip + BLOCK_TILES * owner
            copies.append(
                pltpu.make_async_copy(
                    src.at[pl.ds(owner, BLOCK_TILES - 1), :, src_cols],
                    whole.at[pl.ds(first, BLOCK_TILES - 1), :, pl.ds(col, cols)],
                    out_sems.at[len(copies)],
                )
            )
            copies[-1].start()
            extra = pltpu.make_async_copy(
                src.at[BLOCK_TILES - 1, :, src_cols],
                whole.at[PAIR_TILES * chip + BLOCK_TILES - 1, :, pl.ds(col, cols)],
                out_sems.at[96 + len(extras)],
            )
            pl.when(owner == 0)(extra.start)
            extras.append((owner, extra))
            if stream == 0:
                copies.append(
                    pltpu.make_async_copy(
                        src.at[:, :, :EXTRA], small.at[chip * 2 + owner], out_sems.at[len(copies)]
                    )
                )
                copies[-1].start()
    for copy in copies:
        copy.wait()
    for owner, extra in extras:
        pl.when(owner == 0)(extra.wait)


def place_square(streams, coords):
    sources = [s.reshape(8, BLOCK_TILES, TILE, -1) for s in (*streams[0], *streams[1])]
    size = sum(s.size for s in sources) * 2
    whole, small = pl.pallas_call(
        place_square_kernel,
        in_specs=[pl.BlockSpec(memory_space=pltpu.SMEM)]
        + [pl.BlockSpec(memory_space=pltpu.HBM)] * 8,
        out_specs=[pl.BlockSpec(memory_space=pltpu.HBM)] * 2,
        out_shape=[
            jax.ShapeDtypeStruct((GROUPS * PAIR_TILES, TILE, 3 * D), bf16),
            jax.ShapeDtypeStruct((2 * GROUPS, BLOCK_TILES, TILE, EXTRA), bf16),
        ],
        scratch_shapes=[pltpu.VMEM(s.shape, bf16) for s in sources]
        + [pltpu.SemaphoreType.DMA((8,)), pltpu.SemaphoreType.DMA((160,))],
        compiler_params=pltpu.CompilerParams(vmem_limit_bytes=40 << 20),
        cost_estimate=pl.CostEstimate(flops=0, bytes_accessed=2 * size, transcendentals=0),
        name="place_square",
    )(coords, *sources)
    return whole.reshape(D, 3 * D), small.reshape(2 * GROUPS, -1)


def place_rest_kernel(coords, *refs):
    source, streams, (up, out, down) = refs[0], refs[1:9], refs[9:12]
    held, in_sems, out_sems = refs[12], refs[13], refs[14]
    parts, part_sems = refs[15:23], refs[23]
    core, x, y, z = coords[0], coords[1], coords[2], coords[3]
    arrivals = [
        pltpu.make_async_copy(source.at[i], held.at[i], in_sems.at[i]) for i in range(2 * GROUPS)
    ]
    others = [pltpu.make_async_copy(streams[i], parts[i], part_sems.at[i]) for i in range(8)]
    for arrival in arrivals + others:
        arrival.start()
    copies = []

    def move(one, other):
        copies.append(pltpu.make_async_copy(one, other, out_sems.at[len(copies)]))
        copies[-1].start()

    lead = DOWN_FIRST // TILE
    for device in range(2 * GROUPS):
        chip, owner = device // 2, device % 2
        src = held.at[device]
        arrivals[device].wait()
        count = BLOCK_TILES - owner
        first = PAIR_TILES * chip + BLOCK_TILES * owner
        for piece in range(UP_PIECES):
            cols = min(D, FF_PAD - piece * D)
            move(
                src.at[pl.ds(piece * BLOCK_TILES + owner, count), :, pl.ds(0, cols)],
                up.at[pl.ds(first, count), :, pl.ds(piece * D, cols)],
            )
        base = UP_PIECES * BLOCK_TILES
        move(src.at[pl.ds(base + owner, count)], out.at[pl.ds(first, count)])
        move(src.at[pl.ds(base + BLOCK_TILES, lead)], down.at[device, pl.ds(0, lead)])
    for part, stream in itertools.product(range(4), range(2)):
        others[4 * stream + part].wait()
        for near, dz in itertools.product(range(2), range(4)):
            src = parts[4 * stream + part].at[near * 4 + dz]
            owner = core if part < 2 else 1 - core
            far = part % 2
            dx, dy = (near, far) if stream == 0 else (far, near)
            chip = ((z ^ dz) * 2 + (y ^ dy)) * 2 + (x ^ dx)
            first = lead + (DOWN_CUT // TILE if stream else 0)
            move(src, down.at[chip * 2 + owner, pl.ds(first, src.shape[0])])
    for copy in copies:
        copy.wait()


def place_rest(gathered, streams, coords):
    source = gathered.reshape(2 * GROUPS, REST_ROWS // TILE, TILE, D)
    sources = [s.reshape(8, -1, TILE, D) for s in (*streams[0], *streams[1])]
    up, out, down = pl.pallas_call(
        place_rest_kernel,
        in_specs=[pl.BlockSpec(memory_space=pltpu.SMEM)]
        + [pl.BlockSpec(memory_space=pltpu.HBM)] * 9,
        out_specs=[pl.BlockSpec(memory_space=pltpu.HBM)] * 3,
        out_shape=[
            jax.ShapeDtypeStruct((D // TILE, TILE, FF_PAD), bf16),
            jax.ShapeDtypeStruct((D // TILE, TILE, D), bf16),
            jax.ShapeDtypeStruct((2 * GROUPS, HALF_DOWN // TILE, TILE, D), bf16),
        ],
        scratch_shapes=[
            pltpu.VMEM(source.shape, bf16),
            pltpu.SemaphoreType.DMA((2 * GROUPS,)),
            pltpu.SemaphoreType.DMA((2 * GROUPS * (UP_PIECES + 2) + 64,)),
        ]
        + [pltpu.VMEM(s.shape, bf16) for s in sources]
        + [pltpu.SemaphoreType.DMA((8,))],
        compiler_params=pltpu.CompilerParams(vmem_limit_bytes=60 << 20),
        cost_estimate=pl.CostEstimate(
            flops=0, bytes_accessed=4 * source.size, transcendentals=0
        ),
        name="place_rest",
    )(coords, source, *sources)
    return up.reshape(D, FF_PAD), out.reshape(D, D), down.reshape(FF_PAD, D)


def tie(*values):
    leaves, form = jax.tree.flatten(values)
    return form.unflatten(lax.optimization_barrier(leaves))


def gather_z(block):
    return [block] + [swap(block, 8 * step) for step in (1, 2, 3)]


def gather_near(parts, cut, axis):
    streams = []
    for stream in range(2):
        if axis == 1:
            own = jnp.stack([p[:, :cut] if stream == 0 else p[:, cut:] for p in parts])
        else:
            own = jnp.stack([p[:cut] if stream == 0 else p[cut:] for p in parts])
        streams.append((own, swap(own, 4 if stream else 2)))
    return streams


def gather_far(streams):
    results = []
    for stream in range(2):
        first = jnp.concatenate(streams[stream])
        results.append((first, swap(first, 2 if stream else 4)))
    return results


def gather_core(streams):
    return [(first, second, swap(first, 1), swap(second, 1)) for first, second in streams]


def window(value, starts, sizes):
    rank = value.ndim
    starts = list(starts) + [0] * (rank - len(starts))
    lengths = list(value.shape)
    for axis, size in enumerate(sizes):
        if size is not None:
            lengths[axis] = size
    starts = [jnp.int32(0) if start is None else jnp.int32(start) for start in starts]
    result = lax.dynamic_slice(value, starts, lengths)
    kept = [
        length for axis, length in enumerate(lengths) if axis >= len(sizes) or sizes[axis] != 1
    ]
    return result.reshape(kept)


class Reduction:
    def __init__(self, keeps, streams, coords):
        self.keeps = [k.reshape(4, 2, 2, BLOCK_TILES, TILE, -1) for k in keeps]
        self.streams = streams
        self.coords = coords

    def part(self, arrays, stream, plane):
        sizes = tuple(None if p is None else 1 for p in plane) + (None, None)
        pieces = []
        for number, first, last in self.streams[stream]:
            starts = tuple(plane) + (None, None, first)
            pieces.append(window(arrays[number], starts, sizes + (last - first,)))
        return pieces[0] if len(pieces) == 1 else jnp.concatenate(pieces, axis=-1)

    def terms(self, stream, plane):
        return [self.part(self.keeps, stream, plane), self.part(self.other, stream, plane)]

    def core_step(self, sends):
        return [swap(send.reshape(4, 2, 2, BLOCK_TILES, TILE, -1), 1) for send in sends]

    def far_sends(self, other, streams=(0, 1), pieces=slice(None)):
        core, x, y, z = self.coords
        self.other = other
        sends = []
        every = self.streams
        for stream in streams:
            plane = (None, None, 1 - x) if stream else (None, 1 - y, None)
            self.streams = {stream: every[stream][pieces]}
            sends.append(total_of(self.terms(stream, plane)).astype(bf16))
        self.streams = every
        return sends

    def far_swap(self, sends):
        return [swap(send, 2 if stream else 4) for stream, send in enumerate(sends)]

    def near_sends(self, far):
        core, x, y, z = self.coords
        self.far = far
        sends = []
        for stream in range(2):
            plane = (None, 1 - y, x) if stream else (None, y, 1 - x)
            after = (None, 1 - y) if stream else (None, 1 - x)
            terms = self.terms(stream, plane) + [window(far[stream], after, (None, 1))]
            sends.append(total_of(terms).astype(bf16))
        return sends

    def near_swap(self, sends):
        return [swap(send, 4 if stream else 2) for stream, send in enumerate(sends)]

    def at(self, plane):
        core, x, y, z = self.coords
        pieces = []
        for stream in range(2):
            after = (plane, y) if stream else (plane, x)
            terms = self.terms(stream, (plane, y, x)) + [
                window(self.far[stream], after, (1, 1)),
                window(self.near[stream], (plane,), (1,)),
            ]
            pieces.append(total_of(terms))
        return jnp.concatenate(pieces, axis=-1)

    def z_sends(self, near):
        z = self.coords[3]
        self.near = near
        return [self.at(z ^ step).astype(bf16) for step in (1, 2, 3)]

    def z_swap(self, sends):
        return [swap(send, 8 * step) for step, send in zip((1, 2, 3), sends)]

    def finish(self, arrived):
        core, x, y, z = self.coords
        total = total_of([self.at(z)] + arrived)
        total = total.reshape(BLOCK_TILES * TILE, -1)
        return lax.dynamic_slice_in_dim(
            total, core * (BLOCK_TILES * TILE - OWN_ROWS), OWN_ROWS, 0
        )


def join_rows(keep, send):
    whole = jnp.concatenate([keep, send[:, 2 * BLOCK_ROWS - PAIR_ROWS :]], axis=1)
    return whole.reshape(D, -1)


def total_of(terms):
    total = terms[0].astype(f32)
    for term in terms[1:]:
        total = total + term.astype(f32)
    return total


def fetch_pairs(narrow, core):
    q, k, v, o = (narrow[i].reshape(OWN_ROWS, D) for i in (2, 4, 5, 7))
    up = pad_hidden(narrow[11].reshape(OWN_ROWS, FF))
    down = narrow[13]
    rows = jnp.concatenate([q, k, v, o, up], axis=1)
    spare = BLOCK_TILES * TILE - OWN_ROWS
    lead = D * HALF_DOWN - down.shape[0]
    tail = jnp.pad(down[:lead].reshape(spare, -1), ((0, 0), (0, 512 - lead // spare)))
    is_first = core == 0
    edge = jnp.where(is_first, rows[OWN_ROWS - spare :], rows[:spare])
    got = swap(jnp.concatenate([edge, tail], axis=1), 1)
    edge = got[:, : rows.shape[1]]
    block = jnp.where(is_first, jnp.concatenate([rows, edge]), jnp.concatenate([edge, rows]))
    extra = got[:, rows.shape[1] : rows.shape[1] + lead // spare].reshape(-1)
    end = jnp.zeros((D * HALF_DOWN - (down.shape[0] - lead),), bf16)
    down_block = jnp.where(
        is_first, jnp.concatenate([down, extra]), jnp.concatenate([down[lead:], end])
    ).reshape(HALF_DOWN, D)
    small = jnp.concatenate([narrow[i] for i in VECTORS])
    small = jnp.pad(small, (0, BLOCK_TILES * TILE * EXTRA - small.shape[0]))
    small = small.reshape(BLOCK_TILES * TILE, EXTRA)
    square = jnp.concatenate([small, block[:, : 3 * D]], axis=1)
    up_block = jnp.pad(block[:, 4 * D :], ((0, 0), (0, UP_PIECES * D - FF_PAD)))
    pieces = [up_block[:, i * D : (i + 1) * D] for i in range(UP_PIECES)]
    rest = jnp.concatenate(pieces + [block[:, 3 * D : 4 * D], down_block[:DOWN_FIRST]])
    return square, rest, down_block[DOWN_FIRST:]


def normalize(values):
    centre = jnp.mean(values, axis=-1, keepdims=True)
    centered = values - centre
    spread_sq = jnp.mean(centered * centered, axis=-1, keepdims=True)
    inverse = lax.rsqrt(spread_sq + 1e-06)
    return centered * inverse, inverse


def normalize_back(grad, gain, xhat, inverse):
    scaled = grad * gain
    first = jnp.mean(scaled, axis=-1, keepdims=True)
    second = jnp.mean(scaled * xhat, axis=-1, keepdims=True)
    return inverse * (scaled - first - xhat * second)


def name_vectors(whole, widths):
    count = len(VECTORS) - 1
    width = widths[VECTORS[0]]
    pieces = whole[:, : count * width].reshape(-1, count, width)
    pieces = pieces.transpose(1, 0, 2).reshape(count, -1).astype(f32)
    found = {i: pieces[position : position + 1] for position, i in enumerate(VECTORS[:-1])}
    last = widths[VECTORS[-1]]
    found[VECTORS[-1]] = whole[:, count * width : count * width + last].reshape(-1).astype(f32)
    return found


def pack_vectors(vectors, width, devices):
    rows = jnp.stack(vectors)
    rows = jnp.pad(rows, ((0, 0), (0, width * devices - rows.shape[1])))
    rows = rows.reshape(len(vectors), devices, width)
    return rows.transpose(1, 0, 2).reshape(devices, -1)


def gather_plain(narrow, widths):
    whole = {
        i: lax.all_gather(narrow[i], "fsdp", axis=0, tiled=True) for i in (2, 4, 5, 7, 11, 13)
    }
    square = [whole[i][: D * D].reshape(D, D) for i in (2, 4, 5, 7)]
    up = pad_hidden(whole[11][: D * FF].reshape(D, FF))
    down = pad_hidden(whole[13][: D * FF].reshape(FF, D).T).T
    joined = jnp.concatenate([narrow[i] for i in VECTORS])
    length = joined.shape[0]
    joined = jnp.pad(joined, (0, 2048 - length)).reshape(16, 128)
    joined = lax.all_gather(joined, "fsdp", axis=0, tiled=True).reshape(-1, 2048)
    return jnp.concatenate(square[:3], axis=1), square[3], up, down, name_vectors(joined, widths)


def on_device(*args):
    devices = lax.axis_size("fsdp")
    tokens, image_valid = args[0], args[1]
    shards = args[2:17]
    cotangent = args[17]
    staged = devices == 32
    widths = [piece.shape[0] for piece in shards]
    narrow = [piece.astype(bf16) for piece in shards]
    index = lax.axis_index("fsdp")
    core, x, y, z = index % 2, (index // 2) % 2, (index // 4) % 2, index // 8
    coords = (core, x, y, z)
    image_count = image_valid.shape[0]
    seq_len = tokens.shape[0] // image_count
    weight_img = jnp.repeat(image_valid.astype(f32), seq_len)[:, None]

    grad_out = weight_img * cotangent
    grad_branch = grad_out.astype(bf16)
    grads = {14: jnp.sum(grad_branch.astype(f32), axis=0)}
    xhat_one, inverse_one = normalize(tokens)
    where = jnp.stack(coords if staged else (jnp.int32(0),) * 4).astype(jnp.int32)
    if staged:
        sq, rest, down = fetch_pairs(narrow, core)
        rest = lax.all_gather(rest, "fsdp", axis=0, tiled=True)
        sq, tokens = tie(sq, tokens)
        sq = gather_z(sq)
        xhat_one, inverse_one = normalize(tokens)
        sq, down, xhat_one, inverse_one, grad_branch = tie(
            sq, down, xhat_one, inverse_one, grad_branch
        )
        sq = gather_near(sq, QKV_CUT, 1)
        down = gather_z(down)
        sq = gather_far(sq)
        sq, down = tie(sq, down)
        sq = gather_core(sq)
        down = gather_near(down, DOWN_CUT, 0)
        weight_qkv, small = place_square(sq, where)
        vectors = name_vectors(small, widths)
    else:
        weight_qkv, weight_o, weight_up, weight_down, vectors = gather_plain(narrow, widths)

    vec = lambda i: vectors[i][:, :D]
    gain_one, shift_one, gain_two, shift_two = vec(0), vec(1), vec(9), vec(10)
    bias_qkv = jnp.concatenate([vec(3), jnp.zeros((1, D), f32), vec(6)], axis=1)
    bias_o, bias_down = vec(8), vec(14)
    bias_up = pad_hidden(vectors[12][:FF].reshape(1, FF))

    normed = (xhat_one * gain_one + shift_one).astype(bf16)
    qkv = (product(normed, weight_qkv) + bias_qkv).astype(bf16)
    if staged:
        qkv, down = tie(qkv, down)
        down = [(*pair, swap(pair[0], 1)) for pair in gather_far(down)]
    mixed, lse = attn_fwd(qkv, 2)
    if staged:
        mixed, lse, down = tie(mixed, lse, down)
        down = [(*parts, swap(parts[1], 1)) for parts in down]
        weight_up, weight_o, weight_down = place_rest(rest, down, where)
    resid = tokens + product(mixed, weight_o) + bias_o
    xhat_two, inverse_two = normalize(resid)
    normed_two = (xhat_two * gain_two + shift_two).astype(bf16)
    (
        branch,
        up_keep,
        up_send,
        up_bias_grad,
        down_grad,
        sums_two,
        grad_resid,
        o_keep,
        o_send,
        grad_mixed,
    ) = mlp(
        where,
        normed_two,
        grad_branch,
        weight_up,
        bias_up,
        weight_down,
        xhat_two,
        inverse_two,
        gain_two.reshape(1, D),
        grad_out,
        mixed,
        weight_o,
    )
    up_bias_grad = up_bias_grad.reshape(FF_PAD)
    layer_out = weight_img * (resid + branch + bias_down)
    grads[9], grads[10], grads[8] = sums_two[0], sums_two[1], sums_two[2]
    hidden_grad = trim_hidden(up_bias_grad.reshape(1, FF_PAD)).reshape(FF)
    early = jnp.concatenate(
        [
            pack_vectors([grads[i] for i in VECTORS[4:8]], widths[0], devices),
            pack_vectors([hidden_grad], widths[12], devices),
        ],
        axis=1,
    )
    if staged:
        down_sum = lax.psum_scatter(down_grad, "fsdp", scatter_dimension=0, tiled=True)
    if staged:
        outer = Reduction(
            (up_keep, o_keep), (((0, 0, UP_CUT),), ((0, UP_CUT, FF_PAD), (1, 0, D))), coords
        )
        outer_other = outer.core_step((up_send, o_send))
        early = early.astype(bf16)
        grad_mixed, outer_other, early = tie(grad_mixed, outer_other, early)
        outer_far = outer.far_swap(outer.far_sends(outer_other))
    grad_qkv = attn_bwd(qkv, grad_mixed, lse, 2)
    if staged:
        grad_qkv, outer_far = tie(grad_qkv, outer_far)
        outer_near = outer.near_sends(outer_far)
        grad_qkv, outer_near = tie(grad_qkv, outer_near)
        outer_near = outer.near_swap(outer_near)
    qkv_keep, qkv_send, qkv_bias_grad, norm_sums, tokens_grad = qkv_back(
        where,
        grad_qkv,
        normed,
        weight_qkv,
        xhat_one,
        inverse_one,
        gain_one.reshape(1, D),
        grad_resid,
    )
    if staged:
        qkv_keep, qkv_send, norm_sums, qkv_bias_grad, outer_near = tie(
            qkv_keep, qkv_send, norm_sums, qkv_bias_grad, outer_near
        )
        outer_z = outer.z_sends(outer_near)
        qkv_other = outer.core_step((qkv_send,))[0]
    grads[3], grads[6] = qkv_bias_grad[0, :D], qkv_bias_grad[0, 2 * D :]
    grads[0], grads[1] = norm_sums[0], norm_sums[1]

    late = [grads[i] for i in VECTORS[:4]]
    rows = jnp.concatenate(
        [pack_vectors(late, widths[0], devices).astype(early.dtype), early], axis=1
    )
    owned = [None] * 15
    if staged:
        rows = jnp.pad(rows, ((0, 0), (0, OWN_ROWS * EXTRA - rows.shape[1])))
        rows = rows.reshape(GROUPS, PAIR_ROWS, EXTRA).astype(bf16)
        top, bottom = rows[:, :BLOCK_ROWS], rows[:, PAIR_ROWS - BLOCK_ROWS :]
        rows_keep = jnp.where(core == 0, top, bottom)
        rows_send = jnp.where(core == 0, bottom, top)
        rows_other = outer.core_step((rows_send,))[0]
        cut = QKV_CUT - EXTRA
        inner = Reduction(
            (qkv_keep, rows_keep), (((0, 0, cut), (1, 0, EXTRA)), ((0, cut, 3 * D),)), coords
        )
        qkv_other, rows_other, outer_z = tie(qkv_other, rows_other, outer_z)
        inner_far = inner.far_swap(inner.far_sends((qkv_other, rows_other)))
        outer_z = outer.z_swap(outer_z)
        inner_far, layer_out = tie(inner_far, layer_out)
        inner_near, outer.near = tie(inner.near_sends(inner_far), outer.near)
        inner_near = inner.near_swap(inner_near)
        outer_sum = outer.finish(outer_z)
        owned[11] = trim_hidden(outer_sum[:, :FF_PAD]).reshape(-1)
        owned[7] = outer_sum[:, FF_PAD:].reshape(-1)
        inner_near, down_sum, owned[11], owned[7] = tie(
            inner_near, down_sum, owned[11], owned[7]
        )
        inner_z = inner.z_sends(inner_near)
        inner_z, down_sum = tie(inner_z, down_sum)
        inner_z = inner.z_swap(inner_z)

        flat = down_sum.astype(f32).reshape(-1)
        size = widths[13]
        lead = flat.shape[0] - size
        got = swap(down_sum.reshape(-1)[size:], 1).astype(f32)
        owned[13] = jnp.where(core == 0, flat[:size], jnp.concatenate([got, flat[: size - lead]]))
        inner_sum = inner.finish(inner_z)
        first = QKV_CUT - EXTRA
        owned[2] = inner_sum[:, :D].reshape(-1)
        owned[4] = jnp.concatenate(
            [inner_sum[:, D:first], inner_sum[:, QKV_CUT : 2 * D + EXTRA]], axis=1
        ).reshape(-1)
        owned[5] = inner_sum[:, 2 * D + EXTRA :].reshape(-1)
        small = inner_sum[:, first:QKV_CUT].reshape(-1)
    else:
        scatter = lambda value: lax.psum_scatter(
            value.astype(f32).reshape(-1), "fsdp", scatter_dimension=0, tiled=True
        )
        fill = lambda value, i: jnp.pad(
            value.reshape(-1), (0, widths[i] * devices - value.size)
        )
        qkv_grad = join_rows(qkv_keep, qkv_send)
        for position, i in enumerate((2, 4, 5)):
            owned[i] = scatter(fill(qkv_grad[:, position * D : (position + 1) * D], i))
        owned[7] = scatter(fill(join_rows(o_keep, o_send), 7))
        owned[11] = scatter(fill(trim_hidden(join_rows(up_keep, up_send)), 11))
        owned[13] = scatter(fill(trim_hidden(down_grad.T).T, 13))
        small = scatter(rows)
    position = 0
    for i in VECTORS:
        owned[i] = small[position : position + widths[i]]
        position += widths[i]
    return (layer_out, tokens_grad, *owned)


def solution(mesh):
    row, flat = P("fsdp", None), P("fsdp")
    in_specs = (row, flat) + (flat,) * 15 + (row,)
    out_specs = (row, row) + (flat,) * 15
    return jax.shard_map(
        on_device, mesh=mesh, in_specs=in_specs, out_specs=out_specs, check_vma=False
    )
```

```python
import functools
import itertools
import jax
import jax.numpy as jnp
from jax import lax
from jax.sharding import PartitionSpec as P
from jax.experimental import pallas as pl
from jax.experimental.pallas import tpu as pltpu
D=1152; HEADS=16; HEAD_DIM=72; LANES=128
NEG=-1e30
LOG2E=1.4426950408889634
def nt(a,b): return lax.dot_general(a,b,(((1,),(1,)),((),())),preferred_element_type=jnp.float32)
def nn(a,b): return lax.dot_general(a,b,(((1,),(0,)),((),())),preferred_element_type=jnp.float32)

def fill_heads(dst, src, col, tokens, fill):
    rows=dst.shape[1]
    for h in range(HEADS):
        if fill is not None:
            dst[h]=fill
        dst[h,0:tokens,0:HEAD_DIM]=src[:,col+h*HEAD_DIM:col+(h+1)*HEAD_DIM]

def pad_values(rows, tokens, kind):
    lane=lax.broadcasted_iota(jnp.int32,(rows,LANES),1)
    row=lax.broadcasted_iota(jnp.int32,(rows,LANES),0)
    if kind=="query":
        v=jnp.where(lane==HEAD_DIM,1.0,0.0)
    elif kind=="key":
        v=jnp.where((lane==HEAD_DIM)&(row>=tokens),NEG,0.0)
    else:
        v=jnp.zeros((rows,LANES),jnp.float32)
    return v.astype(jnp.bfloat16)

def fwd_kernel(tokens, krows, qrows, per, qkv_ref, mixed_ref, lse_ref, qs, ks, vs, os):
    step=pl.program_id(0)
    @pl.when(step==0)
    def _():
        fill_heads(qs,qkv_ref,0,tokens,pad_values(qrows,tokens,"query"))
        fill_heads(ks,qkv_ref,D,tokens,pad_values(krows,tokens,"key"))
        zero=pad_values(krows,tokens,"value")
        for h in range(HEADS):
            vs[h]=zero
            vs[h,0:tokens,0:HEAD_DIM]=qkv_ref[:,2*D+h*HEAD_DIM:2*D+(h+1)*HEAD_DIM]
    c=HEAD_DIM**-0.5*LOG2E
    for j in range(per):
        h=step*per+j
        s=nt(ks[h],qs[h])
        m=jnp.max(s,axis=0,keepdims=True)
        e=jnp.exp2((s-m)*c)
        l=jnp.sum(e,axis=0,keepdims=True)
        p=(e*(1.0/l)).astype(jnp.bfloat16)
        vt=vs[h].T
        ot=nn(vt,p)
        os[h]=ot.T.astype(jnp.bfloat16)
        lse_ref[j]=m*c+jnp.log2(l)
    @pl.when(step==pl.num_programs(0)-1)
    def _():
        for h in range(HEADS):
            mixed_ref[:,h*HEAD_DIM:(h+1)*HEAD_DIM]=os[h,0:tokens,0:HEAD_DIM]

def attn_fwd(qkv, per=1):
    tokens=qkv.shape[0]
    krows=-(-tokens//16)*16; qrows=-(-tokens//128)*128
    return pl.pallas_call(functools.partial(fwd_kernel,tokens,krows,qrows,per),
        grid=(HEADS//per,),
        in_specs=[pl.BlockSpec(qkv.shape,lambda i:(0,0),pipeline_mode=pl.Buffered(1))],
        out_specs=[pl.BlockSpec((tokens,D),lambda i:(0,0),pipeline_mode=pl.Buffered(1)),pl.BlockSpec((per,1,qrows),lambda i:(i,0,0))],
        out_shape=[jax.ShapeDtypeStruct((tokens,D),jnp.bfloat16),jax.ShapeDtypeStruct((HEADS,1,qrows),jnp.float32)],
        scratch_shapes=[pltpu.VMEM((HEADS,qrows,LANES),jnp.bfloat16),pltpu.VMEM((HEADS,krows,LANES),jnp.bfloat16),
                        pltpu.VMEM((HEADS,krows,LANES),jnp.bfloat16),pltpu.VMEM((HEADS,qrows,LANES),jnp.bfloat16)],
        compiler_params=pltpu.CompilerParams(vmem_limit_bytes=56<<20,dimension_semantics=("arbitrary",)),
        cost_estimate=pl.CostEstimate(flops=4*HEADS*qrows*krows*LANES,bytes_accessed=4*tokens*D*2,transcendentals=HEADS*qrows*krows),
        name="attention_forward")(qkv)

def bwd_kernel(tokens, krows, qrows, per, qkv_ref, go_ref, lse_ref, dqkv_ref, qs, ks, vs, gs):
    step=pl.program_id(0)
    @pl.when(step==0)
    def _():
        fill_heads(qs,qkv_ref,0,tokens,pad_values(qrows,tokens,"query"))
        fill_heads(ks,qkv_ref,D,tokens,pad_values(krows,tokens,"key"))
        fill_heads(vs,qkv_ref,2*D,tokens,pad_values(krows,tokens,"value"))
        fill_heads(gs,go_ref,0,tokens,pad_values(qrows,tokens,"value"))
    scale=HEAD_DIM**-0.5
    c=scale*LOG2E
    for j in range(per):
        h=step*per+j
        q=qs[h]; k=ks[h]; v=vs[h]; g=gs[h]
        s=nt(k,q)
        p=jnp.exp2(s*c-lse_ref[j])
        dp=nt(v,g)
        dv=nn(p.astype(jnp.bfloat16),g)
        delta=jnp.sum(p*dp,axis=0,keepdims=True)
        ds=(p*(dp-delta)).astype(jnp.bfloat16)
        dk=nn(ds,q)*scale
        dqt=nn(k.T,ds)*scale
        qs[h]=dqt.T.astype(jnp.bfloat16)
        ks[h]=dk.astype(jnp.bfloat16)
        vs[h]=dv.astype(jnp.bfloat16)
    @pl.when(step==pl.num_programs(0)-1)
    def _():
        for i,r in enumerate((qs,ks,vs)):
            for h in range(HEADS):
                dqkv_ref[:,i*D+h*HEAD_DIM:i*D+(h+1)*HEAD_DIM]=r[h,0:tokens,0:HEAD_DIM]

def attn_bwd(qkv, gmixed, lse, per=1):
    tokens=qkv.shape[0]
    krows=-(-tokens//16)*16; qrows=-(-tokens//128)*128
    return pl.pallas_call(functools.partial(bwd_kernel,tokens,krows,qrows,per),
        grid=(HEADS//per,),
        in_specs=[pl.BlockSpec(qkv.shape,lambda i:(0,0),pipeline_mode=pl.Buffered(1)),pl.BlockSpec(gmixed.shape,lambda i:(0,0),pipeline_mode=pl.Buffered(1)),
                  pl.BlockSpec((per,1,qrows),lambda i:(i,0,0))],
        out_specs=pl.BlockSpec((tokens,3*D),lambda i:(0,0),pipeline_mode=pl.Buffered(1)),
        out_shape=jax.ShapeDtypeStruct((tokens,3*D),jnp.bfloat16),
        scratch_shapes=[pltpu.VMEM((HEADS,qrows,LANES),jnp.bfloat16),pltpu.VMEM((HEADS,krows,LANES),jnp.bfloat16),
                        pltpu.VMEM((HEADS,krows,LANES),jnp.bfloat16),pltpu.VMEM((HEADS,qrows,LANES),jnp.bfloat16)],
        compiler_params=pltpu.CompilerParams(vmem_limit_bytes=56<<20,dimension_semantics=("arbitrary",)),
        cost_estimate=pl.CostEstimate(flops=1000000,bytes_accessed=1000000,transcendentals=0),
        name="attention_backward")(qkv,gmixed,lse)


GELU_A = 0.7978845608028654
GELU_B = 0.044715


PAIR_ROWS = D // HEADS
BLOCK_ROWS = 40


def share_rows(core, value, keep_ref, send_ref):
    for chip in range(value.shape[0] // PAIR_ROWS):
        first = value[chip * PAIR_ROWS : chip * PAIR_ROWS + BLOCK_ROWS]
        last = value[(chip + 1) * PAIR_ROWS - BLOCK_ROWS : (chip + 1) * PAIR_ROWS]
        keep_ref[chip] = jnp.where(core == 0, first, last).astype(jnp.bfloat16)
        send_ref[chip] = jnp.where(core == 0, last, first).astype(jnp.bfloat16)


def mlp_kernel(coords, normed_ref, grad_ref, up_ref, bias_ref, down_ref, xhat_ref, inverse_ref, gain_ref,
               grad_out_ref, mixed_ref, output_ref, out_ref, up_keep_ref, up_send_ref, bias_grad_ref,
               down_grad_ref, sums_ref, resid_grad_ref, output_keep_ref, output_send_ref, mixed_grad_ref,
               normed, normed_t, grad, out, back):
    step = pl.program_id(0)
    tokens = normed_ref.shape[0]

    @pl.when(step == 0)
    def _():
        for held, source in ((normed, normed_ref), (grad, grad_ref)):
            held[...] = jnp.zeros_like(held)
            held[0:tokens] = source[...]
        normed_t[...] = normed[...].T
        out[...] = jnp.zeros_like(out)
        back[...] = jnp.zeros_like(back)

    pre = nn(normed[...], up_ref[...]) + bias_ref[...]
    square = pre * pre
    bend = jnp.tanh(pre * (GELU_A + GELU_A * GELU_B * square))
    hidden = (0.5 * pre * (1.0 + bend)).astype(jnp.bfloat16)
    slope = 0.5 * (1.0 + bend) + 0.5 * pre * (1.0 - bend * bend) * (
        GELU_A + 3.0 * GELU_A * GELU_B * square
    )
    grad_pre = (nt(grad[...], down_ref[...]) * slope).astype(jnp.bfloat16)
    out[...] += nn(hidden, down_ref[...])
    back[...] += nt(grad_pre, up_ref[...])
    down_grad_ref[...] = nn(hidden.T, grad[...]).astype(jnp.bfloat16)
    share_rows(coords[0], nn(normed_t[...], grad_pre), up_keep_ref, up_send_ref)
    bias_grad_ref[...] = jnp.sum(grad_pre.astype(jnp.float32), axis=0, keepdims=True)

    @pl.when(step == pl.num_programs(0) - 1)
    def _():
        out_ref[...] = out[0:tokens]
        total = back[0:tokens]
        xhat = xhat_ref[...]
        sums_ref[0:1] = jnp.sum(total * xhat, axis=0, keepdims=True)
        sums_ref[1:2] = jnp.sum(total, axis=0, keepdims=True)
        scaled = total * gain_ref[...]
        first = jnp.mean(scaled, axis=-1, keepdims=True)
        second = jnp.mean(scaled * xhat, axis=-1, keepdims=True)
        resid_grad = grad_out_ref[...] + inverse_ref[...] * (scaled - first - xhat * second)
        resid_grad_ref[...] = resid_grad
        grad[0:tokens] = resid_grad.astype(jnp.bfloat16)
        low = grad[...]
        sums_ref[2:3] = jnp.sum(low.astype(jnp.float32), axis=0, keepdims=True)
        mixed_grad_ref[...] = nt(low, output_ref[...]).astype(jnp.bfloat16)[0:tokens]
        normed[0:tokens] = mixed_ref[...]
        normed_t[...] = normed[...].T
        share_rows(coords[0], nn(normed_t[...], low), output_keep_ref, output_send_ref)


def whole_block(shape):
    return pl.BlockSpec(shape, lambda i: (0, 0), pipeline_mode=pl.Buffered(1))


def mlp(coords, normed, grad, up, bias, down, xhat, inverse, gain, grad_out, mixed, output):
    tokens, hidden = normed.shape[0], up.shape[1]
    rows = -(-tokens // 16) * 16
    tile = 256
    full = whole_block((tokens, D))
    columns = pl.BlockSpec((D, tile), lambda i: (0, i))
    line = pl.BlockSpec((1, tile), lambda i: (0, i))
    band = pl.BlockSpec((tile, D), lambda i: (i, 0))
    square = whole_block((D, D))
    shares = (D // PAIR_ROWS, BLOCK_ROWS)
    part = pl.BlockSpec(shares + (tile,), lambda i: (0, 0, i))
    full_part = pl.BlockSpec(
        shares + (D,), lambda i: (0, 0, 0), pipeline_mode=pl.Buffered(1)
    )
    return pl.pallas_call(
        mlp_kernel,
        grid=(hidden // tile,),
        in_specs=[pl.BlockSpec(memory_space=pltpu.SMEM), full, full, columns, line, band, full, whole_block((tokens, 1)),
                  whole_block((1, D)), full, full, square],
        out_specs=[full, part, part, line, band, whole_block((8, D)), full, full_part, full_part,
                   full],
        out_shape=[
            jax.ShapeDtypeStruct((tokens, D), jnp.float32),
            jax.ShapeDtypeStruct(shares + (hidden,), jnp.bfloat16),
            jax.ShapeDtypeStruct(shares + (hidden,), jnp.bfloat16),
            jax.ShapeDtypeStruct((1, hidden), jnp.float32),
            jax.ShapeDtypeStruct((hidden, D), jnp.bfloat16),
            jax.ShapeDtypeStruct((8, D), jnp.float32),
            jax.ShapeDtypeStruct((tokens, D), jnp.float32),
            jax.ShapeDtypeStruct(shares + (D,), jnp.bfloat16),
            jax.ShapeDtypeStruct(shares + (D,), jnp.bfloat16),
            jax.ShapeDtypeStruct((tokens, D), jnp.bfloat16),
        ],
        scratch_shapes=[
            pltpu.VMEM((rows, D), jnp.bfloat16),
            pltpu.VMEM((D, rows), jnp.bfloat16),
            pltpu.VMEM((rows, D), jnp.bfloat16),
            pltpu.VMEM((rows, D), jnp.float32),
            pltpu.VMEM((rows, D), jnp.float32),
        ],
        compiler_params=pltpu.CompilerParams(
            vmem_limit_bytes=56 << 20, dimension_semantics=("arbitrary",)
        ),
        cost_estimate=pl.CostEstimate(flops=1000000, bytes_accessed=1000000, transcendentals=0),
        name="mlp_forward_backward",
    )(coords, normed, grad, up, bias, down, xhat, inverse, gain, grad_out, mixed, output)


def qkv_back_kernel(coords, grad_ref, normed_ref, weight_ref, xhat_ref, inverse_ref, gain_ref, resid_ref,
                    keep_ref, send_ref, bias_grad_ref, sums_ref, tokens_ref, grad, normed_t, total):
    step = pl.program_id(0)
    tokens = normed_ref.shape[0]

    @pl.when(step == 0)
    def _():
        grad[...] = jnp.zeros_like(grad)
        grad[0:tokens] = normed_ref[...]
        normed_t[...] = grad[...].T
        grad[...] = jnp.zeros_like(grad)
        total[...] = jnp.zeros_like(total)

    grad[0:tokens] = grad_ref[...]
    share_rows(coords[0], nn(normed_t[...], grad[...]), keep_ref, send_ref)
    bias_grad_ref[...] = jnp.sum(grad[...].astype(jnp.float32), axis=0, keepdims=True)
    total[...] += nt(grad[...], weight_ref[...])

    @pl.when(step == pl.num_programs(0) - 1)
    def _():
        back = total[0:tokens]
        xhat = xhat_ref[...]
        sums_ref[0:1] = jnp.sum(back * xhat, axis=0, keepdims=True)
        sums_ref[1:2] = jnp.sum(back, axis=0, keepdims=True)
        scaled = back * gain_ref[...]
        first = jnp.mean(scaled, axis=-1, keepdims=True)
        second = jnp.mean(scaled * xhat, axis=-1, keepdims=True)
        tokens_ref[...] = resid_ref[...] + inverse_ref[...] * (scaled - first - xhat * second)


def qkv_back(coords, grad, normed, weight, xhat, inverse, gain, resid):
    tokens = normed.shape[0]
    rows = -(-tokens // 16) * 16
    whole = lambda shape: pl.BlockSpec(shape, lambda i: (0, 0), pipeline_mode=pl.Buffered(1))
    part = lambda shape: pl.BlockSpec(shape, lambda i: (0, i))
    shares = (D // PAIR_ROWS, BLOCK_ROWS)
    share = pl.BlockSpec(shares + (D,), lambda i: (0, 0, i))
    return pl.pallas_call(
        qkv_back_kernel,
        grid=(3,),
        in_specs=[
            pl.BlockSpec(memory_space=pltpu.SMEM),
            part((tokens, D)),
            whole((tokens, D)),
            part((D, D)),
            whole((tokens, D)),
            whole((tokens, 1)),
            whole((1, D)),
            whole((tokens, D)),
        ],
        out_specs=[share, share, part((1, D)), whole((8, D)), whole((tokens, D))],
        out_shape=[
            jax.ShapeDtypeStruct(shares + (3 * D,), jnp.bfloat16),
            jax.ShapeDtypeStruct(shares + (3 * D,), jnp.bfloat16),
            jax.ShapeDtypeStruct((1, 3 * D), jnp.float32),
            jax.ShapeDtypeStruct((8, D), jnp.float32),
            jax.ShapeDtypeStruct((tokens, D), jnp.float32),
        ],
        scratch_shapes=[
            pltpu.VMEM((rows, D), jnp.bfloat16),
            pltpu.VMEM((D, rows), jnp.bfloat16),
            pltpu.VMEM((rows, D), jnp.float32),
        ],
        compiler_params=pltpu.CompilerParams(
            vmem_limit_bytes=56 << 20, dimension_semantics=("arbitrary",)
        ),
        cost_estimate=pl.CostEstimate(flops=1000000, bytes_accessed=1000000, transcendentals=0),
        name="qkv_backward",
    )(coords, grad, normed, weight, xhat, inverse, gain, resid)


FF = 4304
GROUPS = 16
FF_GROUP = FF // GROUPS
FF_ROWS = 272
FF_PAD = GROUPS * FF_ROWS
HALF_DOWN = FF_ROWS // 2
OWN_ROWS = PAIR_ROWS // 2
TILE = 8
BLOCK_TILES = 5
PAIR_TILES = PAIR_ROWS // TILE
EXTRA = 128
QKV_CUT = 14 * 128
UP_CUT = 22 * 128
UP_PIECES = 4
DOWN_CUT = 40
DOWN_FIRST = 64
REST_ROWS = UP_PIECES * BLOCK_TILES * TILE + BLOCK_TILES * TILE + DOWN_FIRST
VECTORS = (0, 1, 3, 6, 8, 9, 10, 14, 12)
bf16 = jnp.bfloat16
f32 = jnp.float32


def product(left, right):
    return jnp.dot(left, right, preferred_element_type=f32)


def product_t(left, right):
    return lax.dot_general(left, right, (((0,), (0,)), ((), ())), preferred_element_type=f32)


def product_bt(left, right):
    return lax.dot_general(left, right, (((1,), (1,)), ((), ())), preferred_element_type=f32)


def swap(value, mask):
    devices = lax.axis_size("fsdp")
    return lax.ppermute(value, "fsdp", [(i, i ^ mask) for i in range(devices)])


def pad_hidden(columns):
    rows = columns.shape[0]
    grouped = columns.reshape(rows, GROUPS, FF_GROUP)
    return jnp.pad(grouped, ((0, 0), (0, 0), (0, FF_ROWS - FF_GROUP))).reshape(rows, FF_PAD)


def trim_hidden(columns):
    rows = columns.shape[0]
    return columns.reshape(rows, GROUPS, FF_ROWS)[:, :, :FF_GROUP].reshape(rows, FF)


def place_square_kernel(coords, *refs):
    sources, (whole, small) = refs[:8], refs[8:10]
    held, in_sems, out_sems = refs[10:18], refs[18], refs[19]
    core, x, y, z = coords[0], coords[1], coords[2], coords[3]
    arrivals = [pltpu.make_async_copy(sources[i], held[i], in_sems.at[i]) for i in range(8)]
    for arrival in arrivals:
        arrival.start()
    copies, extras = [], []
    for part, stream in itertools.product(range(4), range(2)):
        arrivals[4 * stream + part].wait()
        for near, dz in itertools.product(range(2), range(4)):
            src = held[4 * stream + part].at[near * 4 + dz]
            owner = core if part < 2 else 1 - core
            far = part % 2
            dx, dy = (near, far) if stream == 0 else (far, near)
            chip = ((z ^ dz) * 2 + (y ^ dy)) * 2 + (x ^ dx)
            cols = src.shape[-1] - (0 if stream else EXTRA)
            col = QKV_CUT - EXTRA if stream else 0
            src_cols = pl.ds(0 if stream else EXTRA, cols)
            first = PAIR_TILES * chip + BLOCK_TILES * owner
            copies.append(
                pltpu.make_async_copy(
                    src.at[pl.ds(owner, BLOCK_TILES - 1), :, src_cols],
                    whole.at[pl.ds(first, BLOCK_TILES - 1), :, pl.ds(col, cols)],
                    out_sems.at[len(copies)],
                )
            )
            copies[-1].start()
            extra = pltpu.make_async_copy(
                src.at[BLOCK_TILES - 1, :, src_cols],
                whole.at[PAIR_TILES * chip + BLOCK_TILES - 1, :, pl.ds(col, cols)],
                out_sems.at[96 + len(extras)],
            )
            pl.when(owner == 0)(extra.start)
            extras.append((owner, extra))
            if stream == 0:
                copies.append(
                    pltpu.make_async_copy(
                        src.at[:, :, :EXTRA], small.at[chip * 2 + owner], out_sems.at[len(copies)]
                    )
                )
                copies[-1].start()
    for copy in copies:
        copy.wait()
    for owner, extra in extras:
        pl.when(owner == 0)(extra.wait)


def place_square(streams, coords):
    sources = [s.reshape(8, BLOCK_TILES, TILE, -1) for s in (*streams[0], *streams[1])]
    size = sum(s.size for s in sources) * 2
    whole, small = pl.pallas_call(
        place_square_kernel,
        in_specs=[pl.BlockSpec(memory_space=pltpu.SMEM)]
        + [pl.BlockSpec(memory_space=pltpu.HBM)] * 8,
        out_specs=[pl.BlockSpec(memory_space=pltpu.HBM)] * 2,
        out_shape=[
            jax.ShapeDtypeStruct((GROUPS * PAIR_TILES, TILE, 3 * D), bf16),
            jax.ShapeDtypeStruct((2 * GROUPS, BLOCK_TILES, TILE, EXTRA), bf16),
        ],
        scratch_shapes=[pltpu.VMEM(s.shape, bf16) for s in sources]
        + [pltpu.SemaphoreType.DMA((8,)), pltpu.SemaphoreType.DMA((160,))],
        compiler_params=pltpu.CompilerParams(vmem_limit_bytes=40 << 20),
        cost_estimate=pl.CostEstimate(flops=0, bytes_accessed=2 * size, transcendentals=0),
        name="place_square",
    )(coords, *sources)
    return whole.reshape(D, 3 * D), small.reshape(2 * GROUPS, -1)


def place_rest_kernel(coords, *refs):
    source, streams, (up, out, down) = refs[0], refs[1:9], refs[9:12]
    held, in_sems, out_sems = refs[12], refs[13], refs[14]
    parts, part_sems = refs[15:23], refs[23]
    core, x, y, z = coords[0], coords[1], coords[2], coords[3]
    arrivals = [
        pltpu.make_async_copy(source.at[i], held.at[i], in_sems.at[i]) for i in range(2 * GROUPS)
    ]
    others = [pltpu.make_async_copy(streams[i], parts[i], part_sems.at[i]) for i in range(8)]
    for arrival in arrivals + others:
        arrival.start()
    copies = []

    def move(one, other):
        copies.append(pltpu.make_async_copy(one, other, out_sems.at[len(copies)]))
        copies[-1].start()

    lead = DOWN_FIRST // TILE
    for device in range(2 * GROUPS):
        chip, owner = device // 2, device % 2
        src = held.at[device]
        arrivals[device].wait()
        count = BLOCK_TILES - owner
        first = PAIR_TILES * chip + BLOCK_TILES * owner
        for piece in range(UP_PIECES):
            cols = min(D, FF_PAD - piece * D)
            move(
                src.at[pl.ds(piece * BLOCK_TILES + owner, count), :, pl.ds(0, cols)],
                up.at[pl.ds(first, count), :, pl.ds(piece * D, cols)],
            )
        base = UP_PIECES * BLOCK_TILES
        move(src.at[pl.ds(base + owner, count)], out.at[pl.ds(first, count)])
        move(src.at[pl.ds(base + BLOCK_TILES, lead)], down.at[device, pl.ds(0, lead)])
    for part, stream in itertools.product(range(4), range(2)):
        others[4 * stream + part].wait()
        for near, dz in itertools.product(range(2), range(4)):
            src = parts[4 * stream + part].at[near * 4 + dz]
            owner = core if part < 2 else 1 - core
            far = part % 2
            dx, dy = (near, far) if stream == 0 else (far, near)
            chip = ((z ^ dz) * 2 + (y ^ dy)) * 2 + (x ^ dx)
            first = lead + (DOWN_CUT // TILE if stream else 0)
            move(src, down.at[chip * 2 + owner, pl.ds(first, src.shape[0])])
    for copy in copies:
        copy.wait()


def place_rest(gathered, streams, coords):
    source = gathered.reshape(2 * GROUPS, REST_ROWS // TILE, TILE, D)
    sources = [s.reshape(8, -1, TILE, D) for s in (*streams[0], *streams[1])]
    up, out, down = pl.pallas_call(
        place_rest_kernel,
        in_specs=[pl.BlockSpec(memory_space=pltpu.SMEM)]
        + [pl.BlockSpec(memory_space=pltpu.HBM)] * 9,
        out_specs=[pl.BlockSpec(memory_space=pltpu.HBM)] * 3,
        out_shape=[
            jax.ShapeDtypeStruct((D // TILE, TILE, FF_PAD), bf16),
            jax.ShapeDtypeStruct((D // TILE, TILE, D), bf16),
            jax.ShapeDtypeStruct((2 * GROUPS, HALF_DOWN // TILE, TILE, D), bf16),
        ],
        scratch_shapes=[
            pltpu.VMEM(source.shape, bf16),
            pltpu.SemaphoreType.DMA((2 * GROUPS,)),
            pltpu.SemaphoreType.DMA((2 * GROUPS * (UP_PIECES + 2) + 64,)),
        ]
        + [pltpu.VMEM(s.shape, bf16) for s in sources]
        + [pltpu.SemaphoreType.DMA((8,))],
        compiler_params=pltpu.CompilerParams(vmem_limit_bytes=60 << 20),
        cost_estimate=pl.CostEstimate(
            flops=0, bytes_accessed=4 * source.size, transcendentals=0
        ),
        name="place_rest",
    )(coords, source, *sources)
    return up.reshape(D, FF_PAD), out.reshape(D, D), down.reshape(FF_PAD, D)


def tie(*values):
    leaves, form = jax.tree.flatten(values)
    return form.unflatten(lax.optimization_barrier(leaves))


def gather_z(block):
    return [block] + [swap(block, 8 * step) for step in (1, 2, 3)]


def gather_near(parts, cut, axis):
    streams = []
    for stream in range(2):
        if axis == 1:
            own = jnp.stack([p[:, :cut] if stream == 0 else p[:, cut:] for p in parts])
        else:
            own = jnp.stack([p[:cut] if stream == 0 else p[cut:] for p in parts])
        streams.append((own, swap(own, 4 if stream else 2)))
    return streams


def gather_far(streams):
    results = []
    for stream in range(2):
        first = jnp.concatenate(streams[stream])
        results.append((first, swap(first, 2 if stream else 4)))
    return results


def gather_core(streams):
    return [(first, second, swap(first, 1), swap(second, 1)) for first, second in streams]


def window(value, starts, sizes):
    rank = value.ndim
    starts = list(starts) + [0] * (rank - len(starts))
    lengths = list(value.shape)
    for axis, size in enumerate(sizes):
        if size is not None:
            lengths[axis] = size
    starts = [jnp.int32(0) if start is None else jnp.int32(start) for start in starts]
    result = lax.dynamic_slice(value, starts, lengths)
    kept = [
        length for axis, length in enumerate(lengths) if axis >= len(sizes) or sizes[axis] != 1
    ]
    return result.reshape(kept)


class Reduction:
    def __init__(self, keeps, streams, coords):
        self.keeps = [k.reshape(4, 2, 2, BLOCK_TILES, TILE, -1) for k in keeps]
        self.streams = streams
        self.coords = coords

    def part(self, arrays, stream, plane):
        sizes = tuple(None if p is None else 1 for p in plane) + (None, None)
        pieces = []
        for number, first, last in self.streams[stream]:
            starts = tuple(plane) + (None, None, first)
            pieces.append(window(arrays[number], starts, sizes + (last - first,)))
        return pieces[0] if len(pieces) == 1 else jnp.concatenate(pieces, axis=-1)

    def terms(self, stream, plane):
        return [self.part(self.keeps, stream, plane), self.part(self.other, stream, plane)]

    def core_step(self, sends):
        return [swap(send.reshape(4, 2, 2, BLOCK_TILES, TILE, -1), 1) for send in sends]

    def far_sends(self, other, streams=(0, 1), pieces=slice(None)):
        core, x, y, z = self.coords
        self.other = other
        sends = []
        every = self.streams
        for stream in streams:
            plane = (None, None, 1 - x) if stream else (None, 1 - y, None)
            self.streams = {stream: every[stream][pieces]}
            sends.append(total_of(self.terms(stream, plane)).astype(bf16))
        self.streams = every
        return sends

    def far_swap(self, sends):
        return [swap(send, 2 if stream else 4) for stream, send in enumerate(sends)]

    def near_sends(self, far):
        core, x, y, z = self.coords
        self.far = far
        sends = []
        for stream in range(2):
            plane = (None, 1 - y, x) if stream else (None, y, 1 - x)
            after = (None, 1 - y) if stream else (None, 1 - x)
            terms = self.terms(stream, plane) + [window(far[stream], after, (None, 1))]
            sends.append(total_of(terms).astype(bf16))
        return sends

    def near_swap(self, sends):
        return [swap(send, 4 if stream else 2) for stream, send in enumerate(sends)]

    def at(self, plane):
        core, x, y, z = self.coords
        pieces = []
        for stream in range(2):
            after = (plane, y) if stream else (plane, x)
            terms = self.terms(stream, (plane, y, x)) + [
                window(self.far[stream], after, (1, 1)),
                window(self.near[stream], (plane,), (1,)),
            ]
            pieces.append(total_of(terms))
        return jnp.concatenate(pieces, axis=-1)

    def z_sends(self, near):
        z = self.coords[3]
        self.near = near
        return [self.at(z ^ step).astype(bf16) for step in (1, 2, 3)]

    def z_swap(self, sends):
        return [swap(send, 8 * step) for step, send in zip((1, 2, 3), sends)]

    def finish(self, arrived):
        core, x, y, z = self.coords
        total = total_of([self.at(z)] + arrived)
        total = total.reshape(BLOCK_TILES * TILE, -1)
        return lax.dynamic_slice_in_dim(
            total, core * (BLOCK_TILES * TILE - OWN_ROWS), OWN_ROWS, 0
        )


def join_rows(keep, send):
    whole = jnp.concatenate([keep, send[:, 2 * BLOCK_ROWS - PAIR_ROWS :]], axis=1)
    return whole.reshape(D, -1)


def total_of(terms):
    total = terms[0].astype(f32)
    for term in terms[1:]:
        total = total + term.astype(f32)
    return total


def fetch_pairs(narrow, core):
    q, k, v, o = (narrow[i].reshape(OWN_ROWS, D) for i in (2, 4, 5, 7))
    up = pad_hidden(narrow[11].reshape(OWN_ROWS, FF))
    down = narrow[13]
    rows = jnp.concatenate([q, k, v, o, up], axis=1)
    spare = BLOCK_TILES * TILE - OWN_ROWS
    lead = D * HALF_DOWN - down.shape[0]
    tail = jnp.pad(down[:lead].reshape(spare, -1), ((0, 0), (0, 512 - lead // spare)))
    is_first = core == 0
    edge = jnp.where(is_first, rows[OWN_ROWS - spare :], rows[:spare])
    got = swap(jnp.concatenate([edge, tail], axis=1), 1)
    edge = got[:, : rows.shape[1]]
    block = jnp.where(is_first, jnp.concatenate([rows, edge]), jnp.concatenate([edge, rows]))
    extra = got[:, rows.shape[1] : rows.shape[1] + lead // spare].reshape(-1)
    end = jnp.zeros((D * HALF_DOWN - (down.shape[0] - lead),), bf16)
    down_block = jnp.where(
        is_first, jnp.concatenate([down, extra]), jnp.concatenate([down[lead:], end])
    ).reshape(HALF_DOWN, D)
    small = jnp.concatenate([narrow[i] for i in VECTORS])
    small = jnp.pad(small, (0, BLOCK_TILES * TILE * EXTRA - small.shape[0]))
    small = small.reshape(BLOCK_TILES * TILE, EXTRA)
    square = jnp.concatenate([small, block[:, : 3 * D]], axis=1)
    up_block = jnp.pad(block[:, 4 * D :], ((0, 0), (0, UP_PIECES * D - FF_PAD)))
    pieces = [up_block[:, i * D : (i + 1) * D] for i in range(UP_PIECES)]
    rest = jnp.concatenate(pieces + [block[:, 3 * D : 4 * D], down_block[:DOWN_FIRST]])
    return square, rest, down_block[DOWN_FIRST:]


def normalize(values):
    centre = jnp.mean(values, axis=-1, keepdims=True)
    centered = values - centre
    spread_sq = jnp.mean(centered * centered, axis=-1, keepdims=True)
    inverse = lax.rsqrt(spread_sq + 1e-06)
    return centered * inverse, inverse


def normalize_back(grad, gain, xhat, inverse):
    scaled = grad * gain
    first = jnp.mean(scaled, axis=-1, keepdims=True)
    second = jnp.mean(scaled * xhat, axis=-1, keepdims=True)
    return inverse * (scaled - first - xhat * second)


def name_vectors(whole, widths):
    count = len(VECTORS) - 1
    width = widths[VECTORS[0]]
    pieces = whole[:, : count * width].reshape(-1, count, width)
    pieces = pieces.transpose(1, 0, 2).reshape(count, -1).astype(f32)
    found = {i: pieces[position : position + 1] for position, i in enumerate(VECTORS[:-1])}
    last = widths[VECTORS[-1]]
    found[VECTORS[-1]] = whole[:, count * width : count * width + last].reshape(-1).astype(f32)
    return found


def pack_vectors(vectors, width, devices):
    rows = jnp.stack(vectors)
    rows = jnp.pad(rows, ((0, 0), (0, width * devices - rows.shape[1])))
    rows = rows.reshape(len(vectors), devices, width)
    return rows.transpose(1, 0, 2).reshape(devices, -1)


def gather_plain(narrow, widths):
    whole = {
        i: lax.all_gather(narrow[i], "fsdp", axis=0, tiled=True) for i in (2, 4, 5, 7, 11, 13)
    }
    square = [whole[i][: D * D].reshape(D, D) for i in (2, 4, 5, 7)]
    up = pad_hidden(whole[11][: D * FF].reshape(D, FF))
    down = pad_hidden(whole[13][: D * FF].reshape(FF, D).T).T
    joined = jnp.concatenate([narrow[i] for i in VECTORS])
    length = joined.shape[0]
    joined = jnp.pad(joined, (0, 2048 - length)).reshape(16, 128)
    joined = lax.all_gather(joined, "fsdp", axis=0, tiled=True).reshape(-1, 2048)
    return jnp.concatenate(square[:3], axis=1), square[3], up, down, name_vectors(joined, widths)


def on_device(*args):
    devices = lax.axis_size("fsdp")
    tokens, image_valid = args[0], args[1]
    shards = args[2:17]
    cotangent = args[17]
    staged = devices == 32
    widths = [piece.shape[0] for piece in shards]
    narrow = [piece.astype(bf16) for piece in shards]
    index = lax.axis_index("fsdp")
    core, x, y, z = index % 2, (index // 2) % 2, (index // 4) % 2, index // 8
    coords = (core, x, y, z)
    image_count = image_valid.shape[0]
    seq_len = tokens.shape[0] // image_count
    weight_img = jnp.repeat(image_valid.astype(f32), seq_len)[:, None]

    grad_out = weight_img * cotangent
    grad_branch = grad_out.astype(bf16)
    grads = {14: jnp.sum(grad_branch.astype(f32), axis=0)}
    xhat_one, inverse_one = normalize(tokens)
    where = jnp.stack(coords if staged else (jnp.int32(0),) * 4).astype(jnp.int32)
    if staged:
        sq, rest, down = fetch_pairs(narrow, core)
        rest = lax.all_gather(rest, "fsdp", axis=0, tiled=True)
        sq, tokens = tie(sq, tokens)
        sq = gather_z(sq)
        xhat_one, inverse_one = normalize(tokens)
        sq, down, xhat_one, inverse_one, grad_branch = tie(
            sq, down, xhat_one, inverse_one, grad_branch
        )
        sq = gather_near(sq, QKV_CUT, 1)
        down = gather_z(down)
        sq = gather_far(sq)
        sq, down = tie(sq, down)
        sq = gather_core(sq)
        down = gather_near(down, DOWN_CUT, 0)
        weight_qkv, small = place_square(sq, where)
        vectors = name_vectors(small, widths)
    else:
        weight_qkv, weight_o, weight_up, weight_down, vectors = gather_plain(narrow, widths)

    vec = lambda i: vectors[i][:, :D]
    gain_one, shift_one, gain_two, shift_two = vec(0), vec(1), vec(9), vec(10)
    bias_qkv = jnp.concatenate([vec(3), jnp.zeros((1, D), f32), vec(6)], axis=1)
    bias_o, bias_down = vec(8), vec(14)
    bias_up = pad_hidden(vectors[12][:FF].reshape(1, FF))

    normed = (xhat_one * gain_one + shift_one).astype(bf16)
    qkv = (product(normed, weight_qkv) + bias_qkv).astype(bf16)
    if staged:
        qkv, down = tie(qkv, down)
        down = [(*pair, swap(pair[0], 1)) for pair in gather_far(down)]
    mixed, lse = attn_fwd(qkv, 4)
    if staged:
        mixed, lse, down = tie(mixed, lse, down)
        down = [(*parts, swap(parts[1], 1)) for parts in down]
        weight_up, weight_o, weight_down = place_rest(rest, down, where)
    resid = tokens + product(mixed, weight_o) + bias_o
    xhat_two, inverse_two = normalize(resid)
    normed_two = (xhat_two * gain_two + shift_two).astype(bf16)
    (
        branch,
        up_keep,
        up_send,
        up_bias_grad,
        down_grad,
        sums_two,
        grad_resid,
        o_keep,
        o_send,
        grad_mixed,
    ) = mlp(
        where,
        normed_two,
        grad_branch,
        weight_up,
        bias_up,
        weight_down,
        xhat_two,
        inverse_two,
        gain_two.reshape(1, D),
        grad_out,
        mixed,
        weight_o,
    )
    up_bias_grad = up_bias_grad.reshape(FF_PAD)
    layer_out = weight_img * (resid + branch + bias_down)
    grads[9], grads[10], grads[8] = sums_two[0], sums_two[1], sums_two[2]
    hidden_grad = trim_hidden(up_bias_grad.reshape(1, FF_PAD)).reshape(FF)
    early = jnp.concatenate(
        [
            pack_vectors([grads[i] for i in VECTORS[4:8]], widths[0], devices),
            pack_vectors([hidden_grad], widths[12], devices),
        ],
        axis=1,
    )
    if staged:
        down_sum = lax.psum_scatter(down_grad, "fsdp", scatter_dimension=0, tiled=True)
    if staged:
        outer = Reduction(
            (up_keep, o_keep), (((0, 0, UP_CUT),), ((0, UP_CUT, FF_PAD), (1, 0, D))), coords
        )
        outer_other = outer.core_step((up_send, o_send))
        early = early.astype(bf16)
        grad_mixed, outer_other, early = tie(grad_mixed, outer_other, early)
        outer_far = outer.far_swap(outer.far_sends(outer_other))
    grad_qkv = attn_bwd(qkv, grad_mixed, lse, 4)
    if staged:
        grad_qkv, outer_far = tie(grad_qkv, outer_far)
        outer_near = outer.near_sends(outer_far)
        grad_qkv, outer_near = tie(grad_qkv, outer_near)
        outer_near = outer.near_swap(outer_near)
    qkv_keep, qkv_send, qkv_bias_grad, norm_sums, tokens_grad = qkv_back(
        where,
        grad_qkv,
        normed,
        weight_qkv,
        xhat_one,
        inverse_one,
        gain_one.reshape(1, D),
        grad_resid,
    )
    if staged:
        qkv_keep, qkv_send, norm_sums, qkv_bias_grad, outer_near = tie(
            qkv_keep, qkv_send, norm_sums, qkv_bias_grad, outer_near
        )
        outer_z = outer.z_sends(outer_near)
        qkv_other = outer.core_step((qkv_send,))[0]
    grads[3], grads[6] = qkv_bias_grad[0, :D], qkv_bias_grad[0, 2 * D :]
    grads[0], grads[1] = norm_sums[0], norm_sums[1]

    late = [grads[i] for i in VECTORS[:4]]
    rows = jnp.concatenate(
        [pack_vectors(late, widths[0], devices).astype(early.dtype), early], axis=1
    )
    owned = [None] * 15
    if staged:
        rows = jnp.pad(rows, ((0, 0), (0, OWN_ROWS * EXTRA - rows.shape[1])))
        rows = rows.reshape(GROUPS, PAIR_ROWS, EXTRA).astype(bf16)
        top, bottom = rows[:, :BLOCK_ROWS], rows[:, PAIR_ROWS - BLOCK_ROWS :]
        rows_keep = jnp.where(core == 0, top, bottom)
        rows_send = jnp.where(core == 0, bottom, top)
        rows_other = outer.core_step((rows_send,))[0]
        cut = QKV_CUT - EXTRA
        inner = Reduction(
            (qkv_keep, rows_keep), (((0, 0, cut), (1, 0, EXTRA)), ((0, cut, 3 * D),)), coords
        )
        qkv_other, rows_other, outer_z = tie(qkv_other, rows_other, outer_z)
        inner_far = inner.far_swap(inner.far_sends((qkv_other, rows_other)))
        outer_z = outer.z_swap(outer_z)
        inner_far, layer_out = tie(inner_far, layer_out)
        inner_near, outer.near = tie(inner.near_sends(inner_far), outer.near)
        inner_near = inner.near_swap(inner_near)
        outer_sum = outer.finish(outer_z)
        owned[11] = trim_hidden(outer_sum[:, :FF_PAD]).reshape(-1)
        owned[7] = outer_sum[:, FF_PAD:].reshape(-1)
        inner_near, down_sum, owned[11], owned[7] = tie(
            inner_near, down_sum, owned[11], owned[7]
        )
        inner_z = inner.z_sends(inner_near)
        inner_z, down_sum = tie(inner_z, down_sum)
        inner_z = inner.z_swap(inner_z)

        flat = down_sum.astype(f32).reshape(-1)
        size = widths[13]
        lead = flat.shape[0] - size
        got = swap(down_sum.reshape(-1)[size:], 1).astype(f32)
        owned[13] = jnp.where(core == 0, flat[:size], jnp.concatenate([got, flat[: size - lead]]))
        inner_sum = inner.finish(inner_z)
        first = QKV_CUT - EXTRA
        owned[2] = inner_sum[:, :D].reshape(-1)
        owned[4] = jnp.concatenate(
            [inner_sum[:, D:first], inner_sum[:, QKV_CUT : 2 * D + EXTRA]], axis=1
        ).reshape(-1)
        owned[5] = inner_sum[:, 2 * D + EXTRA :].reshape(-1)
        small = inner_sum[:, first:QKV_CUT].reshape(-1)
    else:
        scatter = lambda value: lax.psum_scatter(
            value.astype(f32).reshape(-1), "fsdp", scatter_dimension=0, tiled=True
        )
        fill = lambda value, i: jnp.pad(
            value.reshape(-1), (0, widths[i] * devices - value.size)
        )
        qkv_grad = join_rows(qkv_keep, qkv_send)
        for position, i in enumerate((2, 4, 5)):
            owned[i] = scatter(fill(qkv_grad[:, position * D : (position + 1) * D], i))
        owned[7] = scatter(fill(join_rows(o_keep, o_send), 7))
        owned[11] = scatter(fill(trim_hidden(join_rows(up_keep, up_send)), 11))
        owned[13] = scatter(fill(trim_hidden(down_grad.T).T, 13))
        small = scatter(rows)
    position = 0
    for i in VECTORS:
        owned[i] = small[position : position + widths[i]]
        position += widths[i]
    return (layer_out, tokens_grad, *owned)


def solution(mesh):
    row, flat = P("fsdp", None), P("fsdp")
    in_specs = (row, flat) + (flat,) * 15 + (row,)
    out_specs = (row, row) + (flat,) * 15
    return jax.shard_map(
        on_device, mesh=mesh, in_specs=in_specs, out_specs=out_specs, check_vma=False
    )
```
